32 devices in a mesh: ctx: 16 (over z, y, x), fsdp: 2 (over core).
Axes of the slice: x: 2, y: 2, z: 4, core: 2. Of those that a mesh axis runs over, the one named last changes fastest.
Arguments:
- tokens: bfloat16 [2, 4096, 1024], P('fsdp', 'ctx'), may hold values from -6 to 6
- seg_ids: int32 [2, 4096], P('fsdp', 'ctx'), may hold values from 0 to 3, as said below
- doc_pos: int32 [2, 4096], P('fsdp', 'ctx'), may hold values from 0 to 1999, as said below
- attn_gain: float32 [1024], replicated, may hold values from 0.5 to 1.5
- w_query: bfloat16 [1024, 1024], P('fsdp'), may hold values from -0.1875 to 0.1875
- w_key: bfloat16 [1024, 512], P('fsdp'), may hold values from -0.1875 to 0.1875
- w_value: bfloat16 [1024, 512], P('fsdp'), may hold values from -0.1875 to 0.1875
- query_gain: float32 [64], replicated, may hold values from 1 to 2
- key_gain: float32 [64], replicated, may hold values from 1 to 2
- w_out: bfloat16 [1024, 1024], P('fsdp'), may hold values from -1.5 to 1.5
- ffn_gain: float32 [1024], replicated, may hold values from 0.5 to 1.5
- w_gate: bfloat16 [1024, 4608], P('fsdp'), may hold values from -0.1875 to 0.1875
- w_up: bfloat16 [1024, 4608], P('fsdp'), may hold values from -0.1875 to 0.1875
- w_down: bfloat16 [4608, 1024], P('fsdp'), may hold values from -0.09375 to 0.09375
- d_output: bfloat16 [2, 4096, 1024], P('fsdp', 'ctx'), may hold values from -6 to 6
Outputs:
- output: bfloat16 [2, 4096, 1024], P('fsdp', 'ctx')
- d_tokens: float32 [2, 4096, 1024], P('fsdp', 'ctx')
- d_attn_gain: float32 [1024], replicated
- d_w_query: float32 [1024, 1024], P('fsdp', 'ctx')
- d_w_key: float32 [1024, 512], P('fsdp', 'ctx')
- d_w_value: float32 [1024, 512], P('fsdp', 'ctx')
- d_query_gain: float32 [64], replicated
- d_key_gain: float32 [64], replicated
- d_w_out: float32 [1024, 1024], P('fsdp', 'ctx')
- d_ffn_gain: float32 [1024], replicated
- d_w_gate: float32 [1024, 4608], P('fsdp', 'ctx')
- d_w_up: float32 [1024, 4608], P('fsdp', 'ctx')
- d_w_down: float32 [4608, 1024], P('fsdp', 'ctx')
The draws below stay inside these ranges and needn't reach their ends.
Inputs may be any that keep to these rules, and one draw needn't show every extreme that they name: `seg_ids`: within each sequence the ids start at 0 and never fall; each run of equal ids is a document of 1 to 2000 tokens, every sequence begins with a document of exactly 2000 tokens, and every sequence holds 4 documents. `doc_pos`: the token's place within its document: 0 at the first token of each run of equal seg_ids, rising by one along it.
All inputs are finite; a program needn't handle non-finite values.
Results may differ from the reference program's by a relative error of at most 0.015.
The reference program's roundings to bfloat16 on the way count: a program that leaves them out, or rounds other values in their place, can miss the bound.
Values may be sent and summed in bfloat16 or wider, within the bound.
A program may use at most 320 MiB of HBM per device.

```python
import jax
import jax.numpy as jnp
from jax import lax

D = 1024
HEADS = 16
KV_HEADS = 8
HEAD_DIM = 64
FF = 4608
DOC_MAX = 2000
DOC_MIN = 200
SEQS = 2
SEQ_LEN = 4096


def documents(key):
    doc_key = jax.random.fold_in(key, 101)
    slot_count = (SEQ_LEN + DOC_MAX - 1) // DOC_MAX

    def one_row(row_key):
        cuts = jax.random.randint(row_key, (slot_count,), DOC_MIN, DOC_MAX - DOC_MIN + 1)
        slot_ids = jnp.arange(slot_count)
        cuts = jnp.where((slot_ids == 0) | (slot_ids == slot_count - 1), DOC_MAX, cuts)
        places = jnp.arange(SEQ_LEN)
        slot_of = places // DOC_MAX
        offset = places % DOC_MAX
        cut_here = jnp.take(cuts, slot_of)
        after_cut = (offset >= cut_here).astype(jnp.int32)
        first_id = jnp.maximum(2 * slot_of - 1, 0)
        seg_out = first_id + after_cut
        pos_out = offset - after_cut * cut_here
        return (seg_out.astype(jnp.int32), pos_out.astype(jnp.int32))
    return jax.vmap(one_row)(jax.random.split(doc_key, SEQS))


def draw_seg_ids(key, part):
    return documents(key)[0]


def draw_doc_pos(key, part):
    return documents(key)[1]


def steps_of(stream_key, shape, shards, low, top_value):
    level, own = 1.0, jax.random.fold_in(stream_key, 6)
    for dim, shards_of in shards:
        heights = jnp.exp(jax.random.uniform(jax.random.fold_in(own, dim), (shards_of,), jnp.float32, low / len(shards), top_value / len(shards)))
        level = level * jnp.repeat(heights, shape[dim] // shards_of).reshape([-1 if axis == dim else 1 for axis in range(len(shape))])
    return level


def normal_values(own_key, extent, deviation, most, cuts=(), kind=jnp.bfloat16):
    entries = jax.random.normal(own_key, extent, jnp.float32) * deviation
    if len(cuts) > 0:
        entries = steps_of(own_key, extent, cuts, -0.22, 0.18) * entries
    return jnp.clip(entries, min=-most, max=most).astype(kind)


def setup_inputs(seed: int = 0) -> dict:
    splits = jax.random.split(jax.random.key(seed), 16)
    tokens = normal_values(splits[0], (SEQS, SEQ_LEN, D), 1.0, 6.0, ((0, 2), (1, 16)))
    seg_ids = draw_seg_ids(jax.random.fold_in(splits[15], 71), 0)
    doc_pos = draw_doc_pos(jax.random.fold_in(splits[15], 71), 0)
    attn_gain = jnp.clip(1.0 + 0.1 * jax.random.normal(splits[3], (D,), jnp.float32), 0.5, 1.5)
    w_query = normal_values(splits[4], (D, HEADS * HEAD_DIM), D ** -0.5, 0.1875, ((0, 2),))
    w_key = normal_values(splits[5], (D, KV_HEADS * HEAD_DIM), D ** -0.5, 0.1875, ((0, 2),))
    w_value = normal_values(splits[6], (D, KV_HEADS * HEAD_DIM), D ** -0.5, 0.1875, ((0, 2),))
    query_gain = jnp.clip(jax.random.uniform(splits[7], (HEAD_DIM,), jnp.float32, 1.0, 2.0), 1.0, 2.0)
    key_gain = jnp.clip(jax.random.uniform(splits[8], (HEAD_DIM,), jnp.float32, 1.0, 2.0), 1.0, 2.0)
    w_out = normal_values(splits[9], (HEADS * HEAD_DIM, D), (HEADS * HEAD_DIM // 64) ** -0.5, 1.5, ((0, 2),))
    ffn_gain = jnp.clip(1.0 + 0.1 * jax.random.normal(splits[10], (D,), jnp.float32), 0.5, 1.5)
    w_gate = normal_values(splits[11], (D, FF), D ** -0.5, 0.1875, ((0, 2),))
    w_up = normal_values(splits[12], (D, FF), D ** -0.5, 0.1875, ((0, 2),))
    w_down = normal_values(splits[13], (FF, D), FF ** -0.5, 0.09375, ((0, 2),))
    d_output = normal_values(splits[14], (SEQS, SEQ_LEN, D), 1.0, 6.0, ((0, 2), (1, 16)))
    return {"tokens": tokens, "seg_ids": seg_ids, "doc_pos": doc_pos, "attn_gain": attn_gain, "w_query": w_query, "w_key": w_key, "w_value": w_value, "query_gain": query_gain, "key_gain": key_gain, "w_out": w_out, "ffn_gain": ffn_gain, "w_gate": w_gate, "w_up": w_up, "w_down": w_down, "d_output": d_output}


@jax.custom_vjp
def low(v):
    return lax.optimization_barrier(v.astype(jnp.bfloat16)).astype(jnp.float32)

@jax.custom_vjp
def low_back(v):
    return v

def low_keep(v):
    return (low(v), None)

def low_pass(kept, grad):
    return (grad,)

def back_keep(v):
    return (v, None)

def back_low(kept, grad):
    return (low(grad),)
low.defvjp(low_keep, low_pass)
low_back.defvjp(back_keep, back_low)
PRECISE = lax.Precision.HIGHEST
EPSILON = 1e-05
THETA = 1000000.0
MASKED = -1e+30

def matmul(left_mat, right_mat):
    return jnp.dot(left_mat, right_mat, precision=PRECISE, preferred_element_type=jnp.float32)

def rms_norm(values, norm_gain):
    return values * lax.rsqrt(lax.optimization_barrier(jnp.mean(values * values, axis=-1, keepdims=True)) + EPSILON) * norm_gain

def rotary(values, positions, turn_sign):
    half_dim = values.shape[-1] // 2
    inverse_freq = THETA ** (-(2.0 / values.shape[-1]) * jnp.arange(half_dim, dtype=jnp.float32))
    angles = positions.astype(jnp.float32)[:, None] * inverse_freq[None, :]
    cosine = jnp.cos(angles)[:, None, :]
    sine_part = turn_sign * jnp.sin(angles)[:, None, :]
    first_half = values[..., :half_dim]
    second_half = values[..., half_dim:]
    return jnp.concatenate([first_half * cosine - second_half * sine_part, second_half * cosine + first_half * sine_part], axis=-1)

def attend(queries, key_heads, values, seg_row):
    length = queries.shape[0]
    block_rows = min(512, length)
    pad_len = (DOC_MAX - 1 + 127) // 128 * 128
    q_per_kv = HEADS // KV_HEADS
    score_scale = HEAD_DIM ** (-0.5)
    keys_pad = jnp.concatenate([jnp.zeros((pad_len, KV_HEADS, HEAD_DIM), jnp.float32), key_heads], axis=0)
    values_pad = jnp.concatenate([jnp.zeros((pad_len, KV_HEADS, HEAD_DIM), jnp.float32), values], axis=0)
    seg_pad = jnp.concatenate([jnp.full((pad_len,), -1, jnp.int32), seg_row.astype(jnp.int32)], axis=0)
    index_pad = jnp.arange(-pad_len, length, dtype=jnp.int32)

    def one_block(block_index):
        block_start = (block_index * block_rows).astype(jnp.int32)
        q_block = lax.dynamic_slice_in_dim(queries, block_start, block_rows, 0)
        q_block = q_block.reshape(block_rows, KV_HEADS, q_per_kv, HEAD_DIM)
        k_block = lax.dynamic_slice_in_dim(keys_pad, block_start, block_rows + pad_len, 0)
        v_block = lax.dynamic_slice_in_dim(values_pad, block_start, block_rows + pad_len, 0)
        seg_key = lax.dynamic_slice_in_dim(seg_pad, block_start, block_rows + pad_len, 0)
        idx_key = lax.dynamic_slice_in_dim(index_pad, block_start, block_rows + pad_len, 0)
        seg_query = lax.dynamic_slice_in_dim(seg_row.astype(jnp.int32), block_start, block_rows, 0)
        idx_query = block_start + jnp.arange(block_rows, dtype=jnp.int32)
        scores = low_back(jnp.einsum('qgrd,kgd->grqk', q_block, k_block, precision=PRECISE) * score_scale)
        allowed = (seg_query[:, None] == seg_key[None, :]) & (idx_key[None, :] <= idx_query[:, None])
        scores = jnp.where(allowed[None, None], scores, MASKED)
        attn_probs = low(jax.nn.softmax(scores, axis=-1))
        mixed = jnp.einsum('grqk,kgd->qgrd', attn_probs, v_block, precision=PRECISE)
        return mixed.reshape(block_rows, HEADS, HEAD_DIM)
    outputs = lax.map(jax.checkpoint(one_block), jnp.arange(length // block_rows, dtype=jnp.int32))
    return outputs.reshape(length, HEADS, HEAD_DIM)

def layer_forward(tokens_float, attn_gain, w_query, w_key, w_value, query_gain, key_gain, w_out, ffn_gain, w_gate, w_up, w_down, seg_row, pos_row):
    length = tokens_float.shape[0]
    normed = low(rms_norm(tokens_float, attn_gain))
    queries = low_back(matmul(normed, w_query)).reshape(length, HEADS, HEAD_DIM)
    key_heads = low_back(matmul(normed, w_key)).reshape(length, KV_HEADS, HEAD_DIM)
    values = low(low_back(matmul(normed, w_value))).reshape(length, KV_HEADS, HEAD_DIM)
    queries = low(rotary(rms_norm(queries, query_gain), pos_row, 1.0))
    key_heads = low(rotary(rms_norm(key_heads, key_gain), pos_row, 1.0))
    mixed = low(low_back(attend(queries, key_heads, values, seg_row))).reshape(length, HEADS * HEAD_DIM)
    middle = tokens_float + low_back(matmul(mixed, w_out))
    normed_two = low(rms_norm(middle, ffn_gain))
    gate_pre = low_back(matmul(normed_two, w_gate))
    up_pre = low_back(matmul(normed_two, w_up))
    hidden = low(jax.nn.silu(gate_pre) * up_pre)
    return middle + matmul(hidden, w_down)

def reference(tokens, seg_ids, doc_pos, attn_gain, w_query, w_key, w_value, query_gain, key_gain, w_out, ffn_gain, w_gate, w_up, w_down, d_output):
    weights = tuple((weight_arg.astype(jnp.float32) for weight_arg in (attn_gain, w_query, w_key, w_value, query_gain, key_gain, w_out, ffn_gain, w_gate, w_up, w_down)))

    def per_sequence(totals, seq_row):
        tokens_in, seg_row, pos_row, cot_row = seq_row

        def forward_fn(tokens_float, *weight_list):
            return layer_forward(tokens_float, *weight_list, seg_row, pos_row)
        layer_out, pull_back = jax.vjp(forward_fn, tokens_in.astype(jnp.float32), *weights)
        gradients = pull_back(cot_row.astype(jnp.float32))
        totals = tuple((running + fresh for running, fresh in zip(totals, gradients[1:])))
        return (totals, (layer_out.astype(jnp.bfloat16), gradients[0]))
    initial = tuple((jnp.zeros_like(weight_arg) for weight_arg in weights))
    totals, (outputs, d_tokens) = lax.scan(per_sequence, initial, (tokens, seg_ids, doc_pos, d_output))
    return (outputs, d_tokens, totals[0], totals[1], totals[2], totals[3], totals[4], totals[5], totals[6], totals[7], totals[8], totals[9], totals[10])
```

```python
import functools

import jax
import jax.numpy as jnp
from jax import lax
from jax.experimental import pallas as pl
from jax.experimental.pallas import tpu as pltpu
from jax.sharding import PartitionSpec as P

HEADS = 16
KV_HEADS = 8
HEAD_DIM = 64
HOPS = 8


EPSILON = 1e-05
THETA = 1000000.0
MASKED = -1e30


def from_behind(block, axis, distance):
    devices = range(lax.axis_size(axis))
    route = [(i - distance, i) for i in devices if i - distance in devices]
    return lax.ppermute(block, axis, route)


def rms_norm(values, norm_gain):
    return (
        values * lax.rsqrt(jnp.mean(values * values, axis=-1, keepdims=True) + EPSILON) * norm_gain
    )


def rms_back(values, norm_gain, upstream):
    inverse = lax.rsqrt(jnp.mean(values * values, axis=-1, keepdims=True) + EPSILON)
    scaled = upstream * norm_gain
    row_width = values.shape[-1]
    d_values = (
        inverse * scaled
        - values * inverse**3 * jnp.sum(scaled * values, axis=-1, keepdims=True) / row_width
    )
    return (d_values, upstream * values * inverse)


def rotary(values, positions, turn_sign):
    half_dim = values.shape[-1] // 2
    inverse_freq = THETA ** (-(2.0 / values.shape[-1]) * jnp.arange(half_dim, dtype=jnp.float32))
    angles = positions.astype(jnp.float32)[:, None] * inverse_freq[None, :]
    cosine = jnp.cos(angles)[:, None, :]
    sine_part = turn_sign * jnp.sin(angles)[:, None, :]
    first_half = values[..., :half_dim]
    second_half = values[..., half_dim:]
    return jnp.concatenate(
        [
            first_half * cosine - second_half * sine_part,
            second_half * cosine + first_half * sine_part,
        ],
        axis=-1,
    )


def outer_product(left_mat, right_mat):
    return lax.dot_general(
        left_mat, right_mat, (((0,), (0,)), ((), ())), preferred_element_type=jnp.float32
    )


def against(left_mat, right_mat):
    return lax.dot_general(
        left_mat, right_mat, (((1,), (1,)), ((), ())), preferred_element_type=jnp.float32
    )


def ring_body(
    tokens,
    seg_ids,
    doc_pos,
    attn_gain,
    w_query,
    w_key,
    w_value,
    query_gain,
    key_gain,
    w_out,
    ffn_gain,
    w_gate,
    w_up,
    w_down,
    d_output,
):
    cycle_place = lax.axis_index("ctx")
    tok_rows = tokens.shape[1]
    resid_in = tokens[0].astype(jnp.float32)
    seg_local = seg_ids[0]
    pos_local = doc_pos[0]
    q_per_kv = HEADS // KV_HEADS
    group_cols = q_per_kv * HEAD_DIM
    score_scale = HEAD_DIM ** (-0.5)
    q_full, k_full, v_full, o_full = (
        lax.all_gather(w_query, "fsdp", axis=0, tiled=True),
        lax.all_gather(w_key, "fsdp", axis=0, tiled=True),
        lax.all_gather(w_value, "fsdp", axis=0, tiled=True),
        lax.all_gather(w_out, "fsdp", axis=0, tiled=True),
    )
    gate_full, up_full, down_full = (
        lax.all_gather(w_gate, "fsdp", axis=0, tiled=True),
        lax.all_gather(w_up, "fsdp", axis=0, tiled=True),
        lax.all_gather(w_down, "fsdp", axis=0, tiled=True),
    )
    normed = rms_norm(resid_in, attn_gain)
    normed_low = normed.astype(jnp.bfloat16)
    query_raw = jnp.dot(normed_low, q_full, preferred_element_type=jnp.float32).reshape(
        tok_rows, HEADS, HEAD_DIM
    )
    key_raw = jnp.dot(normed_low, k_full, preferred_element_type=jnp.float32).reshape(
        tok_rows, KV_HEADS, HEAD_DIM
    )
    value_raw = jnp.dot(normed_low, v_full, preferred_element_type=jnp.float32)
    query_rot = rotary(rms_norm(query_raw, query_gain), pos_local, 1.0)
    key_rot = rotary(rms_norm(key_raw, key_gain), pos_local, 1.0)
    query_low = query_rot.astype(jnp.bfloat16).reshape(tok_rows, HEADS * HEAD_DIM)
    key_low = key_rot.astype(jnp.bfloat16).reshape(tok_rows, KV_HEADS * HEAD_DIM)
    value_low = value_raw.astype(jnp.bfloat16)
    own_kv = (key_low, value_low, seg_local)
    kv_blocks = [own_kv]
    carried = own_kv
    for hop_index in range(HOPS):
        carried = from_behind((carried[0], carried[1], carried[2]), "ctx", 1)
        kv_blocks.append(carried)
    key_all = jnp.concatenate([kv_entry[0] for kv_entry in kv_blocks], axis=0)
    value_all = jnp.concatenate([kv_entry[1] for kv_entry in kv_blocks], axis=0)
    seg_all = jnp.concatenate([kv_entry[2] for kv_entry in kv_blocks], axis=0)
    key_owner = cycle_place - jnp.arange(HOPS + 1, dtype=jnp.int32)
    owner_valid = jnp.repeat(key_owner >= 0, tok_rows)
    key_index = (
        key_owner[:, None] * tok_rows + jnp.arange(tok_rows, dtype=jnp.int32)[None, :]
    ).reshape(-1)
    query_index = cycle_place * tok_rows + jnp.arange(tok_rows, dtype=jnp.int32)
    allowed = (
        (seg_local[:, None] == seg_all[None, :])
        & (key_index[None, :] <= query_index[:, None])
        & owner_valid[None, :]
    )

    def group_scores(kv_group):
        query_part = lax.dynamic_slice_in_dim(query_low, kv_group * group_cols, group_cols, 1)
        query_part = query_part.reshape(tok_rows, q_per_kv, HEAD_DIM)
        key_part = lax.dynamic_slice_in_dim(key_all, kv_group * HEAD_DIM, HEAD_DIM, 1)
        value_part = lax.dynamic_slice_in_dim(value_all, kv_group * HEAD_DIM, HEAD_DIM, 1)
        scores = (
            jnp.einsum("trd,kd->rtk", query_part, key_part, preferred_element_type=jnp.float32)
            * score_scale
        )
        return (jnp.where(allowed[None], scores, MASKED), query_part, key_part, value_part)

    def forward_group(kv_group):
        scores, query_part, key_part, value_part = group_scores(kv_group)
        row_top = jnp.max(scores, axis=-1, keepdims=True)
        log_total = row_top + jnp.log(jnp.sum(jnp.exp(scores - row_top), axis=-1, keepdims=True))
        attn_probs = jnp.exp(scores - log_total)
        mixed_part = jnp.einsum(
            "rtk,kd->trd",
            attn_probs.astype(jnp.bfloat16),
            value_part,
            preferred_element_type=jnp.float32,
        )
        return (mixed_part.reshape(tok_rows, group_cols), log_total[..., 0])

    mixed_groups, total_groups = lax.map(forward_group, jnp.arange(KV_HEADS, dtype=jnp.int32))
    mixed = mixed_groups.transpose(1, 0, 2).reshape(tok_rows, HEADS * HEAD_DIM)
    mixed_low = mixed.astype(jnp.bfloat16)
    middle = resid_in + jnp.dot(mixed_low, o_full, preferred_element_type=jnp.float32)
    ffn_low = rms_norm(middle, ffn_gain).astype(jnp.bfloat16)
    gate_pre = jnp.dot(ffn_low, gate_full, preferred_element_type=jnp.float32)
    up_pre = jnp.dot(ffn_low, up_full, preferred_element_type=jnp.float32)
    gate_sig = jax.nn.sigmoid(gate_pre)
    gate_act = gate_pre * gate_sig
    hidden_low = (gate_act * up_pre).astype(jnp.bfloat16)
    result = middle + jnp.dot(hidden_low, down_full, preferred_element_type=jnp.float32)
    output = result.astype(jnp.bfloat16)[None]
    cot_low = d_output[0]
    cotangent = cot_low.astype(jnp.float32)
    grad_w_down = outer_product(hidden_low, cot_low)
    grad_hidden = against(cot_low, down_full)
    gate_back = (grad_hidden * up_pre * (gate_sig * (1.0 + gate_pre * (1.0 - gate_sig)))).astype(
        jnp.bfloat16
    )
    up_back = (grad_hidden * gate_act).astype(jnp.bfloat16)
    grad_w_gate = outer_product(ffn_low, gate_back)
    grad_w_up = outer_product(ffn_low, up_back)
    grad_ffn_in = against(gate_back, gate_full) + against(up_back, up_full)
    middle_part, ffn_terms = rms_back(middle, ffn_gain, grad_ffn_in)
    grad_middle = cotangent + middle_part
    middle_low = grad_middle.astype(jnp.bfloat16)
    grad_w_out = outer_product(mixed_low, middle_low)
    grad_mixed = against(middle_low, o_full).astype(jnp.bfloat16)

    def backward_group(kv_group):
        scores, query_part, key_part, value_part = group_scores(kv_group)
        attn_probs = jnp.exp(scores - total_groups[kv_group][..., None])
        mixed_grad_part = lax.dynamic_slice_in_dim(grad_mixed, kv_group * group_cols, group_cols, 1)
        mixed_grad_part = mixed_grad_part.reshape(tok_rows, q_per_kv, HEAD_DIM)
        grad_probs = jnp.einsum(
            "trd,kd->rtk", mixed_grad_part, value_part, preferred_element_type=jnp.float32
        )
        grad_value = jnp.einsum(
            "rtk,trd->kd",
            attn_probs.astype(jnp.bfloat16),
            mixed_grad_part,
            preferred_element_type=jnp.float32,
        )
        row_delta = jnp.sum(grad_probs * attn_probs, axis=-1, keepdims=True)
        grad_scores = (attn_probs * (grad_probs - row_delta)).astype(jnp.bfloat16)
        grad_query = (
            jnp.einsum("rtk,kd->trd", grad_scores, key_part, preferred_element_type=jnp.float32)
            * score_scale
        )
        grad_key = (
            jnp.einsum("rtk,trd->kd", grad_scores, query_part, preferred_element_type=jnp.float32)
            * score_scale
        )
        return (grad_query.reshape(tok_rows, group_cols), grad_key, grad_value)

    query_groups, key_groups, value_groups = lax.map(
        backward_group, jnp.arange(KV_HEADS, dtype=jnp.int32)
    )
    grad_query_rot = query_groups.transpose(1, 0, 2).reshape(tok_rows, HEADS, HEAD_DIM)
    key_blocks = key_groups.transpose(1, 0, 2).reshape(HOPS + 1, tok_rows, KV_HEADS * HEAD_DIM)
    value_blocks = value_groups.transpose(1, 0, 2).reshape(HOPS + 1, tok_rows, KV_HEADS * HEAD_DIM)
    home_key = key_blocks[HOPS]
    home_value = value_blocks[HOPS]
    for hop_index in range(HOPS, 0, -1):
        moved_key, moved_value = (
            from_behind(home_key.astype(jnp.bfloat16), "ctx", -1).astype(home_key.dtype),
            from_behind(home_value.astype(jnp.bfloat16), "ctx", -1).astype(home_value.dtype),
        )
        home_key = moved_key + key_blocks[hop_index - 1]
        home_value = moved_value + value_blocks[hop_index - 1]
    query_turned = rotary(grad_query_rot, pos_local, -1.0)
    key_turned = rotary(home_key.reshape(tok_rows, KV_HEADS, HEAD_DIM), pos_local, -1.0)
    query_back, query_terms = rms_back(query_raw, query_gain, query_turned)
    key_back, key_terms = rms_back(key_raw, key_gain, key_turned)
    query_back = query_back.reshape(tok_rows, HEADS * HEAD_DIM).astype(jnp.bfloat16)
    key_back = key_back.reshape(tok_rows, KV_HEADS * HEAD_DIM).astype(jnp.bfloat16)
    value_back = home_value.astype(jnp.bfloat16)
    grad_w_query = outer_product(normed_low, query_back)
    grad_w_key = outer_product(normed_low, key_back)
    grad_w_value = outer_product(normed_low, value_back)
    grad_normed = (
        against(query_back, q_full) + against(key_back, k_full) + against(value_back, v_full)
    )
    input_part, attn_terms = rms_back(resid_in, attn_gain, grad_normed)
    d_tokens = (grad_middle + input_part)[None]
    gain_totals = lax.psum(
        (
            jnp.sum(attn_terms, axis=0),
            jnp.sum(ffn_terms, axis=0),
            jnp.sum(query_terms, axis=(0, 1)),
            jnp.sum(key_terms, axis=(0, 1)),
        ),
        ("ctx", "fsdp"),
    )
    weight_grads = (
        grad_w_query,
        grad_w_key,
        grad_w_value,
        grad_w_out,
        grad_w_gate,
        grad_w_up,
        grad_w_down,
    )
    spread = (
        lax.psum_scatter(
            weight_grads[0].astype(jnp.bfloat16), "fsdp", scatter_dimension=0, tiled=True
        ).astype(jnp.float32),
        lax.psum_scatter(
            weight_grads[1].astype(jnp.bfloat16), "fsdp", scatter_dimension=0, tiled=True
        ).astype(jnp.float32),
        lax.psum_scatter(
            weight_grads[2].astype(jnp.bfloat16), "fsdp", scatter_dimension=0, tiled=True
        ).astype(jnp.float32),
        lax.psum_scatter(
            weight_grads[3].astype(jnp.bfloat16), "fsdp", scatter_dimension=0, tiled=True
        ).astype(jnp.float32),
        lax.psum_scatter(
            weight_grads[4].astype(jnp.bfloat16), "fsdp", scatter_dimension=0, tiled=True
        ).astype(jnp.float32),
        lax.psum_scatter(
            weight_grads[5].astype(jnp.bfloat16), "fsdp", scatter_dimension=0, tiled=True
        ).astype(jnp.float32),
        lax.psum_scatter(
            weight_grads[6].astype(jnp.bfloat16), "fsdp", scatter_dimension=0, tiled=True
        ).astype(jnp.float32),
    )
    shares = (
        lax.psum_scatter(spread[0], "ctx", scatter_dimension=1, tiled=True),
        lax.psum_scatter(spread[1], "ctx", scatter_dimension=1, tiled=True),
        lax.psum_scatter(spread[2], "ctx", scatter_dimension=1, tiled=True),
        lax.psum_scatter(spread[3], "ctx", scatter_dimension=1, tiled=True),
        lax.psum_scatter(spread[4], "ctx", scatter_dimension=1, tiled=True),
        lax.psum_scatter(spread[5], "ctx", scatter_dimension=1, tiled=True),
        lax.psum_scatter(spread[6], "ctx", scatter_dimension=1, tiled=True),
    )
    return (
        output,
        d_tokens,
        gain_totals[0],
        shares[0],
        shares[1],
        shares[2],
        gain_totals[2],
        gain_totals[3],
        shares[3],
        gain_totals[1],
        shares[4],
        shares[5],
        shares[6],
    )


MESH = pl.DeviceIdType.MESH
BLOCK = 256
RING = 16
VMEM_SPEC = pl.BlockSpec(memory_space=pltpu.VMEM)
SMEM_SPEC = pl.BlockSpec(memory_space=pltpu.SMEM)
F32 = jnp.float32
BF16 = jnp.bfloat16


def dot_dims(left_mat, right_mat, left_dim, right_dim):
    return lax.dot_general(
        left_mat, right_mat, (((left_dim,), (right_dim,)), ((), ())), preferred_element_type=F32
    )


def exchange_kernel(src, dst, own_sem, send_sem, recv_sem):
    place, core = lax.axis_index("ctx"), lax.axis_index("fsdp")
    barrier = pltpu.get_barrier_semaphore()
    for step in range(1, RING):
        peer = lax.rem(place + step, RING)
        pl.semaphore_signal(barrier, inc=1, device_id=(peer, core), device_id_type=MESH)
    own = pltpu.make_async_copy(src.at[place], dst.at[place], own_sem)
    own.start()
    pl.semaphore_wait(barrier, RING - 1)
    copies = []
    for step in range(1, RING):
        peer = lax.rem(place + step, RING)
        copy = pltpu.make_async_remote_copy(
            src_ref=src.at[peer],
            dst_ref=dst.at[place],
            send_sem=send_sem.at[step],
            recv_sem=recv_sem.at[step],
            device_id=(peer, core),
            device_id_type=MESH,
        )
        copy.start()
        copies.append(copy)
    own.wait()
    for copy in copies:
        copy.wait()


def exchange(blocks, call_id):
    return pl.pallas_call(
        exchange_kernel,
        out_shape=jax.ShapeDtypeStruct(blocks.shape, blocks.dtype),
        in_specs=[VMEM_SPEC],
        out_specs=VMEM_SPEC,
        scratch_shapes=[
            pltpu.SemaphoreType.DMA,
            pltpu.SemaphoreType.DMA((RING,)),
            pltpu.SemaphoreType.DMA((RING,)),
        ],
        compiler_params=pltpu.CompilerParams(collective_id=call_id, has_side_effects=True),
        name="exchange_heads",
    )(blocks)


def transposed(block):
    return block.astype(F32).T.astype(BF16)


def block_probs(key_nat, query_t, first_key, start, query_place, diagonal, masked):
    scores = jnp.dot(key_nat, query_t, preferred_element_type=F32)
    probs = jnp.exp(scores)
    if masked:
        key_place = first_key + lax.broadcasted_iota(jnp.int32, probs.shape, 0)
        ok = key_place >= start
        if diagonal:
            ok = ok & (key_place <= query_place)
        probs = jnp.where(ok, probs, 0.0)
    return probs


def attend_kernel(first_ref, clear_ref, qkv_ref, start_ref, mixed_ref, inv_ref, key_nat):
    blocks = qkv_ref.shape[0]

    def turn(j, carry):
        key_nat[j] = transposed(qkv_ref[j, HEAD_DIM : 2 * HEAD_DIM, :])
        return carry

    lax.fori_loop(0, blocks, turn, 0)

    def per_query(i, nothing):
        query_t = qkv_ref[i, 0:HEAD_DIM, :] * jnp.asarray(HEAD_DIM**-0.5, BF16)
        start = start_ref[i]
        query_place = i * BLOCK + lax.broadcasted_iota(jnp.int32, (1, BLOCK), 1)

        def step(diagonal, masked, j, carry):
            total, acc = carry
            probs = block_probs(
                key_nat[j], query_t, j * BLOCK, start, query_place, diagonal, masked
            )
            total = total + jnp.sum(probs, axis=0, keepdims=True)
            acc = acc + jnp.dot(
                qkv_ref[j, 2 * HEAD_DIM : 3 * HEAD_DIM, :],
                probs.astype(BF16),
                preferred_element_type=F32,
            )
            return total, acc

        carry = (jnp.zeros((1, BLOCK), F32), jnp.zeros((HEAD_DIM, BLOCK), F32))
        carry = lax.fori_loop(
            first_ref[i], clear_ref[i], functools.partial(step, False, True), carry
        )
        carry = lax.fori_loop(clear_ref[i], i, functools.partial(step, False, False), carry)
        total, acc = step(True, True, i, carry)
        inverse = 1.0 / total
        mixed_ref[i] = (acc * inverse).astype(BF16)
        inv_ref[i] = inverse
        return nothing

    lax.fori_loop(0, blocks, per_query, 0)


def attend(first, clear, qkv, start):
    blocks = qkv.shape[0]
    return pl.pallas_call(
        attend_kernel,
        out_shape=(
            jax.ShapeDtypeStruct((blocks, HEAD_DIM, BLOCK), BF16),
            jax.ShapeDtypeStruct((blocks, 1, BLOCK), F32),
        ),
        in_specs=[SMEM_SPEC, SMEM_SPEC, VMEM_SPEC, VMEM_SPEC],
        out_specs=(VMEM_SPEC, VMEM_SPEC),
        scratch_shapes=[pltpu.VMEM((blocks, BLOCK, HEAD_DIM), BF16)],
        name="attend_forward",
    )(first, clear, qkv, start)


def attend_back_kernel(
    first_ref,
    clear_ref,
    qkv_ref,
    start_ref,
    mixed_ref,
    inv_ref,
    cot_ref,
    out_ref,
    key_nat,
    value_nat,
    key_acc,
    value_acc,
):
    blocks = qkv_ref.shape[0]
    scale = HEAD_DIM**-0.5

    def turn(j, carry):
        key_nat[j] = transposed(qkv_ref[j, HEAD_DIM : 2 * HEAD_DIM, :])
        value_nat[j] = transposed(qkv_ref[j, 2 * HEAD_DIM : 3 * HEAD_DIM, :])
        key_acc[j] = jnp.zeros((BLOCK, HEAD_DIM), F32)
        value_acc[j] = jnp.zeros((BLOCK, HEAD_DIM), F32)
        return carry

    lax.fori_loop(0, blocks, turn, 0)

    def per_query(i, nothing):
        query_t = qkv_ref[i, 0:HEAD_DIM, :] * jnp.asarray(scale, BF16)
        query_nat = transposed(query_t)
        cot_t = cot_ref[i]
        cot_nat = transposed(cot_t)
        start = start_ref[i]
        inverse = inv_ref[i]
        delta = jnp.sum(
            cot_t.astype(F32) * mixed_ref[i].astype(F32), axis=0, keepdims=True
        )
        query_place = i * BLOCK + lax.broadcasted_iota(jnp.int32, (1, BLOCK), 1)

        def step(diagonal, masked, j, acc):
            probs = (
                block_probs(key_nat[j], query_t, j * BLOCK, start, query_place, diagonal, masked)
                * inverse
            )
            grad_probs = jnp.dot(value_nat[j], cot_t, preferred_element_type=F32)
            grad_scores = (probs * (grad_probs - delta)).astype(BF16)
            value_acc[j] += jnp.dot(probs.astype(BF16), cot_nat, preferred_element_type=F32)
            key_acc[j] += jnp.dot(grad_scores, query_nat, preferred_element_type=F32)
            return acc + jnp.dot(
                qkv_ref[j, HEAD_DIM : 2 * HEAD_DIM, :], grad_scores, preferred_element_type=F32
            )

        acc = jnp.zeros((HEAD_DIM, BLOCK), F32)
        acc = lax.fori_loop(first_ref[i], clear_ref[i], functools.partial(step, False, True), acc)
        acc = lax.fori_loop(clear_ref[i], i, functools.partial(step, False, False), acc)
        acc = step(True, True, i, acc)
        out_ref[i, 0:HEAD_DIM, :] = (acc * scale).astype(BF16)
        return nothing

    lax.fori_loop(0, blocks, per_query, 0)

    def flush(j, carry):
        out_ref[j, HEAD_DIM : 2 * HEAD_DIM, :] = key_acc[j].T.astype(BF16)
        out_ref[j, 2 * HEAD_DIM : 3 * HEAD_DIM, :] = value_acc[j].T.astype(BF16)
        return carry

    lax.fori_loop(0, blocks, flush, 0)


def attend_back(first, clear, qkv, start, mixed, inverse, cot):
    blocks = qkv.shape[0]
    return pl.pallas_call(
        attend_back_kernel,
        out_shape=jax.ShapeDtypeStruct(qkv.shape, BF16),
        in_specs=[SMEM_SPEC, SMEM_SPEC] + [VMEM_SPEC] * 5,
        out_specs=VMEM_SPEC,
        scratch_shapes=[
            pltpu.VMEM((blocks, BLOCK, HEAD_DIM), BF16),
            pltpu.VMEM((blocks, BLOCK, HEAD_DIM), BF16),
            pltpu.VMEM((blocks, BLOCK, HEAD_DIM), F32),
            pltpu.VMEM((blocks, BLOCK, HEAD_DIM), F32),
        ],
        name="attend_backward",
    )(first, clear, qkv, start, mixed, inverse, cot)


def spread_kernel(parts, rows, n_in, n_out, *refs):
    inputs, outputs, scratch = refs[:n_in], refs[n_in : n_in + n_out], refs[n_in + n_out :]
    sent = (scratch[0:3], scratch[3:6])
    came = (scratch[6:9], scratch[9:12])
    send_sems, recv_sems = scratch[12], scratch[13]
    compute, finish = parts
    place, core = lax.axis_index("ctx"), lax.axis_index("fsdp")
    x, y, z = lax.rem(place, 2), lax.rem(place // 2, 2), place // 4

    def at(chain, first, second, depth):
        if chain == 0:
            return depth * 4 + second * 2 + first
        return depth * 4 + first * 2 + second

    coords = ((x, y), (y, x))
    barrier = pltpu.get_barrier_semaphore()
    peers = [at(0, 1 - x, y, z), at(0, x, 1 - y, z)]
    peers += [at(0, x, y, lax.rem(z + step, 4)) for step in range(1, 4)]
    for peer in peers:
        pl.semaphore_signal(barrier, inc=1, device_id=(peer, core), device_id_type=MESH)
    pl.semaphore_wait(barrier, len(peers))

    def copy(chain, stage, slot, sem, peer):
        return pltpu.make_async_remote_copy(
            src_ref=sent[chain][stage].at[slot],
            dst_ref=came[chain][stage].at[slot],
            send_sem=send_sems.at[chain, sem],
            recv_sem=recv_sems.at[chain, sem],
            device_id=(peer, core),
            device_id_type=MESH,
        )

    def one(index, nothing):
        turned = 1 - index // 4
        depth = lax.rem(index + 1, 4)
        slot = turned * 4 + depth
        for chain in range(2):
            first, second = coords[chain]
            other = second + turned - 2 * second * turned
            owner = at(chain, 1 - first, other, lax.rem(z + depth, 4))
            for row, value in compute(chain, owner, inputs):
                sent[chain][0][slot, row : row + value.shape[0], :] = value.astype(BF16)
            copy(chain, 0, slot, slot, at(chain, 1 - first, second, z)).start()
        return nothing

    lax.fori_loop(0, 8, one, 0)

    def two(index, nothing):
        depth = lax.rem(index + 1, 4)
        for chain in range(2):
            first, second = coords[chain]
            copy(chain, 0, 4 + depth, 4 + depth, at(chain, 1 - first, second, z)).wait_recv()
            owner = at(chain, first, 1 - second, lax.rem(z + depth, 4))
            for row, value in compute(chain, owner, inputs):
                window = slice(row, row + value.shape[0])
                value = value + came[chain][0][4 + depth, window, :].astype(F32)
                sent[chain][1][depth, window, :] = value.astype(BF16)
            copy(chain, 1, depth, 8 + depth, at(chain, first, 1 - second, z)).start()
        return nothing

    lax.fori_loop(0, 4, two, 0)

    def three(depth, nothing):
        for chain in range(2):
            first, second = coords[chain]
            copy(chain, 0, depth, depth, at(chain, 1 - first, second, z)).wait_recv()
            copy(chain, 1, depth, 8 + depth, at(chain, first, 1 - second, z)).wait_recv()
            far = at(chain, first, second, lax.rem(z + depth, 4))
            for row, value in compute(chain, far, inputs):
                window = slice(row, row + value.shape[0])
                value = value + came[chain][0][depth, window, :].astype(F32)
                value = value + came[chain][1][depth, window, :].astype(F32)
                sent[chain][2][depth - 1, window, :] = value.astype(BF16)
            copy(chain, 2, depth - 1, 11 + depth, far).start()
        return nothing

    lax.fori_loop(1, 4, three, 0)

    for chain in range(2):
        first, second = coords[chain]
        copy(chain, 0, 0, 0, at(chain, 1 - first, second, z)).wait_recv()
        copy(chain, 1, 0, 8, at(chain, first, 1 - second, z)).wait_recv()
        for depth in range(1, 4):
            far = at(chain, first, second, lax.rem(z + depth, 4))
            copy(chain, 2, depth - 1, 11 + depth, far).wait_recv()
        for row, value in compute(chain, place, inputs):
            window = slice(row, row + value.shape[0])
            value = value + came[chain][0][0, window, :].astype(F32)
            value = value + came[chain][1][0, window, :].astype(F32)
            for depth in range(3):
                value = value + came[chain][2][depth, window, :].astype(F32)
            finish(chain, row, value, outputs)
        for slot in range(8):
            copy(chain, 0, slot, slot, at(chain, 1 - first, second, z)).wait_send()
        for depth in range(4):
            copy(chain, 1, depth, 8 + depth, at(chain, first, 1 - second, z)).wait_send()
        for depth in range(1, 4):
            far = at(chain, first, second, lax.rem(z + depth, 4))
            copy(chain, 2, depth - 1, 11 + depth, far).wait_send()


def spread_call(parts, rows, inputs, out_shape, call_id, name):
    lanes = 256
    buffers = [
        pltpu.VMEM((slots, rows[chain], lanes), BF16) for chain in range(2) for slots in (8, 4, 3)
    ]
    return pl.pallas_call(
        functools.partial(spread_kernel, parts, rows, len(inputs), len(out_shape)),
        out_shape=out_shape,
        in_specs=[VMEM_SPEC] * len(inputs),
        out_specs=tuple([VMEM_SPEC] * len(out_shape)),
        scratch_shapes=buffers
        + buffers
        + [pltpu.SemaphoreType.DMA((2, 15)), pltpu.SemaphoreType.DMA((2, 15))],
        compiler_params=pltpu.CompilerParams(
            collective_id=call_id, has_side_effects=True, vmem_limit_bytes=60 << 20
        ),
        name=name,
    )(*inputs)


def rows_of(ref, owner, count, base=0):
    return ref[pl.ds(pl.multiple_of(base + owner * count, 16), count), :]


def ffn_parts():
    def compute(chain, owner, inputs):
        gate_t, up_t, cot_t, mid_t, normed, hidden, mixed = inputs
        lanes = slice(chain * 256, chain * 256 + 256)
        width = gate_t.shape[0] // RING
        values = [
            (0, jnp.dot(rows_of(gate_t, owner, width), normed[:, lanes], preferred_element_type=F32)),
            (width, jnp.dot(rows_of(up_t, owner, width), normed[:, lanes], preferred_element_type=F32)),
        ]
        narrow = cot_t.shape[0] // RING
        down_rows = rows_of(cot_t, owner, narrow)
        row = 2 * width
        for chunk in range(5) if chain == 0 else range(5, 9):
            piece = hidden[:, chunk * 256 : chunk * 256 + 256]
            values.append((row, jnp.dot(down_rows, piece, preferred_element_type=F32)))
            row += narrow
        values.append(
            (row, jnp.dot(rows_of(mid_t, owner, narrow), mixed[:, lanes], preferred_element_type=F32))
        )
        return values

    def finish(chain, row, value, outputs):
        gate, up, down, out = outputs
        lanes = slice(chain * 256, chain * 256 + 256)
        width = gate.shape[0]
        narrow = down.shape[0]
        if row < width:
            gate[:, lanes] = value
        elif row < 2 * width:
            up[:, lanes] = value
        else:
            chunk = (row - 2 * width) // narrow
            if chunk == (5 if chain == 0 else 4):
                out[:, lanes] = value
            else:
                chunk += 5 * chain
                down[:, chunk * 256 : chunk * 256 + 256] = value

    return compute, finish


def qkv_parts():
    def compute(chain, owner, inputs):
        back_t, normed = inputs
        lanes = slice(chain * 256, chain * 256 + 256)
        values = []
        row, base = 0, 0
        for count in (64, 32, 32):
            values.append(
                (
                    row,
                    jnp.dot(
                        rows_of(back_t, owner, count, base),
                        normed[:, lanes],
                        preferred_element_type=F32,
                    ),
                )
            )
            row += count
            base += count * RING
        return values

    def finish(chain, row, value, outputs):
        outputs[0][row : row + value.shape[0], chain * 256 : chain * 256 + 256] = value

    return compute, finish


def turn_heads(values_t, positions, sign):
    half = HEAD_DIM // 2
    inverse_freq = THETA ** (-(2.0 / HEAD_DIM) * jnp.arange(half, dtype=F32))
    angles = inverse_freq[:, None] * positions.astype(F32)[None, :]
    cosine, sine = jnp.cos(angles)[None], sign * jnp.sin(angles)[None]
    first, second = values_t[:, :half], values_t[:, half:]
    return jnp.concatenate(
        [first * cosine - second * sine, second * cosine + first * sine], axis=1
    )


def head_norm(values_t, gain):
    mean = jnp.mean(values_t * values_t, axis=1, keepdims=True)
    return values_t * lax.rsqrt(mean + EPSILON) * gain[None, :, None]


def head_norm_back(values_t, gain, upstream):
    inverse = lax.rsqrt(jnp.mean(values_t * values_t, axis=1, keepdims=True) + EPSILON)
    scaled = upstream * gain[None, :, None]
    d_values = (
        inverse * scaled
        - values_t
        * inverse**3
        * jnp.sum(scaled * values_t, axis=1, keepdims=True)
        / values_t.shape[1]
    )
    return d_values, jnp.sum(upstream * values_t * inverse, axis=(0, 2))


def both(block, axis):
    return lax.all_gather(block, "fsdp", axis=axis, tiled=True)


def heads_body(
    tokens,
    seg_ids,
    doc_pos,
    attn_gain,
    w_query,
    w_key,
    w_value,
    query_gain,
    key_gain,
    w_out,
    ffn_gain,
    w_gate,
    w_up,
    w_down,
    d_output,
):
    place, core = lax.axis_index("ctx"), lax.axis_index("fsdp")
    rows, width = tokens.shape[1], tokens.shape[2]
    resid_in = tokens[0].astype(F32)
    pos_local = doc_pos[0]
    q_full, k_full, v_full, o_full = (
        both(w_query, 0),
        both(w_key, 0),
        both(w_value, 0),
        both(w_out, 0),
    )
    gate_full, up_full, down_full = both(w_gate, 0), both(w_up, 0), both(w_down, 0)
    starts_local = place * rows + jnp.arange(rows, dtype=jnp.int32) - pos_local
    starts = lax.all_gather(starts_local, "ctx", axis=0, tiled=False)
    first = starts[:, 0] // BLOCK
    own_index = jnp.arange(RING, dtype=jnp.int32)
    clear = jnp.minimum((starts[:, -1] + BLOCK - 1) // BLOCK, own_index)
    starts = starts[:, None, :]

    normed_low = rms_norm(resid_in, attn_gain).astype(BF16)
    query_raw = dot_dims(q_full, normed_low, 0, 1).reshape(HEADS, HEAD_DIM, rows)
    key_raw = dot_dims(k_full, normed_low, 0, 1).reshape(KV_HEADS, HEAD_DIM, rows)
    value_raw = dot_dims(v_full, normed_low, 0, 1).reshape(KV_HEADS, HEAD_DIM, rows)
    query_low = turn_heads(head_norm(query_raw, query_gain), pos_local, 1.0).astype(BF16)
    key_low = turn_heads(head_norm(key_raw, key_gain), pos_local, 1.0).astype(BF16)
    value_low = value_raw.astype(BF16)
    group = HEADS // KV_HEADS
    qkv_home = jnp.concatenate(
        [query_low, jnp.repeat(key_low, group, axis=0), jnp.repeat(value_low, group, axis=0)],
        axis=1,
    )
    qkv = exchange(qkv_home, 1)
    mixed_far, inverse_total = attend(first, clear, qkv, starts)
    mixed_t = exchange(mixed_far, 2).reshape(HEADS * HEAD_DIM, rows)

    middle = resid_in + dot_dims(mixed_t, o_full, 0, 0)
    ffn_low = rms_norm(middle, ffn_gain).astype(BF16)
    gate_pre = jnp.dot(ffn_low, gate_full, preferred_element_type=F32)
    up_pre = jnp.dot(ffn_low, up_full, preferred_element_type=F32)
    gate_sig = jax.nn.sigmoid(gate_pre)
    gate_act = gate_pre * gate_sig
    hidden_low = (gate_act * up_pre).astype(BF16)
    result = middle + jnp.dot(hidden_low, down_full, preferred_element_type=F32)
    output = result.astype(BF16)[None]
    cot_low = d_output[0]
    cotangent = cot_low.astype(F32)
    grad_hidden = against(cot_low, down_full)
    gate_back = (grad_hidden * up_pre * (gate_sig * (1.0 + gate_pre * (1.0 - gate_sig)))).astype(
        BF16
    )
    up_back = (grad_hidden * gate_act).astype(BF16)
    grad_ffn_in = against(gate_back, gate_full) + against(up_back, up_full)
    middle_part, ffn_terms = rms_back(middle, ffn_gain, grad_ffn_in)
    grad_middle = cotangent + middle_part
    middle_low = grad_middle.astype(BF16)
    grad_mixed = dot_dims(o_full, middle_low, 1, 1).astype(BF16)

    cot_far = exchange(grad_mixed.reshape(HEADS, HEAD_DIM, rows), 3)
    back_far = attend_back(first, clear, qkv, starts, mixed_far, inverse_total, cot_far)
    back_home = exchange(back_far, 4).astype(F32)

    def half_of(block):
        gathered = both(block, 0)
        part = gathered.shape[1] // 2
        return lax.dynamic_slice_in_dim(gathered, core * part, part, 1)

    wide = gate_back.shape[1] // RING
    narrow = width // RING
    grads_t = spread_call(
        ffn_parts(),
        (2 * wide + 6 * narrow, 2 * wide + 5 * narrow),
        (
            both(gate_back.T, 1),
            both(up_back.T, 1),
            both(cot_low.T, 1),
            both(middle_low.T, 1),
            half_of(ffn_low),
            half_of(hidden_low),
            half_of(mixed_t.T),
        ),
        (
            jax.ShapeDtypeStruct((wide, width // 2), F32),
            jax.ShapeDtypeStruct((wide, width // 2), F32),
            jax.ShapeDtypeStruct((narrow, gate_back.shape[1] // 2), F32),
            jax.ShapeDtypeStruct((narrow, width // 2), F32),
        ),
        5,
        "spread_ffn",
    )

    query_turned = turn_heads(back_home[:, :HEAD_DIM], pos_local, -1.0)
    key_value = back_home[:, HEAD_DIM:].reshape(KV_HEADS, group, 2 * HEAD_DIM, rows).sum(axis=1)
    key_turned = turn_heads(key_value[:, :HEAD_DIM], pos_local, -1.0)
    query_back, query_terms = head_norm_back(query_raw, query_gain, query_turned)
    key_back, key_terms = head_norm_back(key_raw, key_gain, key_turned)
    query_back = query_back.astype(BF16).reshape(HEADS * HEAD_DIM, rows)
    key_back = key_back.astype(BF16).reshape(KV_HEADS * HEAD_DIM, rows)
    value_back = key_value[:, HEAD_DIM:].astype(BF16).reshape(KV_HEADS * HEAD_DIM, rows)
    back_t = jnp.concatenate([query_back, key_back, value_back], axis=0)
    (qkv_grads,) = spread_call(
        qkv_parts(),
        (128, 128),
        (both(back_t, 1), half_of(normed_low)),
        (jax.ShapeDtypeStruct((128, width // 2), F32),),
        6,
        "spread_qkv",
    )
    grad_normed = (
        dot_dims(query_back, q_full, 0, 1)
        + dot_dims(key_back, k_full, 0, 1)
        + dot_dims(value_back, v_full, 0, 1)
    )
    input_part, attn_terms = rms_back(resid_in, attn_gain, grad_normed)
    d_tokens = (grad_middle + input_part)[None]
    gain_totals = lax.psum(
        (jnp.sum(attn_terms, axis=0), jnp.sum(ffn_terms, axis=0), query_terms, key_terms),
        ("ctx", "fsdp"),
    )
    return (
        output,
        d_tokens,
        gain_totals[0],
        qkv_grads[:64].T,
        qkv_grads[64:96].T,
        qkv_grads[96:].T,
        gain_totals[2],
        gain_totals[3],
        grads_t[3].T,
        gain_totals[1],
        grads_t[0].T,
        grads_t[1].T,
        grads_t[2].T,
    )


def solution(mesh):
    in_specs = (
        P("fsdp", "ctx", None),
        P("fsdp", "ctx"),
        P("fsdp", "ctx"),
        P(),
        P("fsdp", None),
        P("fsdp", None),
        P("fsdp", None),
        P(),
        P(),
        P("fsdp", None),
        P(),
        P("fsdp", None),
        P("fsdp", None),
        P("fsdp", None),
        P("fsdp", "ctx", None),
    )
    out_specs = (
        P("fsdp", "ctx", None),
        P("fsdp", "ctx", None),
        P(),
        P("fsdp", "ctx"),
        P("fsdp", "ctx"),
        P("fsdp", "ctx"),
        P(),
        P(),
        P("fsdp", "ctx"),
        P(),
        P("fsdp", "ctx"),
        P("fsdp", "ctx"),
        P("fsdp", "ctx"),
    )
    chosen = heads_body if (mesh.shape["ctx"], mesh.shape["fsdp"]) == (HEADS, 2) else ring_body
    return jax.shard_map(chosen, mesh=mesh, in_specs=in_specs, out_specs=out_specs, check_vma=False)
```

```python
import functools

import jax
import jax.numpy as jnp
from jax import lax
from jax.experimental import pallas as pl
from jax.experimental.pallas import tpu as pltpu
from jax.sharding import PartitionSpec as P

HEADS = 16
KV_HEADS = 8
HEAD_DIM = 64
HOPS = 8


EPSILON = 1e-05
THETA = 1000000.0
MASKED = -1e30


def from_behind(block, axis, distance):
    devices = range(lax.axis_size(axis))
    route = [(i - distance, i) for i in devices if i - distance in devices]
    return lax.ppermute(block, axis, route)


def rms_norm(values, norm_gain):
    return (
        values * lax.rsqrt(jnp.mean(values * values, axis=-1, keepdims=True) + EPSILON) * norm_gain
    )


def rms_back(values, norm_gain, upstream):
    inverse = lax.rsqrt(jnp.mean(values * values, axis=-1, keepdims=True) + EPSILON)
    scaled = upstream * norm_gain
    row_width = values.shape[-1]
    d_values = (
        inverse * scaled
        - values * inverse**3 * jnp.sum(scaled * values, axis=-1, keepdims=True) / row_width
    )
    return (d_values, upstream * values * inverse)


def rotary(values, positions, turn_sign):
    half_dim = values.shape[-1] // 2
    inverse_freq = THETA ** (-(2.0 / values.shape[-1]) * jnp.arange(half_dim, dtype=jnp.float32))
    angles = positions.astype(jnp.float32)[:, None] * inverse_freq[None, :]
    cosine = jnp.cos(angles)[:, None, :]
    sine_part = turn_sign * jnp.sin(angles)[:, None, :]
    first_half = values[..., :half_dim]
    second_half = values[..., half_dim:]
    return jnp.concatenate(
        [
            first_half * cosine - second_half * sine_part,
            second_half * cosine + first_half * sine_part,
        ],
        axis=-1,
    )


def outer_product(left_mat, right_mat):
    return lax.dot_general(
        left_mat, right_mat, (((0,), (0,)), ((), ())), preferred_element_type=jnp.float32
    )


def against(left_mat, right_mat):
    return lax.dot_general(
        left_mat, right_mat, (((1,), (1,)), ((), ())), preferred_element_type=jnp.float32
    )


def ring_body(
    tokens,
    seg_ids,
    doc_pos,
    attn_gain,
    w_query,
    w_key,
    w_value,
    query_gain,
    key_gain,
    w_out,
    ffn_gain,
    w_gate,
    w_up,
    w_down,
    d_output,
):
    cycle_place = lax.axis_index("ctx")
    tok_rows = tokens.shape[1]
    resid_in = tokens[0].astype(jnp.float32)
    seg_local = seg_ids[0]
    pos_local = doc_pos[0]
    q_per_kv = HEADS // KV_HEADS
    group_cols = q_per_kv * HEAD_DIM
    score_scale = HEAD_DIM ** (-0.5)
    q_full, k_full, v_full, o_full = (
        lax.all_gather(w_query, "fsdp", axis=0, tiled=True),
        lax.all_gather(w_key, "fsdp", axis=0, tiled=True),
        lax.all_gather(w_value, "fsdp", axis=0, tiled=True),
        lax.all_gather(w_out, "fsdp", axis=0, tiled=True),
    )
    gate_full, up_full, down_full = (
        lax.all_gather(w_gate, "fsdp", axis=0, tiled=True),
        lax.all_gather(w_up, "fsdp", axis=0, tiled=True),
        lax.all_gather(w_down, "fsdp", axis=0, tiled=True),
    )
    normed = rms_norm(resid_in, attn_gain)
    normed_low = normed.astype(jnp.bfloat16)
    query_raw = jnp.dot(normed_low, q_full, preferred_element_type=jnp.float32).reshape(
        tok_rows, HEADS, HEAD_DIM
    )
    key_raw = jnp.dot(normed_low, k_full, preferred_element_type=jnp.float32).reshape(
        tok_rows, KV_HEADS, HEAD_DIM
    )
    value_raw = jnp.dot(normed_low, v_full, preferred_element_type=jnp.float32)
    query_rot = rotary(rms_norm(query_raw, query_gain), pos_local, 1.0)
    key_rot = rotary(rms_norm(key_raw, key_gain), pos_local, 1.0)
    query_low = query_rot.astype(jnp.bfloat16).reshape(tok_rows, HEADS * HEAD_DIM)
    key_low = key_rot.astype(jnp.bfloat16).reshape(tok_rows, KV_HEADS * HEAD_DIM)
    value_low = value_raw.astype(jnp.bfloat16)
    own_kv = (key_low, value_low, seg_local)
    kv_blocks = [own_kv]
    carried = own_kv
    for hop_index in range(HOPS):
        carried = from_behind((carried[0], carried[1], carried[2]), "ctx", 1)
        kv_blocks.append(carried)
    key_all = jnp.concatenate([kv_entry[0] for kv_entry in kv_blocks], axis=0)
    value_all = jnp.concatenate([kv_entry[1] for kv_entry in kv_blocks], axis=0)
    seg_all = jnp.concatenate([kv_entry[2] for kv_entry in kv_blocks], axis=0)
    key_owner = cycle_place - jnp.arange(HOPS + 1, dtype=jnp.int32)
    owner_valid = jnp.repeat(key_owner >= 0, tok_rows)
    key_index = (
        key_owner[:, None] * tok_rows + jnp.arange(tok_rows, dtype=jnp.int32)[None, :]
    ).reshape(-1)
    query_index = cycle_place * tok_rows + jnp.arange(tok_rows, dtype=jnp.int32)
    allowed = (
        (seg_local[:, None] == seg_all[None, :])
        & (key_index[None, :] <= query_index[:, None])
        & owner_valid[None, :]
    )

    def group_scores(kv_group):
        query_part = lax.dynamic_slice_in_dim(query_low, kv_group * group_cols, group_cols, 1)
        query_part = query_part.reshape(tok_rows, q_per_kv, HEAD_DIM)
        key_part = lax.dynamic_slice_in_dim(key_all, kv_group * HEAD_DIM, HEAD_DIM, 1)
        value_part = lax.dynamic_slice_in_dim(value_all, kv_group * HEAD_DIM, HEAD_DIM, 1)
        scores = (
            jnp.einsum("trd,kd->rtk", query_part, key_part, preferred_element_type=jnp.float32)
            * score_scale
        )
        return (jnp.where(allowed[None], scores, MASKED), query_part, key_part, value_part)

    def forward_group(kv_group):
        scores, query_part, key_part, value_part = group_scores(kv_group)
        row_top = jnp.max(scores, axis=-1, keepdims=True)
        log_total = row_top + jnp.log(jnp.sum(jnp.exp(scores - row_top), axis=-1, keepdims=True))
        attn_probs = jnp.exp(scores - log_total)
        mixed_part = jnp.einsum(
            "rtk,kd->trd",
            attn_probs.astype(jnp.bfloat16),
            value_part,
            preferred_element_type=jnp.float32,
        )
        return (mixed_part.reshape(tok_rows, group_cols), log_total[..., 0])

    mixed_groups, total_groups = lax.map(forward_group, jnp.arange(KV_HEADS, dtype=jnp.int32))
    mixed = mixed_groups.transpose(1, 0, 2).reshape(tok_rows, HEADS * HEAD_DIM)
    mixed_low = mixed.astype(jnp.bfloat16)
    middle = resid_in + jnp.dot(mixed_low, o_full, preferred_element_type=jnp.float32)
    ffn_low = rms_norm(middle, ffn_gain).astype(jnp.bfloat16)
    gate_pre = jnp.dot(ffn_low, gate_full, preferred_element_type=jnp.float32)
    up_pre = jnp.dot(ffn_low, up_full, preferred_element_type=jnp.float32)
    gate_sig = jax.nn.sigmoid(gate_pre)
    gate_act = gate_pre * gate_sig
    hidden_low = (gate_act * up_pre).astype(jnp.bfloat16)
    result = middle + jnp.dot(hidden_low, down_full, preferred_element_type=jnp.float32)
    output = result.astype(jnp.bfloat16)[None]
    cot_low = d_output[0]
    cotangent = cot_low.astype(jnp.float32)
    grad_w_down = outer_product(hidden_low, cot_low)
    grad_hidden = against(cot_low, down_full)
    gate_back = (grad_hidden * up_pre * (gate_sig * (1.0 + gate_pre * (1.0 - gate_sig)))).astype(
        jnp.bfloat16
    )
    up_back = (grad_hidden * gate_act).astype(jnp.bfloat16)
    grad_w_gate = outer_product(ffn_low, gate_back)
    grad_w_up = outer_product(ffn_low, up_back)
    grad_ffn_in = against(gate_back, gate_full) + against(up_back, up_full)
    middle_part, ffn_terms = rms_back(middle, ffn_gain, grad_ffn_in)
    grad_middle = cotangent + middle_part
    middle_low = grad_middle.astype(jnp.bfloat16)
    grad_w_out = outer_product(mixed_low, middle_low)
    grad_mixed = against(middle_low, o_full).astype(jnp.bfloat16)

    def backward_group(kv_group):
        scores, query_part, key_part, value_part = group_scores(kv_group)
        attn_probs = jnp.exp(scores - total_groups[kv_group][..., None])
        mixed_grad_part = lax.dynamic_slice_in_dim(grad_mixed, kv_group * group_cols, group_cols, 1)
        mixed_grad_part = mixed_grad_part.reshape(tok_rows, q_per_kv, HEAD_DIM)
        grad_probs = jnp.einsum(
            "trd,kd->rtk", mixed_grad_part, value_part, preferred_element_type=jnp.float32
        )
        grad_value = jnp.einsum(
            "rtk,trd->kd",
            attn_probs.astype(jnp.bfloat16),
            mixed_grad_part,
            preferred_element_type=jnp.float32,
        )
        row_delta = jnp.sum(grad_probs * attn_probs, axis=-1, keepdims=True)
        grad_scores = (attn_probs * (grad_probs - row_delta)).astype(jnp.bfloat16)
        grad_query = (
            jnp.einsum("rtk,kd->trd", grad_scores, key_part, preferred_element_type=jnp.float32)
            * score_scale
        )
        grad_key = (
            jnp.einsum("rtk,trd->kd", grad_scores, query_part, preferred_element_type=jnp.float32)
            * score_scale
        )
        return (grad_query.reshape(tok_rows, group_cols), grad_key, grad_value)

    query_groups, key_groups, value_groups = lax.map(
        backward_group, jnp.arange(KV_HEADS, dtype=jnp.int32)
    )
    grad_query_rot = query_groups.transpose(1, 0, 2).reshape(tok_rows, HEADS, HEAD_DIM)
    key_blocks = key_groups.transpose(1, 0, 2).reshape(HOPS + 1, tok_rows, KV_HEADS * HEAD_DIM)
    value_blocks = value_groups.transpose(1, 0, 2).reshape(HOPS + 1, tok_rows, KV_HEADS * HEAD_DIM)
    home_key = key_blocks[HOPS]
    home_value = value_blocks[HOPS]
    for hop_index in range(HOPS, 0, -1):
        moved_key, moved_value = (
            from_behind(home_key.astype(jnp.bfloat16), "ctx", -1).astype(home_key.dtype),
            from_behind(home_value.astype(jnp.bfloat16), "ctx", -1).astype(home_value.dtype),
        )
        home_key = moved_key + key_blocks[hop_index - 1]
        home_value = moved_value + value_blocks[hop_index - 1]
    query_turned = rotary(grad_query_rot, pos_local, -1.0)
    key_turned = rotary(home_key.reshape(tok_rows, KV_HEADS, HEAD_DIM), pos_local, -1.0)
    query_back, query_terms = rms_back(query_raw, query_gain, query_turned)
    key_back, key_terms = rms_back(key_raw, key_gain, key_turned)
    query_back = query_back.reshape(tok_rows, HEADS * HEAD_DIM).astype(jnp.bfloat16)
    key_back = key_back.reshape(tok_rows, KV_HEADS * HEAD_DIM).astype(jnp.bfloat16)
    value_back = home_value.astype(jnp.bfloat16)
    grad_w_query = outer_product(normed_low, query_back)
    grad_w_key = outer_product(normed_low, key_back)
    grad_w_value = outer_product(normed_low, value_back)
    grad_normed = (
        against(query_back, q_full) + against(key_back, k_full) + against(value_back, v_full)
    )
    input_part, attn_terms = rms_back(resid_in, attn_gain, grad_normed)
    d_tokens = (grad_middle + input_part)[None]
    gain_totals = lax.psum(
        (
            jnp.sum(attn_terms, axis=0),
            jnp.sum(ffn_terms, axis=0),
            jnp.sum(query_terms, axis=(0, 1)),
            jnp.sum(key_terms, axis=(0, 1)),
        ),
        ("ctx", "fsdp"),
    )
    weight_grads = (
        grad_w_query,
        grad_w_key,
        grad_w_value,
        grad_w_out,
        grad_w_gate,
        grad_w_up,
        grad_w_down,
    )
    spread = (
        lax.psum_scatter(
            weight_grads[0].astype(jnp.bfloat16), "fsdp", scatter_dimension=0, tiled=True
        ).astype(jnp.float32),
        lax.psum_scatter(
            weight_grads[1].astype(jnp.bfloat16), "fsdp", scatter_dimension=0, tiled=True
        ).astype(jnp.float32),
        lax.psum_scatter(
            weight_grads[2].astype(jnp.bfloat16), "fsdp", scatter_dimension=0, tiled=True
        ).astype(jnp.float32),
        lax.psum_scatter(
            weight_grads[3].astype(jnp.bfloat16), "fsdp", scatter_dimension=0, tiled=True
        ).astype(jnp.float32),
        lax.psum_scatter(
            weight_grads[4].astype(jnp.bfloat16), "fsdp", scatter_dimension=0, tiled=True
        ).astype(jnp.float32),
        lax.psum_scatter(
            weight_grads[5].astype(jnp.bfloat16), "fsdp", scatter_dimension=0, tiled=True
        ).astype(jnp.float32),
        lax.psum_scatter(
            weight_grads[6].astype(jnp.bfloat16), "fsdp", scatter_dimension=0, tiled=True
        ).astype(jnp.float32),
    )
    shares = (
        lax.psum_scatter(spread[0], "ctx", scatter_dimension=1, tiled=True),
        lax.psum_scatter(spread[1], "ctx", scatter_dimension=1, tiled=True),
        lax.psum_scatter(spread[2], "ctx", scatter_dimension=1, tiled=True),
        lax.psum_scatter(spread[3], "ctx", scatter_dimension=1, tiled=True),
        lax.psum_scatter(spread[4], "ctx", scatter_dimension=1, tiled=True),
        lax.psum_scatter(spread[5], "ctx", scatter_dimension=1, tiled=True),
        lax.psum_scatter(spread[6], "ctx", scatter_dimension=1, tiled=True),
    )
    return (
        output,
        d_tokens,
        gain_totals[0],
        shares[0],
        shares[1],
        shares[2],
        gain_totals[2],
        gain_totals[3],
        shares[3],
        gain_totals[1],
        shares[4],
        shares[5],
        shares[6],
    )


MESH = pl.DeviceIdType.MESH
BLOCK = 256
RING = 16
VMEM_SPEC = pl.BlockSpec(memory_space=pltpu.VMEM)
SMEM_SPEC = pl.BlockSpec(memory_space=pltpu.SMEM)
F32 = jnp.float32
BF16 = jnp.bfloat16


def dot_dims(left_mat, right_mat, left_dim, right_dim):
    return lax.dot_general(
        left_mat, right_mat, (((left_dim,), (right_dim,)), ((), ())), preferred_element_type=F32
    )


def exchange_kernel(src, dst, own_sem, send_sem, recv_sem):
    place, core = lax.axis_index("ctx"), lax.axis_index("fsdp")
    barrier = pltpu.get_barrier_semaphore()
    for step in range(1, RING):
        peer = lax.rem(place + step, RING)
        pl.semaphore_signal(barrier, inc=1, device_id=(peer, core), device_id_type=MESH)
    own = pltpu.make_async_copy(src.at[place], dst.at[place], own_sem)
    own.start()
    pl.semaphore_wait(barrier, RING - 1)
    copies = []
    for step in range(1, RING):
        peer = lax.rem(place + step, RING)
        copy = pltpu.make_async_remote_copy(
            src_ref=src.at[peer],
            dst_ref=dst.at[place],
            send_sem=send_sem.at[step],
            recv_sem=recv_sem.at[step],
            device_id=(peer, core),
            device_id_type=MESH,
        )
        copy.start()
        copies.append(copy)
    own.wait()
    for copy in copies:
        copy.wait()


def exchange(blocks, call_id):
    return pl.pallas_call(
        exchange_kernel,
        out_shape=jax.ShapeDtypeStruct(blocks.shape, blocks.dtype),
        in_specs=[VMEM_SPEC],
        out_specs=VMEM_SPEC,
        scratch_shapes=[
            pltpu.SemaphoreType.DMA,
            pltpu.SemaphoreType.DMA((RING,)),
            pltpu.SemaphoreType.DMA((RING,)),
        ],
        compiler_params=pltpu.CompilerParams(collective_id=call_id, has_side_effects=True),
        name="exchange_heads",
    )(blocks)


def transposed(block):
    return block.astype(F32).T.astype(BF16)


def block_probs(key_nat, query_t, first_key, start, query_place, diagonal, masked):
    scores = jnp.dot(key_nat, query_t, preferred_element_type=F32)
    probs = jnp.exp(scores)
    if masked:
        key_place = first_key + lax.broadcasted_iota(jnp.int32, probs.shape, 0)
        ok = key_place >= start
        if diagonal:
            ok = ok & (key_place <= query_place)
        probs = jnp.where(ok, probs, 0.0)
    return probs


def attend_kernel(first_ref, clear_ref, qkv_ref, start_ref, mixed_ref, inv_ref, key_nat):
    blocks = qkv_ref.shape[0]

    def turn(j, carry):
        key_nat[j] = transposed(qkv_ref[j, HEAD_DIM : 2 * HEAD_DIM, :])
        return carry

    lax.fori_loop(0, blocks, turn, 0)

    def per_query(i, nothing):
        query_t = qkv_ref[i, 0:HEAD_DIM, :] * jnp.asarray(HEAD_DIM**-0.5, BF16)
        start = start_ref[i]
        query_place = i * BLOCK + lax.broadcasted_iota(jnp.int32, (1, BLOCK), 1)

        def step(diagonal, masked, j, carry):
            total, acc = carry
            probs = block_probs(
                key_nat[j], query_t, j * BLOCK, start, query_place, diagonal, masked
            )
            total = total + jnp.sum(probs, axis=0, keepdims=True)
            acc = acc + jnp.dot(
                qkv_ref[j, 2 * HEAD_DIM : 3 * HEAD_DIM, :],
                probs.astype(BF16),
                preferred_element_type=F32,
            )
            return total, acc

        carry = (jnp.zeros((1, BLOCK), F32), jnp.zeros((HEAD_DIM, BLOCK), F32))
        carry = lax.fori_loop(
            first_ref[i], clear_ref[i], functools.partial(step, False, True), carry
        )
        carry = lax.fori_loop(clear_ref[i], i, functools.partial(step, False, False), carry)
        total, acc = step(True, True, i, carry)
        inverse = 1.0 / total
        mixed_ref[i] = (acc * inverse).astype(BF16)
        inv_ref[i] = inverse
        return nothing

    lax.fori_loop(0, blocks, per_query, 0)


def attend(first, clear, qkv, start):
    blocks = qkv.shape[0]
    return pl.pallas_call(
        attend_kernel,
        out_shape=(
            jax.ShapeDtypeStruct((blocks, HEAD_DIM, BLOCK), BF16),
            jax.ShapeDtypeStruct((blocks, 1, BLOCK), F32),
        ),
        in_specs=[SMEM_SPEC, SMEM_SPEC, VMEM_SPEC, VMEM_SPEC],
        out_specs=(VMEM_SPEC, VMEM_SPEC),
        scratch_shapes=[pltpu.VMEM((blocks, BLOCK, HEAD_DIM), BF16)],
        name="attend_forward",
    )(first, clear, qkv, start)


def flip(bit, turned):
    return bit + turned - 2 * bit * turned


class Spread:
    def __init__(self, chain, compute, sent, came, send_sems, recv_sems):
        place, self.core = lax.axis_index("ctx"), lax.axis_index("fsdp")
        x, y, self.z = lax.rem(place, 2), lax.rem(place // 2, 2), place // 4
        self.chain = chain
        self.first, self.second = (x, y) if chain == 0 else (y, x)
        self.compute, self.sent, self.came = compute, sent, came
        self.send_sems, self.recv_sems = send_sems, recv_sems

    def at(self, first, second, depth):
        low = second * 2 + first if self.chain == 0 else first * 2 + second
        return depth * 4 + low

    def deep(self, depth):
        return lax.rem(self.z + depth, 4)

    def copy(self, stage, slot):
        if stage == 0:
            peer = self.at(1 - self.first, self.second, self.z)
            source, target, sem = self.sent.at[slot], self.came[0].at[slot], slot
        elif stage == 1:
            peer = self.at(self.first, 1 - self.second, self.z)
            source, target, sem = self.came[0].at[4 + slot], self.came[1].at[slot], 8 + slot
        else:
            peer = self.at(self.first, self.second, self.deep(slot))
            source, target, sem = self.came[0].at[slot], self.came[2].at[slot - 1], 11 + slot
        return pltpu.make_async_remote_copy(
            src_ref=source,
            dst_ref=target,
            send_sem=self.send_sems.at[self.chain, sem],
            recv_sem=self.recv_sems.at[self.chain, sem],
            device_id=(peer, self.core),
            device_id_type=MESH,
        )

    def stage_one(self, turned, depth):
        slot = turned * 4 + depth
        owner = self.at(1 - self.first, flip(self.second, turned), self.deep(depth))
        for row, value in self.compute(self.chain, owner):
            self.sent[slot, row : row + value.shape[0], :] = value.astype(BF16)
        self.copy(0, slot).start()

    def stage_two(self, depth):
        self.copy(0, 4 + depth).wait_recv()
        owner = self.at(self.first, 1 - self.second, self.deep(depth))
        for row, value in self.compute(self.chain, owner):
            window = slice(row, row + value.shape[0])
            value = value + self.came[0][4 + depth, window, :].astype(F32)
            self.came[0][4 + depth, window, :] = value.astype(BF16)
        self.copy(1, depth).start()

    def stage_three(self, depth):
        self.copy(0, depth).wait_recv()
        self.copy(1, depth).wait_recv()
        owner = self.at(self.first, self.second, self.deep(depth))
        for row, value in self.compute(self.chain, owner):
            window = slice(row, row + value.shape[0])
            value = value + self.came[0][depth, window, :].astype(F32)
            value = value + self.came[1][depth, window, :].astype(F32)
            self.came[0][depth, window, :] = value.astype(BF16)
        self.copy(2, depth).start()

    def close(self, finish):
        self.copy(0, 0).wait_recv()
        self.copy(1, 0).wait_recv()
        for depth in range(1, 4):
            self.copy(2, depth).wait_recv()
        owner = self.at(self.first, self.second, self.z)
        for row, value in self.compute(self.chain, owner):
            window = slice(row, row + value.shape[0])
            value = value + self.came[0][0, window, :].astype(F32)
            value = value + self.came[1][0, window, :].astype(F32)
            for depth in range(3):
                value = value + self.came[2][depth, window, :].astype(F32)
            finish(self.chain, row, value)

    def drain(self):
        for slot in range(8):
            self.copy(0, slot).wait_send()
        for depth in range(4):
            self.copy(1, depth).wait_send()
        for depth in range(1, 4):
            self.copy(2, depth).wait_send()


def greet(peers):
    barrier = pltpu.get_barrier_semaphore()
    for peer in peers:
        pl.semaphore_signal(barrier, inc=1, device_id=peer, device_id_type=MESH)
    pl.semaphore_wait(barrier, len(peers))


def turn_into(source, put):
    for column in range(0, source.shape[1], 128):
        put(column, source[:, column : column + 128].astype(F32).T.astype(BF16))


def back_kernel(
    gate_ref,
    up_ref,
    hidden_ref,
    cot_ref,
    middle_ref,
    ffn_ref,
    mixed_ref,
    home_ref,
    qkv_ref,
    start_ref,
    part_ref,
    inv_ref,
    gate_out,
    up_out,
    down_out,
    out_out,
    back_out,
    pair_own,
    pair_far,
    side_own,
    side_far,
    hidden_far,
    ffn_far,
    mixed_far,
    cot_far,
    back_own,
    key_value,
    grad_acc,
    sent_a,
    came_a0,
    came_a1,
    came_a2,
    sent_b,
    came_b0,
    came_b1,
    came_b2,
    send_sems,
    recv_sems,
    cot_send,
    cot_recv,
    back_send,
    back_recv,
    core_send,
    core_recv,
):
    place, core = lax.axis_index("ctx"), lax.axis_index("fsdp")
    blocks = qkv_ref.shape[0]
    wide = pair_own.shape[1] // 2
    narrow = side_own.shape[1] // RING
    half_hidden = hidden_far.shape[1]
    half_width = ffn_far.shape[1]
    scale = HEAD_DIM**-0.5

    greet(
        [(lax.rem(place + step, RING), core) for step in range(1, RING)] + [(place, 1 - core)]
    )

    def cot_copy(step, peer):
        return pltpu.make_async_remote_copy(
            src_ref=home_ref.at[peer],
            dst_ref=cot_far.at[place],
            send_sem=cot_send.at[step],
            recv_sem=cot_recv.at[step],
            device_id=(peer, core),
            device_id_type=MESH,
        )

    for step in range(1, RING):
        cot_copy(step, lax.rem(place + step, RING)).start()
    cot_far[place] = home_ref[place]

    def core_copy(source, target, sem):
        return pltpu.make_async_remote_copy(
            src_ref=source,
            dst_ref=target,
            send_sem=core_send.at[sem],
            recv_sem=core_recv.at[sem],
            device_id=(place, 1 - core),
            device_id_type=MESH,
        )

    def half(part, size):
        return pl.ds(pl.multiple_of(part * size, 128), size)

    def pair_copy(turn_x, turn_y, depth):
        x, y, z = lax.rem(place, 2), lax.rem(place // 2, 2), place // 4
        owner = lax.rem(z + depth, 4) * 4 + flip(y, turn_y) * 2 + flip(x, turn_x)
        return core_copy(
            pair_own.at[owner], pair_far.at[owner], 4 + turn_x * 8 + turn_y * 4 + depth
        )

    sides = [
        core_copy(ffn_ref.at[:, half(1 - core, half_width)], ffn_far, 0),
        core_copy(mixed_ref.at[half(1 - core, half_width), :], mixed_far, 1),
        core_copy(hidden_ref.at[:, half(1 - core, half_hidden)], hidden_far, 2),
        core_copy(side_own, side_far, 3),
    ]
    for copy in sides[:3]:
        copy.start()

    def put_side(which):
        def put(column, value):
            side_own[which, column : column + 128, :] = value

        return put

    turn_into(cot_ref, put_side(0))
    turn_into(middle_ref, put_side(1))
    sides[3].start()

    def put_pair(base):
        def put(column, value):
            done = 0
            while done < 128:
                owner, row = divmod(column + done, wide)
                count = min(128 - done, wide - row)
                pair_own[owner, base + row : base + row + count, :] = value[done : done + count]
                done += count

        return put

    turn_into(gate_ref, put_pair(0))
    turn_into(up_ref, put_pair(wide))
    order = [(1, 1, depth) for depth in (1, 2, 3, 0)]
    for depth in (1, 2, 3, 0):
        order += [(1, 0, depth), (0, 1, depth)]
    order += [(0, 0, depth) for depth in range(4)]
    for turn_x, turn_y, depth in order:
        pair_copy(turn_x, turn_y, depth).start()

    def compute(chain, owner):
        lanes = pl.ds(chain * 256, 256)
        own_lanes = pl.ds(pl.multiple_of(core * half_width + chain * 256, 128), 256)
        both_pair = jnp.dot(pair_own[owner], ffn_ref[:, own_lanes], preferred_element_type=F32)
        both_pair += jnp.dot(pair_far[owner], ffn_far[:, lanes], preferred_element_type=F32)
        values = [(0, both_pair)]
        rows = pl.ds(pl.multiple_of(owner * narrow, 16), narrow)
        begin, chunks = (0, 5) if chain == 0 else (5, 4)
        cols = pl.ds(pl.multiple_of(core * half_hidden + begin * 256, 128), chunks * 256)
        down = jnp.dot(side_own[0, rows, :], hidden_ref[:, cols], preferred_element_type=F32)
        down += jnp.dot(
            side_far[0, rows, :],
            hidden_far[:, begin * 256 : (begin + chunks) * 256],
            preferred_element_type=F32,
        )
        row = 2 * wide
        for chunk in range(chunks):
            values.append((row, down[:, chunk * 256 : chunk * 256 + 256]))
            row += narrow
        out = dot_dims(side_own[1, rows, :], mixed_ref[own_lanes, :], 1, 1)
        out += dot_dims(side_far[1, rows, :], mixed_far[lanes, :], 1, 1)
        values.append((row, out))
        return values

    def finish(chain, row, value):
        lanes = slice(chain * 256, chain * 256 + 256)
        if row == 0:
            gate_out[:, lanes] = value[:wide]
            up_out[:, lanes] = value[wide:]
            return
        chunk = (row - 2 * wide) // narrow
        if chunk == 5 - chain:
            out_out[:, lanes] = value
        else:
            chunk += 5 * chain
            down_out[:, chunk * 256 : chunk * 256 + 256] = value

    chains = (
        Spread(0, compute, sent_a, (came_a0, came_a1, came_a2), send_sems, recv_sems),
        Spread(1, compute, sent_b, (came_b0, came_b1, came_b2), send_sems, recv_sems),
    )
    for copy in sides:
        copy.wait_recv()

    def one_near(index, nothing):
        depth = lax.rem(index + 1, 4)
        pair_copy(1, 1, depth).wait_recv()
        for chain in chains:
            chain.stage_one(1, depth)
        return nothing

    def one_far(index, nothing):
        depth = lax.rem(index + 1, 4)
        pair_copy(1, 0, depth).wait_recv()
        pair_copy(0, 1, depth).wait_recv()
        for chain in chains:
            chain.stage_one(0, depth)
        return nothing

    lax.fori_loop(0, 4, one_near, 0)
    lax.fori_loop(0, 4, one_far, 0)

    key_value[0] = jnp.zeros(key_value.shape[1:], BF16)

    def prepare(j, nothing):
        packed = qkv_ref[j, HEAD_DIM : 3 * HEAD_DIM, :].astype(F32)
        key_value[j + 1] = packed.T.astype(BF16)
        grad_acc[j + 1] = jnp.zeros(grad_acc.shape[1:], F32)
        return nothing

    grad_acc[0] = jnp.zeros(grad_acc.shape[1:], F32)
    lax.fori_loop(0, blocks, prepare, 0)

    def back_copy(step, peer):
        return pltpu.make_async_remote_copy(
            src_ref=back_own.at[peer],
            dst_ref=back_out.at[place],
            send_sem=back_send.at[step],
            recv_sem=back_recv.at[step],
            device_id=(peer, core),
            device_id_type=MESH,
        )

    def flush(j):
        turned = grad_acc[j + 1].T.astype(BF16)
        back_own[j, HEAD_DIM : 3 * HEAD_DIM, :] = turned

        @pl.when(j != place)
        def _():
            back_copy(lax.rem(j - place + RING, RING), j).start()

    def per_query(i, nothing):
        @pl.when(i != place)
        def _():
            step = lax.rem(place - i + RING, RING)
            cot_copy(step, lax.rem(place + step, RING)).wait_recv()

        empty = jnp.zeros((HEAD_DIM, BLOCK), BF16)
        query = qkv_ref[i, 0:HEAD_DIM, :] * jnp.asarray(scale, BF16)
        query_t = jnp.concatenate([query, empty], axis=0)
        cot = cot_far[i]
        cot_t = jnp.concatenate([empty, cot], axis=0)
        query_nat = transposed(query_t)
        cot_nat = transposed(cot_t)
        start = start_ref[i]
        inverse = inv_ref[i]
        delta = jnp.sum(cot.astype(F32) * part_ref[i].astype(F32), axis=0, keepdims=True)
        query_place = i * BLOCK + lax.broadcasted_iota(jnp.int32, (1, BLOCK), 1)

        def step(diagonal, j):
            block = key_value[j + 1]
            scores = jnp.dot(block, query_t, preferred_element_type=F32)
            grad_probs = jnp.dot(block, cot_t, preferred_element_type=F32)
            key_place = j * BLOCK + lax.broadcasted_iota(jnp.int32, scores.shape, 0)
            ok = key_place >= start
            if diagonal:
                ok = ok & (key_place <= query_place)
            probs = jnp.where(ok, jnp.exp(scores) * inverse, 0.0)
            grad_scores = (probs * (grad_probs - delta)).astype(BF16)
            update = jnp.dot(grad_scores, query_nat, preferred_element_type=F32)
            update += jnp.dot(probs.astype(BF16), cot_nat, preferred_element_type=F32)
            grad_acc[j + 1] += update
            return jnp.dot(
                qkv_ref[jnp.maximum(j, 0), HEAD_DIM : 2 * HEAD_DIM, :],
                grad_scores,
                preferred_element_type=F32,
            )

        pairs = (jnp.minimum(i, 8) + 1) // 2

        def two(index, acc):
            j = i - 2 * pairs + 2 * index
            return acc + step(False, j) + step(False, j + 1)

        acc = lax.fori_loop(0, pairs, two, step(True, i))
        back_own[i, 0:HEAD_DIM, :] = (acc * scale).astype(BF16)

        @pl.when(i >= 8)
        def _():
            flush(i - 8)

        @pl.when((i >= 8) & (lax.rem(i, 2) == 0))
        def _():
            depth = lax.rem((i - 8) // 2 + 1, 4)
            for chain in chains:
                chain.stage_two(depth)

        return nothing

    lax.fori_loop(0, blocks, per_query, 0)

    def rest(j, nothing):
        flush(j)
        return nothing

    lax.fori_loop(blocks - 8, blocks, rest, 0)
    back_out[place] = back_own[place]
    for depth in range(4):
        pair_copy(0, 0, depth).wait_recv()

    def three(depth, nothing):
        for chain in chains:
            chain.stage_three(depth)
        return nothing

    lax.fori_loop(1, 4, three, 0)
    for chain in chains:
        chain.close(finish)

    def settle(step, nothing):
        peer = lax.rem(place + step, RING)
        back_copy(step, peer).wait()
        cot_copy(step, peer).wait_send()
        return nothing

    lax.fori_loop(1, RING, settle, 0)
    for copy in sides:
        copy.wait_send()
    for turn_x, turn_y, depth in order:
        pair_copy(turn_x, turn_y, depth).wait_send()
    for chain in chains:
        chain.drain()


def back_call(call_id, *inputs):
    gate_back, qkv = inputs[0], inputs[8]
    rows, hidden_width = gate_back.shape
    width = inputs[3].shape[1]
    blocks = qkv.shape[0]
    wide, narrow = hidden_width // RING, width // RING
    chain_rows = (2 * wide + 6 * narrow, 2 * wide + 5 * narrow)
    buffers = [
        pltpu.VMEM((slots, chain_rows[chain], 256), BF16)
        for chain in range(2)
        for slots in (8, 8, 4, 3)
    ]
    return pl.pallas_call(
        back_kernel,
        out_shape=(
            jax.ShapeDtypeStruct((wide, width // 2), F32),
            jax.ShapeDtypeStruct((wide, width // 2), F32),
            jax.ShapeDtypeStruct((narrow, hidden_width // 2), F32),
            jax.ShapeDtypeStruct((narrow, width // 2), F32),
            jax.ShapeDtypeStruct(qkv.shape, BF16),
        ),
        in_specs=[VMEM_SPEC] * len(inputs),
        out_specs=(VMEM_SPEC,) * 5,
        scratch_shapes=[
            pltpu.VMEM((RING, 2 * wide, rows), BF16),
            pltpu.VMEM((RING, 2 * wide, rows), BF16),
            pltpu.VMEM((2, width, rows), BF16),
            pltpu.VMEM((2, width, rows), BF16),
            pltpu.VMEM((rows, hidden_width // 2), BF16),
            pltpu.VMEM((rows, width // 2), BF16),
            pltpu.VMEM((width // 2, rows), BF16),
            pltpu.VMEM((blocks, HEAD_DIM, BLOCK), BF16),
            pltpu.VMEM(qkv.shape, BF16),
            pltpu.VMEM((blocks + 1, BLOCK, 2 * HEAD_DIM), BF16),
            pltpu.VMEM((blocks + 1, BLOCK, 2 * HEAD_DIM), F32),
        ]
        + buffers
        + [
            pltpu.SemaphoreType.DMA((2, 15)),
            pltpu.SemaphoreType.DMA((2, 15)),
            pltpu.SemaphoreType.DMA((RING,)),
            pltpu.SemaphoreType.DMA((RING,)),
            pltpu.SemaphoreType.DMA((RING,)),
            pltpu.SemaphoreType.DMA((RING,)),
            pltpu.SemaphoreType.DMA((20,)),
            pltpu.SemaphoreType.DMA((20,)),
        ],
        compiler_params=pltpu.CompilerParams(
            collective_id=call_id, has_side_effects=True, vmem_limit_bytes=63 << 20
        ),
        name="backward_spread",
    )(*inputs)


def spread_kernel(parts, rows, n_in, n_out, *refs):
    inputs, outputs, scratch = refs[:n_in], refs[n_in : n_in + n_out], refs[n_in + n_out :]
    sent = (scratch[0:3], scratch[3:6])
    came = (scratch[6:9], scratch[9:12])
    send_sems, recv_sems = scratch[12], scratch[13]
    compute, finish = parts
    place, core = lax.axis_index("ctx"), lax.axis_index("fsdp")
    x, y, z = lax.rem(place, 2), lax.rem(place // 2, 2), place // 4

    def at(chain, first, second, depth):
        if chain == 0:
            return depth * 4 + second * 2 + first
        return depth * 4 + first * 2 + second

    coords = ((x, y), (y, x))
    barrier = pltpu.get_barrier_semaphore()
    peers = [at(0, 1 - x, y, z), at(0, x, 1 - y, z)]
    peers += [at(0, x, y, lax.rem(z + step, 4)) for step in range(1, 4)]
    for peer in peers:
        pl.semaphore_signal(barrier, inc=1, device_id=(peer, core), device_id_type=MESH)
    pl.semaphore_wait(barrier, len(peers))

    def copy(chain, stage, slot, sem, peer):
        return pltpu.make_async_remote_copy(
            src_ref=sent[chain][stage].at[slot],
            dst_ref=came[chain][stage].at[slot],
            send_sem=send_sems.at[chain, sem],
            recv_sem=recv_sems.at[chain, sem],
            device_id=(peer, core),
            device_id_type=MESH,
        )

    def one(index, nothing):
        turned = 1 - index // 4
        depth = lax.rem(index + 1, 4)
        slot = turned * 4 + depth
        for chain in range(2):
            first, second = coords[chain]
            other = second + turned - 2 * second * turned
            owner = at(chain, 1 - first, other, lax.rem(z + depth, 4))
            for row, value in compute(chain, owner, inputs):
                sent[chain][0][slot, row : row + value.shape[0], :] = value.astype(BF16)
            copy(chain, 0, slot, slot, at(chain, 1 - first, second, z)).start()
        return nothing

    lax.fori_loop(0, 8, one, 0)

    def two(index, nothing):
        depth = lax.rem(index + 1, 4)
        for chain in range(2):
            first, second = coords[chain]
            copy(chain, 0, 4 + depth, 4 + depth, at(chain, 1 - first, second, z)).wait_recv()
            owner = at(chain, first, 1 - second, lax.rem(z + depth, 4))
            for row, value in compute(chain, owner, inputs):
                window = slice(row, row + value.shape[0])
                value = value + came[chain][0][4 + depth, window, :].astype(F32)
                sent[chain][1][depth, window, :] = value.astype(BF16)
            copy(chain, 1, depth, 8 + depth, at(chain, first, 1 - second, z)).start()
        return nothing

    lax.fori_loop(0, 4, two, 0)

    def three(depth, nothing):
        for chain in range(2):
            first, second = coords[chain]
            copy(chain, 0, depth, depth, at(chain, 1 - first, second, z)).wait_recv()
            copy(chain, 1, depth, 8 + depth, at(chain, first, 1 - second, z)).wait_recv()
            far = at(chain, first, second, lax.rem(z + depth, 4))
            for row, value in compute(chain, far, inputs):
                window = slice(row, row + value.shape[0])
                value = value + came[chain][0][depth, window, :].astype(F32)
                value = value + came[chain][1][depth, window, :].astype(F32)
                sent[chain][2][depth - 1, window, :] = value.astype(BF16)
            copy(chain, 2, depth - 1, 11 + depth, far).start()
        return nothing

    lax.fori_loop(1, 4, three, 0)

    for chain in range(2):
        first, second = coords[chain]
        copy(chain, 0, 0, 0, at(chain, 1 - first, second, z)).wait_recv()
        copy(chain, 1, 0, 8, at(chain, first, 1 - second, z)).wait_recv()
        for depth in range(1, 4):
            far = at(chain, first, second, lax.rem(z + depth, 4))
            copy(chain, 2, depth - 1, 11 + depth, far).wait_recv()
        for row, value in compute(chain, place, inputs):
            window = slice(row, row + value.shape[0])
            value = value + came[chain][0][0, window, :].astype(F32)
            value = value + came[chain][1][0, window, :].astype(F32)
            for depth in range(3):
                value = value + came[chain][2][depth, window, :].astype(F32)
            finish(chain, row, value, outputs)
        for slot in range(8):
            copy(chain, 0, slot, slot, at(chain, 1 - first, second, z)).wait_send()
        for depth in range(4):
            copy(chain, 1, depth, 8 + depth, at(chain, first, 1 - second, z)).wait_send()
        for depth in range(1, 4):
            far = at(chain, first, second, lax.rem(z + depth, 4))
            copy(chain, 2, depth - 1, 11 + depth, far).wait_send()


def spread_call(parts, rows, inputs, out_shape, call_id, name):
    lanes = 256
    buffers = [
        pltpu.VMEM((slots, rows[chain], lanes), BF16) for chain in range(2) for slots in (8, 4, 3)
    ]
    return pl.pallas_call(
        functools.partial(spread_kernel, parts, rows, len(inputs), len(out_shape)),
        out_shape=out_shape,
        in_specs=[VMEM_SPEC] * len(inputs),
        out_specs=tuple([VMEM_SPEC] * len(out_shape)),
        scratch_shapes=buffers
        + buffers
        + [pltpu.SemaphoreType.DMA((2, 15)), pltpu.SemaphoreType.DMA((2, 15))],
        compiler_params=pltpu.CompilerParams(
            collective_id=call_id, has_side_effects=True, vmem_limit_bytes=60 << 20
        ),
        name=name,
    )(*inputs)


def rows_of(ref, owner, count, base=0):
    return ref[pl.ds(pl.multiple_of(base + owner * count, 16), count), :]


def qkv_parts():
    def compute(chain, owner, inputs):
        back_t, normed = inputs
        lanes = slice(chain * 256, chain * 256 + 256)
        values = []
        row, base = 0, 0
        for count in (64, 32, 32):
            values.append(
                (
                    row,
                    jnp.dot(
                        rows_of(back_t, owner, count, base),
                        normed[:, lanes],
                        preferred_element_type=F32,
                    ),
                )
            )
            row += count
            base += count * RING
        return values

    def finish(chain, row, value, outputs):
        outputs[0][row : row + value.shape[0], chain * 256 : chain * 256 + 256] = value

    return compute, finish


def turn_heads(values_t, positions, sign):
    half = HEAD_DIM // 2
    inverse_freq = THETA ** (-(2.0 / HEAD_DIM) * jnp.arange(half, dtype=F32))
    angles = inverse_freq[:, None] * positions.astype(F32)[None, :]
    cosine, sine = jnp.cos(angles)[None], sign * jnp.sin(angles)[None]
    first, second = values_t[:, :half], values_t[:, half:]
    return jnp.concatenate(
        [first * cosine - second * sine, second * cosine + first * sine], axis=1
    )


def head_norm(values_t, gain):
    mean = jnp.mean(values_t * values_t, axis=1, keepdims=True)
    return values_t * lax.rsqrt(mean + EPSILON) * gain[None, :, None]


def head_norm_back(values_t, gain, upstream):
    inverse = lax.rsqrt(jnp.mean(values_t * values_t, axis=1, keepdims=True) + EPSILON)
    scaled = upstream * gain[None, :, None]
    d_values = (
        inverse * scaled
        - values_t
        * inverse**3
        * jnp.sum(scaled * values_t, axis=1, keepdims=True)
        / values_t.shape[1]
    )
    return d_values, jnp.sum(upstream * values_t * inverse, axis=(0, 2))


def both(block, axis):
    return lax.all_gather(block, "fsdp", axis=axis, tiled=True)


def heads_body(
    tokens,
    seg_ids,
    doc_pos,
    attn_gain,
    w_query,
    w_key,
    w_value,
    query_gain,
    key_gain,
    w_out,
    ffn_gain,
    w_gate,
    w_up,
    w_down,
    d_output,
):
    place, core = lax.axis_index("ctx"), lax.axis_index("fsdp")
    rows, width = tokens.shape[1], tokens.shape[2]
    resid_in = tokens[0].astype(F32)
    pos_local = doc_pos[0]
    q_full, k_full, v_full, o_full = (
        both(w_query, 0),
        both(w_key, 0),
        both(w_value, 0),
        both(w_out, 0),
    )
    gate_full, up_full, down_full = both(w_gate, 0), both(w_up, 0), both(w_down, 0)
    starts_local = place * rows + jnp.arange(rows, dtype=jnp.int32) - pos_local
    starts = lax.all_gather(starts_local, "ctx", axis=0, tiled=False)
    first = starts[:, 0] // BLOCK
    own_index = jnp.arange(RING, dtype=jnp.int32)
    clear = jnp.minimum((starts[:, -1] + BLOCK - 1) // BLOCK, own_index)
    starts = starts[:, None, :]

    normed_low = rms_norm(resid_in, attn_gain).astype(BF16)
    query_raw = dot_dims(q_full, normed_low, 0, 1).reshape(HEADS, HEAD_DIM, rows)
    key_raw = dot_dims(k_full, normed_low, 0, 1).reshape(KV_HEADS, HEAD_DIM, rows)
    value_raw = dot_dims(v_full, normed_low, 0, 1).reshape(KV_HEADS, HEAD_DIM, rows)
    query_low = turn_heads(head_norm(query_raw, query_gain), pos_local, 1.0).astype(BF16)
    key_low = turn_heads(head_norm(key_raw, key_gain), pos_local, 1.0).astype(BF16)
    value_low = value_raw.astype(BF16)
    group = HEADS // KV_HEADS
    qkv_home = jnp.concatenate(
        [query_low, jnp.repeat(key_low, group, axis=0), jnp.repeat(value_low, group, axis=0)],
        axis=1,
    )
    qkv = exchange(qkv_home, 1)
    mixed_far, inverse_total = attend(first, clear, qkv, starts)
    mixed_t = exchange(mixed_far, 2).reshape(HEADS * HEAD_DIM, rows)

    middle = resid_in + dot_dims(mixed_t, o_full, 0, 0)
    ffn_low = rms_norm(middle, ffn_gain).astype(BF16)
    gate_pre = jnp.dot(ffn_low, gate_full, preferred_element_type=F32)
    up_pre = jnp.dot(ffn_low, up_full, preferred_element_type=F32)
    gate_sig = jax.nn.sigmoid(gate_pre)
    gate_act = gate_pre * gate_sig
    hidden_low = (gate_act * up_pre).astype(BF16)
    result = middle + jnp.dot(hidden_low, down_full, preferred_element_type=F32)
    output = result.astype(BF16)[None]
    cot_low = d_output[0]
    cotangent = cot_low.astype(F32)
    grad_hidden = against(cot_low, down_full)
    gate_back = (grad_hidden * up_pre * (gate_sig * (1.0 + gate_pre * (1.0 - gate_sig)))).astype(
        BF16
    )
    up_back = (grad_hidden * gate_act).astype(BF16)
    grad_ffn_in = against(gate_back, gate_full) + against(up_back, up_full)
    middle_part, ffn_terms = rms_back(middle, ffn_gain, grad_ffn_in)
    grad_middle = cotangent + middle_part
    middle_low = grad_middle.astype(BF16)
    grad_mixed = dot_dims(o_full, middle_low, 1, 1).astype(BF16)

    gate_t, up_t, down_t, out_t, back_home = back_call(
        3,
        gate_back,
        up_back,
        hidden_low,
        cot_low,
        middle_low,
        ffn_low,
        mixed_t,
        grad_mixed.reshape(HEADS, HEAD_DIM, rows),
        qkv,
        starts,
        mixed_far,
        inverse_total,
    )
    back_home = back_home.astype(F32)

    def half_of(block):
        gathered = both(block, 0)
        part = gathered.shape[1] // 2
        return lax.dynamic_slice_in_dim(gathered, core * part, part, 1)

    query_turned = turn_heads(back_home[:, :HEAD_DIM], pos_local, -1.0)
    key_value = back_home[:, HEAD_DIM:].reshape(KV_HEADS, group, 2 * HEAD_DIM, rows).sum(axis=1)
    key_turned = turn_heads(key_value[:, :HEAD_DIM], pos_local, -1.0)
    query_back, query_terms = head_norm_back(query_raw, query_gain, query_turned)
    key_back, key_terms = head_norm_back(key_raw, key_gain, key_turned)
    query_back = query_back.astype(BF16).reshape(HEADS * HEAD_DIM, rows)
    key_back = key_back.astype(BF16).reshape(KV_HEADS * HEAD_DIM, rows)
    value_back = key_value[:, HEAD_DIM:].astype(BF16).reshape(KV_HEADS * HEAD_DIM, rows)
    back_t = jnp.concatenate([query_back, key_back, value_back], axis=0)
    (qkv_grads,) = spread_call(
        qkv_parts(),
        (128, 128),
        (both(back_t, 1), half_of(normed_low)),
        (jax.ShapeDtypeStruct((128, width // 2), F32),),
        6,
        "spread_qkv",
    )
    grad_normed = (
        dot_dims(query_back, q_full, 0, 1)
        + dot_dims(key_back, k_full, 0, 1)
        + dot_dims(value_back, v_full, 0, 1)
    )
    input_part, attn_terms = rms_back(resid_in, attn_gain, grad_normed)
    d_tokens = (grad_middle + input_part)[None]
    gain_totals = lax.psum(
        (jnp.sum(attn_terms, axis=0), jnp.sum(ffn_terms, axis=0), query_terms, key_terms),
        ("ctx", "fsdp"),
    )
    return (
        output,
        d_tokens,
        gain_totals[0],
        qkv_grads[:64].T,
        qkv_grads[64:96].T,
        qkv_grads[96:].T,
        gain_totals[2],
        gain_totals[3],
        out_t.T,
        gain_totals[1],
        gate_t.T,
        up_t.T,
        down_t.T,
    )


def solution(mesh):
    in_specs = (
        P("fsdp", "ctx", None),
        P("fsdp", "ctx"),
        P("fsdp", "ctx"),
        P(),
        P("fsdp", None),
        P("fsdp", None),
        P("fsdp", None),
        P(),
        P(),
        P("fsdp", None),
        P(),
        P("fsdp", None),
        P("fsdp", None),
        P("fsdp", None),
        P("fsdp", "ctx", None),
    )
    out_specs = (
        P("fsdp", "ctx", None),
        P("fsdp", "ctx", None),
        P(),
        P("fsdp", "ctx"),
        P("fsdp", "ctx"),
        P("fsdp", "ctx"),
        P(),
        P(),
        P("fsdp", "ctx"),
        P(),
        P("fsdp", "ctx"),
        P("fsdp", "ctx"),
        P("fsdp", "ctx"),
    )
    chosen = heads_body if (mesh.shape["ctx"], mesh.shape["fsdp"]) == (HEADS, 2) else ring_body
    return jax.shard_map(chosen, mesh=mesh, in_specs=in_specs, out_specs=out_specs, check_vma=False)
```

```python
import functools

import jax
import jax.numpy as jnp
from jax import lax
from jax.experimental import pallas as pl
from jax.experimental.pallas import tpu as pltpu
from jax.sharding import PartitionSpec as P

HEADS = 16
KV_HEADS = 8
HEAD_DIM = 64
HOPS = 8


EPSILON = 1e-05
THETA = 1000000.0
MASKED = -1e30


def from_behind(block, axis, distance):
    devices = range(lax.axis_size(axis))
    route = [(i - distance, i) for i in devices if i - distance in devices]
    return lax.ppermute(block, axis, route)


def rms_norm(values, norm_gain):
    return (
        values * lax.rsqrt(jnp.mean(values * values, axis=-1, keepdims=True) + EPSILON) * norm_gain
    )


def rms_back(values, norm_gain, upstream):
    inverse = lax.rsqrt(jnp.mean(values * values, axis=-1, keepdims=True) + EPSILON)
    scaled = upstream * norm_gain
    row_width = values.shape[-1]
    d_values = (
        inverse * scaled
        - values * inverse**3 * jnp.sum(scaled * values, axis=-1, keepdims=True) / row_width
    )
    return (d_values, upstream * values * inverse)


def rotary(values, positions, turn_sign):
    half_dim = values.shape[-1] // 2
    inverse_freq = THETA ** (-(2.0 / values.shape[-1]) * jnp.arange(half_dim, dtype=jnp.float32))
    angles = positions.astype(jnp.float32)[:, None] * inverse_freq[None, :]
    cosine = jnp.cos(angles)[:, None, :]
    sine_part = turn_sign * jnp.sin(angles)[:, None, :]
    first_half = values[..., :half_dim]
    second_half = values[..., half_dim:]
    return jnp.concatenate(
        [
            first_half * cosine - second_half * sine_part,
            second_half * cosine + first_half * sine_part,
        ],
        axis=-1,
    )


def outer_product(left_mat, right_mat):
    return lax.dot_general(
        left_mat, right_mat, (((0,), (0,)), ((), ())), preferred_element_type=jnp.float32
    )


def against(left_mat, right_mat):
    return lax.dot_general(
        left_mat, right_mat, (((1,), (1,)), ((), ())), preferred_element_type=jnp.float32
    )


def ring_body(
    tokens,
    seg_ids,
    doc_pos,
    attn_gain,
    w_query,
    w_key,
    w_value,
    query_gain,
    key_gain,
    w_out,
    ffn_gain,
    w_gate,
    w_up,
    w_down,
    d_output,
):
    cycle_place = lax.axis_index("ctx")
    tok_rows = tokens.shape[1]
    resid_in = tokens[0].astype(jnp.float32)
    seg_local = seg_ids[0]
    pos_local = doc_pos[0]
    q_per_kv = HEADS // KV_HEADS
    group_cols = q_per_kv * HEAD_DIM
    score_scale = HEAD_DIM ** (-0.5)
    q_full, k_full, v_full, o_full = (
        lax.all_gather(w_query, "fsdp", axis=0, tiled=True),
        lax.all_gather(w_key, "fsdp", axis=0, tiled=True),
        lax.all_gather(w_value, "fsdp", axis=0, tiled=True),
        lax.all_gather(w_out, "fsdp", axis=0, tiled=True),
    )
    gate_full, up_full, down_full = (
        lax.all_gather(w_gate, "fsdp", axis=0, tiled=True),
        lax.all_gather(w_up, "fsdp", axis=0, tiled=True),
        lax.all_gather(w_down, "fsdp", axis=0, tiled=True),
    )
    normed = rms_norm(resid_in, attn_gain)
    normed_low = normed.astype(jnp.bfloat16)
    query_raw = jnp.dot(normed_low, q_full, preferred_element_type=jnp.float32).reshape(
        tok_rows, HEADS, HEAD_DIM
    )
    key_raw = jnp.dot(normed_low, k_full, preferred_element_type=jnp.float32).reshape(
        tok_rows, KV_HEADS, HEAD_DIM
    )
    value_raw = jnp.dot(normed_low, v_full, preferred_element_type=jnp.float32)
    query_rot = rotary(rms_norm(query_raw, query_gain), pos_local, 1.0)
    key_rot = rotary(rms_norm(key_raw, key_gain), pos_local, 1.0)
    query_low = query_rot.astype(jnp.bfloat16).reshape(tok_rows, HEADS * HEAD_DIM)
    key_low = key_rot.astype(jnp.bfloat16).reshape(tok_rows, KV_HEADS * HEAD_DIM)
    value_low = value_raw.astype(jnp.bfloat16)
    own_kv = (key_low, value_low, seg_local)
    kv_blocks = [own_kv]
    carried = own_kv
    for hop_index in range(HOPS):
        carried = from_behind((carried[0], carried[1], carried[2]), "ctx", 1)
        kv_blocks.append(carried)
    key_all = jnp.concatenate([kv_entry[0] for kv_entry in kv_blocks], axis=0)
    value_all = jnp.concatenate([kv_entry[1] for kv_entry in kv_blocks], axis=0)
    seg_all = jnp.concatenate([kv_entry[2] for kv_entry in kv_blocks], axis=0)
    key_owner = cycle_place - jnp.arange(HOPS + 1, dtype=jnp.int32)
    owner_valid = jnp.repeat(key_owner >= 0, tok_rows)
    key_index = (
        key_owner[:, None] * tok_rows + jnp.arange(tok_rows, dtype=jnp.int32)[None, :]
    ).reshape(-1)
    query_index = cycle_place * tok_rows + jnp.arange(tok_rows, dtype=jnp.int32)
    allowed = (
        (seg_local[:, None] == seg_all[None, :])
        & (key_index[None, :] <= query_index[:, None])
        & owner_valid[None, :]
    )

    def group_scores(kv_group):
        query_part = lax.dynamic_slice_in_dim(query_low, kv_group * group_cols, group_cols, 1)
        query_part = query_part.reshape(tok_rows, q_per_kv, HEAD_DIM)
        key_part = lax.dynamic_slice_in_dim(key_all, kv_group * HEAD_DIM, HEAD_DIM, 1)
        value_part = lax.dynamic_slice_in_dim(value_all, kv_group * HEAD_DIM, HEAD_DIM, 1)
        scores = (
            jnp.einsum("trd,kd->rtk", query_part, key_part, preferred_element_type=jnp.float32)
            * score_scale
        )
        return (jnp.where(allowed[None], scores, MASKED), query_part, key_part, value_part)

    def forward_group(kv_group):
        scores, query_part, key_part, value_part = group_scores(kv_group)
        row_top = jnp.max(scores, axis=-1, keepdims=True)
        log_total = row_top + jnp.log(jnp.sum(jnp.exp(scores - row_top), axis=-1, keepdims=True))
        attn_probs = jnp.exp(scores - log_total)
        mixed_part = jnp.einsum(
            "rtk,kd->trd",
            attn_probs.astype(jnp.bfloat16),
            value_part,
            preferred_element_type=jnp.float32,
        )
        return (mixed_part.reshape(tok_rows, group_cols), log_total[..., 0])

    mixed_groups, total_groups = lax.map(forward_group, jnp.arange(KV_HEADS, dtype=jnp.int32))
    mixed = mixed_groups.transpose(1, 0, 2).reshape(tok_rows, HEADS * HEAD_DIM)
    mixed_low = mixed.astype(jnp.bfloat16)
    middle = resid_in + jnp.dot(mixed_low, o_full, preferred_element_type=jnp.float32)
    ffn_low = rms_norm(middle, ffn_gain).astype(jnp.bfloat16)
    gate_pre = jnp.dot(ffn_low, gate_full, preferred_element_type=jnp.float32)
    up_pre = jnp.dot(ffn_low, up_full, preferred_element_type=jnp.float32)
    gate_sig = jax.nn.sigmoid(gate_pre)
    gate_act = gate_pre * gate_sig
    hidden_low = (gate_act * up_pre).astype(jnp.bfloat16)
    result = middle + jnp.dot(hidden_low, down_full, preferred_element_type=jnp.float32)
    output = result.astype(jnp.bfloat16)[None]
    cot_low = d_output[0]
    cotangent = cot_low.astype(jnp.float32)
    grad_w_down = outer_product(hidden_low, cot_low)
    grad_hidden = against(cot_low, down_full)
    gate_back = (grad_hidden * up_pre * (gate_sig * (1.0 + gate_pre * (1.0 - gate_sig)))).astype(
        jnp.bfloat16
    )
    up_back = (grad_hidden * gate_act).astype(jnp.bfloat16)
    grad_w_gate = outer_product(ffn_low, gate_back)
    grad_w_up = outer_product(ffn_low, up_back)
    grad_ffn_in = against(gate_back, gate_full) + against(up_back, up_full)
    middle_part, ffn_terms = rms_back(middle, ffn_gain, grad_ffn_in)
    grad_middle = cotangent + middle_part
    middle_low = grad_middle.astype(jnp.bfloat16)
    grad_w_out = outer_product(mixed_low, middle_low)
    grad_mixed = against(middle_low, o_full).astype(jnp.bfloat16)

    def backward_group(kv_group):
        scores, query_part, key_part, value_part = group_scores(kv_group)
        attn_probs = jnp.exp(scores - total_groups[kv_group][..., None])
        mixed_grad_part = lax.dynamic_slice_in_dim(grad_mixed, kv_group * group_cols, group_cols, 1)
        mixed_grad_part = mixed_grad_part.reshape(tok_rows, q_per_kv, HEAD_DIM)
        grad_probs = jnp.einsum(
            "trd,kd->rtk", mixed_grad_part, value_part, preferred_element_type=jnp.float32
        )
        grad_value = jnp.einsum(
            "rtk,trd->kd",
            attn_probs.astype(jnp.bfloat16),
            mixed_grad_part,
            preferred_element_type=jnp.float32,
        )
        row_delta = jnp.sum(grad_probs * attn_probs, axis=-1, keepdims=True)
        grad_scores = (attn_probs * (grad_probs - row_delta)).astype(jnp.bfloat16)
        grad_query = (
            jnp.einsum("rtk,kd->trd", grad_scores, key_part, preferred_element_type=jnp.float32)
            * score_scale
        )
        grad_key = (
            jnp.einsum("rtk,trd->kd", grad_scores, query_part, preferred_element_type=jnp.float32)
            * score_scale
        )
        return (grad_query.reshape(tok_rows, group_cols), grad_key, grad_value)

    query_groups, key_groups, value_groups = lax.map(
        backward_group, jnp.arange(KV_HEADS, dtype=jnp.int32)
    )
    grad_query_rot = query_groups.transpose(1, 0, 2).reshape(tok_rows, HEADS, HEAD_DIM)
    key_blocks = key_groups.transpose(1, 0, 2).reshape(HOPS + 1, tok_rows, KV_HEADS * HEAD_DIM)
    value_blocks = value_groups.transpose(1, 0, 2).reshape(HOPS + 1, tok_rows, KV_HEADS * HEAD_DIM)
    home_key = key_blocks[HOPS]
    home_value = value_blocks[HOPS]
    for hop_index in range(HOPS, 0, -1):
        moved_key, moved_value = (
            from_behind(home_key.astype(jnp.bfloat16), "ctx", -1).astype(home_key.dtype),
            from_behind(home_value.astype(jnp.bfloat16), "ctx", -1).astype(home_value.dtype),
        )
        home_key = moved_key + key_blocks[hop_index - 1]
        home_value = moved_value + value_blocks[hop_index - 1]
    query_turned = rotary(grad_query_rot, pos_local, -1.0)
    key_turned = rotary(home_key.reshape(tok_rows, KV_HEADS, HEAD_DIM), pos_local, -1.0)
    query_back, query_terms = rms_back(query_raw, query_gain, query_turned)
    key_back, key_terms = rms_back(key_raw, key_gain, key_turned)
    query_back = query_back.reshape(tok_rows, HEADS * HEAD_DIM).astype(jnp.bfloat16)
    key_back = key_back.reshape(tok_rows, KV_HEADS * HEAD_DIM).astype(jnp.bfloat16)
    value_back = home_value.astype(jnp.bfloat16)
    grad_w_query = outer_product(normed_low, query_back)
    grad_w_key = outer_product(normed_low, key_back)
    grad_w_value = outer_product(normed_low, value_back)
    grad_normed = (
        against(query_back, q_full) + against(key_back, k_full) + against(value_back, v_full)
    )
    input_part, attn_terms = rms_back(resid_in, attn_gain, grad_normed)
    d_tokens = (grad_middle + input_part)[None]
    gain_totals = lax.psum(
        (
            jnp.sum(attn_terms, axis=0),
            jnp.sum(ffn_terms, axis=0),
            jnp.sum(query_terms, axis=(0, 1)),
            jnp.sum(key_terms, axis=(0, 1)),
        ),
        ("ctx", "fsdp"),
    )
    weight_grads = (
        grad_w_query,
        grad_w_key,
        grad_w_value,
        grad_w_out,
        grad_w_gate,
        grad_w_up,
        grad_w_down,
    )
    spread = (
        lax.psum_scatter(
            weight_grads[0].astype(jnp.bfloat16), "fsdp", scatter_dimension=0, tiled=True
        ).astype(jnp.float32),
        lax.psum_scatter(
            weight_grads[1].astype(jnp.bfloat16), "fsdp", scatter_dimension=0, tiled=True
        ).astype(jnp.float32),
        lax.psum_scatter(
            weight_grads[2].astype(jnp.bfloat16), "fsdp", scatter_dimension=0, tiled=True
        ).astype(jnp.float32),
        lax.psum_scatter(
            weight_grads[3].astype(jnp.bfloat16), "fsdp", scatter_dimension=0, tiled=True
        ).astype(jnp.float32),
        lax.psum_scatter(
            weight_grads[4].astype(jnp.bfloat16), "fsdp", scatter_dimension=0, tiled=True
        ).astype(jnp.float32),
        lax.psum_scatter(
            weight_grads[5].astype(jnp.bfloat16), "fsdp", scatter_dimension=0, tiled=True
        ).astype(jnp.float32),
        lax.psum_scatter(
            weight_grads[6].astype(jnp.bfloat16), "fsdp", scatter_dimension=0, tiled=True
        ).astype(jnp.float32),
    )
    shares = (
        lax.psum_scatter(spread[0], "ctx", scatter_dimension=1, tiled=True),
        lax.psum_scatter(spread[1], "ctx", scatter_dimension=1, tiled=True),
        lax.psum_scatter(spread[2], "ctx", scatter_dimension=1, tiled=True),
        lax.psum_scatter(spread[3], "ctx", scatter_dimension=1, tiled=True),
        lax.psum_scatter(spread[4], "ctx", scatter_dimension=1, tiled=True),
        lax.psum_scatter(spread[5], "ctx", scatter_dimension=1, tiled=True),
        lax.psum_scatter(spread[6], "ctx", scatter_dimension=1, tiled=True),
    )
    return (
        output,
        d_tokens,
        gain_totals[0],
        shares[0],
        shares[1],
        shares[2],
        gain_totals[2],
        gain_totals[3],
        shares[3],
        gain_totals[1],
        shares[4],
        shares[5],
        shares[6],
    )


MESH = pl.DeviceIdType.MESH
BLOCK = 256
RING = 16
VMEM_SPEC = pl.BlockSpec(memory_space=pltpu.VMEM)
SMEM_SPEC = pl.BlockSpec(memory_space=pltpu.SMEM)
F32 = jnp.float32
BF16 = jnp.bfloat16


def dot_dims(left_mat, right_mat, left_dim, right_dim):
    return lax.dot_general(
        left_mat, right_mat, (((left_dim,), (right_dim,)), ((), ())), preferred_element_type=F32
    )


def exchange_kernel(src, dst, own_sem, send_sem, recv_sem):
    place, core = lax.axis_index("ctx"), lax.axis_index("fsdp")
    barrier = pltpu.get_barrier_semaphore()
    for step in range(1, RING):
        peer = lax.rem(place + step, RING)
        pl.semaphore_signal(barrier, inc=1, device_id=(peer, core), device_id_type=MESH)
    own = pltpu.make_async_copy(src.at[place], dst.at[place], own_sem)
    own.start()
    pl.semaphore_wait(barrier, RING - 1)
    copies = []
    for step in range(1, RING):
        peer = lax.rem(place + step, RING)
        copy = pltpu.make_async_remote_copy(
            src_ref=src.at[peer],
            dst_ref=dst.at[place],
            send_sem=send_sem.at[step],
            recv_sem=recv_sem.at[step],
            device_id=(peer, core),
            device_id_type=MESH,
        )
        copy.start()
        copies.append(copy)
    own.wait()
    for copy in copies:
        copy.wait()


def exchange(blocks, call_id):
    return pl.pallas_call(
        exchange_kernel,
        out_shape=jax.ShapeDtypeStruct(blocks.shape, blocks.dtype),
        in_specs=[VMEM_SPEC],
        out_specs=VMEM_SPEC,
        scratch_shapes=[
            pltpu.SemaphoreType.DMA,
            pltpu.SemaphoreType.DMA((RING,)),
            pltpu.SemaphoreType.DMA((RING,)),
        ],
        compiler_params=pltpu.CompilerParams(collective_id=call_id, has_side_effects=True),
        name="exchange_heads",
    )(blocks)


def transposed(block):
    return block.astype(F32).T.astype(BF16)


def block_probs(key_nat, query_t, first_key, start, query_place, diagonal, masked):
    scores = jnp.dot(key_nat, query_t, preferred_element_type=F32)
    probs = jnp.exp(scores)
    if masked:
        key_place = first_key + lax.broadcasted_iota(jnp.int32, probs.shape, 0)
        ok = key_place >= start
        if diagonal:
            ok = ok & (key_place <= query_place)
        probs = jnp.where(ok, probs, 0.0)
    return probs


def attend_kernel(first_ref, clear_ref, qkv_ref, start_ref, mixed_ref, inv_ref, key_nat):
    blocks = qkv_ref.shape[0]

    def turn(j, carry):
        key_nat[j] = transposed(qkv_ref[j, HEAD_DIM : 2 * HEAD_DIM, :])
        return carry

    lax.fori_loop(0, blocks, turn, 0)

    def per_query(i, nothing):
        query_t = qkv_ref[i, 0:HEAD_DIM, :] * jnp.asarray(HEAD_DIM**-0.5, BF16)
        start = start_ref[i]
        query_place = i * BLOCK + lax.broadcasted_iota(jnp.int32, (1, BLOCK), 1)

        def step(diagonal, masked, j, carry):
            total, acc = carry
            probs = block_probs(
                key_nat[j], query_t, j * BLOCK, start, query_place, diagonal, masked
            )
            total = total + jnp.sum(probs, axis=0, keepdims=True)
            acc = acc + jnp.dot(
                qkv_ref[j, 2 * HEAD_DIM : 3 * HEAD_DIM, :],
                probs.astype(BF16),
                preferred_element_type=F32,
            )
            return total, acc

        carry = (jnp.zeros((1, BLOCK), F32), jnp.zeros((HEAD_DIM, BLOCK), F32))
        carry = lax.fori_loop(
            first_ref[i], clear_ref[i], functools.partial(step, False, True), carry
        )
        carry = lax.fori_loop(clear_ref[i], i, functools.partial(step, False, False), carry)
        total, acc = step(True, True, i, carry)
        inverse = 1.0 / total
        mixed_ref[i] = (acc * inverse).astype(BF16)
        inv_ref[i] = inverse
        return nothing

    lax.fori_loop(0, blocks, per_query, 0)


def attend(first, clear, qkv, start):
    blocks = qkv.shape[0]
    return pl.pallas_call(
        attend_kernel,
        out_shape=(
            jax.ShapeDtypeStruct((blocks, HEAD_DIM, BLOCK), BF16),
            jax.ShapeDtypeStruct((blocks, 1, BLOCK), F32),
        ),
        in_specs=[SMEM_SPEC, SMEM_SPEC, VMEM_SPEC, VMEM_SPEC],
        out_specs=(VMEM_SPEC, VMEM_SPEC),
        scratch_shapes=[pltpu.VMEM((blocks, BLOCK, HEAD_DIM), BF16)],
        name="attend_forward",
    )(first, clear, qkv, start)


def flip(bit, turned):
    return bit + turned - 2 * bit * turned


class Spread:
    def __init__(self, chain, compute, sent, came, send_sems, recv_sems):
        place, self.core = lax.axis_index("ctx"), lax.axis_index("fsdp")
        x, y, self.z = lax.rem(place, 2), lax.rem(place // 2, 2), place // 4
        self.chain = chain
        self.first, self.second = (x, y) if chain == 0 else (y, x)
        self.compute, self.sent, self.came = compute, sent, came
        self.send_sems, self.recv_sems = send_sems, recv_sems

    def at(self, first, second, depth):
        low = second * 2 + first if self.chain == 0 else first * 2 + second
        return depth * 4 + low

    def deep(self, depth):
        return lax.rem(self.z + depth, 4)

    def copy(self, stage, slot):
        if stage == 0:
            peer = self.at(1 - self.first, self.second, self.z)
            source, target, sem = self.sent.at[slot], self.came[0].at[slot], slot
        elif stage == 1:
            peer = self.at(self.first, 1 - self.second, self.z)
            source, target, sem = self.came[0].at[4 + slot], self.came[1].at[slot], 8 + slot
        else:
            peer = self.at(self.first, self.second, self.deep(slot))
            source, target, sem = self.came[0].at[slot], self.came[2].at[slot - 1], 11 + slot
        return pltpu.make_async_remote_copy(
            src_ref=source,
            dst_ref=target,
            send_sem=self.send_sems.at[self.chain, sem],
            recv_sem=self.recv_sems.at[self.chain, sem],
            device_id=(peer, self.core),
            device_id_type=MESH,
        )

    def stage_one(self, turned, depth):
        slot = turned * 4 + depth
        owner = self.at(1 - self.first, flip(self.second, turned), self.deep(depth))
        for row, value in self.compute(self.chain, owner):
            self.sent[slot, row : row + value.shape[0], :] = value.astype(BF16)
        self.copy(0, slot).start()

    def stage_two(self, depth):
        self.copy(0, 4 + depth).wait_recv()
        owner = self.at(self.first, 1 - self.second, self.deep(depth))
        for row, value in self.compute(self.chain, owner):
            window = slice(row, row + value.shape[0])
            value = value + self.came[0][4 + depth, window, :].astype(F32)
            self.came[0][4 + depth, window, :] = value.astype(BF16)
        self.copy(1, depth).start()

    def stage_three(self, depth):
        self.copy(0, depth).wait_recv()
        self.copy(1, depth).wait_recv()
        owner = self.at(self.first, self.second, self.deep(depth))
        for row, value in self.compute(self.chain, owner):
            window = slice(row, row + value.shape[0])
            value = value + self.came[0][depth, window, :].astype(F32)
            value = value + self.came[1][depth, window, :].astype(F32)
            self.came[0][depth, window, :] = value.astype(BF16)
        self.copy(2, depth).start()

    def close(self, finish):
        self.copy(0, 0).wait_recv()
        self.copy(1, 0).wait_recv()
        for depth in range(1, 4):
            self.copy(2, depth).wait_recv()
        owner = self.at(self.first, self.second, self.z)
        for row, value in self.compute(self.chain, owner):
            window = slice(row, row + value.shape[0])
            value = value + self.came[0][0, window, :].astype(F32)
            value = value + self.came[1][0, window, :].astype(F32)
            for depth in range(3):
                value = value + self.came[2][depth, window, :].astype(F32)
            finish(self.chain, row, value)

    def drain(self):
        for slot in range(8):
            self.copy(0, slot).wait_send()
        for depth in range(4):
            self.copy(1, depth).wait_send()
        for depth in range(1, 4):
            self.copy(2, depth).wait_send()


def greet(peers):
    barrier = pltpu.get_barrier_semaphore()
    for peer in peers:
        pl.semaphore_signal(barrier, inc=1, device_id=peer, device_id_type=MESH)
    pl.semaphore_wait(barrier, len(peers))


def turn_into(source, put):
    for column in range(0, source.shape[1], 128):
        put(column, source[:, column : column + 128].astype(F32).T.astype(BF16))


def back_kernel(
    gate_ref,
    up_ref,
    hidden_ref,
    cot_ref,
    middle_ref,
    ffn_ref,
    mixed_ref,
    home_ref,
    qkv_ref,
    start_ref,
    part_ref,
    inv_ref,
    gate_out,
    up_out,
    down_out,
    out_out,
    back_out,
    pair_own,
    pair_far,
    side_own,
    side_far,
    hidden_far,
    ffn_far,
    mixed_far,
    cot_far,
    back_own,
    key_value,
    grad_acc,
    sent_a,
    came_a0,
    came_a1,
    came_a2,
    sent_b,
    came_b0,
    came_b1,
    came_b2,
    send_sems,
    recv_sems,
    cot_send,
    cot_recv,
    back_send,
    back_recv,
    core_send,
    core_recv,
):
    place, core = lax.axis_index("ctx"), lax.axis_index("fsdp")
    blocks = qkv_ref.shape[0]
    wide = pair_own.shape[1] // 2
    narrow = side_own.shape[1] // RING
    half_hidden = hidden_far.shape[1]
    half_width = ffn_far.shape[1]
    scale = HEAD_DIM**-0.5

    greet(
        [(lax.rem(place + step, RING), core) for step in range(1, RING)] + [(place, 1 - core)]
    )

    def cot_copy(step, peer):
        return pltpu.make_async_remote_copy(
            src_ref=home_ref.at[peer],
            dst_ref=cot_far.at[place],
            send_sem=cot_send.at[step],
            recv_sem=cot_recv.at[step],
            device_id=(peer, core),
            device_id_type=MESH,
        )

    for step in range(1, RING):
        cot_copy(step, lax.rem(place + step, RING)).start()
    cot_far[place] = home_ref[place]

    def core_copy(source, target, sem):
        return pltpu.make_async_remote_copy(
            src_ref=source,
            dst_ref=target,
            send_sem=core_send.at[sem],
            recv_sem=core_recv.at[sem],
            device_id=(place, 1 - core),
            device_id_type=MESH,
        )

    def half(part, size):
        return pl.ds(pl.multiple_of(part * size, 128), size)

    def pair_copy(turn_x, turn_y, depth):
        x, y, z = lax.rem(place, 2), lax.rem(place // 2, 2), place // 4
        owner = lax.rem(z + depth, 4) * 4 + flip(y, turn_y) * 2 + flip(x, turn_x)
        return core_copy(
            pair_own.at[owner], pair_far.at[owner], 4 + turn_x * 8 + turn_y * 4 + depth
        )

    sides = [
        core_copy(ffn_ref.at[:, half(1 - core, half_width)], ffn_far, 0),
        core_copy(mixed_ref.at[half(1 - core, half_width), :], mixed_far, 1),
        core_copy(hidden_ref.at[:, half(1 - core, half_hidden)], hidden_far, 2),
        core_copy(side_own, side_far, 3),
    ]
    for copy in sides[:3]:
        copy.start()

    def put_side(which):
        def put(column, value):
            side_own[which, column : column + 128, :] = value

        return put

    turn_into(cot_ref, put_side(0))
    turn_into(middle_ref, put_side(1))
    sides[3].start()

    def put_pair(base):
        def put(column, value):
            done = 0
            while done < 128:
                owner, row = divmod(column + done, wide)
                count = min(128 - done, wide - row)
                pair_own[owner, base + row : base + row + count, :] = value[done : done + count]
                done += count

        return put

    turn_into(gate_ref, put_pair(0))
    turn_into(up_ref, put_pair(wide))
    order = []
    for depth in (1, 2, 3, 0):
        order += [(1, 1, depth), (1, 0, depth), (0, 1, depth)]
    order += [(0, 0, depth) for depth in (1, 2, 3, 0)]
    for turn_x, turn_y, depth in order:
        pair_copy(turn_x, turn_y, depth).start()

    def compute(chain, owner):
        lanes = pl.ds(chain * 256, 256)
        own_lanes = pl.ds(pl.multiple_of(core * half_width + chain * 256, 128), 256)
        both_pair = jnp.dot(pair_own[owner], ffn_ref[:, own_lanes], preferred_element_type=F32)
        both_pair += jnp.dot(pair_far[owner], ffn_far[:, lanes], preferred_element_type=F32)
        values = [(0, both_pair)]
        rows = pl.ds(pl.multiple_of(owner * narrow, 16), narrow)
        begin, chunks = (0, 5) if chain == 0 else (5, 4)
        cols = pl.ds(pl.multiple_of(core * half_hidden + begin * 256, 128), chunks * 256)
        down = jnp.dot(side_own[0, rows, :], hidden_ref[:, cols], preferred_element_type=F32)
        down += jnp.dot(
            side_far[0, rows, :],
            hidden_far[:, begin * 256 : (begin + chunks) * 256],
            preferred_element_type=F32,
        )
        row = 2 * wide
        for chunk in range(chunks):
            values.append((row, down[:, chunk * 256 : chunk * 256 + 256]))
            row += narrow
        out = dot_dims(side_own[1, rows, :], mixed_ref[own_lanes, :], 1, 1)
        out += dot_dims(side_far[1, rows, :], mixed_far[lanes, :], 1, 1)
        values.append((row, out))
        return values

    def finish(chain, row, value):
        lanes = slice(chain * 256, chain * 256 + 256)
        if row == 0:
            gate_out[:, lanes] = value[:wide]
            up_out[:, lanes] = value[wide:]
            return
        chunk = (row - 2 * wide) // narrow
        if chunk == 5 - chain:
            out_out[:, lanes] = value
        else:
            chunk += 5 * chain
            down_out[:, chunk * 256 : chunk * 256 + 256] = value

    chains = (
        Spread(0, compute, sent_a, (came_a0, came_a1, came_a2), send_sems, recv_sems),
        Spread(1, compute, sent_b, (came_b0, came_b1, came_b2), send_sems, recv_sems),
    )
    for copy in sides:
        copy.wait_recv()

    def near(depth):
        pair_copy(1, 1, depth).wait_recv()
        for chain in chains:
            chain.stage_one(1, depth)

    def far(depth):
        pair_copy(1, 0, depth).wait_recv()
        pair_copy(0, 1, depth).wait_recv()
        for chain in chains:
            chain.stage_one(0, depth)

    def event(number):
        @pl.when(lax.rem(number, 2) == 1)
        def _():
            for chain in chains:
                chain.stage_two(lax.rem((number + 1) // 2, 4))

        @pl.when((lax.rem(number, 2) == 1) & (number >= 3))
        def _():
            depth = (number - 1) // 2
            pair_copy(0, 0, depth).wait_recv()
            for chain in chains:
                chain.stage_three(depth)

        @pl.when((lax.rem(number, 2) == 1) & (number <= 5))
        def _():
            far(lax.rem(number // 2 + 2, 4))

        @pl.when((lax.rem(number, 2) == 0) & (number <= 5))
        def _():
            near(lax.rem(number // 2 + 2, 4))

    near(1)
    far(1)
    near(2)

    key_value[0] = jnp.zeros(key_value.shape[1:], BF16)

    def prepare(j, nothing):
        packed = qkv_ref[j, HEAD_DIM : 3 * HEAD_DIM, :].astype(F32)
        key_value[j + 1] = packed.T.astype(BF16)
        grad_acc[j + 1] = jnp.zeros(grad_acc.shape[1:], F32)
        return nothing

    grad_acc[0] = jnp.zeros(grad_acc.shape[1:], F32)
    lax.fori_loop(0, blocks, prepare, 0)

    def back_copy(step, peer):
        return pltpu.make_async_remote_copy(
            src_ref=back_own.at[peer],
            dst_ref=back_out.at[place],
            send_sem=back_send.at[step],
            recv_sem=back_recv.at[step],
            device_id=(peer, core),
            device_id_type=MESH,
        )

    def flush(j):
        turned = grad_acc[j + 1].T.astype(BF16)
        back_own[j, HEAD_DIM : 3 * HEAD_DIM, :] = turned

        @pl.when(j != place)
        def _():
            back_copy(lax.rem(j - place + RING, RING), j).start()

    def per_query(i):
        @pl.when(i != place)
        def _():
            step = lax.rem(place - i + RING, RING)
            cot_copy(step, lax.rem(place + step, RING)).wait_recv()

        empty = jnp.zeros((HEAD_DIM, BLOCK), BF16)
        query = qkv_ref[i, 0:HEAD_DIM, :] * jnp.asarray(scale, BF16)
        query_t = jnp.concatenate([query, empty], axis=0)
        cot = cot_far[i]
        cot_t = jnp.concatenate([empty, cot], axis=0)
        query_nat = transposed(query_t)
        cot_nat = transposed(cot_t)
        start = start_ref[i]
        inverse = inv_ref[i]
        delta = jnp.sum(cot.astype(F32) * part_ref[i].astype(F32), axis=0, keepdims=True)
        query_place = i * BLOCK + lax.broadcasted_iota(jnp.int32, (1, BLOCK), 1)

        def step(diagonal, j):
            block = key_value[j + 1]
            scores = jnp.dot(block, query_t, preferred_element_type=F32)
            grad_probs = jnp.dot(block, cot_t, preferred_element_type=F32)
            key_place = j * BLOCK + lax.broadcasted_iota(jnp.int32, scores.shape, 0)
            ok = key_place >= start
            if diagonal:
                ok = ok & (key_place <= query_place)
            probs = jnp.where(ok, jnp.exp(scores) * inverse, 0.0)
            grad_scores = (probs * (grad_probs - delta)).astype(BF16)
            update = jnp.dot(grad_scores, query_nat, preferred_element_type=F32)
            update += jnp.dot(probs.astype(BF16), cot_nat, preferred_element_type=F32)
            grad_acc[j + 1] += update
            return jnp.dot(
                qkv_ref[jnp.maximum(j, 0), HEAD_DIM : 2 * HEAD_DIM, :],
                grad_scores,
                preferred_element_type=F32,
            )

        pairs = (jnp.minimum(i, 8) + 1) // 2

        def two(index, acc):
            j = i - 2 * pairs + 2 * index
            return acc + step(False, j) + step(False, j + 1)

        acc = lax.fori_loop(0, pairs, two, step(True, i))
        back_own[i, 0:HEAD_DIM, :] = (acc * scale).astype(BF16)

        @pl.when(i >= 8)
        def _():
            flush(i - 8)

    def rest(j, nothing):
        flush(j)
        return nothing

    def per_step(i, nothing):
        @pl.when(i < blocks)
        def _():
            per_query(i)

        @pl.when(i == blocks - 1)
        def _():
            lax.fori_loop(blocks - 8, blocks, rest, 0)

        @pl.when((i >= 6) & (lax.rem(i, 3) == 0))
        def _():
            event(i // 3 - 1)

        return nothing

    lax.fori_loop(0, 25, per_step, 0)
    back_out[place] = back_own[place]
    pair_copy(0, 0, 0).wait_recv()
    for chain in chains:
        chain.close(finish)

    def settle(step, nothing):
        peer = lax.rem(place + step, RING)
        back_copy(step, peer).wait()
        cot_copy(step, peer).wait_send()
        return nothing

    lax.fori_loop(1, RING, settle, 0)
    for copy in sides:
        copy.wait_send()
    for turn_x, turn_y, depth in order:
        pair_copy(turn_x, turn_y, depth).wait_send()
    for chain in chains:
        chain.drain()


def back_call(call_id, *inputs):
    gate_back, qkv = inputs[0], inputs[8]
    rows, hidden_width = gate_back.shape
    width = inputs[3].shape[1]
    blocks = qkv.shape[0]
    wide, narrow = hidden_width // RING, width // RING
    chain_rows = (2 * wide + 6 * narrow, 2 * wide + 5 * narrow)
    buffers = [
        pltpu.VMEM((slots, chain_rows[chain], 256), BF16)
        for chain in range(2)
        for slots in (8, 8, 4, 3)
    ]
    return pl.pallas_call(
        back_kernel,
        out_shape=(
            jax.ShapeDtypeStruct((wide, width // 2), F32),
            jax.ShapeDtypeStruct((wide, width // 2), F32),
            jax.ShapeDtypeStruct((narrow, hidden_width // 2), F32),
            jax.ShapeDtypeStruct((narrow, width // 2), F32),
            jax.ShapeDtypeStruct(qkv.shape, BF16),
        ),
        in_specs=[VMEM_SPEC] * len(inputs),
        out_specs=(VMEM_SPEC,) * 5,
        scratch_shapes=[
            pltpu.VMEM((RING, 2 * wide, rows), BF16),
            pltpu.VMEM((RING, 2 * wide, rows), BF16),
            pltpu.VMEM((2, width, rows), BF16),
            pltpu.VMEM((2, width, rows), BF16),
            pltpu.VMEM((rows, hidden_width // 2), BF16),
            pltpu.VMEM((rows, width // 2), BF16),
            pltpu.VMEM((width // 2, rows), BF16),
            pltpu.VMEM((blocks, HEAD_DIM, BLOCK), BF16),
            pltpu.VMEM(qkv.shape, BF16),
            pltpu.VMEM((blocks + 1, BLOCK, 2 * HEAD_DIM), BF16),
            pltpu.VMEM((blocks + 1, BLOCK, 2 * HEAD_DIM), F32),
        ]
        + buffers
        + [
            pltpu.SemaphoreType.DMA((2, 15)),
            pltpu.SemaphoreType.DMA((2, 15)),
            pltpu.SemaphoreType.DMA((RING,)),
            pltpu.SemaphoreType.DMA((RING,)),
            pltpu.SemaphoreType.DMA((RING,)),
            pltpu.SemaphoreType.DMA((RING,)),
            pltpu.SemaphoreType.DMA((20,)),
            pltpu.SemaphoreType.DMA((20,)),
        ],
        compiler_params=pltpu.CompilerParams(
            collective_id=call_id, has_side_effects=True, vmem_limit_bytes=63 << 20
        ),
        name="backward_spread",
    )(*inputs)


def turn_back(values, cosine, sine):
    half = HEAD_DIM // 2
    first, second = values[:half], values[half:]
    return jnp.concatenate(
        [first * cosine + second * sine, second * cosine - first * sine], axis=0
    )


def column_norm_back(values, gain, upstream):
    inverse = lax.rsqrt(jnp.mean(values * values, axis=0, keepdims=True) + EPSILON)
    scaled = upstream * gain
    total = jnp.sum(scaled * values, axis=0, keepdims=True) / values.shape[0]
    return inverse * scaled - values * inverse**3 * total, upstream * values * inverse


def tail_kernel(
    back_ref,
    query_ref,
    key_ref,
    cosine_ref,
    sine_ref,
    query_gain_ref,
    key_gain_ref,
    weights_ref,
    normed_ref,
    tokens_ref,
    attn_gain_ref,
    middle_ref,
    ffn_terms_ref,
    tokens_out,
    grads_out,
    gains_out,
    turned_own,
    turned_far,
    normed_far,
    natural,
    summed,
    gain_own,
    gain_came,
    gain_deep,
    sent_a,
    came_a0,
    came_a1,
    came_a2,
    sent_b,
    came_b0,
    came_b1,
    came_b2,
    send_sems,
    recv_sems,
    core_send,
    core_recv,
    gain_send,
    gain_recv,
):
    place, core = lax.axis_index("ctx"), lax.axis_index("fsdp")
    x, y, z = lax.rem(place, 2), lax.rem(place // 2, 2), place // 4
    near_x = (place + 1 - 2 * x, core)
    near_y = (place + 2 - 4 * y, core)
    partner = (place, 1 - core)
    deep = [(lax.rem(place + 4 * step, RING), core) for step in range(1, 4)]
    greet([near_x, near_y, partner] + deep)
    half_width = normed_far.shape[1]
    heads, pairs = query_ref.shape[0], key_ref.shape[0]
    group = heads // pairs

    def core_copy(source, target, sem):
        return pltpu.make_async_remote_copy(
            src_ref=source,
            dst_ref=target,
            send_sem=core_send.at[sem],
            recv_sem=core_recv.at[sem],
            device_id=partner,
            device_id_type=MESH,
        )

    other = pl.ds(pl.multiple_of((1 - core) * half_width, 128), half_width)
    sides = [
        core_copy(normed_ref.at[:, other], normed_far, 0),
        core_copy(turned_own, turned_far, 1),
    ]
    sides[0].start()
    cosine, sine = cosine_ref[...], sine_ref[...]

    def query_head(head, total):
        upstream = turn_back(back_ref[head, 0:HEAD_DIM, :].astype(F32), cosine, sine)
        back, terms = column_norm_back(query_ref[head], query_gain_ref[...], upstream)
        rows = pl.ds(pl.multiple_of(head * HEAD_DIM, HEAD_DIM), HEAD_DIM)
        turned_own[rows, :] = back.astype(BF16)
        return total + terms

    def key_head(pair, total):
        upstream = jnp.zeros((2 * HEAD_DIM, back_ref.shape[2]), F32)
        for member in range(group):
            upstream += back_ref[group * pair + member, HEAD_DIM : 3 * HEAD_DIM, :].astype(F32)
        back, terms = column_norm_back(
            key_ref[pair],
            key_gain_ref[...],
            turn_back(upstream[:HEAD_DIM], cosine, sine),
        )
        base = heads * HEAD_DIM
        rows = pl.ds(pl.multiple_of(base + pair * HEAD_DIM, HEAD_DIM), HEAD_DIM)
        turned_own[rows, :] = back.astype(BF16)
        base += pairs * HEAD_DIM
        rows = pl.ds(pl.multiple_of(base + pair * HEAD_DIM, HEAD_DIM), HEAD_DIM)
        turned_own[rows, :] = upstream[HEAD_DIM:].astype(BF16)
        return total + terms

    nothing = jnp.zeros((HEAD_DIM, back_ref.shape[2]), F32)
    query_terms = lax.fori_loop(0, heads, query_head, nothing)
    key_terms = lax.fori_loop(0, pairs, key_head, nothing)
    sides[1].start()

    def compute(chain, owner):
        lanes = slice(chain * 256, chain * 256 + 256)
        own_lanes = pl.ds(pl.multiple_of(core * half_width + chain * 256, 128), 256)
        values, row, base = [], 0, 0
        for size in (heads, pairs, pairs):
            count = size * HEAD_DIM // RING
            rows = pl.ds(pl.multiple_of(base + owner * count, 16), count)
            value = jnp.dot(turned_own[rows, :], normed_ref[:, own_lanes], preferred_element_type=F32)
            value += jnp.dot(turned_far[rows, :], normed_far[:, lanes], preferred_element_type=F32)
            values.append((row, value))
            row += count
            base += size * HEAD_DIM
        return values

    def finish(chain, row, value):
        grads_out[row : row + value.shape[0], chain * 256 : chain * 256 + 256] = value

    chains = (
        Spread(0, compute, sent_a, (came_a0, came_a1, came_a2), send_sems, recv_sems),
        Spread(1, compute, sent_b, (came_b0, came_b1, came_b2), send_sems, recv_sems),
    )
    for copy in sides:
        copy.wait_recv()

    def one(index, carry):
        for chain in chains:
            chain.stage_one(1 - index // 4, lax.rem(index + 1, 4))
        return carry

    lax.fori_loop(0, 8, one, 0)

    natural[...] = jnp.zeros(natural.shape, BF16)
    for row in range(0, turned_own.shape[0], 128):
        natural[:, row : row + 128] = turned_own[row : row + 128, :].astype(F32).T.astype(BF16)

    def two(index, carry):
        for chain in chains:
            chain.stage_two(lax.rem(index + 1, 4))
        return carry

    lax.fori_loop(0, 4, two, 0)

    cut = 2 * pairs * HEAD_DIM
    upstream = dot_dims(natural[:, : heads * HEAD_DIM], weights_ref[:, cut:], 1, 1)
    upstream += dot_dims(natural[:, heads * HEAD_DIM :], weights_ref[:, :cut], 1, 1)
    summed[...] = upstream

    def three(depth, carry):
        for chain in chains:
            chain.stage_three(depth)
        return carry

    lax.fori_loop(1, 4, three, 0)

    def token_rows(index, total):
        rows = pl.ds(pl.multiple_of(index * 32, 32), 32)
        values, upstream = tokens_ref[rows, :].astype(F32), summed[rows, :]
        inverse = lax.rsqrt(jnp.mean(values * values, axis=-1, keepdims=True) + EPSILON)
        scaled = upstream * attn_gain_ref[...]
        weight = jnp.sum(scaled * values, axis=-1, keepdims=True) / values.shape[1]
        tokens_out[rows, :] = (
            middle_ref[rows, :] + inverse * scaled - values * inverse**3 * weight
        )
        return total + jnp.sum(upstream * values * inverse, axis=0, keepdims=True)

    terms = lax.fori_loop(
        0, tokens_ref.shape[0] // 32, token_rows, jnp.zeros((1, tokens_ref.shape[1]), F32)
    )
    gain_own[0] = jnp.zeros(gain_own.shape[1:], F32)
    gain_own[0, 0:1, :] = terms
    gain_own[0, 1:2, :] = ffn_terms_ref[...]
    gain_own[0, 2:3, 0:HEAD_DIM] = jnp.sum(query_terms.T, axis=0, keepdims=True)
    gain_own[0, 3:4, 0:HEAD_DIM] = jnp.sum(key_terms.T, axis=0, keepdims=True)

    def gain_copy(source, target, sem, peer):
        return pltpu.make_async_remote_copy(
            src_ref=source,
            dst_ref=target,
            send_sem=gain_send.at[sem],
            recv_sem=gain_recv.at[sem],
            device_id=peer,
            device_id_type=MESH,
        )

    gain_copies = []
    for stage, peer in enumerate((near_x, near_y, partner)):
        copy = gain_copy(gain_own.at[stage], gain_came.at[stage], stage, peer)
        copy.start()
        gain_copies.append(copy)
        copy.wait_recv()
        gain_own[stage + 1] = gain_own[stage] + gain_came[stage]
    gain_deep[z] = gain_own[3]
    for step in range(1, 4):
        copy = gain_copy(gain_own.at[3], gain_deep.at[z], 2 + step, deep[step - 1])
        copy.start()
        gain_copies.append(copy)

    for chain in chains:
        chain.close(finish)
    for copy in gain_copies[3:]:
        copy.wait_recv()
    gains_out[...] = (gain_deep[0] + gain_deep[1]) + (gain_deep[2] + gain_deep[3])
    for copy in sides + gain_copies:
        copy.wait_send()
    for chain in chains:
        chain.drain()


def tail_call(call_id, *inputs):
    rows, width = inputs[8].shape
    total = (HEADS + 2 * KV_HEADS) * HEAD_DIM
    block_rows = total // RING
    buffers = [
        pltpu.VMEM((slots, block_rows, 256), BF16) for chain in range(2) for slots in (8, 8, 4, 3)
    ]
    return pl.pallas_call(
        tail_kernel,
        out_shape=(
            jax.ShapeDtypeStruct((rows, width), F32),
            jax.ShapeDtypeStruct((block_rows, width // 2), F32),
            jax.ShapeDtypeStruct((4, width), F32),
        ),
        in_specs=[VMEM_SPEC] * len(inputs),
        out_specs=(VMEM_SPEC,) * 3,
        scratch_shapes=[
            pltpu.VMEM((total, rows), BF16),
            pltpu.VMEM((total, rows), BF16),
            pltpu.VMEM((rows, width // 2), BF16),
            pltpu.VMEM((rows, total), BF16),
            pltpu.VMEM((rows, width), F32),
            pltpu.VMEM((4, 4, width), F32),
            pltpu.VMEM((3, 4, width), F32),
            pltpu.VMEM((4, 4, width), F32),
        ]
        + buffers
        + [
            pltpu.SemaphoreType.DMA((2, 15)),
            pltpu.SemaphoreType.DMA((2, 15)),
            pltpu.SemaphoreType.DMA((2,)),
            pltpu.SemaphoreType.DMA((2,)),
            pltpu.SemaphoreType.DMA((6,)),
            pltpu.SemaphoreType.DMA((6,)),
        ],
        compiler_params=pltpu.CompilerParams(
            collective_id=call_id, has_side_effects=True, vmem_limit_bytes=60 << 20
        ),
        name="backward_tail",
    )(*inputs)


def angle_parts(positions):
    half = HEAD_DIM // 2
    inverse_freq = THETA ** (-(2.0 / HEAD_DIM) * jnp.arange(half, dtype=F32))
    angles = inverse_freq[:, None] * positions.astype(F32)[None, :]
    return jnp.cos(angles), jnp.sin(angles)


def front_kernel(
    tokens_ref,
    gain_ref,
    w_query_ref,
    w_key_ref,
    w_value_ref,
    query_gain_ref,
    key_gain_ref,
    cosine_ref,
    sine_ref,
    own_start_ref,
    qkv_out,
    starts_out,
    query_out,
    key_out,
    normed_out,
    weights_out,
    home,
    own_sem,
    send_sem,
    recv_sem,
    start_send,
    start_recv,
    core_send,
    core_recv,
):
    place, core = lax.axis_index("ctx"), lax.axis_index("fsdp")
    rows = tokens_ref.shape[0]
    depth = w_query_ref.shape[0]
    partner = (place, 1 - core)
    greet([partner] + [(lax.rem(place + step, RING), core) for step in range(1, RING)])

    def own_rows(part):
        return pl.ds(pl.multiple_of(part * depth, 128), depth)

    copies, locals_, column = [], [], 0
    for index, source in enumerate((w_key_ref, w_value_ref, w_query_ref)):
        window = pl.ds(column, source.shape[1])
        target = weights_out.at[own_rows(core), window]
        copy = pltpu.make_async_remote_copy(
            src_ref=source,
            dst_ref=target,
            send_sem=core_send.at[index],
            recv_sem=core_recv.at[index],
            device_id=partner,
            device_id_type=MESH,
        )
        copy.start()
        copies.append(copy)
        near = pltpu.make_async_copy(source, target, own_sem.at[index])
        near.start()
        locals_.append(near)
        column += source.shape[1]

    def start_copy(step):
        peer = lax.rem(place + step, RING)
        return pltpu.make_async_remote_copy(
            src_ref=own_start_ref,
            dst_ref=starts_out.at[place],
            send_sem=start_send.at[step],
            recv_sem=start_recv.at[step],
            device_id=(peer, core),
            device_id_type=MESH,
        )

    for step in range(1, RING):
        start_copy(step).start()
    starts_out[place] = own_start_ref[...]

    def norm_rows(index, nothing):
        window = pl.ds(pl.multiple_of(index * 32, 32), 32)
        values = tokens_ref[window, :].astype(F32)
        inverse = lax.rsqrt(jnp.mean(values * values, axis=-1, keepdims=True) + EPSILON)
        normed_out[window, :] = (values * inverse * gain_ref[...]).astype(BF16)
        return nothing

    lax.fori_loop(0, rows // 32, norm_rows, 0)
    cosine, sine = cosine_ref[...], sine_ref[...]
    half = HEAD_DIM // 2

    def project(column, count):
        window = pl.ds(column, count)
        product = jnp.dot(normed_out[...], weights_out[:, window], preferred_element_type=F32)
        return product.T

    def turned(values, gain):
        mean = jnp.mean(values * values, axis=0, keepdims=True)
        values = values * lax.rsqrt(mean + EPSILON) * gain
        first, second = values[:half], values[half:]
        return jnp.concatenate(
            [first * cosine - second * sine, second * cosine + first * sine], axis=0
        ).astype(BF16)

    group = HEADS // KV_HEADS
    kv_width = KV_HEADS * HEAD_DIM
    copies[0].wait_recv()
    locals_[0].wait()

    def key_chunk(index, nothing):
        products = project(pl.multiple_of(index * 256, 256), 256)
        for member in range(4):
            raw = products[member * HEAD_DIM : (member + 1) * HEAD_DIM]
            pair = index * 4 + member
            key_out[pair] = raw
            key = turned(raw, key_gain_ref[...])
            for twin in range(group):
                home[group * pair + twin, HEAD_DIM : 2 * HEAD_DIM, :] = key
        return nothing

    lax.fori_loop(0, KV_HEADS // 4, key_chunk, 0)
    copies[1].wait_recv()
    locals_[1].wait()

    def value_chunk(index, nothing):
        products = project(pl.multiple_of(kv_width + index * 256, 256), 256)
        for member in range(4):
            value = products[member * HEAD_DIM : (member + 1) * HEAD_DIM].astype(BF16)
            for twin in range(group):
                home[group * (index * 4 + member) + twin, 2 * HEAD_DIM : 3 * HEAD_DIM, :] = value
        return nothing

    lax.fori_loop(0, KV_HEADS // 4, value_chunk, 0)
    copies[2].wait_recv()
    locals_[2].wait()

    def block_copy(step):
        peer = lax.rem(place + step, RING)
        return pltpu.make_async_remote_copy(
            src_ref=home.at[peer],
            dst_ref=qkv_out.at[place],
            send_sem=send_sem.at[step],
            recv_sem=recv_sem.at[step],
            device_id=(peer, core),
            device_id_type=MESH,
        )

    def query_chunk(index, nothing):
        products = project(pl.multiple_of(2 * kv_width + index * 256, 256), 256)
        for member in range(4):
            raw = products[member * HEAD_DIM : (member + 1) * HEAD_DIM]
            head = index * 4 + member
            query_out[head] = raw
            home[head, 0:HEAD_DIM, :] = turned(raw, query_gain_ref[...])

            @pl.when(head != place)
            def _():
                block_copy(lax.rem(head - place + RING, RING)).start()

        return nothing

    lax.fori_loop(0, HEADS // 4, query_chunk, 0)
    qkv_out[place] = home[place]

    def settle(step, nothing):
        block_copy(step).wait()
        start_copy(step).wait()
        return nothing

    lax.fori_loop(1, RING, settle, 0)
    for copy in copies:
        copy.wait_send()


def front_call(call_id, *inputs):
    rows, width = inputs[0].shape
    total = (HEADS + 2 * KV_HEADS) * HEAD_DIM
    return pl.pallas_call(
        front_kernel,
        out_shape=(
            jax.ShapeDtypeStruct((RING, 3 * HEAD_DIM, rows), BF16),
            jax.ShapeDtypeStruct((RING, 1, rows), jnp.int32),
            jax.ShapeDtypeStruct((HEADS, HEAD_DIM, rows), F32),
            jax.ShapeDtypeStruct((KV_HEADS, HEAD_DIM, rows), F32),
            jax.ShapeDtypeStruct((rows, width), BF16),
            jax.ShapeDtypeStruct((width, total), BF16),
        ),
        in_specs=[VMEM_SPEC] * len(inputs),
        out_specs=(VMEM_SPEC,) * 6,
        scratch_shapes=[
            pltpu.VMEM((RING, 3 * HEAD_DIM, rows), BF16),
            pltpu.SemaphoreType.DMA((3,)),
            pltpu.SemaphoreType.DMA((RING,)),
            pltpu.SemaphoreType.DMA((RING,)),
            pltpu.SemaphoreType.DMA((RING,)),
            pltpu.SemaphoreType.DMA((RING,)),
            pltpu.SemaphoreType.DMA((3,)),
            pltpu.SemaphoreType.DMA((3,)),
        ],
        compiler_params=pltpu.CompilerParams(
            collective_id=call_id, has_side_effects=True, vmem_limit_bytes=48 << 20
        ),
        name="front_heads",
    )(*inputs)


def both(block, axis):
    return lax.all_gather(block, "fsdp", axis=axis, tiled=True)


def heads_body(
    tokens,
    seg_ids,
    doc_pos,
    attn_gain,
    w_query,
    w_key,
    w_value,
    query_gain,
    key_gain,
    w_out,
    ffn_gain,
    w_gate,
    w_up,
    w_down,
    d_output,
):
    place, core = lax.axis_index("ctx"), lax.axis_index("fsdp")
    rows, width = tokens.shape[1], tokens.shape[2]
    resid_in = tokens[0].astype(F32)
    pos_local = doc_pos[0]
    o_full, gate_full = both(w_out, 0), both(w_gate, 0)
    up_full, down_full = both(w_up, 0), both(w_down, 0)
    own_starts = place * rows + jnp.arange(rows, dtype=jnp.int32) - pos_local
    cosine, sine = angle_parts(pos_local)
    qkv, starts, query_raw, key_raw, normed_low, kvq_full = front_call(
        1,
        tokens[0],
        attn_gain[None, :],
        w_query,
        w_key,
        w_value,
        query_gain[:, None],
        key_gain[:, None],
        cosine,
        sine,
        own_starts[None, :],
    )
    first = starts[:, 0, 0] // BLOCK
    own_index = jnp.arange(RING, dtype=jnp.int32)
    clear = jnp.minimum((starts[:, 0, -1] + BLOCK - 1) // BLOCK, own_index)
    mixed_far, inverse_total = attend(first, clear, qkv, starts)
    mixed_t = exchange(mixed_far, 2).reshape(HEADS * HEAD_DIM, rows)

    middle = resid_in + dot_dims(mixed_t, o_full, 0, 0)
    ffn_low = rms_norm(middle, ffn_gain).astype(BF16)
    gate_pre = jnp.dot(ffn_low, gate_full, preferred_element_type=F32)
    up_pre = jnp.dot(ffn_low, up_full, preferred_element_type=F32)
    gate_sig = jax.nn.sigmoid(gate_pre)
    gate_act = gate_pre * gate_sig
    hidden_low = (gate_act * up_pre).astype(BF16)
    result = middle + jnp.dot(hidden_low, down_full, preferred_element_type=F32)
    output = result.astype(BF16)[None]
    cot_low = d_output[0]
    cotangent = cot_low.astype(F32)
    grad_hidden = against(cot_low, down_full)
    gate_back = (grad_hidden * up_pre * (gate_sig * (1.0 + gate_pre * (1.0 - gate_sig)))).astype(
        BF16
    )
    up_back = (grad_hidden * gate_act).astype(BF16)
    grad_ffn_in = against(gate_back, gate_full) + against(up_back, up_full)
    middle_part, ffn_terms = rms_back(middle, ffn_gain, grad_ffn_in)
    grad_middle = cotangent + middle_part
    middle_low = grad_middle.astype(BF16)
    grad_mixed = dot_dims(o_full, middle_low, 1, 1).astype(BF16)

    gate_t, up_t, down_t, out_t, back_home = back_call(
        3,
        gate_back,
        up_back,
        hidden_low,
        cot_low,
        middle_low,
        ffn_low,
        mixed_t,
        grad_mixed.reshape(HEADS, HEAD_DIM, rows),
        qkv,
        starts,
        mixed_far,
        inverse_total,
    )
    d_tokens, qkv_grads, gain_totals = tail_call(
        4,
        back_home,
        query_raw,
        key_raw,
        cosine,
        sine,
        query_gain[:, None],
        key_gain[:, None],
        kvq_full,
        normed_low,
        tokens[0],
        attn_gain[None, :],
        grad_middle,
        jnp.sum(ffn_terms, axis=0, keepdims=True),
    )
    return (
        output,
        d_tokens[None],
        gain_totals[0],
        qkv_grads[:64].T,
        qkv_grads[64:96].T,
        qkv_grads[96:].T,
        gain_totals[2, :HEAD_DIM],
        gain_totals[3, :HEAD_DIM],
        out_t.T,
        gain_totals[1],
        gate_t.T,
        up_t.T,
        down_t.T,
    )


def solution(mesh):
    in_specs = (
        P("fsdp", "ctx", None),
        P("fsdp", "ctx"),
        P("fsdp", "ctx"),
        P(),
        P("fsdp", None),
        P("fsdp", None),
        P("fsdp", None),
        P(),
        P(),
        P("fsdp", None),
        P(),
        P("fsdp", None),
        P("fsdp", None),
        P("fsdp", None),
        P("fsdp", "ctx", None),
    )
    out_specs = (
        P("fsdp", "ctx", None),
        P("fsdp", "ctx", None),
        P(),
        P("fsdp", "ctx"),
        P("fsdp", "ctx"),
        P("fsdp", "ctx"),
        P(),
        P(),
        P("fsdp", "ctx"),
        P(),
        P("fsdp", "ctx"),
        P("fsdp", "ctx"),
        P("fsdp", "ctx"),
    )
    chosen = heads_body if (mesh.shape["ctx"], mesh.shape["fsdp"]) == (HEADS, 2) else ring_body
    return jax.shard_map(chosen, mesh=mesh, in_specs=in_specs, out_specs=out_specs, check_vma=False)
```

```python
import functools

import jax
import jax.numpy as jnp
from jax import lax
from jax.experimental import pallas as pl
from jax.experimental.pallas import tpu as pltpu
from jax.sharding import PartitionSpec as P

HEADS = 16
KV_HEADS = 8
HEAD_DIM = 64
HOPS = 8


EPSILON = 1e-05
THETA = 1000000.0
MASKED = -1e30


def from_behind(block, axis, distance):
    devices = range(lax.axis_size(axis))
    route = [(i - distance, i) for i in devices if i - distance in devices]
    return lax.ppermute(block, axis, route)


def rms_norm(values, norm_gain):
    return (
        values * lax.rsqrt(jnp.mean(values * values, axis=-1, keepdims=True) + EPSILON) * norm_gain
    )


def rms_back(values, norm_gain, upstream):
    inverse = lax.rsqrt(jnp.mean(values * values, axis=-1, keepdims=True) + EPSILON)
    scaled = upstream * norm_gain
    row_width = values.shape[-1]
    d_values = (
        inverse * scaled
        - values * inverse**3 * jnp.sum(scaled * values, axis=-1, keepdims=True) / row_width
    )
    return (d_values, upstream * values * inverse)


def rotary(values, positions, turn_sign):
    half_dim = values.shape[-1] // 2
    inverse_freq = THETA ** (-(2.0 / values.shape[-1]) * jnp.arange(half_dim, dtype=jnp.float32))
    angles = positions.astype(jnp.float32)[:, None] * inverse_freq[None, :]
    cosine = jnp.cos(angles)[:, None, :]
    sine_part = turn_sign * jnp.sin(angles)[:, None, :]
    first_half = values[..., :half_dim]
    second_half = values[..., half_dim:]
    return jnp.concatenate(
        [
            first_half * cosine - second_half * sine_part,
            second_half * cosine + first_half * sine_part,
        ],
        axis=-1,
    )


def outer_product(left_mat, right_mat):
    return lax.dot_general(
        left_mat, right_mat, (((0,), (0,)), ((), ())), preferred_element_type=jnp.float32
    )


def against(left_mat, right_mat):
    return lax.dot_general(
        left_mat, right_mat, (((1,), (1,)), ((), ())), preferred_element_type=jnp.float32
    )


def ring_body(
    tokens,
    seg_ids,
    doc_pos,
    attn_gain,
    w_query,
    w_key,
    w_value,
    query_gain,
    key_gain,
    w_out,
    ffn_gain,
    w_gate,
    w_up,
    w_down,
    d_output,
):
    cycle_place = lax.axis_index("ctx")
    tok_rows = tokens.shape[1]
    resid_in = tokens[0].astype(jnp.float32)
    seg_local = seg_ids[0]
    pos_local = doc_pos[0]
    q_per_kv = HEADS // KV_HEADS
    group_cols = q_per_kv * HEAD_DIM
    score_scale = HEAD_DIM ** (-0.5)
    q_full, k_full, v_full, o_full = (
        lax.all_gather(w_query, "fsdp", axis=0, tiled=True),
        lax.all_gather(w_key, "fsdp", axis=0, tiled=True),
        lax.all_gather(w_value, "fsdp", axis=0, tiled=True),
        lax.all_gather(w_out, "fsdp", axis=0, tiled=True),
    )
    gate_full, up_full, down_full = (
        lax.all_gather(w_gate, "fsdp", axis=0, tiled=True),
        lax.all_gather(w_up, "fsdp", axis=0, tiled=True),
        lax.all_gather(w_down, "fsdp", axis=0, tiled=True),
    )
    normed = rms_norm(resid_in, attn_gain)
    normed_low = normed.astype(jnp.bfloat16)
    query_raw = jnp.dot(normed_low, q_full, preferred_element_type=jnp.float32).reshape(
        tok_rows, HEADS, HEAD_DIM
    )
    key_raw = jnp.dot(normed_low, k_full, preferred_element_type=jnp.float32).reshape(
        tok_rows, KV_HEADS, HEAD_DIM
    )
    value_raw = jnp.dot(normed_low, v_full, preferred_element_type=jnp.float32)
    query_rot = rotary(rms_norm(query_raw, query_gain), pos_local, 1.0)
    key_rot = rotary(rms_norm(key_raw, key_gain), pos_local, 1.0)
    query_low = query_rot.astype(jnp.bfloat16).reshape(tok_rows, HEADS * HEAD_DIM)
    key_low = key_rot.astype(jnp.bfloat16).reshape(tok_rows, KV_HEADS * HEAD_DIM)
    value_low = value_raw.astype(jnp.bfloat16)
    own_kv = (key_low, value_low, seg_local)
    kv_blocks = [own_kv]
    carried = own_kv
    for hop_index in range(HOPS):
        carried = from_behind((carried[0], carried[1], carried[2]), "ctx", 1)
        kv_blocks.append(carried)
    key_all = jnp.concatenate([kv_entry[0] for kv_entry in kv_blocks], axis=0)
    value_all = jnp.concatenate([kv_entry[1] for kv_entry in kv_blocks], axis=0)
    seg_all = jnp.concatenate([kv_entry[2] for kv_entry in kv_blocks], axis=0)
    key_owner = cycle_place - jnp.arange(HOPS + 1, dtype=jnp.int32)
    owner_valid = jnp.repeat(key_owner >= 0, tok_rows)
    key_index = (
        key_owner[:, None] * tok_rows + jnp.arange(tok_rows, dtype=jnp.int32)[None, :]
    ).reshape(-1)
    query_index = cycle_place * tok_rows + jnp.arange(tok_rows, dtype=jnp.int32)
    allowed = (
        (seg_local[:, None] == seg_all[None, :])
        & (key_index[None, :] <= query_index[:, None])
        & owner_valid[None, :]
    )

    def group_scores(kv_group):
        query_part = lax.dynamic_slice_in_dim(query_low, kv_group * group_cols, group_cols, 1)
        query_part = query_part.reshape(tok_rows, q_per_kv, HEAD_DIM)
        key_part = lax.dynamic_slice_in_dim(key_all, kv_group * HEAD_DIM, HEAD_DIM, 1)
        value_part = lax.dynamic_slice_in_dim(value_all, kv_group * HEAD_DIM, HEAD_DIM, 1)
        scores = (
            jnp.einsum("trd,kd->rtk", query_part, key_part, preferred_element_type=jnp.float32)
            * score_scale
        )
        return (jnp.where(allowed[None], scores, MASKED), query_part, key_part, value_part)

    def forward_group(kv_group):
        scores, query_part, key_part, value_part = group_scores(kv_group)
        row_top = jnp.max(scores, axis=-1, keepdims=True)
        log_total = row_top + jnp.log(jnp.sum(jnp.exp(scores - row_top), axis=-1, keepdims=True))
        attn_probs = jnp.exp(scores - log_total)
        mixed_part = jnp.einsum(
            "rtk,kd->trd",
            attn_probs.astype(jnp.bfloat16),
            value_part,
            preferred_element_type=jnp.float32,
        )
        return (mixed_part.reshape(tok_rows, group_cols), log_total[..., 0])

    mixed_groups, total_groups = lax.map(forward_group, jnp.arange(KV_HEADS, dtype=jnp.int32))
    mixed = mixed_groups.transpose(1, 0, 2).reshape(tok_rows, HEADS * HEAD_DIM)
    mixed_low = mixed.astype(jnp.bfloat16)
    middle = resid_in + jnp.dot(mixed_low, o_full, preferred_element_type=jnp.float32)
    ffn_low = rms_norm(middle, ffn_gain).astype(jnp.bfloat16)
    gate_pre = jnp.dot(ffn_low, gate_full, preferred_element_type=jnp.float32)
    up_pre = jnp.dot(ffn_low, up_full, preferred_element_type=jnp.float32)
    gate_sig = jax.nn.sigmoid(gate_pre)
    gate_act = gate_pre * gate_sig
    hidden_low = (gate_act * up_pre).astype(jnp.bfloat16)
    result = middle + jnp.dot(hidden_low, down_full, preferred_element_type=jnp.float32)
    output = result.astype(jnp.bfloat16)[None]
    cot_low = d_output[0]
    cotangent = cot_low.astype(jnp.float32)
    grad_w_down = outer_product(hidden_low, cot_low)
    grad_hidden = against(cot_low, down_full)
    gate_back = (grad_hidden * up_pre * (gate_sig * (1.0 + gate_pre * (1.0 - gate_sig)))).astype(
        jnp.bfloat16
    )
    up_back = (grad_hidden * gate_act).astype(jnp.bfloat16)
    grad_w_gate = outer_product(ffn_low, gate_back)
    grad_w_up = outer_product(ffn_low, up_back)
    grad_ffn_in = against(gate_back, gate_full) + against(up_back, up_full)
    middle_part, ffn_terms = rms_back(middle, ffn_gain, grad_ffn_in)
    grad_middle = cotangent + middle_part
    middle_low = grad_middle.astype(jnp.bfloat16)
    grad_w_out = outer_product(mixed_low, middle_low)
    grad_mixed = against(middle_low, o_full).astype(jnp.bfloat16)

    def backward_group(kv_group):
        scores, query_part, key_part, value_part = group_scores(kv_group)
        attn_probs = jnp.exp(scores - total_groups[kv_group][..., None])
        mixed_grad_part = lax.dynamic_slice_in_dim(grad_mixed, kv_group * group_cols, group_cols, 1)
        mixed_grad_part = mixed_grad_part.reshape(tok_rows, q_per_kv, HEAD_DIM)
        grad_probs = jnp.einsum(
            "trd,kd->rtk", mixed_grad_part, value_part, preferred_element_type=jnp.float32
        )
        grad_value = jnp.einsum(
            "rtk,trd->kd",
            attn_probs.astype(jnp.bfloat16),
            mixed_grad_part,
            preferred_element_type=jnp.float32,
        )
        row_delta = jnp.sum(grad_probs * attn_probs, axis=-1, keepdims=True)
        grad_scores = (attn_probs * (grad_probs - row_delta)).astype(jnp.bfloat16)
        grad_query = (
            jnp.einsum("rtk,kd->trd", grad_scores, key_part, preferred_element_type=jnp.float32)
            * score_scale
        )
        grad_key = (
            jnp.einsum("rtk,trd->kd", grad_scores, query_part, preferred_element_type=jnp.float32)
            * score_scale
        )
        return (grad_query.reshape(tok_rows, group_cols), grad_key, grad_value)

    query_groups, key_groups, value_groups = lax.map(
        backward_group, jnp.arange(KV_HEADS, dtype=jnp.int32)
    )
    grad_query_rot = query_groups.transpose(1, 0, 2).reshape(tok_rows, HEADS, HEAD_DIM)
    key_blocks = key_groups.transpose(1, 0, 2).reshape(HOPS + 1, tok_rows, KV_HEADS * HEAD_DIM)
    value_blocks = value_groups.transpose(1, 0, 2).reshape(HOPS + 1, tok_rows, KV_HEADS * HEAD_DIM)
    home_key = key_blocks[HOPS]
    home_value = value_blocks[HOPS]
    for hop_index in range(HOPS, 0, -1):
        moved_key, moved_value = (
            from_behind(home_key.astype(jnp.bfloat16), "ctx", -1).astype(home_key.dtype),
            from_behind(home_value.astype(jnp.bfloat16), "ctx", -1).astype(home_value.dtype),
        )
        home_key = moved_key + key_blocks[hop_index - 1]
        home_value = moved_value + value_blocks[hop_index - 1]
    query_turned = rotary(grad_query_rot, pos_local, -1.0)
    key_turned = rotary(home_key.reshape(tok_rows, KV_HEADS, HEAD_DIM), pos_local, -1.0)
    query_back, query_terms = rms_back(query_raw, query_gain, query_turned)
    key_back, key_terms = rms_back(key_raw, key_gain, key_turned)
    query_back = query_back.reshape(tok_rows, HEADS * HEAD_DIM).astype(jnp.bfloat16)
    key_back = key_back.reshape(tok_rows, KV_HEADS * HEAD_DIM).astype(jnp.bfloat16)
    value_back = home_value.astype(jnp.bfloat16)
    grad_w_query = outer_product(normed_low, query_back)
    grad_w_key = outer_product(normed_low, key_back)
    grad_w_value = outer_product(normed_low, value_back)
    grad_normed = (
        against(query_back, q_full) + against(key_back, k_full) + against(value_back, v_full)
    )
    input_part, attn_terms = rms_back(resid_in, attn_gain, grad_normed)
    d_tokens = (grad_middle + input_part)[None]
    gain_totals = lax.psum(
        (
            jnp.sum(attn_terms, axis=0),
            jnp.sum(ffn_terms, axis=0),
            jnp.sum(query_terms, axis=(0, 1)),
            jnp.sum(key_terms, axis=(0, 1)),
        ),
        ("ctx", "fsdp"),
    )
    weight_grads = (
        grad_w_query,
        grad_w_key,
        grad_w_value,
        grad_w_out,
        grad_w_gate,
        grad_w_up,
        grad_w_down,
    )
    spread = (
        lax.psum_scatter(
            weight_grads[0].astype(jnp.bfloat16), "fsdp", scatter_dimension=0, tiled=True
        ).astype(jnp.float32),
        lax.psum_scatter(
            weight_grads[1].astype(jnp.bfloat16), "fsdp", scatter_dimension=0, tiled=True
        ).astype(jnp.float32),
        lax.psum_scatter(
            weight_grads[2].astype(jnp.bfloat16), "fsdp", scatter_dimension=0, tiled=True
        ).astype(jnp.float32),
        lax.psum_scatter(
            weight_grads[3].astype(jnp.bfloat16), "fsdp", scatter_dimension=0, tiled=True
        ).astype(jnp.float32),
        lax.psum_scatter(
            weight_grads[4].astype(jnp.bfloat16), "fsdp", scatter_dimension=0, tiled=True
        ).astype(jnp.float32),
        lax.psum_scatter(
            weight_grads[5].astype(jnp.bfloat16), "fsdp", scatter_dimension=0, tiled=True
        ).astype(jnp.float32),
        lax.psum_scatter(
            weight_grads[6].astype(jnp.bfloat16), "fsdp", scatter_dimension=0, tiled=True
        ).astype(jnp.float32),
    )
    shares = (
        lax.psum_scatter(spread[0], "ctx", scatter_dimension=1, tiled=True),
        lax.psum_scatter(spread[1], "ctx", scatter_dimension=1, tiled=True),
        lax.psum_scatter(spread[2], "ctx", scatter_dimension=1, tiled=True),
        lax.psum_scatter(spread[3], "ctx", scatter_dimension=1, tiled=True),
        lax.psum_scatter(spread[4], "ctx", scatter_dimension=1, tiled=True),
        lax.psum_scatter(spread[5], "ctx", scatter_dimension=1, tiled=True),
        lax.psum_scatter(spread[6], "ctx", scatter_dimension=1, tiled=True),
    )
    return (
        output,
        d_tokens,
        gain_totals[0],
        shares[0],
        shares[1],
        shares[2],
        gain_totals[2],
        gain_totals[3],
        shares[3],
        gain_totals[1],
        shares[4],
        shares[5],
        shares[6],
    )


MESH = pl.DeviceIdType.MESH
BLOCK = 256
RING = 16
VMEM_SPEC = pl.BlockSpec(memory_space=pltpu.VMEM)
HBM_SPEC = pl.BlockSpec(memory_space=pltpu.HBM)
SMEM_SPEC = pl.BlockSpec(memory_space=pltpu.SMEM)
F32 = jnp.float32
BF16 = jnp.bfloat16


def dot_dims(left_mat, right_mat, left_dim, right_dim):
    return lax.dot_general(
        left_mat, right_mat, (((left_dim,), (right_dim,)), ((), ())), preferred_element_type=F32
    )


def exchange_kernel(src, dst, own_sem, send_sem, recv_sem):
    place, core = lax.axis_index("ctx"), lax.axis_index("fsdp")
    barrier = pltpu.get_barrier_semaphore()
    for step in range(1, RING):
        peer = lax.rem(place + step, RING)
        pl.semaphore_signal(barrier, inc=1, device_id=(peer, core), device_id_type=MESH)
    own = pltpu.make_async_copy(src.at[place], dst.at[place], own_sem)
    own.start()
    pl.semaphore_wait(barrier, RING - 1)
    copies = []
    for step in range(1, RING):
        peer = lax.rem(place + step, RING)
        copy = pltpu.make_async_remote_copy(
            src_ref=src.at[peer],
            dst_ref=dst.at[place],
            send_sem=send_sem.at[step],
            recv_sem=recv_sem.at[step],
            device_id=(peer, core),
            device_id_type=MESH,
        )
        copy.start()
        copies.append(copy)
    own.wait()
    for copy in copies:
        copy.wait()


def exchange(blocks, call_id):
    return pl.pallas_call(
        exchange_kernel,
        out_shape=jax.ShapeDtypeStruct(blocks.shape, blocks.dtype),
        in_specs=[VMEM_SPEC],
        out_specs=VMEM_SPEC,
        scratch_shapes=[
            pltpu.SemaphoreType.DMA,
            pltpu.SemaphoreType.DMA((RING,)),
            pltpu.SemaphoreType.DMA((RING,)),
        ],
        compiler_params=pltpu.CompilerParams(collective_id=call_id, has_side_effects=True),
        name="exchange_heads",
    )(blocks)


def transposed(block):
    return block.astype(F32).T.astype(BF16)


def block_probs(key_nat, query_t, first_key, start, query_place, diagonal, masked):
    scores = jnp.dot(key_nat, query_t, preferred_element_type=F32)
    probs = jnp.exp(scores)
    if masked:
        key_place = first_key + lax.broadcasted_iota(jnp.int32, probs.shape, 0)
        ok = key_place >= start
        if diagonal:
            ok = ok & (key_place <= query_place)
        probs = jnp.where(ok, probs, 0.0)
    return probs


def attend_kernel(first_ref, clear_ref, qkv_ref, start_ref, mixed_ref, inv_ref, key_nat):
    blocks = qkv_ref.shape[0]

    def turn(j, carry):
        key_nat[j] = transposed(qkv_ref[j, HEAD_DIM : 2 * HEAD_DIM, :])
        return carry

    lax.fori_loop(0, blocks, turn, 0)

    def per_query(i, nothing):
        query_t = qkv_ref[i, 0:HEAD_DIM, :] * jnp.asarray(HEAD_DIM**-0.5, BF16)
        start = start_ref[i]
        query_place = i * BLOCK + lax.broadcasted_iota(jnp.int32, (1, BLOCK), 1)

        def step(diagonal, masked, j, carry):
            total, acc = carry
            probs = block_probs(
                key_nat[j], query_t, j * BLOCK, start, query_place, diagonal, masked
            )
            total = total + jnp.sum(probs, axis=0, keepdims=True)
            acc = acc + jnp.dot(
                qkv_ref[j, 2 * HEAD_DIM : 3 * HEAD_DIM, :],
                probs.astype(BF16),
                preferred_element_type=F32,
            )
            return total, acc

        carry = (jnp.zeros((1, BLOCK), F32), jnp.zeros((HEAD_DIM, BLOCK), F32))
        carry = lax.fori_loop(
            first_ref[i], clear_ref[i], functools.partial(step, False, True), carry
        )
        carry = lax.fori_loop(clear_ref[i], i, functools.partial(step, False, False), carry)
        total, acc = step(True, True, i, carry)
        inverse = 1.0 / total
        mixed_ref[i] = (acc * inverse).astype(BF16)
        inv_ref[i] = inverse
        return nothing

    lax.fori_loop(0, blocks, per_query, 0)


def attend(first, clear, qkv, start):
    blocks = qkv.shape[0]
    return pl.pallas_call(
        attend_kernel,
        out_shape=(
            jax.ShapeDtypeStruct((blocks, HEAD_DIM, BLOCK), BF16),
            jax.ShapeDtypeStruct((blocks, 1, BLOCK), F32),
        ),
        in_specs=[SMEM_SPEC, SMEM_SPEC, VMEM_SPEC, VMEM_SPEC],
        out_specs=(VMEM_SPEC, VMEM_SPEC),
        scratch_shapes=[pltpu.VMEM((blocks, BLOCK, HEAD_DIM), BF16)],
        name="attend_forward",
    )(first, clear, qkv, start)


def flip(bit, turned):
    return bit + turned - 2 * bit * turned


class Spread:
    def __init__(self, chain, compute, sent, came, send_sems, recv_sems):
        place, self.core = lax.axis_index("ctx"), lax.axis_index("fsdp")
        x, y, self.z = lax.rem(place, 2), lax.rem(place // 2, 2), place // 4
        self.chain = chain
        self.first, self.second = (x, y) if chain == 0 else (y, x)
        self.compute, self.sent, self.came = compute, sent, came
        self.send_sems, self.recv_sems = send_sems, recv_sems

    def at(self, first, second, depth):
        low = second * 2 + first if self.chain == 0 else first * 2 + second
        return depth * 4 + low

    def deep(self, depth):
        return lax.rem(self.z + depth, 4)

    def copy(self, stage, slot):
        if stage == 0:
            peer = self.at(1 - self.first, self.second, self.z)
            source, target, sem = self.sent.at[slot], self.came[0].at[slot], slot
        elif stage == 1:
            peer = self.at(self.first, 1 - self.second, self.z)
            source, target, sem = self.came[0].at[4 + slot], self.came[1].at[slot], 8 + slot
        else:
            peer = self.at(self.first, self.second, self.deep(slot))
            source, target, sem = self.came[0].at[slot], self.came[2].at[slot - 1], 11 + slot
        return pltpu.make_async_remote_copy(
            src_ref=source,
            dst_ref=target,
            send_sem=self.send_sems.at[self.chain, sem],
            recv_sem=self.recv_sems.at[self.chain, sem],
            device_id=(peer, self.core),
            device_id_type=MESH,
        )

    def stage_one(self, turned, depth):
        slot = turned * 4 + depth
        owner = self.at(1 - self.first, flip(self.second, turned), self.deep(depth))
        for row, value in self.compute(self.chain, owner):
            self.sent[slot, row : row + value.shape[0], :] = value.astype(BF16)
        self.copy(0, slot).start()

    def stage_two(self, depth):
        self.copy(0, 4 + depth).wait_recv()
        owner = self.at(self.first, 1 - self.second, self.deep(depth))
        for row, value in self.compute(self.chain, owner):
            window = slice(row, row + value.shape[0])
            value = value + self.came[0][4 + depth, window, :].astype(F32)
            self.came[0][4 + depth, window, :] = value.astype(BF16)
        self.copy(1, depth).start()

    def stage_three(self, depth):
        self.copy(0, depth).wait_recv()
        self.copy(1, depth).wait_recv()
        owner = self.at(self.first, self.second, self.deep(depth))
        for row, value in self.compute(self.chain, owner):
            window = slice(row, row + value.shape[0])
            value = value + self.came[0][depth, window, :].astype(F32)
            value = value + self.came[1][depth, window, :].astype(F32)
            self.came[0][depth, window, :] = value.astype(BF16)
        self.copy(2, depth).start()

    def close(self, finish):
        self.copy(0, 0).wait_recv()
        self.copy(1, 0).wait_recv()
        for depth in range(1, 4):
            self.copy(2, depth).wait_recv()
        owner = self.at(self.first, self.second, self.z)
        for row, value in self.compute(self.chain, owner):
            window = slice(row, row + value.shape[0])
            value = value + self.came[0][0, window, :].astype(F32)
            value = value + self.came[1][0, window, :].astype(F32)
            for depth in range(3):
                value = value + self.came[2][depth, window, :].astype(F32)
            finish(self.chain, row, value)

    def drain_first(self):
        for slot in range(8):
            self.copy(0, slot).wait_send()

    def drain_last(self):
        for depth in range(4):
            self.copy(1, depth).wait_send()
        for depth in range(1, 4):
            self.copy(2, depth).wait_send()


def greet(peers):
    barrier = pltpu.get_barrier_semaphore()
    for peer in peers:
        pl.semaphore_signal(barrier, inc=1, device_id=peer, device_id_type=MESH)
    pl.semaphore_wait(barrier, len(peers))


def turn_back(values, cosine, sine):
    half = HEAD_DIM // 2
    first, second = values[:half], values[half:]
    return jnp.concatenate(
        [first * cosine + second * sine, second * cosine - first * sine], axis=0
    )


def column_norm_back(values, gain, upstream):
    inverse = lax.rsqrt(jnp.mean(values * values, axis=0, keepdims=True) + EPSILON)
    scaled = upstream * gain
    total = jnp.sum(scaled * values, axis=0, keepdims=True) / values.shape[0]
    return inverse * scaled - values * inverse**3 * total, upstream * values * inverse


def back_kernel(
    pair_own,
    hidden_hbm,
    side_own,
    ffn_ref,
    mixed_ref,
    home_ref,
    qkv_ref,
    start_ref,
    part_ref,
    inv_ref,
    cosine_ref,
    sine_ref,
    query_gain_ref,
    key_gain_ref,
    normed_ref,
    attn_gain_ref,
    ffn_terms_ref,
    tokens_hbm,
    query_hbm,
    key_hbm,
    weights_hbm,
    middle_hbm,
    gate_out,
    up_out,
    down_out,
    out_out,
    grads_out,
    tokens_out,
    gains_out,
    pair_far,
    side_far,
    hidden_own,
    hidden_far,
    ffn_far,
    mixed_far,
    normed_far,
    cot_far,
    back_own,
    back_far,
    turned_own,
    turned_far,
    gain_own,
    gain_came,
    gain_deep,
    sent_a,
    came_a0,
    came_a1,
    came_a2,
    sent_b,
    came_b0,
    came_b1,
    came_b2,
    tail_sent_a,
    tail_came_a0,
    tail_came_a1,
    tail_came_a2,
    tail_sent_b,
    tail_came_b0,
    tail_came_b1,
    tail_came_b2,
    send_sems,
    recv_sems,
    tail_send,
    tail_recv,
    cot_send,
    cot_recv,
    back_send,
    back_recv,
    core_send,
    core_recv,
    gain_send,
    gain_recv,
    load_sem,
    weight_sem,
):
    place, core = lax.axis_index("ctx"), lax.axis_index("fsdp")
    x, y, z = lax.rem(place, 2), lax.rem(place // 2, 2), place // 4
    blocks = qkv_ref.shape[0]
    wide = pair_own.shape[1] // 2
    narrow = side_own.shape[1] // RING
    half_hidden = hidden_far.shape[1]
    half_width = ffn_far.shape[1]
    heads, pairs = query_hbm.shape[0], key_hbm.shape[0]
    group = heads // pairs
    scale = HEAD_DIM**-0.5
    partner = (place, 1 - core)

    def half(part, size):
        return pl.ds(pl.multiple_of(part * size, 128), size)

    own_hidden = pltpu.make_async_copy(
        hidden_hbm.at[:, half(core, half_hidden)], hidden_own, load_sem.at[0]
    )
    own_hidden.start()
    middle_load = pltpu.make_async_copy(middle_hbm, tokens_out, load_sem.at[1])
    middle_load.start()
    greet([(lax.rem(place + step, RING), core) for step in range(1, RING)] + [partner])

    def remote(source, target, send, recv, peer):
        return pltpu.make_async_remote_copy(
            src_ref=source,
            dst_ref=target,
            send_sem=send,
            recv_sem=recv,
            device_id=peer,
            device_id_type=MESH,
        )

    def cot_copy(step, peer):
        return remote(
            home_ref.at[peer], cot_far.at[place], cot_send.at[step], cot_recv.at[step], (peer, core)
        )

    def core_copy(source, target, sem):
        return remote(source, target, core_send.at[sem], core_recv.at[sem], partner)

    def pair_copy(turn_x, turn_y, depth):
        owner = lax.rem(z + depth, 4) * 4 + flip(y, turn_y) * 2 + flip(x, turn_x)
        return core_copy(
            pair_own.at[owner], pair_far.at[owner], 6 + turn_x * 8 + turn_y * 4 + depth
        )

    sides = [
        core_copy(ffn_ref.at[:, half(1 - core, half_width)], ffn_far, 0),
        core_copy(mixed_ref.at[half(1 - core, half_width), :], mixed_far, 1),
        core_copy(side_own, side_far, 2),
        core_copy(hidden_hbm.at[:, half(1 - core, half_hidden)], hidden_far, 3),
    ]
    order = []
    for depth in (2, 1, 3, 0):
        order += [(1, 1, depth), (1, 0, depth), (0, 1, depth)]
    order += [(0, 0, depth) for depth in (2, 1, 3, 0)]
    for copy in sides:
        copy.start()
    pair_copy(*order[0]).start()
    for step in range(1, RING):
        cot_copy(step, lax.rem(place + step, RING)).start()
    for turn_x, turn_y, depth in order[1:]:
        pair_copy(turn_x, turn_y, depth).start()
    normed_copy = core_copy(normed_ref.at[:, half(1 - core, half_width)], normed_far, 4)
    normed_copy.start()
    cot_far[place] = home_ref[place]

    def compute(chain, owner):
        lanes = pl.ds(chain * 256, 256)
        own_lanes = pl.ds(pl.multiple_of(core * half_width + chain * 256, 128), 256)
        both_pair = jnp.dot(pair_own[owner], ffn_ref[:, own_lanes], preferred_element_type=F32)
        both_pair += jnp.dot(pair_far[owner], ffn_far[:, lanes], preferred_element_type=F32)
        values = [(0, both_pair)]
        rows = pl.ds(pl.multiple_of(owner * narrow, 16), narrow)
        begin, chunks = (0, 5) if chain == 0 else (5, 4)
        cols = slice(begin * 256, (begin + chunks) * 256)
        down = jnp.dot(side_own[0, rows, :], hidden_own[:, cols], preferred_element_type=F32)
        down += jnp.dot(side_far[0, rows, :], hidden_far[:, cols], preferred_element_type=F32)
        row = 2 * wide
        for chunk in range(chunks):
            values.append((row, down[:, chunk * 256 : chunk * 256 + 256]))
            row += narrow
        out = dot_dims(side_own[1, rows, :], mixed_ref[own_lanes, :], 1, 1)
        out += dot_dims(side_far[1, rows, :], mixed_far[lanes, :], 1, 1)
        values.append((row, out))
        return values

    def finish(chain, row, value):
        lanes = slice(chain * 256, chain * 256 + 256)
        if row == 0:
            gate_out[:, lanes] = value[:wide]
            up_out[:, lanes] = value[wide:]
            return
        chunk = (row - 2 * wide) // narrow
        if chunk == 5 - chain:
            out_out[:, lanes] = value
        else:
            chunk += 5 * chain
            down_out[:, chunk * 256 : chunk * 256 + 256] = value

    chains = (
        Spread(0, compute, sent_a, (came_a0, came_a1, came_a2), send_sems, recv_sems),
        Spread(1, compute, sent_b, (came_b0, came_b1, came_b2), send_sems, recv_sems),
    )
    own_hidden.wait()
    for copy in sides:
        copy.wait_recv()

    def near(depth):
        pair_copy(1, 1, depth).wait_recv()
        for chain in chains:
            chain.stage_one(1, depth)

    def far(depth):
        pair_copy(1, 0, depth).wait_recv()
        pair_copy(0, 1, depth).wait_recv()
        for chain in chains:
            chain.stage_one(0, depth)

    def onward(depth):
        for chain in chains:
            chain.stage_two(depth)

    def deeper(depth):
        pair_copy(0, 0, depth).wait_recv()
        for chain in chains:
            chain.stage_three(depth)

    near(2)
    far(2)
    near(1)

    def back_copy(step, peer):
        return remote(
            back_own.at[peer],
            back_far.at[place],
            back_send.at[step],
            back_recv.at[step],
            (peer, core),
        )

    def attention(scaled, natural, delta_ref, query_acc, key_nat, value_nat, pair_acc):
        def prepare(i):
            @pl.when(i != place)
            def _():
                step = lax.rem(place - i + RING, RING)
                cot_copy(step, lax.rem(place + step, RING)).wait_recv()

            query = qkv_ref[i, 0:HEAD_DIM, :] * jnp.asarray(scale, BF16)
            cot = cot_far[i]
            scaled[i] = query
            natural[i] = transposed(jnp.concatenate([query, cot], axis=0))
            delta_ref[i] = jnp.sum(
                cot.astype(F32) * part_ref[i].astype(F32), axis=0, keepdims=True
            )
            query_acc[i] = jnp.zeros(query_acc.shape[1:], F32)

        def prepare_one(i, nothing):
            prepare(i)
            return nothing

        def per_key(j, nothing):
            @pl.when(j + 8 < blocks)
            def _():
                prepare(j + 8)

            key_nat[...] = transposed(qkv_ref[j, HEAD_DIM : 2 * HEAD_DIM, :])
            value_nat[...] = transposed(qkv_ref[j, 2 * HEAD_DIM : 3 * HEAD_DIM, :])
            key_place = j * BLOCK + lax.broadcasted_iota(jnp.int32, (BLOCK, BLOCK), 0)

            def step(diagonal, i):
                inside = jnp.minimum(i, blocks - 1)
                start = start_ref[inside] + (i // blocks) * (blocks * BLOCK)
                scores = jnp.dot(key_nat[...], scaled[inside], preferred_element_type=F32)
                grad_probs = jnp.dot(value_nat[...], cot_far[inside], preferred_element_type=F32)
                ok = key_place >= start
                if diagonal:
                    query_place = i * BLOCK + lax.broadcasted_iota(jnp.int32, (1, BLOCK), 1)
                    ok = ok & (key_place <= query_place)
                probs = jnp.where(ok, jnp.exp(scores) * inv_ref[inside], 0.0)
                grad_scores = (probs * (grad_probs - delta_ref[inside])).astype(BF16)
                both_low = jnp.concatenate([grad_scores, probs.astype(BF16)], axis=0)
                query_acc[i] += jnp.dot(
                    qkv_ref[j, HEAD_DIM : 2 * HEAD_DIM, :],
                    grad_scores,
                    preferred_element_type=F32,
                )
                return jnp.dot(both_low, natural[inside], preferred_element_type=F32)

            pair_acc[...] = step(True, j)
            count = (jnp.minimum(8, blocks - 1 - j) + 1) // 2

            def two(index, carry):
                i = j + 1 + 2 * index
                pair_acc[...] += step(False, i) + step(False, i + 1)
                return carry

            lax.fori_loop(0, count, two, 0)
            back_own[j, 0:HEAD_DIM, :] = (query_acc[j] * scale).astype(BF16)
            first = lax.broadcasted_iota(jnp.int32, (BLOCK, 2 * HEAD_DIM), 1) < HEAD_DIM
            merged = jnp.where(first, pair_acc[0:BLOCK, :], pair_acc[BLOCK:, :])
            back_own[j, HEAD_DIM : 3 * HEAD_DIM, :] = merged.T.astype(BF16)

            @pl.when(j != place)
            def _():
                back_copy(lax.rem(j - place + RING, RING), j).start()

            @pl.when(j == 4)
            def _():
                onward(2)
                far(1)

            @pl.when(j == 9)
            def _():
                near(3)

            return nothing

        lax.fori_loop(0, 8, prepare_one, 0)
        lax.fori_loop(0, blocks, per_key, 0)
        back_far[place] = back_own[place]

    pl.run_scoped(
        attention,
        pltpu.VMEM((blocks, HEAD_DIM, BLOCK), BF16),
        pltpu.VMEM((blocks, BLOCK, 2 * HEAD_DIM), BF16),
        pltpu.VMEM((blocks, 1, BLOCK), F32),
        pltpu.VMEM((blocks + 1, HEAD_DIM, BLOCK), F32),
        pltpu.VMEM((BLOCK, HEAD_DIM), BF16),
        pltpu.VMEM((BLOCK, HEAD_DIM), BF16),
        pltpu.VMEM((2 * BLOCK, 2 * HEAD_DIM), F32),
    )

    turned_copy = core_copy(turned_own, turned_far, 5)

    def tail_compute(chain, owner):
        lanes = slice(chain * 256, chain * 256 + 256)
        own_lanes = pl.ds(pl.multiple_of(core * half_width + chain * 256, 128), 256)
        values, row = [], 0
        for size, base in ((heads, 2 * pairs), (pairs, 0), (pairs, pairs)):
            count = size * HEAD_DIM // RING
            rows = pl.ds(pl.multiple_of(base * HEAD_DIM + owner * count, 16), count)
            value = jnp.dot(
                turned_own[rows, :], normed_ref[:, own_lanes], preferred_element_type=F32
            )
            value += jnp.dot(turned_far[rows, :], normed_far[:, lanes], preferred_element_type=F32)
            values.append((row, value))
            row += count
        return values

    def tail_finish(chain, row, value):
        grads_out[row : row + value.shape[0], chain * 256 : chain * 256 + 256] = value

    tails = (
        Spread(
            0,
            tail_compute,
            tail_sent_a,
            (tail_came_a0, tail_came_a1, tail_came_a2),
            tail_send,
            tail_recv,
        ),
        Spread(
            1,
            tail_compute,
            tail_sent_b,
            (tail_came_b0, tail_came_b1, tail_came_b2),
            tail_send,
            tail_recv,
        ),
    )

    near_x = (place + 1 - 2 * x, core)
    near_y = (place + 2 - 4 * y, core)

    def finish_all(natural, summed, query_ref, key_ref, tokens_ref):
        loads = [
            pltpu.make_async_copy(query_hbm, query_ref, load_sem.at[2]),
            pltpu.make_async_copy(key_hbm, key_ref, load_sem.at[3]),
            pltpu.make_async_copy(tokens_hbm, tokens_ref, load_sem.at[4]),
        ]
        for copy in loads:
            copy.start()
        cosine, sine = cosine_ref[...], sine_ref[...]

        def head_rows(index):
            return pl.ds(pl.multiple_of(index * HEAD_DIM, HEAD_DIM), HEAD_DIM)

        def query_head(head, total):
            upstream = turn_back(back_far[head, 0:HEAD_DIM, :].astype(F32), cosine, sine)
            back, terms = column_norm_back(query_ref[head], query_gain_ref[...], upstream)
            turned_own[head_rows(2 * pairs + head), :] = back.astype(BF16)
            return total + terms

        def key_head(pair, total):
            upstream = jnp.zeros((2 * HEAD_DIM, BLOCK), F32)
            for member in range(group):
                upstream += back_far[group * pair + member, HEAD_DIM : 3 * HEAD_DIM, :].astype(F32)
            back, terms = column_norm_back(
                key_ref[pair],
                key_gain_ref[...],
                turn_back(upstream[:HEAD_DIM], cosine, sine),
            )
            turned_own[head_rows(pair), :] = back.astype(BF16)
            turned_own[head_rows(pairs + pair), :] = upstream[HEAD_DIM:].astype(BF16)
            return total + terms

        def weight_load(part, column):
            slot = (sent_a, sent_b)[part]
            return pltpu.make_async_copy(
                weights_hbm.at[pl.ds(part * 512, 512), pl.ds(pl.multiple_of(column * 256, 256), 256)],
                slot.at[column, pl.ds(0, 512), :],
                weight_sem.at[part, column],
            )

        onward(1)
        deeper(2)
        far(3)
        near(0)

        def arrive(step, nothing):
            back_copy(step, lax.rem(place + step, RING)).wait_recv()
            return nothing

        lax.fori_loop(1, RING, arrive, 0)
        for copy in loads:
            copy.wait()
        nothing = jnp.zeros((HEAD_DIM, BLOCK), F32)
        query_terms = lax.fori_loop(0, heads, query_head, nothing)
        key_terms = lax.fori_loop(0, pairs, key_head, nothing)
        turned_copy.start()
        onward(3)
        deeper(1)
        far(0)
        for row in range(0, turned_own.shape[0], 128):
            natural[:, row : row + 128] = turned_own[row : row + 128, :].astype(F32).T.astype(BF16)
        normed_copy.wait_recv()
        turned_copy.wait_recv()

        def tail_one(index, carry):
            for chain in tails:
                chain.stage_one(1 - index // 4, lax.rem(index + 1, 4))
            return carry

        lax.fori_loop(0, 8, tail_one, 0)
        onward(0)

        def tail_two(index, carry):
            for chain in tails:
                chain.stage_two(lax.rem(index + 1, 4))
            return carry

        lax.fori_loop(0, 4, tail_two, 0)
        deeper(3)
        for chain in chains:
            chain.drain_first()
        for part in range(2):
            for column in range(8):
                weight_load(part, column).start()

        for part, slots in enumerate((sent_a, sent_b)):
            total = None
            for column in range(8):
                weight_load(part, column).wait()
                term = dot_dims(
                    natural[:, column * 256 : column * 256 + 256], slots[column, 0:512, :], 1, 1
                )
                total = term if total is None else total + term
            summed[:, part * 512 : part * 512 + 512] = total
        middle_load.wait()

        def token_rows(index, total):
            rows = pl.ds(pl.multiple_of(index * 32, 32), 32)
            values, upstream = tokens_ref[rows, :].astype(F32), summed[rows, :]
            inverse = lax.rsqrt(jnp.mean(values * values, axis=-1, keepdims=True) + EPSILON)
            scaled = upstream * attn_gain_ref[...]
            weight = jnp.sum(scaled * values, axis=-1, keepdims=True) / values.shape[1]
            tokens_out[rows, :] += inverse * scaled - values * inverse**3 * weight
            return total + jnp.sum(upstream * values * inverse, axis=0, keepdims=True)

        terms = lax.fori_loop(
            0, BLOCK // 32, token_rows, jnp.zeros((1, tokens_ref.shape[1]), F32)
        )
        gain_own[0] = jnp.zeros(gain_own.shape[1:], F32)
        gain_own[0, 0:1, :] = terms
        gain_own[0, 1:2, :] = ffn_terms_ref[...]
        gain_own[0, 2:3, 0:HEAD_DIM] = jnp.sum(query_terms.T, axis=0, keepdims=True)
        gain_own[0, 3:4, 0:HEAD_DIM] = jnp.sum(key_terms.T, axis=0, keepdims=True)

    width = normed_ref.shape[1]
    pl.run_scoped(
        finish_all,
        pltpu.VMEM((BLOCK, turned_own.shape[0]), BF16),
        pltpu.VMEM((BLOCK, width), F32),
        pltpu.VMEM((heads, HEAD_DIM, BLOCK), F32),
        pltpu.VMEM((pairs, HEAD_DIM, BLOCK), F32),
        pltpu.VMEM((BLOCK, width), BF16),
    )

    gain_copies = []

    def gain_copy(source, target, sem, peer):
        copy = remote(source, target, gain_send.at[sem], gain_recv.at[sem], peer)
        copy.start()
        gain_copies.append(copy)

    gain_copy(gain_own.at[0], gain_came.at[0], 0, near_x)

    def tail_three(depth, carry):
        for chain in tails:
            chain.stage_three(depth)
        return carry

    lax.fori_loop(1, 4, tail_three, 0)
    gain_copies[0].wait_recv()
    gain_own[1] = gain_own[0] + gain_came[0]
    gain_copy(gain_own.at[1], gain_came.at[1], 1, near_y)
    pair_copy(0, 0, 0).wait_recv()
    chains[0].close(finish)
    gain_copies[1].wait_recv()
    gain_own[2] = gain_own[1] + gain_came[1]
    gain_copy(gain_own.at[2], gain_came.at[2], 2, partner)
    chains[1].close(finish)
    gain_copies[2].wait_recv()
    gain_own[3] = gain_own[2] + gain_came[2]
    gain_deep[z] = gain_own[3]
    for step in range(1, 4):
        deep = (lax.rem(place + 4 * step, RING), core)
        gain_copy(gain_own.at[3], gain_deep.at[z], 2 + step, deep)
    for chain in tails:
        chain.close(tail_finish)
    for copy in gain_copies[3:]:
        copy.wait_recv()
    gains_out[...] = (gain_deep[0] + gain_deep[1]) + (gain_deep[2] + gain_deep[3])

    def settle(step, nothing):
        peer = lax.rem(place + step, RING)
        back_copy(step, peer).wait_send()
        cot_copy(step, peer).wait_send()
        return nothing

    lax.fori_loop(1, RING, settle, 0)
    for copy in sides + [normed_copy, turned_copy] + gain_copies:
        copy.wait_send()
    for turn_x, turn_y, depth in order:
        pair_copy(turn_x, turn_y, depth).wait_send()
    for chain in chains:
        chain.drain_last()
    for chain in tails:
        chain.drain_first()
        chain.drain_last()


def back_call(call_id, inputs, loads):
    pair, hidden, side, ffn_low, qkv = (inputs[k] for k in (0, 1, 2, 3, 6))
    rows, hidden_width = hidden.shape
    width = ffn_low.shape[1]
    blocks = qkv.shape[0]
    wide, narrow = hidden_width // RING, width // RING
    total = (HEADS + 2 * KV_HEADS) * HEAD_DIM

    def buffers(sizes):
        return [
            pltpu.VMEM((slots, sizes[chain], 256), BF16)
            for chain in range(2)
            for slots in (8, 8, 4, 3)
        ]

    dma = pltpu.SemaphoreType.DMA
    specs = [VMEM_SPEC] * (len(inputs) + len(loads))
    specs[1] = HBM_SPEC
    for index in range(len(inputs), len(specs)):
        specs[index] = HBM_SPEC
    return pl.pallas_call(
        back_kernel,
        out_shape=(
            jax.ShapeDtypeStruct((wide, width // 2), F32),
            jax.ShapeDtypeStruct((wide, width // 2), F32),
            jax.ShapeDtypeStruct((narrow, hidden_width // 2), F32),
            jax.ShapeDtypeStruct((narrow, width // 2), F32),
            jax.ShapeDtypeStruct((total // RING, width // 2), F32),
            jax.ShapeDtypeStruct((rows, width), F32),
            jax.ShapeDtypeStruct((4, width), F32),
        ),
        in_specs=specs,
        out_specs=(VMEM_SPEC,) * 7,
        scratch_shapes=[
            pltpu.VMEM(pair.shape, BF16),
            pltpu.VMEM(side.shape, BF16),
            pltpu.VMEM((rows, hidden_width // 2), BF16),
            pltpu.VMEM((rows, hidden_width // 2), BF16),
            pltpu.VMEM((rows, width // 2), BF16),
            pltpu.VMEM((width // 2, rows), BF16),
            pltpu.VMEM((rows, width // 2), BF16),
            pltpu.VMEM((blocks, HEAD_DIM, BLOCK), BF16),
            pltpu.VMEM(qkv.shape, BF16),
            pltpu.VMEM(qkv.shape, BF16),
            pltpu.VMEM((total, rows), BF16),
            pltpu.VMEM((total, rows), BF16),
            pltpu.VMEM((4, 4, width), F32),
            pltpu.VMEM((3, 4, width), F32),
            pltpu.VMEM((4, 4, width), F32),
        ]
        + buffers((2 * wide + 6 * narrow, 2 * wide + 5 * narrow))
        + buffers((total // RING, total // RING))
        + [dma((2, 15))] * 4
        + [dma((RING,))] * 4
        + [dma((22,))] * 2
        + [dma((6,))] * 2
        + [dma((5,)), dma((2, 8))],
        compiler_params=pltpu.CompilerParams(
            collective_id=call_id, has_side_effects=True, vmem_limit_bytes=63 << 20
        ),
        name="backward_spread",
    )(*inputs, *loads)


def angle_parts(positions):
    half = HEAD_DIM // 2
    inverse_freq = THETA ** (-(2.0 / HEAD_DIM) * jnp.arange(half, dtype=F32))
    angles = inverse_freq[:, None] * positions.astype(F32)[None, :]
    return jnp.cos(angles), jnp.sin(angles)


def front_kernel(
    tokens_ref,
    gain_ref,
    w_query_ref,
    w_key_ref,
    w_value_ref,
    query_gain_ref,
    key_gain_ref,
    cosine_ref,
    sine_ref,
    own_start_ref,
    qkv_out,
    starts_out,
    query_out,
    key_out,
    normed_out,
    weights_out,
    home,
    own_sem,
    send_sem,
    recv_sem,
    start_send,
    start_recv,
    core_send,
    core_recv,
):
    place, core = lax.axis_index("ctx"), lax.axis_index("fsdp")
    rows = tokens_ref.shape[0]
    depth = w_query_ref.shape[0]
    partner = (place, 1 - core)
    greet([partner] + [(lax.rem(place + step, RING), core) for step in range(1, RING)])

    def own_rows(part):
        return pl.ds(pl.multiple_of(part * depth, 128), depth)

    copies, locals_, column = [], [], 0
    for index, source in enumerate((w_key_ref, w_value_ref, w_query_ref)):
        window = pl.ds(column, source.shape[1])
        target = weights_out.at[own_rows(core), window]
        copy = pltpu.make_async_remote_copy(
            src_ref=source,
            dst_ref=target,
            send_sem=core_send.at[index],
            recv_sem=core_recv.at[index],
            device_id=partner,
            device_id_type=MESH,
        )
        copy.start()
        copies.append(copy)
        near = pltpu.make_async_copy(source, target, own_sem.at[index])
        near.start()
        locals_.append(near)
        column += source.shape[1]

    def start_copy(step):
        peer = lax.rem(place + step, RING)
        return pltpu.make_async_remote_copy(
            src_ref=own_start_ref,
            dst_ref=starts_out.at[place],
            send_sem=start_send.at[step],
            recv_sem=start_recv.at[step],
            device_id=(peer, core),
            device_id_type=MESH,
        )

    for step in range(1, RING):
        start_copy(step).start()
    starts_out[place] = own_start_ref[...]

    def norm_rows(index, nothing):
        window = pl.ds(pl.multiple_of(index * 32, 32), 32)
        values = tokens_ref[window, :].astype(F32)
        inverse = lax.rsqrt(jnp.mean(values * values, axis=-1, keepdims=True) + EPSILON)
        normed_out[window, :] = (values * inverse * gain_ref[...]).astype(BF16)
        return nothing

    lax.fori_loop(0, rows // 32, norm_rows, 0)
    cosine, sine = cosine_ref[...], sine_ref[...]
    half = HEAD_DIM // 2

    def project(column, count):
        window = pl.ds(column, count)
        product = jnp.dot(normed_out[...], weights_out[:, window], preferred_element_type=F32)
        return product.T

    def turned(values, gain):
        mean = jnp.mean(values * values, axis=0, keepdims=True)
        values = values * lax.rsqrt(mean + EPSILON) * gain
        first, second = values[:half], values[half:]
        return jnp.concatenate(
            [first * cosine - second * sine, second * cosine + first * sine], axis=0
        ).astype(BF16)

    group = HEADS // KV_HEADS
    kv_width = KV_HEADS * HEAD_DIM
    copies[0].wait_recv()
    locals_[0].wait()

    def key_chunk(index, nothing):
        products = project(pl.multiple_of(index * 256, 256), 256)
        for member in range(4):
            raw = products[member * HEAD_DIM : (member + 1) * HEAD_DIM]
            pair = index * 4 + member
            key_out[pair] = raw
            key = turned(raw, key_gain_ref[...])
            for twin in range(group):
                home[group * pair + twin, HEAD_DIM : 2 * HEAD_DIM, :] = key
        return nothing

    lax.fori_loop(0, KV_HEADS // 4, key_chunk, 0)
    copies[1].wait_recv()
    locals_[1].wait()

    def value_chunk(index, nothing):
        products = project(pl.multiple_of(kv_width + index * 256, 256), 256)
        for member in range(4):
            value = products[member * HEAD_DIM : (member + 1) * HEAD_DIM].astype(BF16)
            for twin in range(group):
                home[group * (index * 4 + member) + twin, 2 * HEAD_DIM : 3 * HEAD_DIM, :] = value
        return nothing

    lax.fori_loop(0, KV_HEADS // 4, value_chunk, 0)
    copies[2].wait_recv()
    locals_[2].wait()

    def block_copy(step):
        peer = lax.rem(place + step, RING)
        return pltpu.make_async_remote_copy(
            src_ref=home.at[peer],
            dst_ref=qkv_out.at[place],
            send_sem=send_sem.at[step],
            recv_sem=recv_sem.at[step],
            device_id=(peer, core),
            device_id_type=MESH,
        )

    def query_chunk(index, nothing):
        products = project(pl.multiple_of(2 * kv_width + index * 256, 256), 256)
        for member in range(4):
            raw = products[member * HEAD_DIM : (member + 1) * HEAD_DIM]
            head = index * 4 + member
            query_out[head] = raw
            home[head, 0:HEAD_DIM, :] = turned(raw, query_gain_ref[...])

            @pl.when(head != place)
            def _():
                block_copy(lax.rem(head - place + RING, RING)).start()

        return nothing

    lax.fori_loop(0, HEADS // 4, query_chunk, 0)
    qkv_out[place] = home[place]

    def settle(step, nothing):
        block_copy(step).wait()
        start_copy(step).wait()
        return nothing

    lax.fori_loop(1, RING, settle, 0)
    for copy in copies:
        copy.wait_send()


def front_call(call_id, *inputs):
    rows, width = inputs[0].shape
    total = (HEADS + 2 * KV_HEADS) * HEAD_DIM
    return pl.pallas_call(
        front_kernel,
        out_shape=(
            jax.ShapeDtypeStruct((RING, 3 * HEAD_DIM, rows), BF16),
            jax.ShapeDtypeStruct((RING, 1, rows), jnp.int32),
            jax.ShapeDtypeStruct((HEADS, HEAD_DIM, rows), F32),
            jax.ShapeDtypeStruct((KV_HEADS, HEAD_DIM, rows), F32),
            jax.ShapeDtypeStruct((rows, width), BF16),
            jax.ShapeDtypeStruct((width, total), BF16),
        ),
        in_specs=[VMEM_SPEC] * len(inputs),
        out_specs=(VMEM_SPEC,) * 6,
        scratch_shapes=[
            pltpu.VMEM((RING, 3 * HEAD_DIM, rows), BF16),
            pltpu.SemaphoreType.DMA((3,)),
            pltpu.SemaphoreType.DMA((RING,)),
            pltpu.SemaphoreType.DMA((RING,)),
            pltpu.SemaphoreType.DMA((RING,)),
            pltpu.SemaphoreType.DMA((RING,)),
            pltpu.SemaphoreType.DMA((3,)),
            pltpu.SemaphoreType.DMA((3,)),
        ],
        compiler_params=pltpu.CompilerParams(
            collective_id=call_id, has_side_effects=True, vmem_limit_bytes=48 << 20
        ),
        name="front_heads",
    )(*inputs)


def ffn_kernel(
    tokens_ref,
    mixed_ref,
    w_out_ref,
    gain_ref,
    cot_ref,
    gate_ref,
    up_ref,
    down_ref,
    pair_out,
    hidden_out,
    output_out,
    ffn_out,
    side_out,
    mixed_back_out,
    grad_middle_out,
    terms_out,
    middle,
    result,
    upstream,
    middle_low,
):
    step = pl.program_id(0)
    rows, width = tokens_ref.shape
    strip = 32

    def strips(work):
        def one(index, carry):
            return work(pl.ds(pl.multiple_of(index * strip, strip), strip), carry)

        return one

    @pl.when(step == 0)
    def _():
        mixed = mixed_ref[...].astype(F32).T.astype(BF16)
        middle[...] = tokens_ref[...].astype(F32) + jnp.dot(
            mixed, w_out_ref[...], preferred_element_type=F32
        )

        def norm(window, carry):
            values = middle[window, :]
            inverse = lax.rsqrt(jnp.mean(values * values, axis=-1, keepdims=True) + EPSILON)
            ffn_out[window, :] = (values * inverse * gain_ref[...]).astype(BF16)
            result[window, :] = values
            return carry

        lax.fori_loop(0, rows // strip, strips(norm), 0)
        upstream[...] = jnp.zeros(upstream.shape, F32)
        side_out[0] = cot_ref[...].astype(F32).T.astype(BF16)

    gate_pre = jnp.dot(ffn_out[...], gate_ref[...], preferred_element_type=F32)
    up_pre = jnp.dot(ffn_out[...], up_ref[...], preferred_element_type=F32)
    grad_hidden = dot_dims(cot_ref[...], down_ref[...], 1, 1)
    gate_sig = jax.nn.sigmoid(gate_pre)
    gate_act = gate_pre * gate_sig
    hidden_out[...] = (gate_act * up_pre).astype(BF16)
    gate_back = (grad_hidden * up_pre * (gate_sig * (1.0 + gate_pre * (1.0 - gate_sig)))).astype(
        BF16
    )
    up_back = (grad_hidden * gate_act).astype(BF16)
    result[...] += jnp.dot(hidden_out[...], down_ref[...], preferred_element_type=F32)
    upstream[...] += dot_dims(gate_back, gate_ref[...], 1, 1) + dot_dims(
        up_back, up_ref[...], 1, 1
    )
    wide = pair_out.shape[1] // 2
    for base, back in ((0, gate_back), (wide, up_back)):
        turned = back.astype(F32).T.astype(BF16)
        for owner in range(pair_out.shape[0]):
            pair_out[owner, base : base + wide, :] = turned[owner * wide : (owner + 1) * wide]

    @pl.when(step == pl.num_programs(0) - 1)
    def _():
        output_out[...] = result[...].astype(BF16)

        def back(window, total):
            values, grads = middle[window, :], upstream[window, :]
            inverse = lax.rsqrt(jnp.mean(values * values, axis=-1, keepdims=True) + EPSILON)
            scaled = grads * gain_ref[...]
            weight = jnp.sum(scaled * values, axis=-1, keepdims=True) / width
            grad_middle = cot_ref[window, :].astype(F32) + (
                inverse * scaled - values * inverse**3 * weight
            )
            grad_middle_out[window, :] = grad_middle
            middle_low[window, :] = grad_middle.astype(BF16)
            return total + jnp.sum(grads * values * inverse, axis=0, keepdims=True)

        terms_out[...] = lax.fori_loop(
            0, rows // strip, strips(back), jnp.zeros((1, width), F32)
        )
        mixed_back_out[...] = dot_dims(w_out_ref[...], middle_low[...], 1, 1).astype(BF16)
        side_out[1] = middle_low[...].astype(F32).T.astype(BF16)


def ffn_call(tokens, mixed_t, w_out, gain, cot, gate, up, down):
    rows, width = tokens.shape
    hidden_width = gate.shape[1]
    steps = 4
    chunk = hidden_width // steps
    owners = RING // steps
    wide = hidden_width // RING

    def whole(*shape):
        return pl.BlockSpec(shape, lambda i: (0,) * len(shape))

    return pl.pallas_call(
        ffn_kernel,
        grid=(steps,),
        out_shape=(
            jax.ShapeDtypeStruct((RING, 2 * wide, rows), BF16),
            jax.ShapeDtypeStruct((rows, hidden_width), BF16),
            jax.ShapeDtypeStruct((rows, width), BF16),
            jax.ShapeDtypeStruct((rows, width), BF16),
            jax.ShapeDtypeStruct((2, width, rows), BF16),
            jax.ShapeDtypeStruct((width, rows), BF16),
            jax.ShapeDtypeStruct((rows, width), F32),
            jax.ShapeDtypeStruct((1, width), F32),
        ),
        in_specs=[
            whole(rows, width),
            whole(width, rows),
            whole(width, width),
            whole(1, width),
            whole(rows, width),
            pl.BlockSpec((width, chunk), lambda i: (0, i)),
            pl.BlockSpec((width, chunk), lambda i: (0, i)),
            pl.BlockSpec((chunk, width), lambda i: (i, 0)),
        ],
        out_specs=(
            pl.BlockSpec((owners, 2 * wide, rows), lambda i: (i, 0, 0)),
            pl.BlockSpec((rows, chunk), lambda i: (0, i)),
            whole(rows, width),
            whole(rows, width),
            whole(2, width, rows),
            whole(width, rows),
            whole(rows, width),
            whole(1, width),
        ),
        scratch_shapes=[pltpu.VMEM((rows, width), F32)] * 3 + [pltpu.VMEM((rows, width), BF16)],
        compiler_params=pltpu.CompilerParams(vmem_limit_bytes=56 << 20),
        name="ffn_both_ways",
    )(tokens, mixed_t, w_out, gain, cot, gate, up, down)


def both(block, axis):
    return lax.all_gather(block, "fsdp", axis=axis, tiled=True)


def heads_body(
    tokens,
    seg_ids,
    doc_pos,
    attn_gain,
    w_query,
    w_key,
    w_value,
    query_gain,
    key_gain,
    w_out,
    ffn_gain,
    w_gate,
    w_up,
    w_down,
    d_output,
):
    place, core = lax.axis_index("ctx"), lax.axis_index("fsdp")
    rows, width = tokens.shape[1], tokens.shape[2]
    pos_local = doc_pos[0]
    o_full, gate_full = both(w_out, 0), both(w_gate, 0)
    up_full, down_full = both(w_up, 0), both(w_down, 0)
    own_starts = place * rows + jnp.arange(rows, dtype=jnp.int32) - pos_local
    cosine, sine = angle_parts(pos_local)
    qkv, starts, query_raw, key_raw, normed_low, kvq_full = front_call(
        1,
        tokens[0],
        attn_gain[None, :],
        w_query,
        w_key,
        w_value,
        query_gain[:, None],
        key_gain[:, None],
        cosine,
        sine,
        own_starts[None, :],
    )
    first = starts[:, 0, 0] // BLOCK
    own_index = jnp.arange(RING, dtype=jnp.int32)
    clear = jnp.minimum((starts[:, 0, -1] + BLOCK - 1) // BLOCK, own_index)
    mixed_far, inverse_total = attend(first, clear, qkv, starts)
    mixed_t = exchange(mixed_far, 2).reshape(HEADS * HEAD_DIM, rows)

    cot_low = d_output[0]
    (
        pair,
        hidden_low,
        output,
        ffn_low,
        side,
        grad_mixed,
        grad_middle,
        ffn_terms,
    ) = ffn_call(
        tokens[0], mixed_t, o_full, ffn_gain[None, :], cot_low, gate_full, up_full, down_full
    )
    gate_t, up_t, down_t, out_t, qkv_grads, d_tokens, gain_totals = back_call(
        3,
        (
            pair,
            hidden_low,
            side,
            ffn_low,
            mixed_t,
            grad_mixed.reshape(HEADS, HEAD_DIM, rows),
            qkv,
            starts,
            mixed_far,
            inverse_total,
            cosine,
            sine,
            query_gain[:, None],
            key_gain[:, None],
            normed_low,
            attn_gain[None, :],
            ffn_terms,
        ),
        (tokens[0], query_raw, key_raw, kvq_full, grad_middle),
    )
    return (
        output[None],
        d_tokens[None],
        gain_totals[0],
        qkv_grads[:64].T,
        qkv_grads[64:96].T,
        qkv_grads[96:].T,
        gain_totals[2, :HEAD_DIM],
        gain_totals[3, :HEAD_DIM],
        out_t.T,
        gain_totals[1],
        gate_t.T,
        up_t.T,
        down_t.T,
    )


def solution(mesh):
    in_specs = (
        P("fsdp", "ctx", None),
        P("fsdp", "ctx"),
        P("fsdp", "ctx"),
        P(),
        P("fsdp", None),
        P("fsdp", None),
        P("fsdp", None),
        P(),
        P(),
        P("fsdp", None),
        P(),
        P("fsdp", None),
        P("fsdp", None),
        P("fsdp", None),
        P("fsdp", "ctx", None),
    )
    out_specs = (
        P("fsdp", "ctx", None),
        P("fsdp", "ctx", None),
        P(),
        P("fsdp", "ctx"),
        P("fsdp", "ctx"),
        P("fsdp", "ctx"),
        P(),
        P(),
        P("fsdp", "ctx"),
        P(),
        P("fsdp", "ctx"),
        P("fsdp", "ctx"),
        P("fsdp", "ctx"),
    )
    chosen = heads_body if (mesh.shape["ctx"], mesh.shape["fsdp"]) == (HEADS, 2) else ring_body
    return jax.shard_map(chosen, mesh=mesh, in_specs=in_specs, out_specs=out_specs, check_vma=False)
```

```python
import functools

import jax
import jax.numpy as jnp
from jax import lax
from jax.experimental import pallas as pl
from jax.experimental.pallas import tpu as pltpu
from jax.sharding import PartitionSpec as P

HEADS = 16
KV_HEADS = 8
HEAD_DIM = 64
HOPS = 8


EPSILON = 1e-05
THETA = 1000000.0
MASKED = -1e30


def from_behind(block, axis, distance):
    devices = range(lax.axis_size(axis))
    route = [(i - distance, i) for i in devices if i - distance in devices]
    return lax.ppermute(block, axis, route)


def rms_norm(values, norm_gain):
    return (
        values * lax.rsqrt(jnp.mean(values * values, axis=-1, keepdims=True) + EPSILON) * norm_gain
    )


def rms_back(values, norm_gain, upstream):
    inverse = lax.rsqrt(jnp.mean(values * values, axis=-1, keepdims=True) + EPSILON)
    scaled = upstream * norm_gain
    row_width = values.shape[-1]
    d_values = (
        inverse * scaled
        - values * inverse**3 * jnp.sum(scaled * values, axis=-1, keepdims=True) / row_width
    )
    return (d_values, upstream * values * inverse)


def rotary(values, positions, turn_sign):
    half_dim = values.shape[-1] // 2
    inverse_freq = THETA ** (-(2.0 / values.shape[-1]) * jnp.arange(half_dim, dtype=jnp.float32))
    angles = positions.astype(jnp.float32)[:, None] * inverse_freq[None, :]
    cosine = jnp.cos(angles)[:, None, :]
    sine_part = turn_sign * jnp.sin(angles)[:, None, :]
    first_half = values[..., :half_dim]
    second_half = values[..., half_dim:]
    return jnp.concatenate(
        [
            first_half * cosine - second_half * sine_part,
            second_half * cosine + first_half * sine_part,
        ],
        axis=-1,
    )


def outer_product(left_mat, right_mat):
    return lax.dot_general(
        left_mat, right_mat, (((0,), (0,)), ((), ())), preferred_element_type=jnp.float32
    )


def against(left_mat, right_mat):
    return lax.dot_general(
        left_mat, right_mat, (((1,), (1,)), ((), ())), preferred_element_type=jnp.float32
    )


def ring_body(
    tokens,
    seg_ids,
    doc_pos,
    attn_gain,
    w_query,
    w_key,
    w_value,
    query_gain,
    key_gain,
    w_out,
    ffn_gain,
    w_gate,
    w_up,
    w_down,
    d_output,
):
    cycle_place = lax.axis_index("ctx")
    tok_rows = tokens.shape[1]
    resid_in = tokens[0].astype(jnp.float32)
    seg_local = seg_ids[0]
    pos_local = doc_pos[0]
    q_per_kv = HEADS // KV_HEADS
    group_cols = q_per_kv * HEAD_DIM
    score_scale = HEAD_DIM ** (-0.5)
    q_full, k_full, v_full, o_full = (
        lax.all_gather(w_query, "fsdp", axis=0, tiled=True),
        lax.all_gather(w_key, "fsdp", axis=0, tiled=True),
        lax.all_gather(w_value, "fsdp", axis=0, tiled=True),
        lax.all_gather(w_out, "fsdp", axis=0, tiled=True),
    )
    gate_full, up_full, down_full = (
        lax.all_gather(w_gate, "fsdp", axis=0, tiled=True),
        lax.all_gather(w_up, "fsdp", axis=0, tiled=True),
        lax.all_gather(w_down, "fsdp", axis=0, tiled=True),
    )
    normed = rms_norm(resid_in, attn_gain)
    normed_low = normed.astype(jnp.bfloat16)
    query_raw = jnp.dot(normed_low, q_full, preferred_element_type=jnp.float32).reshape(
        tok_rows, HEADS, HEAD_DIM
    )
    key_raw = jnp.dot(normed_low, k_full, preferred_element_type=jnp.float32).reshape(
        tok_rows, KV_HEADS, HEAD_DIM
    )
    value_raw = jnp.dot(normed_low, v_full, preferred_element_type=jnp.float32)
    query_rot = rotary(rms_norm(query_raw, query_gain), pos_local, 1.0)
    key_rot = rotary(rms_norm(key_raw, key_gain), pos_local, 1.0)
    query_low = query_rot.astype(jnp.bfloat16).reshape(tok_rows, HEADS * HEAD_DIM)
    key_low = key_rot.astype(jnp.bfloat16).reshape(tok_rows, KV_HEADS * HEAD_DIM)
    value_low = value_raw.astype(jnp.bfloat16)
    own_kv = (key_low, value_low, seg_local)
    kv_blocks = [own_kv]
    carried = own_kv
    for hop_index in range(HOPS):
        carried = from_behind((carried[0], carried[1], carried[2]), "ctx", 1)
        kv_blocks.append(carried)
    key_all = jnp.concatenate([kv_entry[0] for kv_entry in kv_blocks], axis=0)
    value_all = jnp.concatenate([kv_entry[1] for kv_entry in kv_blocks], axis=0)
    seg_all = jnp.concatenate([kv_entry[2] for kv_entry in kv_blocks], axis=0)
    key_owner = cycle_place - jnp.arange(HOPS + 1, dtype=jnp.int32)
    owner_valid = jnp.repeat(key_owner >= 0, tok_rows)
    key_index = (
        key_owner[:, None] * tok_rows + jnp.arange(tok_rows, dtype=jnp.int32)[None, :]
    ).reshape(-1)
    query_index = cycle_place * tok_rows + jnp.arange(tok_rows, dtype=jnp.int32)
    allowed = (
        (seg_local[:, None] == seg_all[None, :])
        & (key_index[None, :] <= query_index[:, None])
        & owner_valid[None, :]
    )

    def group_scores(kv_group):
        query_part = lax.dynamic_slice_in_dim(query_low, kv_group * group_cols, group_cols, 1)
        query_part = query_part.reshape(tok_rows, q_per_kv, HEAD_DIM)
        key_part = lax.dynamic_slice_in_dim(key_all, kv_group * HEAD_DIM, HEAD_DIM, 1)
        value_part = lax.dynamic_slice_in_dim(value_all, kv_group * HEAD_DIM, HEAD_DIM, 1)
        scores = (
            jnp.einsum("trd,kd->rtk", query_part, key_part, preferred_element_type=jnp.float32)
            * score_scale
        )
        return (jnp.where(allowed[None], scores, MASKED), query_part, key_part, value_part)

    def forward_group(kv_group):
        scores, query_part, key_part, value_part = group_scores(kv_group)
        row_top = jnp.max(scores, axis=-1, keepdims=True)
        log_total = row_top + jnp.log(jnp.sum(jnp.exp(scores - row_top), axis=-1, keepdims=True))
        attn_probs = jnp.exp(scores - log_total)
        mixed_part = jnp.einsum(
            "rtk,kd->trd",
            attn_probs.astype(jnp.bfloat16),
            value_part,
            preferred_element_type=jnp.float32,
        )
        return (mixed_part.reshape(tok_rows, group_cols), log_total[..., 0])

    mixed_groups, total_groups = lax.map(forward_group, jnp.arange(KV_HEADS, dtype=jnp.int32))
    mixed = mixed_groups.transpose(1, 0, 2).reshape(tok_rows, HEADS * HEAD_DIM)
    mixed_low = mixed.astype(jnp.bfloat16)
    middle = resid_in + jnp.dot(mixed_low, o_full, preferred_element_type=jnp.float32)
    ffn_low = rms_norm(middle, ffn_gain).astype(jnp.bfloat16)
    gate_pre = jnp.dot(ffn_low, gate_full, preferred_element_type=jnp.float32)
    up_pre = jnp.dot(ffn_low, up_full, preferred_element_type=jnp.float32)
    gate_sig = jax.nn.sigmoid(gate_pre)
    gate_act = gate_pre * gate_sig
    hidden_low = (gate_act * up_pre).astype(jnp.bfloat16)
    result = middle + jnp.dot(hidden_low, down_full, preferred_element_type=jnp.float32)
    output = result.astype(jnp.bfloat16)[None]
    cot_low = d_output[0]
    cotangent = cot_low.astype(jnp.float32)
    grad_w_down = outer_product(hidden_low, cot_low)
    grad_hidden = against(cot_low, down_full)
    gate_back = (grad_hidden * up_pre * (gate_sig * (1.0 + gate_pre * (1.0 - gate_sig)))).astype(
        jnp.bfloat16
    )
    up_back = (grad_hidden * gate_act).astype(jnp.bfloat16)
    grad_w_gate = outer_product(ffn_low, gate_back)
    grad_w_up = outer_product(ffn_low, up_back)
    grad_ffn_in = against(gate_back, gate_full) + against(up_back, up_full)
    middle_part, ffn_terms = rms_back(middle, ffn_gain, grad_ffn_in)
    grad_middle = cotangent + middle_part
    middle_low = grad_middle.astype(jnp.bfloat16)
    grad_w_out = outer_product(mixed_low, middle_low)
    grad_mixed = against(middle_low, o_full).astype(jnp.bfloat16)

    def backward_group(kv_group):
        scores, query_part, key_part, value_part = group_scores(kv_group)
        attn_probs = jnp.exp(scores - total_groups[kv_group][..., None])
        mixed_grad_part = lax.dynamic_slice_in_dim(grad_mixed, kv_group * group_cols, group_cols, 1)
        mixed_grad_part = mixed_grad_part.reshape(tok_rows, q_per_kv, HEAD_DIM)
        grad_probs = jnp.einsum(
            "trd,kd->rtk", mixed_grad_part, value_part, preferred_element_type=jnp.float32
        )
        grad_value = jnp.einsum(
            "rtk,trd->kd",
            attn_probs.astype(jnp.bfloat16),
            mixed_grad_part,
            preferred_element_type=jnp.float32,
        )
        row_delta = jnp.sum(grad_probs * attn_probs, axis=-1, keepdims=True)
        grad_scores = (attn_probs * (grad_probs - row_delta)).astype(jnp.bfloat16)
        grad_query = (
            jnp.einsum("rtk,kd->trd", grad_scores, key_part, preferred_element_type=jnp.float32)
            * score_scale
        )
        grad_key = (
            jnp.einsum("rtk,trd->kd", grad_scores, query_part, preferred_element_type=jnp.float32)
            * score_scale
        )
        return (grad_query.reshape(tok_rows, group_cols), grad_key, grad_value)

    query_groups, key_groups, value_groups = lax.map(
        backward_group, jnp.arange(KV_HEADS, dtype=jnp.int32)
    )
    grad_query_rot = query_groups.transpose(1, 0, 2).reshape(tok_rows, HEADS, HEAD_DIM)
    key_blocks = key_groups.transpose(1, 0, 2).reshape(HOPS + 1, tok_rows, KV_HEADS * HEAD_DIM)
    value_blocks = value_groups.transpose(1, 0, 2).reshape(HOPS + 1, tok_rows, KV_HEADS * HEAD_DIM)
    home_key = key_blocks[HOPS]
    home_value = value_blocks[HOPS]
    for hop_index in range(HOPS, 0, -1):
        moved_key, moved_value = (
            from_behind(home_key.astype(jnp.bfloat16), "ctx", -1).astype(home_key.dtype),
            from_behind(home_value.astype(jnp.bfloat16), "ctx", -1).astype(home_value.dtype),
        )
        home_key = moved_key + key_blocks[hop_index - 1]
        home_value = moved_value + value_blocks[hop_index - 1]
    query_turned = rotary(grad_query_rot, pos_local, -1.0)
    key_turned = rotary(home_key.reshape(tok_rows, KV_HEADS, HEAD_DIM), pos_local, -1.0)
    query_back, query_terms = rms_back(query_raw, query_gain, query_turned)
    key_back, key_terms = rms_back(key_raw, key_gain, key_turned)
    query_back = query_back.reshape(tok_rows, HEADS * HEAD_DIM).astype(jnp.bfloat16)
    key_back = key_back.reshape(tok_rows, KV_HEADS * HEAD_DIM).astype(jnp.bfloat16)
    value_back = home_value.astype(jnp.bfloat16)
    grad_w_query = outer_product(normed_low, query_back)
    grad_w_key = outer_product(normed_low, key_back)
    grad_w_value = outer_product(normed_low, value_back)
    grad_normed = (
        against(query_back, q_full) + against(key_back, k_full) + against(value_back, v_full)
    )
    input_part, attn_terms = rms_back(resid_in, attn_gain, grad_normed)
    d_tokens = (grad_middle + input_part)[None]
    gain_totals = lax.psum(
        (
            jnp.sum(attn_terms, axis=0),
            jnp.sum(ffn_terms, axis=0),
            jnp.sum(query_terms, axis=(0, 1)),
            jnp.sum(key_terms, axis=(0, 1)),
        ),
        ("ctx", "fsdp"),
    )
    weight_grads = (
        grad_w_query,
        grad_w_key,
        grad_w_value,
        grad_w_out,
        grad_w_gate,
        grad_w_up,
        grad_w_down,
    )
    spread = (
        lax.psum_scatter(
            weight_grads[0].astype(jnp.bfloat16), "fsdp", scatter_dimension=0, tiled=True
        ).astype(jnp.float32),
        lax.psum_scatter(
            weight_grads[1].astype(jnp.bfloat16), "fsdp", scatter_dimension=0, tiled=True
        ).astype(jnp.float32),
        lax.psum_scatter(
            weight_grads[2].astype(jnp.bfloat16), "fsdp", scatter_dimension=0, tiled=True
        ).astype(jnp.float32),
        lax.psum_scatter(
            weight_grads[3].astype(jnp.bfloat16), "fsdp", scatter_dimension=0, tiled=True
        ).astype(jnp.float32),
        lax.psum_scatter(
            weight_grads[4].astype(jnp.bfloat16), "fsdp", scatter_dimension=0, tiled=True
        ).astype(jnp.float32),
        lax.psum_scatter(
            weight_grads[5].astype(jnp.bfloat16), "fsdp", scatter_dimension=0, tiled=True
        ).astype(jnp.float32),
        lax.psum_scatter(
            weight_grads[6].astype(jnp.bfloat16), "fsdp", scatter_dimension=0, tiled=True
        ).astype(jnp.float32),
    )
    shares = (
        lax.psum_scatter(spread[0], "ctx", scatter_dimension=1, tiled=True),
        lax.psum_scatter(spread[1], "ctx", scatter_dimension=1, tiled=True),
        lax.psum_scatter(spread[2], "ctx", scatter_dimension=1, tiled=True),
        lax.psum_scatter(spread[3], "ctx", scatter_dimension=1, tiled=True),
        lax.psum_scatter(spread[4], "ctx", scatter_dimension=1, tiled=True),
        lax.psum_scatter(spread[5], "ctx", scatter_dimension=1, tiled=True),
        lax.psum_scatter(spread[6], "ctx", scatter_dimension=1, tiled=True),
    )
    return (
        output,
        d_tokens,
        gain_totals[0],
        shares[0],
        shares[1],
        shares[2],
        gain_totals[2],
        gain_totals[3],
        shares[3],
        gain_totals[1],
        shares[4],
        shares[5],
        shares[6],
    )


MESH = pl.DeviceIdType.MESH
BLOCK = 256
RING = 16
HALF = 8
VMEM_SPEC = pl.BlockSpec(memory_space=pltpu.VMEM)
HBM_SPEC = pl.BlockSpec(memory_space=pltpu.HBM)
SMEM_SPEC = pl.BlockSpec(memory_space=pltpu.SMEM)
F32 = jnp.float32
BF16 = jnp.bfloat16


def dot_dims(left_mat, right_mat, left_dim, right_dim):
    return lax.dot_general(
        left_mat, right_mat, (((left_dim,), (right_dim,)), ((), ())), preferred_element_type=F32
    )


def transposed(block):
    return block.astype(F32).T.astype(BF16)


def flip(bit, turned):
    return bit + turned - 2 * bit * turned


class Spread:
    def __init__(self, chain, compute, sent, came, send_sems, recv_sems):
        place, self.core = lax.axis_index("ctx"), lax.axis_index("fsdp")
        x, y, self.z = lax.rem(place, 2), lax.rem(place // 2, 2), place // 4
        self.chain = chain
        self.first, self.second = (x, y) if chain == 0 else (y, x)
        self.compute, self.sent, self.came = compute, sent, came
        self.send_sems, self.recv_sems = send_sems, recv_sems

    def at(self, first, second, depth):
        low = second * 2 + first if self.chain == 0 else first * 2 + second
        return depth * 4 + low

    def deep(self, depth):
        return lax.rem(self.z + depth, 4)

    def copy(self, stage, slot):
        if stage == 0:
            peer = self.at(1 - self.first, self.second, self.z)
            source, target, sem = self.sent.at[slot], self.came[0].at[slot], slot
        elif stage == 1:
            peer = self.at(self.first, 1 - self.second, self.z)
            source, target, sem = self.came[0].at[4 + slot], self.came[1].at[slot], 8 + slot
        else:
            peer = self.at(self.first, self.second, self.deep(slot))
            source, target, sem = self.came[0].at[slot], self.came[2].at[slot - 1], 11 + slot
        return pltpu.make_async_remote_copy(
            src_ref=source,
            dst_ref=target,
            send_sem=self.send_sems.at[self.chain, sem],
            recv_sem=self.recv_sems.at[self.chain, sem],
            device_id=(peer, self.core),
            device_id_type=MESH,
        )

    def stage_one(self, turned, depth):
        slot = turned * 4 + depth
        owner = self.at(1 - self.first, flip(self.second, turned), self.deep(depth))
        for row, value in self.compute(self.chain, owner):
            self.sent[slot, row : row + value.shape[0], :] = value.astype(BF16)
        self.copy(0, slot).start()

    def stage_two(self, depth):
        self.copy(0, 4 + depth).wait_recv()
        owner = self.at(self.first, 1 - self.second, self.deep(depth))
        for row, value in self.compute(self.chain, owner):
            window = slice(row, row + value.shape[0])
            value = value + self.came[0][4 + depth, window, :].astype(F32)
            self.came[0][4 + depth, window, :] = value.astype(BF16)
        self.copy(1, depth).start()

    def stage_three(self, depth):
        self.copy(0, depth).wait_recv()
        self.copy(1, depth).wait_recv()
        owner = self.at(self.first, self.second, self.deep(depth))
        for row, value in self.compute(self.chain, owner):
            window = slice(row, row + value.shape[0])
            value = value + self.came[0][depth, window, :].astype(F32)
            value = value + self.came[1][depth, window, :].astype(F32)
            self.came[0][depth, window, :] = value.astype(BF16)
        self.copy(2, depth).start()

    def close(self, finish):
        self.copy(0, 0).wait_recv()
        self.copy(1, 0).wait_recv()
        for depth in range(1, 4):
            self.copy(2, depth).wait_recv()
        owner = self.at(self.first, self.second, self.z)
        for row, value in self.compute(self.chain, owner):
            window = slice(row, row + value.shape[0])
            value = value + self.came[0][0, window, :].astype(F32)
            value = value + self.came[1][0, window, :].astype(F32)
            for depth in range(3):
                value = value + self.came[2][depth, window, :].astype(F32)
            finish(self.chain, row, value)

    def drain(self):
        for slot in range(8):
            self.copy(0, slot).wait_send()
        for depth in range(4):
            self.copy(1, depth).wait_send()
        for depth in range(1, 4):
            self.copy(2, depth).wait_send()


def greet(peers):
    barrier = pltpu.get_barrier_semaphore()
    for peer in peers:
        pl.semaphore_signal(barrier, inc=1, device_id=peer, device_id_type=MESH)
    pl.semaphore_wait(barrier, len(peers))


def turn_back(values, cosine, sine):
    half = HEAD_DIM // 2
    first, second = values[:half], values[half:]
    return jnp.concatenate(
        [first * cosine + second * sine, second * cosine - first * sine], axis=0
    )


def column_norm_back(values, gain, upstream):
    inverse = lax.rsqrt(jnp.mean(values * values, axis=0, keepdims=True) + EPSILON)
    scaled = upstream * gain
    total = jnp.sum(scaled * values, axis=0, keepdims=True) / values.shape[0]
    return inverse * scaled - values * inverse**3 * total, upstream * values * inverse


def back_kernel(
    pair_own,
    hidden_hbm,
    side_own,
    ffn_ref,
    mixed_ref,
    home_ref,
    qkv_ref,
    start_ref,
    part_ref,
    inv_ref,
    table_ref,
    normed_ref,
    attn_gain_ref,
    ffn_terms_ref,
    tokens_hbm,
    query_hbm,
    key_hbm,
    weights_hbm,
    middle_hbm,
    gate_out,
    up_out,
    down_out,
    out_out,
    grads_out,
    tokens_out,
    gains_out,
    pair_far,
    side_far,
    hidden_own,
    hidden_far,
    ffn_far,
    mixed_far,
    normed_far,
    cot_far,
    back_own,
    back_far,
    extra_own,
    extra_far,
    turned_own,
    turned_far,
    gain_own,
    gain_came,
    gain_all,
    sent_a,
    came_a0,
    came_a1,
    came_a2,
    sent_b,
    came_b0,
    came_b1,
    came_b2,
    tail_sent_a,
    tail_came_a0,
    tail_came_a1,
    tail_came_a2,
    tail_sent_b,
    tail_came_b0,
    tail_came_b1,
    tail_came_b2,
    send_sems,
    recv_sems,
    tail_send,
    tail_recv,
    cot_send,
    cot_recv,
    back_send,
    back_recv,
    core_send,
    core_recv,
    gain_send,
    gain_recv,
    extra_send,
    extra_recv,
    load_sem,
):
    place, core = lax.axis_index("ctx"), lax.axis_index("fsdp")
    part, member = place // HALF, lax.rem(place, HALF)
    base = part * HALF - 1
    x, y, z = lax.rem(place, 2), lax.rem(place // 2, 2), place // 4
    wide = pair_own.shape[1] // 2
    narrow = side_own.shape[1] // RING
    half_hidden = hidden_far.shape[1]
    half_width = ffn_far.shape[1]
    heads, pairs = query_hbm.shape[0], key_hbm.shape[0]
    scale = HEAD_DIM**-0.5
    partner = (place, 1 - core)

    def half(part, size):
        return pl.ds(pl.multiple_of(part * size, 128), size)

    own_hidden = pltpu.make_async_copy(
        hidden_hbm.at[:, half(core, half_hidden)], hidden_own, load_sem.at[0]
    )
    own_hidden.start()
    middle_load = pltpu.make_async_copy(middle_hbm, tokens_out, load_sem.at[1])
    middle_load.start()
    greet([(lax.rem(place + step, RING), core) for step in range(1, RING)] + [partner])

    def remote(source, target, send, recv, peer):
        return pltpu.make_async_remote_copy(
            src_ref=source,
            dst_ref=target,
            send_sem=send,
            recv_sem=recv,
            device_id=peer,
            device_id_type=MESH,
        )

    def mate(step):
        return (part * HALF + lax.rem(member + step, HALF), core)

    def cot_copy(step):
        return remote(
            home_ref.at[lax.rem(member + step, HALF)],
            cot_far.at[member],
            cot_send.at[step],
            cot_recv.at[step],
            mate(step),
        )

    def core_copy(source, target, sem):
        return remote(source, target, core_send.at[sem], core_recv.at[sem], partner)

    def pair_copy(turn_x, turn_y, depth):
        owner = lax.rem(z + depth, 4) * 4 + flip(y, turn_y) * 2 + flip(x, turn_x)
        return core_copy(
            pair_own.at[owner], pair_far.at[owner], 6 + turn_x * 8 + turn_y * 4 + depth
        )

    sides = [
        core_copy(ffn_ref.at[:, half(1 - core, half_width)], ffn_far, 0),
        core_copy(mixed_ref.at[half(1 - core, half_width), :], mixed_far, 1),
        core_copy(side_own, side_far, 2),
        core_copy(hidden_hbm.at[:, half(1 - core, half_hidden)], hidden_far, 3),
    ]
    order = []
    for depth in (2, 1, 3, 0):
        order += [(1, 1, depth), (1, 0, depth), (0, 1, depth)]
    order += [(0, 0, depth) for depth in (2, 1, 3, 0)]
    for copy in sides:
        copy.start()
    pair_copy(*order[0]).start()
    for step in range(1, HALF):
        cot_copy(step).start()
    for turn_x, turn_y, depth in order[1:]:
        pair_copy(turn_x, turn_y, depth).start()
    normed_copy = core_copy(normed_ref.at[:, half(1 - core, half_width)], normed_far, 4)
    normed_copy.start()
    cot_far[member] = home_ref[member]

    def compute(chain, owner):
        lanes = pl.ds(chain * 256, 256)
        own_lanes = pl.ds(pl.multiple_of(core * half_width + chain * 256, 128), 256)
        both_pair = jnp.dot(pair_own[owner], ffn_ref[:, own_lanes], preferred_element_type=F32)
        both_pair += jnp.dot(pair_far[owner], ffn_far[:, lanes], preferred_element_type=F32)
        values = [(0, both_pair)]
        rows = pl.ds(pl.multiple_of(owner * narrow, 16), narrow)
        begin, chunks = (0, 5) if chain == 0 else (5, 4)
        cols = slice(begin * 256, (begin + chunks) * 256)
        down = jnp.dot(side_own[0, rows, :], hidden_own[:, cols], preferred_element_type=F32)
        down += jnp.dot(side_far[0, rows, :], hidden_far[:, cols], preferred_element_type=F32)
        row = 2 * wide
        for chunk in range(chunks):
            values.append((row, down[:, chunk * 256 : chunk * 256 + 256]))
            row += narrow
        out = dot_dims(side_own[1, rows, :], mixed_ref[own_lanes, :], 1, 1)
        out += dot_dims(side_far[1, rows, :], mixed_far[lanes, :], 1, 1)
        values.append((row, out))
        return values

    def finish(chain, row, value):
        lanes = slice(chain * 256, chain * 256 + 256)
        if row == 0:
            gate_out[:, lanes] = value[:wide]
            up_out[:, lanes] = value[wide:]
            return
        chunk = (row - 2 * wide) // narrow
        if chunk == 5 - chain:
            out_out[:, lanes] = value
        else:
            chunk += 5 * chain
            down_out[:, chunk * 256 : chunk * 256 + 256] = value

    chains = (
        Spread(0, compute, sent_a, (came_a0, came_a1, came_a2), send_sems, recv_sems),
        Spread(1, compute, sent_b, (came_b0, came_b1, came_b2), send_sems, recv_sems),
    )
    own_hidden.wait()
    for copy in sides:
        copy.wait_recv()

    def near(depth):
        pair_copy(1, 1, depth).wait_recv()
        for chain in chains:
            chain.stage_one(1, depth)

    def far(depth):
        pair_copy(1, 0, depth).wait_recv()
        pair_copy(0, 1, depth).wait_recv()
        for chain in chains:
            chain.stage_one(0, depth)

    def onward(depth):
        for chain in chains:
            chain.stage_two(depth)

    def deeper(depth):
        pair_copy(0, 0, depth).wait_recv()
        for chain in chains:
            chain.stage_three(depth)

    near(2)
    far(2)
    near(1)

    def back_copy(step):
        return remote(
            back_own.at[lax.rem(member + step, HALF)],
            back_far.at[member],
            back_send.at[step],
            back_recv.at[step],
            mate(step),
        )

    def extra_copy(group):
        return remote(
            extra_own,
            extra_far.at[group],
            extra_send.at[group],
            extra_recv.at[group],
            (HALF - 1, core),
        )

    def attention(
        scaled, cots, natural, delta_ref, query_acc, key_nat, value_nat, pair_acc
    ):
        def widen(ref, i, row):
            return jnp.concatenate(
                [ref[i, row : row + HEAD_DIM, :], ref[i, row + HEAD_DIM : row + 2 * HEAD_DIM, :]],
                axis=1,
            )

        def prepare(i, nothing):
            @pl.when(i != member)
            def _():
                cot_copy(lax.rem(member - i + HALF, HALF)).wait_recv()

            query = widen(qkv_ref, i + 1, 0) * jnp.asarray(scale, BF16)
            cot = widen(cot_far, i, 0)
            scaled[i] = query
            cots[i] = cot
            natural[i] = transposed(jnp.concatenate([query, cot], axis=0))
            delta_ref[i] = jnp.sum(
                cot.astype(F32) * widen(part_ref, i, 0).astype(F32), axis=0, keepdims=True
            )
            query_acc[i] = jnp.zeros(query_acc.shape[1:], F32)
            return nothing

        def per_key(j, nothing):
            key_t = qkv_ref[j, 2 * HEAD_DIM : 3 * HEAD_DIM, :]
            key_nat[...] = transposed(key_t)
            value_nat[...] = transposed(qkv_ref[j, 3 * HEAD_DIM : 4 * HEAD_DIM, :])
            shape = (BLOCK, 2 * BLOCK)
            key_place = (base + j) * BLOCK + lax.broadcasted_iota(jnp.int32, shape, 0)

            def step(diagonal, i):
                start = jnp.concatenate([start_ref[i - 1]] * 2, axis=1)
                scores = jnp.dot(key_nat[...], scaled[i - 1], preferred_element_type=F32)
                grad_probs = jnp.dot(value_nat[...], cots[i - 1], preferred_element_type=F32)
                ok = key_place >= start
                if diagonal:
                    places = (base + i) * BLOCK + lax.broadcasted_iota(jnp.int32, (1, BLOCK), 1)
                    ok = ok & (key_place <= jnp.concatenate([places] * 2, axis=1))
                probs = jnp.where(ok, jnp.exp(scores) * inv_ref[i - 1], 0.0)
                grad_scores = (probs * (grad_probs - delta_ref[i - 1])).astype(BF16)
                both_low = jnp.concatenate([grad_scores, probs.astype(BF16)], axis=0)
                query_acc[i - 1] += jnp.dot(
                    qkv_ref[j, 2 * HEAD_DIM : 3 * HEAD_DIM, :],
                    grad_scores,
                    preferred_element_type=F32,
                )
                return jnp.dot(both_low, natural[i - 1], preferred_element_type=F32)

            @pl.when(j == 0)
            def _():
                pair_acc[...] = jnp.zeros(pair_acc.shape, F32)

            @pl.when(j > 0)
            def _():
                pair_acc[...] = step(True, j)

            def one(i, carry):
                pair_acc[...] += step(False, i)
                return carry

            lax.fori_loop(j + 1, HALF + 1, one, 0)
            first = lax.broadcasted_iota(jnp.int32, (BLOCK, 2 * HEAD_DIM), 1) < HEAD_DIM
            merged = jnp.where(first, pair_acc[0:BLOCK, :], pair_acc[BLOCK:, :]).T.astype(BF16)

            @pl.when(j == 0)
            def _():
                extra_own[...] = merged
                extra_copy(member).start()

            @pl.when(j > 0)
            def _():
                query_grad = (query_acc[j - 1] * scale).astype(BF16)
                back_own[j - 1, 0:HEAD_DIM, :] = query_grad[:, :BLOCK]
                back_own[j - 1, HEAD_DIM : 2 * HEAD_DIM, :] = query_grad[:, BLOCK:]
                back_own[j - 1, 2 * HEAD_DIM : 4 * HEAD_DIM, :] = merged

            @pl.when((j > 0) & (j - 1 != member))
            def _():
                back_copy(lax.rem(j - 1 - member + HALF, HALF)).start()

            @pl.when(j == 4)
            def _():
                onward(2)
                far(1)

            @pl.when(j == HALF)
            def _():
                near(3)

            return nothing

        lax.fori_loop(0, HALF, prepare, 0)
        lax.fori_loop(1 - part, HALF + 1, per_key, 0)
        back_far[member] = back_own[member]

    pl.run_scoped(
        attention,
        pltpu.VMEM((HALF, HEAD_DIM, 2 * BLOCK), BF16),
        pltpu.VMEM((HALF, HEAD_DIM, 2 * BLOCK), BF16),
        pltpu.VMEM((HALF, 2 * BLOCK, 2 * HEAD_DIM), BF16),
        pltpu.VMEM((HALF, 1, 2 * BLOCK), F32),
        pltpu.VMEM((HALF, HEAD_DIM, 2 * BLOCK), F32),
        pltpu.VMEM((BLOCK, HEAD_DIM), BF16),
        pltpu.VMEM((BLOCK, HEAD_DIM), BF16),
        pltpu.VMEM((2 * BLOCK, 2 * HEAD_DIM), F32),
    )

    turned_copy = core_copy(turned_own, turned_far, 5)

    def tail_compute(chain, owner):
        lanes = slice(chain * 256, chain * 256 + 256)
        own_lanes = pl.ds(pl.multiple_of(core * half_width + chain * 256, 128), 256)
        values, row = [], 0
        for size, base in ((heads, 2 * pairs), (pairs, 0), (pairs, pairs)):
            count = size * HEAD_DIM // RING
            rows = pl.ds(pl.multiple_of(base * HEAD_DIM + owner * count, 16), count)
            value = jnp.dot(
                turned_own[rows, :], normed_ref[:, own_lanes], preferred_element_type=F32
            )
            value += jnp.dot(turned_far[rows, :], normed_far[:, lanes], preferred_element_type=F32)
            values.append((row, value))
            row += count
        return values

    def tail_finish(chain, row, value):
        grads_out[row : row + value.shape[0], chain * 256 : chain * 256 + 256] = value

    tails = (
        Spread(
            0,
            tail_compute,
            tail_sent_a,
            (tail_came_a0, tail_came_a1, tail_came_a2),
            tail_send,
            tail_recv,
        ),
        Spread(
            1,
            tail_compute,
            tail_sent_b,
            (tail_came_b0, tail_came_b1, tail_came_b2),
            tail_send,
            tail_recv,
        ),
    )

    def finish_all(natural, summed, query_ref, key_ref, tokens_ref, weights_ref):
        loads = [
            pltpu.make_async_copy(query_hbm, query_ref, load_sem.at[2]),
            pltpu.make_async_copy(key_hbm, key_ref, load_sem.at[3]),
            pltpu.make_async_copy(tokens_hbm, tokens_ref, load_sem.at[4]),
            pltpu.make_async_copy(weights_hbm, weights_ref, load_sem.at[5]),
        ]
        for copy in loads:
            copy.start()
        half_dim = HEAD_DIM // 2
        cosine, sine = table_ref[0:half_dim, :], table_ref[half_dim:HEAD_DIM, :]
        query_gain = table_ref[HEAD_DIM : 2 * HEAD_DIM, :]
        key_gain = table_ref[2 * HEAD_DIM : 3 * HEAD_DIM, :]

        def head_rows(index):
            return pl.ds(pl.multiple_of(index * HEAD_DIM, HEAD_DIM), HEAD_DIM)

        def query_head(head, total):
            low = pl.multiple_of(lax.rem(head, 2) * HEAD_DIM, HEAD_DIM)
            upstream = turn_back(
                back_far[head // 2, pl.ds(low, HEAD_DIM), :].astype(F32), cosine, sine
            )
            back, terms = column_norm_back(query_ref[head], query_gain, upstream)
            turned_own[head_rows(2 * pairs + head), :] = back.astype(BF16)
            return total + terms

        def key_head(pair, total):
            upstream = back_far[pair, 2 * HEAD_DIM : 4 * HEAD_DIM, :].astype(F32)
            upstream += extra_far[pair].astype(F32)
            back, terms = column_norm_back(
                key_ref[pair],
                key_gain,
                turn_back(upstream[:HEAD_DIM], cosine, sine),
            )
            turned_own[head_rows(pair), :] = back.astype(BF16)
            turned_own[head_rows(pairs + pair), :] = upstream[HEAD_DIM:].astype(BF16)
            return total + terms

        onward(1)
        far(3)

        def arrive(step, nothing):
            back_copy(step).wait_recv()
            return nothing

        lax.fori_loop(1, HALF, arrive, 0)

        def extra_arrive(group, nothing):
            extra_copy(group).wait_recv()
            return nothing

        @pl.when(place == HALF - 1)
        def _():
            lax.fori_loop(0, HALF, extra_arrive, 0)

        @pl.when(place != HALF - 1)
        def _():
            extra_far[...] = jnp.zeros(extra_far.shape, BF16)

        for copy in loads:
            copy.wait()
        nothing = jnp.zeros((HEAD_DIM, BLOCK), F32)
        query_terms = lax.fori_loop(0, heads, query_head, nothing)
        key_terms = lax.fori_loop(0, pairs, key_head, nothing)
        turned_copy.start()
        for row in range(0, turned_own.shape[0], 128):
            natural[:, row : row + 128] = turned_own[row : row + 128, :].astype(F32).T.astype(BF16)
        deeper(2)
        normed_copy.wait_recv()
        turned_copy.wait_recv()

        def tail_one(index, carry):
            for chain in tails:
                chain.stage_one(1 - index // 4, lax.rem(index + 1, 4))
            return carry

        lax.fori_loop(0, 8, tail_one, 0)
        near(0)
        summed[...] = dot_dims(natural[...], weights_ref[...], 1, 1)
        middle_load.wait()

        def token_rows(index, total):
            rows = pl.ds(pl.multiple_of(index * 32, 32), 32)
            values, upstream = tokens_ref[rows, :].astype(F32), summed[rows, :]
            inverse = lax.rsqrt(jnp.mean(values * values, axis=-1, keepdims=True) + EPSILON)
            scaled = upstream * attn_gain_ref[...]
            weight = jnp.sum(scaled * values, axis=-1, keepdims=True) / values.shape[1]
            tokens_out[rows, :] += inverse * scaled - values * inverse**3 * weight
            return total + jnp.sum(upstream * values * inverse, axis=0, keepdims=True)

        terms = lax.fori_loop(
            0, BLOCK // 32, token_rows, jnp.zeros((1, tokens_ref.shape[1]), F32)
        )
        gain_own[...] = jnp.zeros(gain_own.shape, F32)
        gain_own[0:1, :] = terms
        gain_own[1:2, :] = ffn_terms_ref[...]
        gain_own[2:3, 0:HEAD_DIM] = jnp.sum(query_terms.T, axis=0, keepdims=True)
        gain_own[3:4, 0:HEAD_DIM] = jnp.sum(key_terms.T, axis=0, keepdims=True)

    width = normed_ref.shape[1]
    pl.run_scoped(
        finish_all,
        pltpu.VMEM((BLOCK, turned_own.shape[0]), BF16),
        pltpu.VMEM((BLOCK, width), F32),
        pltpu.VMEM((heads, HEAD_DIM, BLOCK), F32),
        pltpu.VMEM((pairs, HEAD_DIM, BLOCK), F32),
        pltpu.VMEM((BLOCK, width), BF16),
        pltpu.VMEM(weights_hbm.shape, BF16),
    )

    def tail_two(index, carry):
        for chain in tails:
            chain.stage_two(lax.rem(index + 1, 4))
        return carry

    def tail_three(depth, carry):
        for chain in tails:
            chain.stage_three(depth)
        return carry

    gain_swap = core_copy(gain_own, gain_came, 22)
    gain_swap.start()

    def gain_copy(step):
        peer = (lax.rem(place + step, RING), core)
        return remote(
            gain_all.at[place], gain_all.at[place], gain_send.at[step], gain_recv.at[step], peer
        )

    def gain_start(step, carry):
        gain_copy(step).start()
        return carry

    def gain_arrive(step, carry):
        gain_copy(step).wait()
        return carry

    onward(3)
    deeper(1)
    far(0)
    gain_swap.wait()
    gain_all[place] = gain_own[...] + gain_came[...]
    lax.fori_loop(1, RING, gain_start, 0)
    lax.fori_loop(0, 4, tail_two, 0)
    onward(0)
    deeper(3)
    lax.fori_loop(1, 4, tail_three, 0)
    pair_copy(0, 0, 0).wait_recv()
    for chain in chains:
        chain.close(finish)
    for chain in tails:
        chain.close(tail_finish)
    lax.fori_loop(1, RING, gain_arrive, 0)

    def gain_sum(index, total):
        return total + gain_all[index]

    gains_out[...] = lax.fori_loop(1, RING, gain_sum, gain_all[0])

    def settle(step, nothing):
        back_copy(step).wait_send()
        cot_copy(step).wait_send()
        return nothing

    lax.fori_loop(1, HALF, settle, 0)

    @pl.when(part == 1)
    def _():
        extra_copy(member).wait_send()

    for copy in sides + [normed_copy, turned_copy]:
        copy.wait_send()
    for turn_x, turn_y, depth in order:
        pair_copy(turn_x, turn_y, depth).wait_send()
    for chain in chains + tails:
        chain.drain()


def back_call(call_id, inputs, loads):
    pair, hidden, side, ffn_low = inputs[:4]
    rows, hidden_width = hidden.shape
    width = ffn_low.shape[1]
    wide, narrow = hidden_width // RING, width // RING
    total = (HEADS + 2 * KV_HEADS) * HEAD_DIM

    def buffers(sizes):
        return [
            pltpu.VMEM((slots, sizes[chain], 256), BF16)
            for chain in range(2)
            for slots in (8, 8, 4, 3)
        ]

    dma = pltpu.SemaphoreType.DMA
    specs = [VMEM_SPEC] * (len(inputs) + len(loads))
    specs[1] = HBM_SPEC
    for index in range(len(inputs), len(specs)):
        specs[index] = HBM_SPEC
    return pl.pallas_call(
        back_kernel,
        out_shape=(
            jax.ShapeDtypeStruct((wide, width // 2), F32),
            jax.ShapeDtypeStruct((wide, width // 2), F32),
            jax.ShapeDtypeStruct((narrow, hidden_width // 2), F32),
            jax.ShapeDtypeStruct((narrow, width // 2), F32),
            jax.ShapeDtypeStruct((total // RING, width // 2), F32),
            jax.ShapeDtypeStruct((rows, width), F32),
            jax.ShapeDtypeStruct((4, width), F32),
        ),
        in_specs=specs,
        out_specs=(VMEM_SPEC,) * 7,
        scratch_shapes=[
            pltpu.VMEM(pair.shape, BF16),
            pltpu.VMEM(side.shape, BF16),
            pltpu.VMEM((rows, hidden_width // 2), BF16),
            pltpu.VMEM((rows, hidden_width // 2), BF16),
            pltpu.VMEM((rows, width // 2), BF16),
            pltpu.VMEM((width // 2, rows), BF16),
            pltpu.VMEM((rows, width // 2), BF16),
            pltpu.VMEM((HALF, 2 * HEAD_DIM, rows), BF16),
            pltpu.VMEM((HALF, 4 * HEAD_DIM, rows), BF16),
            pltpu.VMEM((HALF, 4 * HEAD_DIM, rows), BF16),
            pltpu.VMEM((2 * HEAD_DIM, rows), BF16),
            pltpu.VMEM((HALF, 2 * HEAD_DIM, rows), BF16),
            pltpu.VMEM((total, rows), BF16),
            pltpu.VMEM((total, rows), BF16),
            pltpu.VMEM((4, width), F32),
            pltpu.VMEM((4, width), F32),
            pltpu.VMEM((RING, 4, width), F32),
        ]
        + buffers((2 * wide + 6 * narrow, 2 * wide + 5 * narrow))
        + buffers((total // RING, total // RING))
        + [dma((2, 15))] * 4
        + [dma((HALF,))] * 4
        + [dma((23,))] * 2
        + [dma((RING,))] * 2
        + [dma((HALF,))] * 2
        + [dma((6,))],
        compiler_params=pltpu.CompilerParams(
            collective_id=call_id, has_side_effects=True, vmem_limit_bytes=63 << 20
        ),
        name="backward_spread",
    )(*inputs, *loads)


def head_table(positions, query_gain, key_gain):
    half = HEAD_DIM // 2
    inverse_freq = THETA ** (-(2.0 / HEAD_DIM) * jnp.arange(half, dtype=F32))
    angles = inverse_freq[:, None] * positions.astype(F32)[None, :]
    shape = (HEAD_DIM, positions.shape[0])
    return jnp.concatenate(
        [
            jnp.cos(angles),
            jnp.sin(angles),
            jnp.broadcast_to(query_gain[:, None], shape),
            jnp.broadcast_to(key_gain[:, None], shape),
        ],
        axis=0,
    )


def front_kernel(
    gain_ref,
    table_ref,
    own_start_ref,
    tokens_hbm,
    w_query_hbm,
    w_key_hbm,
    w_value_hbm,
    w_out_hbm,
    w_gate_hbm,
    w_up_hbm,
    w_down_hbm,
    qkv_out,
    starts_out,
    normed_out,
    part_out,
    mixed_out,
    inv_out,
    out_full,
    query_hbm,
    key_hbm,
    weights_hbm,
    gate_far,
    up_far,
    down_far,
    home,
    key_nat,
    tokens_ref,
    query_out,
    key_out,
    weights_out,
    keep_sem,
    own_sem,
    send_sem,
    recv_sem,
    start_send,
    start_recv,
    mixed_send,
    mixed_recv,
    extra_send,
    extra_recv,
    core_send,
    core_recv,
):
    place, core = lax.axis_index("ctx"), lax.axis_index("fsdp")
    part, member = place // HALF, lax.rem(place, HALF)
    rows = tokens_ref.shape[0]
    depth = w_query_hbm.shape[0]
    partner = (place, 1 - core)
    tokens_load = pltpu.make_async_copy(tokens_hbm, tokens_ref, keep_sem.at[0])
    tokens_load.start()
    greet([partner] + [(lax.rem(place + step, RING), core) for step in range(1, RING)])

    def remote(source, target, send, recv, peer):
        return pltpu.make_async_remote_copy(
            src_ref=source,
            dst_ref=target,
            send_sem=send,
            recv_sem=recv,
            device_id=peer,
            device_id_type=MESH,
        )

    def mate(step):
        return (part * HALF + lax.rem(member + step, HALF), core)

    copies, near_copies = [], []

    def share(source, target, near_target=None):
        index = len(copies)
        copy = remote(source, target, core_send.at[index], core_recv.at[index], partner)
        copy.start()
        copies.append(copy)
        if near_target is not None:
            near = pltpu.make_async_copy(source, near_target, own_sem.at[index])
            near.start()
            near_copies.append(near)

    column = 0
    own_depth = pl.ds(pl.multiple_of(core * depth, 128), depth)
    for source in (w_key_hbm, w_value_hbm, w_query_hbm):
        window = pl.ds(column, source.shape[1])
        target = weights_out.at[own_depth, window]
        share(source, target, target)
        column += source.shape[1]

    target = out_full.at[own_depth, :]
    share(w_out_hbm, target, target)
    for source, target in ((w_gate_hbm, gate_far), (w_up_hbm, up_far), (w_down_hbm, down_far)):
        share(source, target)

    def start_copy(step):
        return remote(
            own_start_ref,
            starts_out.at[member],
            start_send.at[step],
            start_recv.at[step],
            mate(step),
        )

    for step in range(1, HALF):
        start_copy(step).start()
    starts_out[member] = own_start_ref[...]

    def norm_rows(index, nothing):
        window = pl.ds(pl.multiple_of(index * 32, 32), 32)
        values = tokens_ref[window, :].astype(F32)
        inverse = lax.rsqrt(jnp.mean(values * values, axis=-1, keepdims=True) + EPSILON)
        normed_out[window, :] = (values * inverse * gain_ref[...]).astype(BF16)
        return nothing

    tokens_load.wait()
    lax.fori_loop(0, rows // 32, norm_rows, 0)
    half = HEAD_DIM // 2
    cosine, sine = table_ref[0:half, :], table_ref[half:HEAD_DIM, :]
    query_gain = table_ref[HEAD_DIM : 2 * HEAD_DIM, :]
    key_gain = table_ref[2 * HEAD_DIM : 3 * HEAD_DIM, :]

    def project(column, count):
        window = pl.ds(column, count)
        product = jnp.dot(normed_out[...], weights_out[:, window], preferred_element_type=F32)
        return product.T

    def turned(values, gain):
        mean = jnp.mean(values * values, axis=0, keepdims=True)
        values = values * lax.rsqrt(mean + EPSILON) * gain
        first, second = values[:half], values[half:]
        return jnp.concatenate(
            [first * cosine - second * sine, second * cosine + first * sine], axis=0
        ).astype(BF16)

    kv_width = KV_HEADS * HEAD_DIM
    copies[0].wait_recv()
    near_copies[0].wait()

    def key_chunk(index, nothing):
        products = project(pl.multiple_of(index * 256, 256), 256)
        for offset in range(4):
            raw = products[offset * HEAD_DIM : (offset + 1) * HEAD_DIM]
            group = index * 4 + offset
            key_out[group] = raw
            home[group, 2 * HEAD_DIM : 3 * HEAD_DIM, :] = turned(raw, key_gain)
        return nothing

    lax.fori_loop(0, KV_HEADS // 4, key_chunk, 0)
    copies[1].wait_recv()
    near_copies[1].wait()

    def value_chunk(index, nothing):
        products = project(pl.multiple_of(kv_width + index * 256, 256), 256)
        for offset in range(4):
            value = products[offset * HEAD_DIM : (offset + 1) * HEAD_DIM].astype(BF16)
            home[index * 4 + offset, 3 * HEAD_DIM : 4 * HEAD_DIM, :] = value
        return nothing

    lax.fori_loop(0, KV_HEADS // 4, value_chunk, 0)

    def extra_copy(group):
        window = pl.ds(2 * HEAD_DIM, 2 * HEAD_DIM)
        return remote(
            home.at[group, window],
            qkv_out.at[0, window],
            extra_send.at[group],
            extra_recv.at[group],
            (HALF + group, core),
        )

    def extra_start(group, nothing):
        extra_copy(group).start()
        return nothing

    @pl.when(place == HALF - 1)
    def _():
        lax.fori_loop(0, HALF, extra_start, 0)

    copies[2].wait_recv()
    near_copies[2].wait()

    def block_copy(step):
        peer = mate(step)
        return remote(
            home.at[lax.rem(member + step, HALF)],
            qkv_out.at[1 + member],
            send_sem.at[step],
            recv_sem.at[step],
            peer,
        )

    def query_chunk(index, nothing):
        products = project(pl.multiple_of(2 * kv_width + index * 256, 256), 256)
        for offset in range(4):
            raw = products[offset * HEAD_DIM : (offset + 1) * HEAD_DIM]
            query_out[index * 4 + offset] = raw
            low = (offset % 2) * HEAD_DIM
            home[index * 2 + offset // 2, low : low + HEAD_DIM, :] = turned(
                raw, query_gain
            )
        for offset in range(2):
            group = index * 2 + offset

            @pl.when(group != member)
            def _():
                block_copy(lax.rem(group - member + HALF, HALF)).start()

        return nothing

    lax.fori_loop(0, HEADS // 4, query_chunk, 0)
    keeps = [
        pltpu.make_async_copy(source, target, keep_sem.at[1 + index])
        for index, (source, target) in enumerate(
            ((query_out, query_hbm), (key_out, key_hbm), (weights_out, weights_hbm))
        )
    ]
    for keep in keeps:
        keep.start()
    qkv_out[1 + member] = home[member]
    base = part * HALF - 1

    @pl.when(part == 1)
    def _():
        extra_copy(member).wait_recv()
        key_nat[0] = transposed(qkv_out[0, 2 * HEAD_DIM : 3 * HEAD_DIM, :])

    def mixed_copy(step):
        peer = mate(step)
        return remote(
            part_out.at[lax.rem(member + step, HALF)],
            mixed_out.at[member],
            mixed_send.at[step],
            mixed_recv.at[step],
            peer,
        )

    def per_query(i, nothing):
        @pl.when(i - 1 != member)
        def _():
            step = lax.rem(member - i + 1 + HALF, HALF)
            block_copy(step).wait_recv()
            start_copy(step).wait_recv()

        key_nat[i] = transposed(qkv_out[i, 2 * HEAD_DIM : 3 * HEAD_DIM, :])
        query_t = jnp.concatenate(
            [qkv_out[i, 0:HEAD_DIM, :], qkv_out[i, HEAD_DIM : 2 * HEAD_DIM, :]], axis=1
        ) * jnp.asarray(HEAD_DIM**-0.5, BF16)
        start = jnp.concatenate([starts_out[i - 1]] * 2, axis=1)
        places = (base + i) * BLOCK + lax.broadcasted_iota(jnp.int32, (1, BLOCK), 1)
        query_place = jnp.concatenate([places] * 2, axis=1)

        def step(diagonal, j, carry):
            total, acc = carry
            scores = jnp.dot(key_nat[j], query_t, preferred_element_type=F32)
            key_place = (base + j) * BLOCK + lax.broadcasted_iota(jnp.int32, scores.shape, 0)
            ok = key_place >= start
            if diagonal:
                ok = ok & (key_place <= query_place)
            probs = jnp.where(ok, jnp.exp(scores), 0.0)
            total = total + jnp.sum(probs, axis=0, keepdims=True)
            acc = acc + jnp.dot(
                qkv_out[j, 3 * HEAD_DIM : 4 * HEAD_DIM, :],
                probs.astype(BF16),
                preferred_element_type=F32,
            )
            return total, acc

        carry = (jnp.zeros((1, 2 * BLOCK), F32), jnp.zeros((HEAD_DIM, 2 * BLOCK), F32))
        carry = lax.fori_loop(1 - part, i, functools.partial(step, False), carry)
        total, acc = step(True, i, carry)
        inverse = 1.0 / total
        low = (acc * inverse).astype(BF16)
        part_out[i - 1, 0:HEAD_DIM, :] = low[:, :BLOCK]
        part_out[i - 1, HEAD_DIM:, :] = low[:, BLOCK:]
        inv_out[i - 1] = inverse

        @pl.when(i - 1 != member)
        def _():
            mixed_copy(lax.rem(i - 1 - member + HALF, HALF)).start()

        return nothing

    lax.fori_loop(1, HALF + 1, per_query, 0)
    mixed_out[member] = part_out[member]

    def settle(step, nothing):
        block_copy(step).wait_send()
        start_copy(step).wait_send()
        mixed_copy(step).wait()
        return nothing

    lax.fori_loop(1, HALF, settle, 0)

    def extra_settle(group, nothing):
        extra_copy(group).wait_send()
        return nothing

    @pl.when(place == HALF - 1)
    def _():
        lax.fori_loop(0, HALF, extra_settle, 0)

    for copy in copies[:3]:
        copy.wait_send()
    for copy in copies[3:]:
        copy.wait()
    for near in near_copies[3:] + keeps:
        near.wait()


def front_call(call_id, inputs, loads):
    rows, width = loads[0].shape
    half_depth, hidden_width = loads[5].shape
    total = (HEADS + 2 * KV_HEADS) * HEAD_DIM
    dma = pltpu.SemaphoreType.DMA
    query_raw = (HEADS, HEAD_DIM, rows)
    key_raw = (KV_HEADS, HEAD_DIM, rows)
    return pl.pallas_call(
        front_kernel,
        out_shape=(
            jax.ShapeDtypeStruct((HALF + 1, 4 * HEAD_DIM, rows), BF16),
            jax.ShapeDtypeStruct((HALF, 1, rows), jnp.int32),
            jax.ShapeDtypeStruct((rows, width), BF16),
            jax.ShapeDtypeStruct((HALF, 2 * HEAD_DIM, rows), BF16),
            jax.ShapeDtypeStruct((HALF, 2 * HEAD_DIM, rows), BF16),
            jax.ShapeDtypeStruct((HALF, 1, 2 * rows), F32),
            jax.ShapeDtypeStruct((width, width), BF16),
            jax.ShapeDtypeStruct(query_raw, F32),
            jax.ShapeDtypeStruct(key_raw, F32),
            jax.ShapeDtypeStruct((width, total), BF16),
            jax.ShapeDtypeStruct((half_depth, hidden_width), BF16),
            jax.ShapeDtypeStruct((half_depth, hidden_width), BF16),
            jax.ShapeDtypeStruct((hidden_width // 2, width), BF16),
        ),
        in_specs=[VMEM_SPEC] * len(inputs) + [HBM_SPEC] * len(loads),
        out_specs=(VMEM_SPEC,) * 7 + (HBM_SPEC,) * 6,
        scratch_shapes=[
            pltpu.VMEM((HALF, 4 * HEAD_DIM, rows), BF16),
            pltpu.VMEM((HALF + 1, rows, HEAD_DIM), BF16),
            pltpu.VMEM((rows, width), BF16),
            pltpu.VMEM(query_raw, F32),
            pltpu.VMEM(key_raw, F32),
            pltpu.VMEM((width, total), BF16),
            dma((4,)),
            dma((4,)),
        ]
        + [dma((HALF,))] * 8
        + [dma((7,))] * 2,
        compiler_params=pltpu.CompilerParams(
            collective_id=call_id, has_side_effects=True, vmem_limit_bytes=63 << 20
        ),
        name="front_heads",
    )(*inputs, *loads)


def ffn_kernel(
    core_ref,
    tokens_ref,
    mixed_ref,
    w_out_ref,
    gain_ref,
    cot_ref,
    gate_own,
    gate_far,
    up_own,
    up_far,
    down_own,
    down_far,
    pair_out,
    hidden_out,
    output_out,
    ffn_out,
    side_out,
    mixed_back_out,
    grad_middle_out,
    terms_out,
    middle,
    result,
    upstream,
    middle_low,
):
    step = pl.program_id(0)
    rows, width = tokens_ref.shape
    strip = 32

    def strips(work):
        def one(index, carry):
            return work(pl.ds(pl.multiple_of(index * strip, strip), strip), carry)

        return one

    @pl.when(step == 0)
    def _():
        mixed = mixed_ref[...].astype(F32).T.astype(BF16)
        middle[...] = tokens_ref[...].astype(F32) + jnp.dot(
            mixed, w_out_ref[...], preferred_element_type=F32
        )

        def norm(window, carry):
            values = middle[window, :]
            inverse = lax.rsqrt(jnp.mean(values * values, axis=-1, keepdims=True) + EPSILON)
            ffn_out[window, :] = (values * inverse * gain_ref[...]).astype(BF16)
            result[window, :] = values
            return carry

        lax.fori_loop(0, rows // strip, strips(norm), 0)
        upstream[...] = jnp.zeros(upstream.shape, F32)
        side_out[0] = cot_ref[...].astype(F32).T.astype(BF16)

    depth = gate_own.shape[0]
    own = pl.ds(pl.multiple_of(core_ref[0] * depth, 128), depth)
    far = pl.ds(pl.multiple_of((1 - core_ref[0]) * depth, 128), depth)

    def strip_of_hidden(down_ref):
        def ahead(near_ref, far_ref):
            return jnp.dot(ffn_out[:, own], near_ref[...], preferred_element_type=F32) + jnp.dot(
                ffn_out[:, far], far_ref[...], preferred_element_type=F32
            )

        gate_pre, up_pre = ahead(gate_own, gate_far), ahead(up_own, up_far)
        grad_hidden = dot_dims(cot_ref[...], down_ref[...], 1, 1)
        gate_sig = jax.nn.sigmoid(gate_pre)
        gate_act = gate_pre * gate_sig
        hidden_out[...] = (gate_act * up_pre).astype(BF16)
        gate_back = (
            grad_hidden * up_pre * (gate_sig * (1.0 + gate_pre * (1.0 - gate_sig)))
        ).astype(BF16)
        up_back = (grad_hidden * gate_act).astype(BF16)
        result[...] += jnp.dot(hidden_out[...], down_ref[...], preferred_element_type=F32)
        for window, gate_ref, up_ref in ((own, gate_own, up_own), (far, gate_far, up_far)):
            upstream[:, window] += dot_dims(gate_back, gate_ref[...], 1, 1) + dot_dims(
                up_back, up_ref[...], 1, 1
            )
        wide = pair_out.shape[1] // 2
        for base, back in ((0, gate_back), (wide, up_back)):
            turned = back.astype(F32).T.astype(BF16)
            for owner in range(pair_out.shape[0]):
                pair_out[owner, base : base + wide, :] = turned[owner * wide : (owner + 1) * wide]

    @pl.when(step < 2)
    def _():
        strip_of_hidden(down_own)

    @pl.when(step >= 2)
    def _():
        strip_of_hidden(down_far)

    @pl.when(step == pl.num_programs(0) - 1)
    def _():
        output_out[...] = result[...].astype(BF16)

        def back(window, total):
            values, grads = middle[window, :], upstream[window, :]
            inverse = lax.rsqrt(jnp.mean(values * values, axis=-1, keepdims=True) + EPSILON)
            scaled = grads * gain_ref[...]
            weight = jnp.sum(scaled * values, axis=-1, keepdims=True) / width
            grad_middle = cot_ref[window, :].astype(F32) + (
                inverse * scaled - values * inverse**3 * weight
            )
            grad_middle_out[window, :] = grad_middle
            middle_low[window, :] = grad_middle.astype(BF16)
            return total + jnp.sum(grads * values * inverse, axis=0, keepdims=True)

        terms_out[...] = lax.fori_loop(
            0, rows // strip, strips(back), jnp.zeros((1, width), F32)
        )
        mixed_back_out[...] = dot_dims(w_out_ref[...], middle_low[...], 1, 1).astype(BF16)
        side_out[1] = middle_low[...].astype(F32).T.astype(BF16)


def ffn_call(core, tokens, mixed_t, w_out, gain, cot, gate, up, down):
    rows, width = tokens.shape
    half_depth, hidden_width = gate[0].shape
    steps = 4
    chunk = hidden_width // steps
    owners = RING // steps
    wide = hidden_width // RING

    def whole(*shape):
        return pl.BlockSpec(shape, lambda i, core_ref: (0,) * len(shape))

    def turn(i, core_ref):
        return lax.rem(i + 2 * core_ref[0], steps)

    columns = pl.BlockSpec((half_depth, chunk), lambda i, core_ref: (0, turn(i, core_ref)))
    return pl.pallas_call(
        ffn_kernel,
        grid_spec=pltpu.PrefetchScalarGridSpec(
            num_scalar_prefetch=1,
            grid=(steps,),
            in_specs=[
                whole(rows, width),
                whole(width, rows),
                whole(width, width),
                whole(1, width),
                whole(rows, width),
                columns,
                columns,
                columns,
                columns,
                pl.BlockSpec((chunk, width), lambda i, core_ref: (jnp.minimum(i, 1), 0)),
                pl.BlockSpec((chunk, width), lambda i, core_ref: (jnp.maximum(i - 2, 0), 0)),
            ],
            out_specs=(
                pl.BlockSpec(
                    (owners, 2 * wide, rows), lambda i, core_ref: (turn(i, core_ref), 0, 0)
                ),
                pl.BlockSpec((rows, chunk), lambda i, core_ref: (0, turn(i, core_ref))),
                whole(rows, width),
                whole(rows, width),
                whole(2, width, rows),
                whole(width, rows),
                whole(rows, width),
                whole(1, width),
            ),
            scratch_shapes=[pltpu.VMEM((rows, width), F32)] * 3
            + [pltpu.VMEM((rows, width), BF16)],
        ),
        out_shape=(
            jax.ShapeDtypeStruct((RING, 2 * wide, rows), BF16),
            jax.ShapeDtypeStruct((rows, hidden_width), BF16),
            jax.ShapeDtypeStruct((rows, width), BF16),
            jax.ShapeDtypeStruct((rows, width), BF16),
            jax.ShapeDtypeStruct((2, width, rows), BF16),
            jax.ShapeDtypeStruct((width, rows), BF16),
            jax.ShapeDtypeStruct((rows, width), F32),
            jax.ShapeDtypeStruct((1, width), F32),
        ),
        compiler_params=pltpu.CompilerParams(vmem_limit_bytes=63 << 20),
        name="ffn_both_ways",
    )(core, tokens, mixed_t, w_out, gain, cot, *gate, *up, *down)


def settle_kernel(*refs):
    count = 6
    sources, gains, rest = refs[:count], refs[count], refs[count + 1 :]
    targets, gain_targets, rest = rest[: count + 2], rest[count + 2 : count + 6], rest[count + 6 :]
    held, in_sem, out_sem = rest[:count], rest[count], rest[count + 1]
    loads = [
        pltpu.make_async_copy(source, hold, in_sem.at[index])
        for index, (source, hold) in enumerate(zip(sources, held))
    ]
    for load in loads:
        load.start()
    stores, row = [], 0
    for index, load in enumerate(loads):
        load.wait()
        if index < count - 1:
            pieces = [(held[index], targets[index])]
        else:
            pieces = []
            for target in targets[index:]:
                pieces.append((held[index].at[pl.ds(row, target.shape[0])], target))
                row += target.shape[0]
        for piece, target in pieces:
            store = pltpu.make_async_copy(piece, target, out_sem.at[len(stores)])
            store.start()
            stores.append(store)
    for index, target in enumerate(gain_targets):
        target[...] = gains[index : index + 1, 0 : target.shape[1]]
    for store in stores:
        store.wait()


def settle_call(tokens, gate_t, up_t, down_t, out_t, qkv_t, gains):
    sources = (tokens, gate_t, up_t, down_t, out_t, qkv_t)
    lanes = qkv_t.shape[1]
    query = HEADS * HEAD_DIM // RING
    pair = KV_HEADS * HEAD_DIM // RING
    shapes = [source.shape for source in sources[:-1]]
    shapes += [(query, lanes), (pair, lanes), (pair, lanes)]
    gain_shapes = [(1, gains.shape[1])] * 2 + [(1, HEAD_DIM)] * 2
    return pl.pallas_call(
        settle_kernel,
        out_shape=tuple(jax.ShapeDtypeStruct(shape, F32) for shape in shapes + gain_shapes),
        in_specs=[HBM_SPEC] * len(sources) + [VMEM_SPEC],
        out_specs=(HBM_SPEC,) * len(shapes) + (VMEM_SPEC,) * 4,
        scratch_shapes=[pltpu.VMEM(source.shape, F32) for source in sources]
        + [pltpu.SemaphoreType.DMA((6,)), pltpu.SemaphoreType.DMA((8,))],
        compiler_params=pltpu.CompilerParams(vmem_limit_bytes=63 << 20),
        name="settle_results",
    )(*sources, gains)


def heads_body(
    tokens,
    seg_ids,
    doc_pos,
    attn_gain,
    w_query,
    w_key,
    w_value,
    query_gain,
    key_gain,
    w_out,
    ffn_gain,
    w_gate,
    w_up,
    w_down,
    d_output,
):
    place = lax.axis_index("ctx")
    rows = tokens.shape[1]
    pos_local = doc_pos[0]
    own_starts = place * rows + jnp.arange(rows, dtype=jnp.int32) - pos_local
    table = head_table(pos_local, query_gain, key_gain)
    (
        qkv,
        starts,
        normed_low,
        mixed_far,
        mixed_home,
        inverse_total,
        o_full,
        query_raw,
        key_raw,
        kvq_full,
        gate_far,
        up_far,
        down_far,
    ) = front_call(
        1,
        (attn_gain[None, :], table, own_starts[None, :]),
        (tokens[0], w_query, w_key, w_value, w_out, w_gate, w_up, w_down),
    )
    mixed_t = mixed_home.reshape(HEADS * HEAD_DIM, rows)
    cot_low = d_output[0]
    (
        pair,
        hidden_low,
        output,
        ffn_low,
        side,
        grad_mixed,
        grad_middle,
        ffn_terms,
    ) = ffn_call(
        lax.axis_index("fsdp").astype(jnp.int32)[None],
        tokens[0],
        mixed_t,
        o_full,
        ffn_gain[None, :],
        cot_low,
        (w_gate, gate_far),
        (w_up, up_far),
        (w_down, down_far),
    )
    gate_t, up_t, down_t, out_t, qkv_grads, d_tokens, gain_totals = back_call(
        3,
        (
            pair,
            hidden_low,
            side,
            ffn_low,
            mixed_t,
            grad_mixed.reshape(HALF, 2 * HEAD_DIM, rows),
            qkv,
            starts,
            mixed_far,
            inverse_total,
            table,
            normed_low,
            attn_gain[None, :],
            ffn_terms,
        ),
        (tokens[0], query_raw, key_raw, kvq_full, grad_middle),
    )
    d_tokens, gate, up, down, out, query, key, value, attn, ffn, query_gains, key_gains = (
        settle_call(d_tokens, gate_t, up_t, down_t, out_t, qkv_grads, gain_totals)
    )
    return (
        output[None],
        d_tokens[None],
        attn[0],
        query.T,
        key.T,
        value.T,
        query_gains[0],
        key_gains[0],
        out.T,
        ffn[0],
        gate.T,
        up.T,
        down.T,
    )


def solution(mesh):
    in_specs = (
        P("fsdp", "ctx", None),
        P("fsdp", "ctx"),
        P("fsdp", "ctx"),
        P(),
        P("fsdp", None),
        P("fsdp", None),
        P("fsdp", None),
        P(),
        P(),
        P("fsdp", None),
        P(),
        P("fsdp", None),
        P("fsdp", None),
        P("fsdp", None),
        P("fsdp", "ctx", None),
    )
    out_specs = (
        P("fsdp", "ctx", None),
        P("fsdp", "ctx", None),
        P(),
        P("fsdp", "ctx"),
        P("fsdp", "ctx"),
        P("fsdp", "ctx"),
        P(),
        P(),
        P("fsdp", "ctx"),
        P(),
        P("fsdp", "ctx"),
        P("fsdp", "ctx"),
        P("fsdp", "ctx"),
    )
    chosen = heads_body if (mesh.shape["ctx"], mesh.shape["fsdp"]) == (HEADS, 2) else ring_body
    return jax.shard_map(chosen, mesh=mesh, in_specs=in_specs, out_specs=out_specs, check_vma=False)
```

```python
import functools

import jax
import jax.numpy as jnp
import numpy as np
from jax import lax
from jax.experimental import pallas as pl
from jax.experimental.pallas import tpu as pltpu
from jax.sharding import PartitionSpec as P

HEADS = 16
KV_HEADS = 8
HEAD_DIM = 64
HOPS = 8


EPSILON = 1e-05
THETA = 1000000.0
MASKED = -1e30


def from_behind(block, axis, distance):
    devices = range(lax.axis_size(axis))
    route = [(i - distance, i) for i in devices if i - distance in devices]
    return lax.ppermute(block, axis, route)


def rms_norm(values, norm_gain):
    return (
        values * lax.rsqrt(jnp.mean(values * values, axis=-1, keepdims=True) + EPSILON) * norm_gain
    )


def rms_back(values, norm_gain, upstream):
    inverse = lax.rsqrt(jnp.mean(values * values, axis=-1, keepdims=True) + EPSILON)
    scaled = upstream * norm_gain
    row_width = values.shape[-1]
    d_values = (
        inverse * scaled
        - values * inverse**3 * jnp.sum(scaled * values, axis=-1, keepdims=True) / row_width
    )
    return (d_values, upstream * values * inverse)


def rotary(values, positions, turn_sign):
    half_dim = values.shape[-1] // 2
    inverse_freq = THETA ** (-(2.0 / values.shape[-1]) * jnp.arange(half_dim, dtype=jnp.float32))
    angles = positions.astype(jnp.float32)[:, None] * inverse_freq[None, :]
    cosine = jnp.cos(angles)[:, None, :]
    sine_part = turn_sign * jnp.sin(angles)[:, None, :]
    first_half = values[..., :half_dim]
    second_half = values[..., half_dim:]
    return jnp.concatenate(
        [
            first_half * cosine - second_half * sine_part,
            second_half * cosine + first_half * sine_part,
        ],
        axis=-1,
    )


def outer_product(left_mat, right_mat):
    return lax.dot_general(
        left_mat, right_mat, (((0,), (0,)), ((), ())), preferred_element_type=jnp.float32
    )


def against(left_mat, right_mat):
    return lax.dot_general(
        left_mat, right_mat, (((1,), (1,)), ((), ())), preferred_element_type=jnp.float32
    )


def ring_body(
    tokens,
    seg_ids,
    doc_pos,
    attn_gain,
    w_query,
    w_key,
    w_value,
    query_gain,
    key_gain,
    w_out,
    ffn_gain,
    w_gate,
    w_up,
    w_down,
    d_output,
):
    cycle_place = lax.axis_index("ctx")
    tok_rows = tokens.shape[1]
    resid_in = tokens[0].astype(jnp.float32)
    seg_local = seg_ids[0]
    pos_local = doc_pos[0]
    q_per_kv = HEADS // KV_HEADS
    group_cols = q_per_kv * HEAD_DIM
    score_scale = HEAD_DIM ** (-0.5)
    q_full, k_full, v_full, o_full = (
        lax.all_gather(w_query, "fsdp", axis=0, tiled=True),
        lax.all_gather(w_key, "fsdp", axis=0, tiled=True),
        lax.all_gather(w_value, "fsdp", axis=0, tiled=True),
        lax.all_gather(w_out, "fsdp", axis=0, tiled=True),
    )
    gate_full, up_full, down_full = (
        lax.all_gather(w_gate, "fsdp", axis=0, tiled=True),
        lax.all_gather(w_up, "fsdp", axis=0, tiled=True),
        lax.all_gather(w_down, "fsdp", axis=0, tiled=True),
    )
    normed = rms_norm(resid_in, attn_gain)
    normed_low = normed.astype(jnp.bfloat16)
    query_raw = jnp.dot(normed_low, q_full, preferred_element_type=jnp.float32).reshape(
        tok_rows, HEADS, HEAD_DIM
    )
    key_raw = jnp.dot(normed_low, k_full, preferred_element_type=jnp.float32).reshape(
        tok_rows, KV_HEADS, HEAD_DIM
    )
    value_raw = jnp.dot(normed_low, v_full, preferred_element_type=jnp.float32)
    query_rot = rotary(rms_norm(query_raw, query_gain), pos_local, 1.0)
    key_rot = rotary(rms_norm(key_raw, key_gain), pos_local, 1.0)
    query_low = query_rot.astype(jnp.bfloat16).reshape(tok_rows, HEADS * HEAD_DIM)
    key_low = key_rot.astype(jnp.bfloat16).reshape(tok_rows, KV_HEADS * HEAD_DIM)
    value_low = value_raw.astype(jnp.bfloat16)
    own_kv = (key_low, value_low, seg_local)
    kv_blocks = [own_kv]
    carried = own_kv
    for hop_index in range(HOPS):
        carried = from_behind((carried[0], carried[1], carried[2]), "ctx", 1)
        kv_blocks.append(carried)
    key_all = jnp.concatenate([kv_entry[0] for kv_entry in kv_blocks], axis=0)
    value_all = jnp.concatenate([kv_entry[1] for kv_entry in kv_blocks], axis=0)
    seg_all = jnp.concatenate([kv_entry[2] for kv_entry in kv_blocks], axis=0)
    key_owner = cycle_place - jnp.arange(HOPS + 1, dtype=jnp.int32)
    owner_valid = jnp.repeat(key_owner >= 0, tok_rows)
    key_index = (
        key_owner[:, None] * tok_rows + jnp.arange(tok_rows, dtype=jnp.int32)[None, :]
    ).reshape(-1)
    query_index = cycle_place * tok_rows + jnp.arange(tok_rows, dtype=jnp.int32)
    allowed = (
        (seg_local[:, None] == seg_all[None, :])
        & (key_index[None, :] <= query_index[:, None])
        & owner_valid[None, :]
    )

    def group_scores(kv_group):
        query_part = lax.dynamic_slice_in_dim(query_low, kv_group * group_cols, group_cols, 1)
        query_part = query_part.reshape(tok_rows, q_per_kv, HEAD_DIM)
        key_part = lax.dynamic_slice_in_dim(key_all, kv_group * HEAD_DIM, HEAD_DIM, 1)
        value_part = lax.dynamic_slice_in_dim(value_all, kv_group * HEAD_DIM, HEAD_DIM, 1)
        scores = (
            jnp.einsum("trd,kd->rtk", query_part, key_part, preferred_element_type=jnp.float32)
            * score_scale
        )
        return (jnp.where(allowed[None], scores, MASKED), query_part, key_part, value_part)

    def forward_group(kv_group):
        scores, query_part, key_part, value_part = group_scores(kv_group)
        row_top = jnp.max(scores, axis=-1, keepdims=True)
        log_total = row_top + jnp.log(jnp.sum(jnp.exp(scores - row_top), axis=-1, keepdims=True))
        attn_probs = jnp.exp(scores - log_total)
        mixed_part = jnp.einsum(
            "rtk,kd->trd",
            attn_probs.astype(jnp.bfloat16),
            value_part,
            preferred_element_type=jnp.float32,
        )
        return (mixed_part.reshape(tok_rows, group_cols), log_total[..., 0])

    mixed_groups, total_groups = lax.map(forward_group, jnp.arange(KV_HEADS, dtype=jnp.int32))
    mixed = mixed_groups.transpose(1, 0, 2).reshape(tok_rows, HEADS * HEAD_DIM)
    mixed_low = mixed.astype(jnp.bfloat16)
    middle = resid_in + jnp.dot(mixed_low, o_full, preferred_element_type=jnp.float32)
    ffn_low = rms_norm(middle, ffn_gain).astype(jnp.bfloat16)
    gate_pre = jnp.dot(ffn_low, gate_full, preferred_element_type=jnp.float32)
    up_pre = jnp.dot(ffn_low, up_full, preferred_element_type=jnp.float32)
    gate_sig = jax.nn.sigmoid(gate_pre)
    gate_act = gate_pre * gate_sig
    hidden_low = (gate_act * up_pre).astype(jnp.bfloat16)
    result = middle + jnp.dot(hidden_low, down_full, preferred_element_type=jnp.float32)
    output = result.astype(jnp.bfloat16)[None]
    cot_low = d_output[0]
    cotangent = cot_low.astype(jnp.float32)
    grad_w_down = outer_product(hidden_low, cot_low)
    grad_hidden = against(cot_low, down_full)
    gate_back = (grad_hidden * up_pre * (gate_sig * (1.0 + gate_pre * (1.0 - gate_sig)))).astype(
        jnp.bfloat16
    )
    up_back = (grad_hidden * gate_act).astype(jnp.bfloat16)
    grad_w_gate = outer_product(ffn_low, gate_back)
    grad_w_up = outer_product(ffn_low, up_back)
    grad_ffn_in = against(gate_back, gate_full) + against(up_back, up_full)
    middle_part, ffn_terms = rms_back(middle, ffn_gain, grad_ffn_in)
    grad_middle = cotangent + middle_part
    middle_low = grad_middle.astype(jnp.bfloat16)
    grad_w_out = outer_product(mixed_low, middle_low)
    grad_mixed = against(middle_low, o_full).astype(jnp.bfloat16)

    def backward_group(kv_group):
        scores, query_part, key_part, value_part = group_scores(kv_group)
        attn_probs = jnp.exp(scores - total_groups[kv_group][..., None])
        mixed_grad_part = lax.dynamic_slice_in_dim(grad_mixed, kv_group * group_cols, group_cols, 1)
        mixed_grad_part = mixed_grad_part.reshape(tok_rows, q_per_kv, HEAD_DIM)
        grad_probs = jnp.einsum(
            "trd,kd->rtk", mixed_grad_part, value_part, preferred_element_type=jnp.float32
        )
        grad_value = jnp.einsum(
            "rtk,trd->kd",
            attn_probs.astype(jnp.bfloat16),
            mixed_grad_part,
            preferred_element_type=jnp.float32,
        )
        row_delta = jnp.sum(grad_probs * attn_probs, axis=-1, keepdims=True)
        grad_scores = (attn_probs * (grad_probs - row_delta)).astype(jnp.bfloat16)
        grad_query = (
            jnp.einsum("rtk,kd->trd", grad_scores, key_part, preferred_element_type=jnp.float32)
            * score_scale
        )
        grad_key = (
            jnp.einsum("rtk,trd->kd", grad_scores, query_part, preferred_element_type=jnp.float32)
            * score_scale
        )
        return (grad_query.reshape(tok_rows, group_cols), grad_key, grad_value)

    query_groups, key_groups, value_groups = lax.map(
        backward_group, jnp.arange(KV_HEADS, dtype=jnp.int32)
    )
    grad_query_rot = query_groups.transpose(1, 0, 2).reshape(tok_rows, HEADS, HEAD_DIM)
    key_blocks = key_groups.transpose(1, 0, 2).reshape(HOPS + 1, tok_rows, KV_HEADS * HEAD_DIM)
    value_blocks = value_groups.transpose(1, 0, 2).reshape(HOPS + 1, tok_rows, KV_HEADS * HEAD_DIM)
    home_key = key_blocks[HOPS]
    home_value = value_blocks[HOPS]
    for hop_index in range(HOPS, 0, -1):
        moved_key, moved_value = (
            from_behind(home_key.astype(jnp.bfloat16), "ctx", -1).astype(home_key.dtype),
            from_behind(home_value.astype(jnp.bfloat16), "ctx", -1).astype(home_value.dtype),
        )
        home_key = moved_key + key_blocks[hop_index - 1]
        home_value = moved_value + value_blocks[hop_index - 1]
    query_turned = rotary(grad_query_rot, pos_local, -1.0)
    key_turned = rotary(home_key.reshape(tok_rows, KV_HEADS, HEAD_DIM), pos_local, -1.0)
    query_back, query_terms = rms_back(query_raw, query_gain, query_turned)
    key_back, key_terms = rms_back(key_raw, key_gain, key_turned)
    query_back = query_back.reshape(tok_rows, HEADS * HEAD_DIM).astype(jnp.bfloat16)
    key_back = key_back.reshape(tok_rows, KV_HEADS * HEAD_DIM).astype(jnp.bfloat16)
    value_back = home_value.astype(jnp.bfloat16)
    grad_w_query = outer_product(normed_low, query_back)
    grad_w_key = outer_product(normed_low, key_back)
    grad_w_value = outer_product(normed_low, value_back)
    grad_normed = (
        against(query_back, q_full) + against(key_back, k_full) + against(value_back, v_full)
    )
    input_part, attn_terms = rms_back(resid_in, attn_gain, grad_normed)
    d_tokens = (grad_middle + input_part)[None]
    gain_totals = lax.psum(
        (
            jnp.sum(attn_terms, axis=0),
            jnp.sum(ffn_terms, axis=0),
            jnp.sum(query_terms, axis=(0, 1)),
            jnp.sum(key_terms, axis=(0, 1)),
        ),
        ("ctx", "fsdp"),
    )
    weight_grads = (
        grad_w_query,
        grad_w_key,
        grad_w_value,
        grad_w_out,
        grad_w_gate,
        grad_w_up,
        grad_w_down,
    )
    spread = (
        lax.psum_scatter(
            weight_grads[0].astype(jnp.bfloat16), "fsdp", scatter_dimension=0, tiled=True
        ).astype(jnp.float32),
        lax.psum_scatter(
            weight_grads[1].astype(jnp.bfloat16), "fsdp", scatter_dimension=0, tiled=True
        ).astype(jnp.float32),
        lax.psum_scatter(
            weight_grads[2].astype(jnp.bfloat16), "fsdp", scatter_dimension=0, tiled=True
        ).astype(jnp.float32),
        lax.psum_scatter(
            weight_grads[3].astype(jnp.bfloat16), "fsdp", scatter_dimension=0, tiled=True
        ).astype(jnp.float32),
        lax.psum_scatter(
            weight_grads[4].astype(jnp.bfloat16), "fsdp", scatter_dimension=0, tiled=True
        ).astype(jnp.float32),
        lax.psum_scatter(
            weight_grads[5].astype(jnp.bfloat16), "fsdp", scatter_dimension=0, tiled=True
        ).astype(jnp.float32),
        lax.psum_scatter(
            weight_grads[6].astype(jnp.bfloat16), "fsdp", scatter_dimension=0, tiled=True
        ).astype(jnp.float32),
    )
    shares = (
        lax.psum_scatter(spread[0], "ctx", scatter_dimension=1, tiled=True),
        lax.psum_scatter(spread[1], "ctx", scatter_dimension=1, tiled=True),
        lax.psum_scatter(spread[2], "ctx", scatter_dimension=1, tiled=True),
        lax.psum_scatter(spread[3], "ctx", scatter_dimension=1, tiled=True),
        lax.psum_scatter(spread[4], "ctx", scatter_dimension=1, tiled=True),
        lax.psum_scatter(spread[5], "ctx", scatter_dimension=1, tiled=True),
        lax.psum_scatter(spread[6], "ctx", scatter_dimension=1, tiled=True),
    )
    return (
        output,
        d_tokens,
        gain_totals[0],
        shares[0],
        shares[1],
        shares[2],
        gain_totals[2],
        gain_totals[3],
        shares[3],
        gain_totals[1],
        shares[4],
        shares[5],
        shares[6],
    )


MESH = pl.DeviceIdType.MESH
BLOCK = 256
RING = 16
HALF = 8
EDGE = 128
DOWN_CHUNKS = ((0, 3), (3, 2), (5, 4))
VMEM_SPEC = pl.BlockSpec(memory_space=pltpu.VMEM)
HBM_SPEC = pl.BlockSpec(memory_space=pltpu.HBM)
SMEM_SPEC = pl.BlockSpec(memory_space=pltpu.SMEM)
F32 = jnp.float32
BF16 = jnp.bfloat16


def dot_dims(left_mat, right_mat, left_dim, right_dim):
    return lax.dot_general(
        left_mat, right_mat, (((left_dim,), (right_dim,)), ((), ())), preferred_element_type=F32
    )


def transposed(block):
    return block.astype(F32).T.astype(BF16)


def flip(bit, turned):
    return bit + turned - 2 * bit * turned


class Spread:
    def __init__(self, chain, compute, sent, came, send_sems, recv_sems):
        place, self.core = lax.axis_index("ctx"), lax.axis_index("fsdp")
        x, y, self.z = lax.rem(place, 2), lax.rem(place // 2, 2), place // 4
        self.chain = chain
        self.first, self.second = (x, y) if chain == 0 else (y, x)
        self.compute, self.sent, self.came = compute, sent, came
        self.send_sems, self.recv_sems = send_sems, recv_sems

    def at(self, first, second, depth):
        low = second * 2 + first if self.chain == 0 else first * 2 + second
        return depth * 4 + low

    def deep(self, depth):
        return lax.rem(self.z + depth, 4)

    def copy(self, stage, slot):
        if stage == 0:
            peer = self.at(1 - self.first, self.second, self.z)
            source, target, sem = self.sent.at[slot], self.came[0].at[slot], slot
        elif stage == 1:
            peer = self.at(self.first, 1 - self.second, self.z)
            source, target, sem = self.came[0].at[4 + slot], self.came[1].at[slot], 8 + slot
        else:
            peer = self.at(self.first, self.second, self.deep(slot))
            source, target, sem = self.came[0].at[slot], self.came[2].at[slot - 1], 11 + slot
        return pltpu.make_async_remote_copy(
            src_ref=source,
            dst_ref=target,
            send_sem=self.send_sems.at[self.chain, sem],
            recv_sem=self.recv_sems.at[self.chain, sem],
            device_id=(peer, self.core),
            device_id_type=MESH,
        )

    def stage_one(self, turned, depth):
        slot = turned * 4 + depth
        owner = self.at(1 - self.first, flip(self.second, turned), self.deep(depth))
        for row, value in self.compute(self.chain, owner):
            self.sent[slot, row : row + value.shape[0], :] = value.astype(BF16)
        self.copy(0, slot).start()

    def stage_two(self, depth):
        self.copy(0, 4 + depth).wait_recv()
        owner = self.at(self.first, 1 - self.second, self.deep(depth))
        for row, value in self.compute(self.chain, owner):
            window = slice(row, row + value.shape[0])
            value = value + self.came[0][4 + depth, window, :].astype(F32)
            self.came[0][4 + depth, window, :] = value.astype(BF16)
        self.copy(1, depth).start()

    def stage_three(self, depth):
        self.copy(0, depth).wait_recv()
        self.copy(1, depth).wait_recv()
        owner = self.at(self.first, self.second, self.deep(depth))
        for row, value in self.compute(self.chain, owner):
            window = slice(row, row + value.shape[0])
            value = value + self.came[0][depth, window, :].astype(F32)
            value = value + self.came[1][depth, window, :].astype(F32)
            self.came[0][depth, window, :] = value.astype(BF16)
        self.copy(2, depth).start()

    def close(self, finish):
        self.copy(0, 0).wait_recv()
        self.copy(1, 0).wait_recv()
        for depth in range(1, 4):
            self.copy(2, depth).wait_recv()
        owner = self.at(self.first, self.second, self.z)
        for row, value in self.compute(self.chain, owner):
            window = slice(row, row + value.shape[0])
            value = value + self.came[0][0, window, :].astype(F32)
            value = value + self.came[1][0, window, :].astype(F32)
            for depth in range(3):
                value = value + self.came[2][depth, window, :].astype(F32)
            finish(self.chain, row, value)

    def drain(self):
        for slot in range(8):
            self.copy(0, slot).wait_send()
        for depth in range(4):
            self.copy(1, depth).wait_send()
        for depth in range(1, 4):
            self.copy(2, depth).wait_send()


class DeepSpread:
    def __init__(self, compute, sent, came, send_sems, recv_sems):
        self.place, self.core = lax.axis_index("ctx"), lax.axis_index("fsdp")
        self.x, self.y = lax.rem(self.place, 2), lax.rem(self.place // 2, 2)
        self.compute, self.sent, self.came = compute, sent, came
        self.send_sems, self.recv_sems = send_sems, recv_sems

    def copy(self, stage, slot):
        if stage == 0:
            peer = lax.rem(self.place + 4 * slot, RING)
            source, target, sem = self.sent.at[slot - 1], self.came[0].at[slot - 1], slot - 1
        elif stage == 1:
            peer = self.place + 1 - 2 * self.x
            local = flip(self.y, slot) * 2 + 1 - self.x
            source, target, sem = self.came[0].at[0, local], self.came[1].at[slot], 3 + slot
        else:
            peer = self.place + 2 - 4 * self.y
            local = (1 - self.y) * 2 + self.x
            source, target, sem = self.came[0].at[0, local], self.came[2].at[0], 5
        return pltpu.make_async_remote_copy(
            src_ref=source,
            dst_ref=target,
            send_sem=self.send_sems.at[sem],
            recv_sem=self.recv_sems.at[sem],
            device_id=(peer, self.core),
            device_id_type=MESH,
        )

    def stage_one(self, slot):
        first = lax.rem(self.place // 4 + slot, 4) * 4
        value = self.compute(first, 4)
        rows = value.shape[0] // 4
        for local in range(4):
            for chunk in range(value.shape[1] // 256):
                self.sent[slot - 1, local, chunk * rows : (chunk + 1) * rows, :] = value[
                    local * rows : (local + 1) * rows, chunk * 256 : (chunk + 1) * 256
                ].astype(BF16)
        self.copy(0, slot).start()

    def arrived(self, local):
        value = self.compute(self.place - lax.rem(self.place, 4) + local, 1)
        rows = value.shape[0]
        for chunk in range(value.shape[1] // 256):
            window = slice(chunk * rows, (chunk + 1) * rows)
            total = value[:, chunk * 256 : (chunk + 1) * 256]
            for slot in range(3):
                total = total + self.came[0][slot, local, window, :].astype(F32)
            yield window, total

    def stage_two(self):
        for slot in range(1, 4):
            self.copy(0, slot).wait_recv()
        for slot in (1, 0):
            local = flip(self.y, slot) * 2 + 1 - self.x
            for window, total in self.arrived(local):
                self.came[0][0, local, window, :] = total.astype(BF16)
            self.copy(1, slot).start()

    def stage_three(self):
        self.copy(1, 1).wait_recv()
        local = (1 - self.y) * 2 + self.x
        for window, total in self.arrived(local):
            total = total + self.came[1][1, window, :].astype(F32)
            self.came[0][0, local, window, :] = total.astype(BF16)
        self.copy(2, 0).start()

    def close(self, finish):
        self.copy(1, 0).wait_recv()
        self.copy(2, 0).wait_recv()
        for window, total in self.arrived(lax.rem(self.place, 4)):
            total = total + self.came[1][0, window, :].astype(F32)
            finish(window, total + self.came[2][0, window, :].astype(F32))

    def drain(self):
        for slot in range(1, 4):
            self.copy(0, slot).wait_send()
        for slot in range(2):
            self.copy(1, slot).wait_send()
        self.copy(2, 0).wait_send()


def greet(peers):
    barrier = pltpu.get_barrier_semaphore()
    for peer in peers:
        pl.semaphore_signal(barrier, inc=1, device_id=peer, device_id_type=MESH)
    pl.semaphore_wait(barrier, len(peers))


def turn_back(values, cosine, sine):
    half = HEAD_DIM // 2
    first, second = values[:half], values[half:]
    return jnp.concatenate(
        [first * cosine + second * sine, second * cosine - first * sine], axis=0
    )


def column_norm_back(values, gain, upstream):
    inverse = lax.rsqrt(jnp.mean(values * values, axis=0, keepdims=True) + EPSILON)
    scaled = upstream * gain
    total = jnp.sum(scaled * values, axis=0, keepdims=True) / values.shape[0]
    return inverse * scaled - values * inverse**3 * total, upstream * values * inverse


def back_kernel(
    pair_hbm,
    hidden_hbm,
    side_hbm,
    ffn_hbm,
    mixed_hbm,
    home_hbm,
    qkv_hbm,
    start_ref,
    part_hbm,
    inv_ref,
    table_ref,
    normed_hbm,
    attn_gain_ref,
    ffn_terms_ref,
    tokens_hbm,
    query_hbm,
    key_hbm,
    weights_hbm,
    middle_hbm,
    gate_out,
    up_out,
    down_out,
    out_out,
    grads_out,
    tokens_out,
    gains_out,
    pair_own,
    side_own,
    ffn_ref,
    mixed_ref,
    home_ref,
    qkv_ref,
    part_ref,
    normed_ref,
    pair_far,
    side_far,
    hidden_own,
    hidden_far,
    ffn_far,
    mixed_far,
    normed_far,
    cot_far,
    back_own,
    back_far,
    extra_own,
    extra_far,
    turned_own,
    turned_far,
    gain_own,
    gain_came,
    gain_all,
    sent_a,
    came_a0,
    came_a1,
    came_a2,
    sent_b,
    came_b0,
    came_b1,
    came_b2,
    sent_c,
    came_c0,
    came_c1,
    came_c2,
    deep_send,
    deep_recv,
    tail_sent_a,
    tail_came_a0,
    tail_came_a1,
    tail_came_a2,
    tail_sent_b,
    tail_came_b0,
    tail_came_b1,
    tail_came_b2,
    send_sems,
    recv_sems,
    tail_send,
    tail_recv,
    cot_send,
    cot_recv,
    back_send,
    back_recv,
    core_send,
    core_recv,
    gain_send,
    gain_recv,
    extra_send,
    extra_recv,
    load_sem,
    stage_sem,
):
    place, core = lax.axis_index("ctx"), lax.axis_index("fsdp")
    part, member = place // HALF, lax.rem(place, HALF)
    base = part * HALF - 1
    x, y, z = lax.rem(place, 2), lax.rem(place // 2, 2), place // 4
    wide = pair_own.shape[1] // 2
    narrow = side_own.shape[1] // RING
    half_hidden = hidden_far.shape[1]
    half_width = ffn_far.shape[1]
    heads, pairs = query_hbm.shape[0], key_hbm.shape[0]
    scale = HEAD_DIM**-0.5
    partner = (place, 1 - core)

    def half(part, size):
        return pl.ds(pl.multiple_of(part * size, 128), size)

    stages = [
        pltpu.make_async_copy(source, target, stage_sem.at[index])
        for index, (source, target) in enumerate(
            (
                (home_hbm, home_ref),
                (pair_hbm, pair_own),
                (side_hbm, side_own),
                (ffn_hbm, ffn_ref),
                (mixed_hbm, mixed_ref),
                (qkv_hbm, qkv_ref),
                (part_hbm, part_ref),
                (normed_hbm, normed_ref),
            )
        )
    ]
    own_hidden = pltpu.make_async_copy(
        hidden_hbm.at[:, half(core, half_hidden)], hidden_own, load_sem.at[0]
    )
    for stage in stages[:5]:
        stage.start()
    own_hidden.start()
    for stage in stages[5:]:
        stage.start()
    middle_load = pltpu.make_async_copy(middle_hbm, tokens_out, load_sem.at[1])
    middle_load.start()
    greet([(lax.rem(place + step, RING), core) for step in range(1, RING)] + [partner])

    def remote(source, target, send, recv, peer):
        return pltpu.make_async_remote_copy(
            src_ref=source,
            dst_ref=target,
            send_sem=send,
            recv_sem=recv,
            device_id=peer,
            device_id_type=MESH,
        )

    def mate(step):
        return (part * HALF + lax.rem(member + step, HALF), core)

    def cot_copy(step):
        return remote(
            home_ref.at[lax.rem(member + step, HALF)],
            cot_far.at[member],
            cot_send.at[step],
            cot_recv.at[step],
            mate(step),
        )

    def core_copy(source, target, sem):
        return remote(source, target, core_send.at[sem], core_recv.at[sem], partner)

    def pair_copy(turn_x, turn_y, depth):
        owner = lax.rem(z + depth, 4) * 4 + flip(y, turn_y) * 2 + flip(x, turn_x)
        return core_copy(
            pair_hbm.at[owner], pair_far.at[owner], 6 + turn_x * 8 + turn_y * 4 + depth
        )

    sides = [
        core_copy(ffn_hbm.at[:, half(1 - core, half_width)], ffn_far, 0),
        core_copy(mixed_hbm.at[half(1 - core, half_width), :], mixed_far, 1),
        core_copy(side_hbm, side_far, 2),
        core_copy(hidden_hbm.at[:, half(1 - core, half_hidden)], hidden_far, 3),
    ]
    order = []
    for depth in (2, 1, 3, 0):
        order += [(1, 1, depth), (1, 0, depth), (0, 1, depth)]
    order += [(0, 0, depth) for depth in (2, 1, 3, 0)]
    for copy in sides:
        copy.start()
    pair_copy(*order[0]).start()
    stages[0].wait()
    for step in range(1, HALF):
        cot_copy(step).start()
    for turn_x, turn_y, depth in order[1:]:
        pair_copy(turn_x, turn_y, depth).start()
    normed_copy = core_copy(normed_hbm.at[:, half(1 - core, half_width)], normed_far, 4)
    normed_copy.start()
    cot_far[member] = home_ref[member]

    def down_product(rows, split):
        cols = slice(split[0] * 256, (split[0] + split[1]) * 256)
        down = jnp.dot(side_own[0, rows, :], hidden_own[:, cols], preferred_element_type=F32)
        return down + jnp.dot(side_far[0, rows, :], hidden_far[:, cols], preferred_element_type=F32)

    def deep_compute(owner, count):
        rows = pl.ds(pl.multiple_of(owner * narrow, 16), count * narrow)
        return down_product(rows, DOWN_CHUNKS[2])

    def deep_finish(window, value):
        chunk = DOWN_CHUNKS[2][0] + window.start // narrow
        down_out[:, chunk * 256 : chunk * 256 + 256] = value

    def compute(chain, owner):
        lanes = pl.ds(chain * 256, 256)
        own_lanes = pl.ds(pl.multiple_of(core * half_width + chain * 256, 128), 256)
        both_pair = jnp.dot(pair_own[owner], ffn_ref[:, own_lanes], preferred_element_type=F32)
        both_pair += jnp.dot(pair_far[owner], ffn_far[:, lanes], preferred_element_type=F32)
        values = [(0, both_pair)]
        rows = pl.ds(pl.multiple_of(owner * narrow, 16), narrow)
        chunks = DOWN_CHUNKS[chain][1]
        down = down_product(rows, DOWN_CHUNKS[chain])
        row = 2 * wide
        for chunk in range(chunks):
            values.append((row, down[:, chunk * 256 : chunk * 256 + 256]))
            row += narrow
        out = dot_dims(side_own[1, rows, :], mixed_ref[own_lanes, :], 1, 1)
        out += dot_dims(side_far[1, rows, :], mixed_far[lanes, :], 1, 1)
        values.append((row, out))
        return values

    def finish(chain, row, value):
        lanes = slice(chain * 256, chain * 256 + 256)
        if row == 0:
            gate_out[:, lanes] = value[:wide]
            up_out[:, lanes] = value[wide:]
            return
        chunk = (row - 2 * wide) // narrow
        if chunk == DOWN_CHUNKS[chain][1]:
            out_out[:, lanes] = value
        else:
            chunk += DOWN_CHUNKS[chain][0]
            down_out[:, chunk * 256 : chunk * 256 + 256] = value

    chains = (
        Spread(0, compute, sent_a, (came_a0, came_a1, came_a2), send_sems, recv_sems),
        Spread(1, compute, sent_b, (came_b0, came_b1, came_b2), send_sems, recv_sems),
    )
    own_hidden.wait()
    for stage in stages[1:5]:
        stage.wait()
    for copy in sides:
        copy.wait_recv()

    def near(depth):
        pair_copy(1, 1, depth).wait_recv()
        for chain in chains:
            chain.stage_one(1, depth)

    def far(depth):
        pair_copy(1, 0, depth).wait_recv()
        pair_copy(0, 1, depth).wait_recv()
        for chain in chains:
            chain.stage_one(0, depth)

    def onward(depth):
        for chain in chains:
            chain.stage_two(depth)

    def deeper(depth):
        pair_copy(0, 0, depth).wait_recv()
        for chain in chains:
            chain.stage_three(depth)

    along = DeepSpread(
        deep_compute, sent_c, (came_c0, came_c1, came_c2), deep_send, deep_recv
    )
    near(2)
    for slot in (2, 1, 3):
        along.stage_one(slot)
    far(2)
    near(1)
    for stage in stages[5:]:
        stage.wait()

    def back_copy(step):
        return remote(
            back_own.at[lax.rem(member + step, HALF)],
            back_far.at[member],
            back_send.at[step],
            back_recv.at[step],
            mate(step),
        )

    def extra_copy(group):
        return remote(
            extra_own,
            extra_far.at[group],
            extra_send.at[group],
            extra_recv.at[group],
            (HALF - 1, core),
        )

    def attention(
        scaled, cots, natural, delta_ref, query_acc, key_nat, value_nat, pair_acc
    ):
        def widen(ref, i, row):
            return jnp.concatenate(
                [ref[i, row : row + HEAD_DIM, :], ref[i, row + HEAD_DIM : row + 2 * HEAD_DIM, :]],
                axis=1,
            )

        def prepare(i, nothing):
            @pl.when(i != member)
            def _():
                cot_copy(lax.rem(member - i + HALF, HALF)).wait_recv()

            query = widen(qkv_ref, i + 1, 0) * jnp.asarray(scale, BF16)
            cot = widen(cot_far, i, 0)
            scaled[i] = query
            cots[i] = cot
            natural[i] = transposed(jnp.concatenate([query, cot], axis=0))
            delta_ref[i] = jnp.sum(
                cot.astype(F32) * widen(part_ref, i, 0).astype(F32), axis=0, keepdims=True
            )
            query_acc[i] = jnp.zeros(query_acc.shape[1:], F32)
            return nothing

        def per_key(j, nothing):
            key_t = qkv_ref[j, 2 * HEAD_DIM : 3 * HEAD_DIM, :]
            key_nat[...] = transposed(key_t)
            value_nat[...] = transposed(qkv_ref[j, 3 * HEAD_DIM : 4 * HEAD_DIM, :])
            shape = (BLOCK, 2 * BLOCK)
            key_place = (base + j) * BLOCK + lax.broadcasted_iota(jnp.int32, shape, 0)

            def step(diagonal, i):
                start = jnp.concatenate([start_ref[i - 1]] * 2, axis=1)
                scores = jnp.dot(key_nat[...], scaled[i - 1], preferred_element_type=F32)
                grad_probs = jnp.dot(value_nat[...], cots[i - 1], preferred_element_type=F32)
                ok = key_place >= start
                if diagonal:
                    places = (base + i) * BLOCK + lax.broadcasted_iota(jnp.int32, (1, BLOCK), 1)
                    ok = ok & (key_place <= jnp.concatenate([places] * 2, axis=1))
                probs = jnp.where(ok, jnp.exp(scores) * inv_ref[i - 1], 0.0)
                grad_scores = (probs * (grad_probs - delta_ref[i - 1])).astype(BF16)
                both_low = jnp.concatenate([grad_scores, probs.astype(BF16)], axis=0)
                query_acc[i - 1] += jnp.dot(
                    qkv_ref[j, 2 * HEAD_DIM : 3 * HEAD_DIM, :],
                    grad_scores,
                    preferred_element_type=F32,
                )
                return jnp.dot(both_low, natural[i - 1], preferred_element_type=F32)

            @pl.when(j == 0)
            def _():
                pair_acc[...] = jnp.zeros(pair_acc.shape, F32)

            @pl.when(j > 0)
            def _():
                pair_acc[...] = step(True, j)

            def one(i, carry):
                pair_acc[...] += step(False, i)
                return carry

            def two(index, carry):
                i = j + 1 + 2 * index
                pair_acc[...] += step(False, i) + step(False, i + 1)
                return carry

            count = (HALF - j) // 2
            lax.fori_loop(0, count, two, 0)
            lax.fori_loop(j + 1 + 2 * count, HALF + 1, one, 0)
            first = lax.broadcasted_iota(jnp.int32, (BLOCK, 2 * HEAD_DIM), 1) < HEAD_DIM
            merged = jnp.where(first, pair_acc[0:BLOCK, :], pair_acc[BLOCK:, :]).T.astype(BF16)

            @pl.when(j == 0)
            def _():
                extra_own[...] = merged
                extra_copy(member).start()

            @pl.when(j > 0)
            def _():
                query_grad = (query_acc[j - 1] * scale).astype(BF16)
                back_own[j - 1, 0:HEAD_DIM, :] = query_grad[:, :BLOCK]
                back_own[j - 1, HEAD_DIM : 2 * HEAD_DIM, :] = query_grad[:, BLOCK:]
                back_own[j - 1, 2 * HEAD_DIM : 4 * HEAD_DIM, :] = merged

            @pl.when((j > 0) & (j - 1 != member))
            def _():
                back_copy(lax.rem(j - 1 - member + HALF, HALF)).start()

            @pl.when(j == 4)
            def _():
                onward(2)
                far(1)

            @pl.when(j == HALF)
            def _():
                near(3)

            return nothing

        lax.fori_loop(0, HALF, prepare, 0)
        lax.fori_loop(1 - part, HALF + 1, per_key, 0)
        back_far[member] = back_own[member]

    pl.run_scoped(
        attention,
        pltpu.VMEM((HALF, HEAD_DIM, 2 * BLOCK), BF16),
        pltpu.VMEM((HALF, HEAD_DIM, 2 * BLOCK), BF16),
        pltpu.VMEM((HALF, 2 * BLOCK, 2 * HEAD_DIM), BF16),
        pltpu.VMEM((HALF, 1, 2 * BLOCK), F32),
        pltpu.VMEM((HALF, HEAD_DIM, 2 * BLOCK), F32),
        pltpu.VMEM((BLOCK, HEAD_DIM), BF16),
        pltpu.VMEM((BLOCK, HEAD_DIM), BF16),
        pltpu.VMEM((2 * BLOCK, 2 * HEAD_DIM), F32),
    )

    turned_copy = core_copy(turned_own, turned_far, 5)

    def tail_compute(chain, owner):
        lanes = slice(chain * 256, chain * 256 + 256)
        own_lanes = pl.ds(pl.multiple_of(core * half_width + chain * 256, 128), 256)
        values, row = [], 0
        for size, base in ((heads, 2 * pairs), (pairs, 0), (pairs, pairs)):
            count = size * HEAD_DIM // RING
            rows = pl.ds(pl.multiple_of(base * HEAD_DIM + owner * count, 16), count)
            value = jnp.dot(
                turned_own[rows, :], normed_ref[:, own_lanes], preferred_element_type=F32
            )
            value += jnp.dot(turned_far[rows, :], normed_far[:, lanes], preferred_element_type=F32)
            values.append((row, value))
            row += count
        return values

    def tail_finish(chain, row, value):
        grads_out[row : row + value.shape[0], chain * 256 : chain * 256 + 256] = value

    tails = (
        Spread(
            0,
            tail_compute,
            tail_sent_a,
            (tail_came_a0, tail_came_a1, tail_came_a2),
            tail_send,
            tail_recv,
        ),
        Spread(
            1,
            tail_compute,
            tail_sent_b,
            (tail_came_b0, tail_came_b1, tail_came_b2),
            tail_send,
            tail_recv,
        ),
    )

    def finish_all(natural, summed, query_ref, key_ref, tokens_ref, weights_ref):
        loads = [
            pltpu.make_async_copy(query_hbm, query_ref, load_sem.at[2]),
            pltpu.make_async_copy(key_hbm, key_ref, load_sem.at[3]),
            pltpu.make_async_copy(tokens_hbm, tokens_ref, load_sem.at[4]),
            pltpu.make_async_copy(weights_hbm, weights_ref, load_sem.at[5]),
        ]
        for copy in loads:
            copy.start()
        half_dim = HEAD_DIM // 2
        cosine, sine = table_ref[0:half_dim, :], table_ref[half_dim:HEAD_DIM, :]
        query_gain = table_ref[HEAD_DIM : 2 * HEAD_DIM, :]
        key_gain = table_ref[2 * HEAD_DIM : 3 * HEAD_DIM, :]

        def head_rows(index):
            return pl.ds(pl.multiple_of(index * HEAD_DIM, HEAD_DIM), HEAD_DIM)

        def query_head(head, total):
            low = pl.multiple_of(lax.rem(head, 2) * HEAD_DIM, HEAD_DIM)
            upstream = turn_back(
                back_far[head // 2, pl.ds(low, HEAD_DIM), :].astype(F32), cosine, sine
            )
            back, terms = column_norm_back(query_ref[head], query_gain, upstream)
            turned_own[head_rows(2 * pairs + head), :] = back.astype(BF16)
            return total + terms

        def key_head(pair, total):
            upstream = back_far[pair, 2 * HEAD_DIM : 4 * HEAD_DIM, :].astype(F32)
            upstream += extra_far[pair].astype(F32)
            back, terms = column_norm_back(
                key_ref[pair],
                key_gain,
                turn_back(upstream[:HEAD_DIM], cosine, sine),
            )
            turned_own[head_rows(pair), :] = back.astype(BF16)
            turned_own[head_rows(pairs + pair), :] = upstream[HEAD_DIM:].astype(BF16)
            return total + terms

        onward(1)
        far(3)

        def arrive(step, nothing):
            back_copy(step).wait_recv()
            return nothing

        lax.fori_loop(1, HALF, arrive, 0)

        def extra_arrive(group, nothing):
            extra_copy(group).wait_recv()
            return nothing

        @pl.when(place == HALF - 1)
        def _():
            lax.fori_loop(0, HALF, extra_arrive, 0)

        @pl.when(place != HALF - 1)
        def _():
            extra_far[...] = jnp.zeros(extra_far.shape, BF16)

        for copy in loads:
            copy.wait()
        nothing = jnp.zeros((HEAD_DIM, BLOCK), F32)
        query_terms = lax.fori_loop(0, heads, query_head, nothing)
        key_terms = lax.fori_loop(0, pairs, key_head, nothing)
        turned_copy.start()
        for row in range(0, turned_own.shape[0], 128):
            natural[:, row : row + 128] = turned_own[row : row + 128, :].astype(F32).T.astype(BF16)
        deeper(2)
        normed_copy.wait_recv()
        turned_copy.wait_recv()

        def tail_one(index, carry):
            for chain in tails:
                chain.stage_one(1 - index // 4, lax.rem(index + 1, 4))
            return carry

        lax.fori_loop(0, 8, tail_one, 0)
        near(0)
        summed[...] = dot_dims(natural[...], weights_ref[...], 1, 1)
        middle_load.wait()

        def token_rows(index, total):
            rows = pl.ds(pl.multiple_of(index * 32, 32), 32)
            values, upstream = tokens_ref[rows, :].astype(F32), summed[rows, :]
            inverse = lax.rsqrt(jnp.mean(values * values, axis=-1, keepdims=True) + EPSILON)
            scaled = upstream * attn_gain_ref[...]
            weight = jnp.sum(scaled * values, axis=-1, keepdims=True) / values.shape[1]
            tokens_out[rows, :] += inverse * scaled - values * inverse**3 * weight
            return total + jnp.sum(upstream * values * inverse, axis=0, keepdims=True)

        terms = lax.fori_loop(
            0, BLOCK // 32, token_rows, jnp.zeros((1, tokens_ref.shape[1]), F32)
        )
        gain_own[...] = jnp.zeros(gain_own.shape, F32)
        gain_own[0:1, :] = terms
        gain_own[1:2, :] = ffn_terms_ref[...]
        gain_own[2:3, 0:HEAD_DIM] = jnp.sum(query_terms.T, axis=0, keepdims=True)
        gain_own[3:4, 0:HEAD_DIM] = jnp.sum(key_terms.T, axis=0, keepdims=True)

    width = normed_ref.shape[1]
    pl.run_scoped(
        finish_all,
        pltpu.VMEM((BLOCK, turned_own.shape[0]), BF16),
        pltpu.VMEM((BLOCK, width), F32),
        pltpu.VMEM((heads, HEAD_DIM, BLOCK), F32),
        pltpu.VMEM((pairs, HEAD_DIM, BLOCK), F32),
        pltpu.VMEM((BLOCK, width), BF16),
        pltpu.VMEM(weights_hbm.shape, BF16),
    )

    def tail_two(index, carry):
        for chain in tails:
            chain.stage_two(lax.rem(index + 1, 4))
        return carry

    def tail_three(depth, carry):
        for chain in tails:
            chain.stage_three(depth)
        return carry

    gain_swap = core_copy(gain_own, gain_came, 22)
    gain_swap.start()
    along.stage_two()

    def gain_copy(step):
        peer = (lax.rem(place + step, RING), core)
        return remote(
            gain_all.at[place], gain_all.at[place], gain_send.at[step], gain_recv.at[step], peer
        )

    def gain_start(step, carry):
        gain_copy(step).start()
        return carry

    def gain_arrive(step, carry):
        gain_copy(step).wait()
        return carry

    onward(3)
    deeper(1)
    far(0)
    gain_swap.wait()
    gain_all[place] = gain_own[...] + gain_came[...]
    lax.fori_loop(1, RING, gain_start, 0)
    lax.fori_loop(0, 4, tail_two, 0)
    along.stage_three()
    onward(0)
    deeper(3)
    lax.fori_loop(1, 4, tail_three, 0)
    pair_copy(0, 0, 0).wait_recv()
    along.close(deep_finish)
    for chain in chains:
        chain.close(finish)
    for chain in tails:
        chain.close(tail_finish)
    lax.fori_loop(1, RING, gain_arrive, 0)

    def gain_sum(index, total):
        return total + gain_all[index]

    gains_out[...] = lax.fori_loop(1, RING, gain_sum, gain_all[0])

    def settle(step, nothing):
        back_copy(step).wait_send()
        cot_copy(step).wait_send()
        return nothing

    lax.fori_loop(1, HALF, settle, 0)

    @pl.when(part == 1)
    def _():
        extra_copy(member).wait_send()

    for copy in sides + [normed_copy, turned_copy]:
        copy.wait_send()
    for turn_x, turn_y, depth in order:
        pair_copy(turn_x, turn_y, depth).wait_send()
    for chain in chains + tails + (along,):
        chain.drain()


def back_call(call_id, inputs, loads):
    pair, hidden, side, ffn_low = inputs[:4]
    rows, hidden_width = hidden.shape
    width = ffn_low.shape[1]
    wide, narrow = hidden_width // RING, width // RING
    total = (HEADS + 2 * KV_HEADS) * HEAD_DIM

    def buffers(sizes):
        return [
            pltpu.VMEM((slots, sizes[chain], 256), BF16)
            for chain in range(2)
            for slots in (8, 8, 4, 3)
        ]

    dma = pltpu.SemaphoreType.DMA
    specs = [VMEM_SPEC] * (len(inputs) + len(loads))
    staged = (0, 2, 3, 4, 5, 6, 8, 11)
    for index in (1, *staged, *range(len(inputs), len(specs))):
        specs[index] = HBM_SPEC
    return pl.pallas_call(
        back_kernel,
        out_shape=(
            jax.ShapeDtypeStruct((wide, width // 2), F32),
            jax.ShapeDtypeStruct((wide, width // 2), F32),
            jax.ShapeDtypeStruct((narrow, hidden_width // 2), F32),
            jax.ShapeDtypeStruct((narrow, width // 2), F32),
            jax.ShapeDtypeStruct((total // RING, width // 2), F32),
            jax.ShapeDtypeStruct((rows, width), F32),
            jax.ShapeDtypeStruct((4, width), F32),
        ),
        in_specs=specs,
        out_specs=(VMEM_SPEC,) * 7,
        scratch_shapes=[pltpu.VMEM(inputs[index].shape, BF16) for index in staged]
        + [
            pltpu.VMEM(pair.shape, BF16),
            pltpu.VMEM(side.shape, BF16),
            pltpu.VMEM((rows, hidden_width // 2), BF16),
            pltpu.VMEM((rows, hidden_width // 2), BF16),
            pltpu.VMEM((rows, width // 2), BF16),
            pltpu.VMEM((width // 2, rows), BF16),
            pltpu.VMEM((rows, width // 2), BF16),
            pltpu.VMEM((HALF, 2 * HEAD_DIM, rows), BF16),
            pltpu.VMEM((HALF, 4 * HEAD_DIM, rows), BF16),
            pltpu.VMEM((HALF, 4 * HEAD_DIM, rows), BF16),
            pltpu.VMEM((2 * HEAD_DIM, rows), BF16),
            pltpu.VMEM((HALF, 2 * HEAD_DIM, rows), BF16),
            pltpu.VMEM((total, rows), BF16),
            pltpu.VMEM((total, rows), BF16),
            pltpu.VMEM((4, width), F32),
            pltpu.VMEM((4, width), F32),
            pltpu.VMEM((RING, 4, width), F32),
        ]
        + buffers([2 * wide + (split[1] + 1) * narrow for split in DOWN_CHUNKS[:2]])
        + [pltpu.VMEM((*lead, DOWN_CHUNKS[2][1] * narrow, 256), BF16) for lead in ((3, 4), (3, 4), (2,), (1,))]
        + [dma((6,)), dma((6,))]
        + buffers((total // RING, total // RING))
        + [dma((2, 15))] * 4
        + [dma((HALF,))] * 4
        + [dma((23,))] * 2
        + [dma((RING,))] * 2
        + [dma((HALF,))] * 2
        + [dma((6,)), dma((8,))],
        compiler_params=pltpu.CompilerParams(
            collective_id=call_id, has_side_effects=True, vmem_limit_bytes=63 << 20
        ),
        name="backward_spread",
    )(*inputs, *loads)


def head_frequencies(rows):
    half = HEAD_DIM // 2
    frequencies = THETA ** (-(2.0 / HEAD_DIM) * np.arange(half, dtype=np.float32))
    return jnp.asarray(np.repeat(frequencies.astype(np.float32)[:, None], rows, axis=1))


def front_kernel(
    gain_ref,
    place_ref,
    query_gain_ref,
    key_gain_ref,
    frequency_ref,
    tokens_hbm,
    w_query_hbm,
    w_key_hbm,
    w_value_hbm,
    w_out_hbm,
    w_gate_hbm,
    w_up_hbm,
    w_down_hbm,
    qkv_out,
    starts_out,
    normed_out,
    part_out,
    mixed_out,
    inv_out,
    out_full,
    table_ref,
    query_hbm,
    key_hbm,
    weights_hbm,
    gate_far,
    up_far,
    down_far,
    home,
    key_nat,
    totals,
    accs,
    tokens_ref,
    query_out,
    key_out,
    weights_out,
    own_start_ref,
    keep_sem,
    own_sem,
    send_sem,
    recv_sem,
    start_send,
    start_recv,
    mixed_send,
    mixed_recv,
    kv_send,
    kv_recv,
    extra_send,
    extra_recv,
    core_send,
    core_recv,
):
    place, core = lax.axis_index("ctx"), lax.axis_index("fsdp")
    part, member = place // HALF, lax.rem(place, HALF)
    rows = tokens_ref.shape[0]
    depth = w_query_hbm.shape[0]
    partner = (place, 1 - core)
    tokens_load = pltpu.make_async_copy(tokens_hbm, tokens_ref, keep_sem.at[0])
    tokens_load.start()
    places = place * rows + lax.broadcasted_iota(jnp.int32, (1, rows), 1)
    own_start_ref[...] = places - place_ref[...]
    angles = frequency_ref[...] * place_ref[...].astype(F32)
    half = HEAD_DIM // 2
    table_ref[0:half, :] = jnp.cos(angles)
    table_ref[half:HEAD_DIM, :] = jnp.sin(angles)
    for index, source in enumerate((query_gain_ref, key_gain_ref)):
        table_ref[(index + 1) * HEAD_DIM : (index + 2) * HEAD_DIM, :] = jnp.broadcast_to(
            source[...], (rows, HEAD_DIM)
        ).T
    greet([partner] + [(lax.rem(place + step, RING), core) for step in range(1, RING)])

    def remote(source, target, send, recv, peer):
        return pltpu.make_async_remote_copy(
            src_ref=source,
            dst_ref=target,
            send_sem=send,
            recv_sem=recv,
            device_id=peer,
            device_id_type=MESH,
        )

    def mate(step):
        return (part * HALF + lax.rem(member + step, HALF), core)

    copies, near_copies = [], []

    def share(source, target, near_target=None):
        index = len(copies)
        copy = remote(source, target, core_send.at[index], core_recv.at[index], partner)
        copy.start()
        copies.append(copy)
        if near_target is not None:
            near = pltpu.make_async_copy(source, near_target, own_sem.at[index])
            near.start()
            near_copies.append(near)

    column = 0
    own_depth = pl.ds(pl.multiple_of(core * depth, 128), depth)
    for source in (w_key_hbm, w_value_hbm, w_query_hbm):
        window = pl.ds(column, source.shape[1])
        target = weights_out.at[own_depth, window]
        share(source, target, target)
        column += source.shape[1]

    target = out_full.at[own_depth, :]
    share(w_out_hbm, target, target)
    for source, target in ((w_gate_hbm, gate_far), (w_up_hbm, up_far), (w_down_hbm, down_far)):
        share(source, target)

    def start_copy(step):
        return remote(
            own_start_ref,
            starts_out.at[member],
            start_send.at[step],
            start_recv.at[step],
            mate(step),
        )

    for step in range(1, HALF):
        start_copy(step).start()
    starts_out[member] = own_start_ref[...]

    def norm_rows(index, nothing):
        window = pl.ds(pl.multiple_of(index * 32, 32), 32)
        values = tokens_ref[window, :].astype(F32)
        inverse = lax.rsqrt(jnp.mean(values * values, axis=-1, keepdims=True) + EPSILON)
        normed_out[window, :] = (values * inverse * gain_ref[...]).astype(BF16)
        return nothing

    tokens_load.wait()
    lax.fori_loop(0, rows // 32, norm_rows, 0)
    cosine, sine = table_ref[0:half, :], table_ref[half:HEAD_DIM, :]
    query_gain = table_ref[HEAD_DIM : 2 * HEAD_DIM, :]
    key_gain = table_ref[2 * HEAD_DIM : 3 * HEAD_DIM, :]

    def project(column, count):
        window = pl.ds(column, count)
        product = jnp.dot(normed_out[...], weights_out[:, window], preferred_element_type=F32)
        return product.T

    def turned(values, gain):
        mean = jnp.mean(values * values, axis=0, keepdims=True)
        values = values * lax.rsqrt(mean + EPSILON) * gain
        first, second = values[:half], values[half:]
        return jnp.concatenate(
            [first * cosine - second * sine, second * cosine + first * sine], axis=0
        ).astype(BF16)

    kv_width = KV_HEADS * HEAD_DIM
    copies[0].wait_recv()
    near_copies[0].wait()

    def key_chunk(index, nothing):
        products = project(pl.multiple_of(index * 256, 256), 256)
        for offset in range(4):
            raw = products[offset * HEAD_DIM : (offset + 1) * HEAD_DIM]
            group = index * 4 + offset
            key_out[group] = raw
            home[group, 2 * HEAD_DIM : 3 * HEAD_DIM, :] = turned(raw, key_gain)
        return nothing

    lax.fori_loop(0, KV_HEADS // 4, key_chunk, 0)
    copies[1].wait_recv()
    near_copies[1].wait()

    def value_chunk(index, nothing):
        products = project(pl.multiple_of(kv_width + index * 256, 256), 256)
        for offset in range(4):
            value = products[offset * HEAD_DIM : (offset + 1) * HEAD_DIM].astype(BF16)
            home[index * 4 + offset, 3 * HEAD_DIM : 4 * HEAD_DIM, :] = value
        return nothing

    lax.fori_loop(0, KV_HEADS // 4, value_chunk, 0)

    window = pl.ds(2 * HEAD_DIM, 2 * HEAD_DIM)

    def kv_copy(step):
        return remote(
            home.at[lax.rem(member + step, HALF), window],
            qkv_out.at[1 + member, window],
            kv_send.at[step],
            kv_recv.at[step],
            mate(step),
        )

    def kv_start(step, nothing):
        kv_copy(HALF - step).start()
        return nothing

    def extra_copy(group):
        return remote(
            home.at[group, window, pl.ds(rows - EDGE, EDGE)],
            qkv_out.at[0, window, pl.ds(rows - EDGE, EDGE)],
            extra_send.at[group],
            extra_recv.at[group],
            (HALF + group, core),
        )

    def extra_start(group, nothing):
        extra_copy(group).start()
        return nothing

    @pl.when(place == HALF - 1)
    def _():
        lax.fori_loop(0, HALF, extra_start, 0)

    lax.fori_loop(1, HALF, kv_start, 0)
    copies[2].wait_recv()
    near_copies[2].wait()

    def block_copy(step):
        peer = mate(step)
        return remote(
            home.at[lax.rem(member + step, HALF), pl.ds(0, 2 * HEAD_DIM)],
            qkv_out.at[1 + member, pl.ds(0, 2 * HEAD_DIM)],
            send_sem.at[step],
            recv_sem.at[step],
            peer,
        )

    def query_chunk(turn, nothing):
        index = lax.rem(member // 2 - turn + 4, 4)
        products = project(pl.multiple_of(2 * kv_width + index * 256, 256), 256)
        for offset in range(4):
            raw = products[offset * HEAD_DIM : (offset + 1) * HEAD_DIM]
            query_out[index * 4 + offset] = raw
            low = (offset % 2) * HEAD_DIM
            home[index * 2 + offset // 2, low : low + HEAD_DIM, :] = turned(
                raw, query_gain
            )
        for offset in range(2):
            group = index * 2 + offset

            @pl.when(group != member)
            def _():
                block_copy(lax.rem(group - member + HALF, HALF)).start()

        return nothing

    lax.fori_loop(0, HEADS // 4, query_chunk, 0)
    keeps = [
        pltpu.make_async_copy(source, target, keep_sem.at[1 + index])
        for index, (source, target) in enumerate(
            ((query_out, query_hbm), (key_out, key_hbm), (weights_out, weights_hbm))
        )
    ]
    for keep in keeps:
        keep.start()
    qkv_out[1 + member] = home[member]
    base = part * HALF - 1

    def mixed_copy(step):
        peer = mate(step)
        return remote(
            part_out.at[lax.rem(member + step, HALF)],
            mixed_out.at[member],
            mixed_send.at[step],
            mixed_recv.at[step],
            peer,
        )

    def query_of(i):
        query_t = jnp.concatenate(
            [qkv_out[i, 0:HEAD_DIM, :], qkv_out[i, HEAD_DIM : 2 * HEAD_DIM, :]], axis=1
        ) * jnp.asarray(HEAD_DIM**-0.5, BF16)
        return query_t, jnp.concatenate([starts_out[i - 1]] * 2, axis=1)

    def meet(query_t, keys, values, ok, carry):
        total, acc = carry
        probs = jnp.exp(jnp.dot(keys, query_t, preferred_element_type=F32))
        probs = jnp.where(ok(lax.broadcasted_iota(jnp.int32, probs.shape, 0)), probs, 0.0)
        total = total + jnp.sum(probs, axis=0, keepdims=True)
        return total, acc + jnp.dot(values, probs.astype(BF16), preferred_element_type=F32)

    def inner(i):
        @pl.when(i - 1 != member)
        def _():
            step = lax.rem(member - i + 1 + HALF, HALF)
            start_copy(step).wait_recv()
            kv_copy(step).wait_recv()
            block_copy(step).wait_recv()

        key_nat[i] = transposed(qkv_out[i, 2 * HEAD_DIM : 3 * HEAD_DIM, :])
        query_t, start = query_of(i)
        places = (base + i) * BLOCK + lax.broadcasted_iota(jnp.int32, (1, BLOCK), 1)
        query_place = jnp.concatenate([places] * 2, axis=1)

        def step(diagonal, j, carry):
            def ok(offset):
                key_place = (base + j) * BLOCK + offset
                if diagonal:
                    return (key_place >= start) & (key_place <= query_place)
                return key_place >= start

            values = qkv_out[j, 3 * HEAD_DIM : 4 * HEAD_DIM, :]
            return meet(query_t, key_nat[j], values, ok, carry)

        carry = (jnp.zeros((1, 2 * BLOCK), F32), jnp.zeros((HEAD_DIM, 2 * BLOCK), F32))
        pairs = (i - 1) // 2

        def two(index, carry):
            return step(False, 2 * index + 2, step(False, 2 * index + 1, carry))

        carry = lax.fori_loop(0, pairs, two, carry)
        carry = lax.fori_loop(2 * pairs + 1, i, functools.partial(step, False), carry)
        totals[i - 1], accs[i - 1] = step(True, i, carry)

    def outer(i):
        @pl.when((part == 1) & (i == 1))
        def _():
            extra_copy(member).wait_recv()
            qkv_out[0, 2 * HEAD_DIM :, 0 : rows - EDGE] = jnp.zeros(
                (2 * HEAD_DIM, rows - EDGE), BF16
            )
            key_nat[0] = transposed(qkv_out[0, 2 * HEAD_DIM : 3 * HEAD_DIM, :])

        @pl.when(part == 1)
        def _():
            query_t, start = query_of(i)

            def ok(offset):
                return HALF * BLOCK - EDGE + offset >= start

            values = qkv_out[0, 3 * HEAD_DIM : 4 * HEAD_DIM, rows - EDGE :]
            totals[i - 1], accs[i - 1] = meet(
                query_t, key_nat[0, rows - EDGE :, :], values, ok, (totals[i - 1], accs[i - 1])
            )

        inverse = 1.0 / totals[i - 1]
        low = (accs[i - 1] * inverse).astype(BF16)
        part_out[i - 1, 0:HEAD_DIM, :] = low[:, :BLOCK]
        part_out[i - 1, HEAD_DIM:, :] = low[:, BLOCK:]
        inv_out[i - 1] = inverse

        @pl.when(i - 1 != member)
        def _():
            mixed_copy(lax.rem(i - 1 - member + HALF, HALF)).start()

    def per_query(i, nothing):
        @pl.when(i <= HALF)
        def _():
            inner(i)

        @pl.when(i > lag)
        def _():
            outer(i - lag)

        return nothing

    lag = 3
    lax.fori_loop(1, HALF + lag + 1, per_query, 0)
    mixed_out[member] = part_out[member]

    def settle(step, nothing):
        block_copy(step).wait_send()
        kv_copy(step).wait_send()
        start_copy(step).wait_send()
        mixed_copy(step).wait()
        return nothing

    lax.fori_loop(1, HALF, settle, 0)

    def extra_settle(group, nothing):
        extra_copy(group).wait_send()
        return nothing

    @pl.when(place == HALF - 1)
    def _():
        lax.fori_loop(0, HALF, extra_settle, 0)

    for copy in copies[:3]:
        copy.wait_send()
    for copy in copies[3:]:
        copy.wait()
    for near in near_copies[3:] + keeps:
        near.wait()


def front_call(call_id, inputs, loads):
    rows, width = loads[0].shape
    half_depth, hidden_width = loads[5].shape
    total = (HEADS + 2 * KV_HEADS) * HEAD_DIM
    dma = pltpu.SemaphoreType.DMA
    query_raw = (HEADS, HEAD_DIM, rows)
    key_raw = (KV_HEADS, HEAD_DIM, rows)
    return pl.pallas_call(
        front_kernel,
        out_shape=(
            jax.ShapeDtypeStruct((HALF + 1, 4 * HEAD_DIM, rows), BF16),
            jax.ShapeDtypeStruct((HALF, 1, rows), jnp.int32),
            jax.ShapeDtypeStruct((rows, width), BF16),
            jax.ShapeDtypeStruct((HALF, 2 * HEAD_DIM, rows), BF16),
            jax.ShapeDtypeStruct((HALF, 2 * HEAD_DIM, rows), BF16),
            jax.ShapeDtypeStruct((HALF, 1, 2 * rows), F32),
            jax.ShapeDtypeStruct((width, width), BF16),
            jax.ShapeDtypeStruct((3 * HEAD_DIM, rows), F32),
            jax.ShapeDtypeStruct(query_raw, F32),
            jax.ShapeDtypeStruct(key_raw, F32),
            jax.ShapeDtypeStruct((width, total), BF16),
            jax.ShapeDtypeStruct((half_depth, hidden_width), BF16),
            jax.ShapeDtypeStruct((half_depth, hidden_width), BF16),
            jax.ShapeDtypeStruct((hidden_width // 2, width), BF16),
        ),
        in_specs=[VMEM_SPEC] * len(inputs) + [HBM_SPEC] * len(loads),
        out_specs=(VMEM_SPEC,) * 8 + (HBM_SPEC,) * 6,
        scratch_shapes=[
            pltpu.VMEM((HALF, 4 * HEAD_DIM, rows), BF16),
            pltpu.VMEM((HALF + 1, rows, HEAD_DIM), BF16),
            pltpu.VMEM((HALF, 1, 2 * rows), F32),
            pltpu.VMEM((HALF, HEAD_DIM, 2 * rows), F32),
            pltpu.VMEM((rows, width), BF16),
            pltpu.VMEM(query_raw, F32),
            pltpu.VMEM(key_raw, F32),
            pltpu.VMEM((width, total), BF16),
            pltpu.VMEM((1, rows), jnp.int32),
            dma((4,)),
            dma((4,)),
        ]
        + [dma((HALF,))] * 10
        + [dma((7,))] * 2,
        compiler_params=pltpu.CompilerParams(
            collective_id=call_id, has_side_effects=True, vmem_limit_bytes=63 << 20
        ),
        name="front_heads",
    )(*inputs, *loads)


def ffn_kernel(
    core_ref,
    tokens_ref,
    mixed_ref,
    w_out_ref,
    gain_ref,
    cot_ref,
    gate_own,
    gate_far,
    up_own,
    up_far,
    down_own,
    down_far,
    pair_out,
    hidden_out,
    output_out,
    ffn_out,
    side_out,
    mixed_back_out,
    grad_middle_out,
    terms_out,
    middle,
    result,
    upstream,
    middle_low,
):
    step = pl.program_id(0)
    rows, width = tokens_ref.shape
    strip = 32

    def strips(work):
        def one(index, carry):
            return work(pl.ds(pl.multiple_of(index * strip, strip), strip), carry)

        return one

    @pl.when(step == 0)
    def _():
        mixed = mixed_ref[...].astype(F32).T.astype(BF16)
        middle[...] = tokens_ref[...].astype(F32) + jnp.dot(
            mixed, w_out_ref[...], preferred_element_type=F32
        )

        def norm(window, carry):
            values = middle[window, :]
            inverse = lax.rsqrt(jnp.mean(values * values, axis=-1, keepdims=True) + EPSILON)
            ffn_out[window, :] = (values * inverse * gain_ref[...]).astype(BF16)
            result[window, :] = values
            return carry

        lax.fori_loop(0, rows // strip, strips(norm), 0)
        upstream[...] = jnp.zeros(upstream.shape, F32)
        side_out[0] = cot_ref[...].astype(F32).T.astype(BF16)

    depth = gate_own.shape[0]
    own = pl.ds(pl.multiple_of(core_ref[0] * depth, 128), depth)
    far = pl.ds(pl.multiple_of((1 - core_ref[0]) * depth, 128), depth)

    def strip_of_hidden(down_ref):
        def ahead(near_ref, far_ref):
            return jnp.dot(ffn_out[:, own], near_ref[...], preferred_element_type=F32) + jnp.dot(
                ffn_out[:, far], far_ref[...], preferred_element_type=F32
            )

        gate_pre, up_pre = ahead(gate_own, gate_far), ahead(up_own, up_far)
        grad_hidden = dot_dims(cot_ref[...], down_ref[...], 1, 1)
        gate_sig = jax.nn.sigmoid(gate_pre)
        gate_act = gate_pre * gate_sig
        hidden_out[...] = (gate_act * up_pre).astype(BF16)
        gate_back = (
            grad_hidden * up_pre * (gate_sig * (1.0 + gate_pre * (1.0 - gate_sig)))
        ).astype(BF16)
        up_back = (grad_hidden * gate_act).astype(BF16)
        result[...] += jnp.dot(hidden_out[...], down_ref[...], preferred_element_type=F32)
        for window, gate_ref, up_ref in ((own, gate_own, up_own), (far, gate_far, up_far)):
            upstream[:, window] += dot_dims(gate_back, gate_ref[...], 1, 1) + dot_dims(
                up_back, up_ref[...], 1, 1
            )
        wide = pair_out.shape[1] // 2
        for base, back in ((0, gate_back), (wide, up_back)):
            turned = back.astype(F32).T.astype(BF16)
            for owner in range(pair_out.shape[0]):
                pair_out[owner, base : base + wide, :] = turned[owner * wide : (owner + 1) * wide]

    @pl.when(step < 2)
    def _():
        strip_of_hidden(down_own)

    @pl.when(step >= 2)
    def _():
        strip_of_hidden(down_far)

    @pl.when(step == pl.num_programs(0) - 1)
    def _():
        output_out[...] = result[...].astype(BF16)

        def back(window, total):
            values, grads = middle[window, :], upstream[window, :]
            inverse = lax.rsqrt(jnp.mean(values * values, axis=-1, keepdims=True) + EPSILON)
            scaled = grads * gain_ref[...]
            weight = jnp.sum(scaled * values, axis=-1, keepdims=True) / width
            grad_middle = cot_ref[window, :].astype(F32) + (
                inverse * scaled - values * inverse**3 * weight
            )
            grad_middle_out[window, :] = grad_middle
            middle_low[window, :] = grad_middle.astype(BF16)
            return total + jnp.sum(grads * values * inverse, axis=0, keepdims=True)

        terms_out[...] = lax.fori_loop(
            0, rows // strip, strips(back), jnp.zeros((1, width), F32)
        )
        mixed_back_out[...] = dot_dims(w_out_ref[...], middle_low[...], 1, 1).astype(BF16)
        side_out[1] = middle_low[...].astype(F32).T.astype(BF16)


def ffn_call(core, tokens, mixed_t, w_out, gain, cot, gate, up, down):
    rows, width = tokens.shape
    half_depth, hidden_width = gate[0].shape
    steps = 4
    chunk = hidden_width // steps
    owners = RING // steps
    wide = hidden_width // RING

    def whole(*shape):
        return pl.BlockSpec(shape, lambda i, core_ref: (0,) * len(shape))

    def turn(i, core_ref):
        return lax.rem(i + 2 * core_ref[0], steps)

    columns = pl.BlockSpec((half_depth, chunk), lambda i, core_ref: (0, turn(i, core_ref)))
    return pl.pallas_call(
        ffn_kernel,
        grid_spec=pltpu.PrefetchScalarGridSpec(
            num_scalar_prefetch=1,
            grid=(steps,),
            in_specs=[
                whole(rows, width),
                whole(width, rows),
                whole(width, width),
                whole(1, width),
                whole(rows, width),
                columns,
                columns,
                columns,
                columns,
                pl.BlockSpec((chunk, width), lambda i, core_ref: (jnp.minimum(i, 1), 0)),
                pl.BlockSpec((chunk, width), lambda i, core_ref: (jnp.maximum(i - 2, 0), 0)),
            ],
            out_specs=(
                pl.BlockSpec(
                    (owners, 2 * wide, rows), lambda i, core_ref: (turn(i, core_ref), 0, 0)
                ),
                pl.BlockSpec((rows, chunk), lambda i, core_ref: (0, turn(i, core_ref))),
                whole(rows, width),
                whole(rows, width),
                whole(2, width, rows),
                whole(width, rows),
                whole(rows, width),
                whole(1, width),
            ),
            scratch_shapes=[pltpu.VMEM((rows, width), F32)] * 3
            + [pltpu.VMEM((rows, width), BF16)],
        ),
        out_shape=(
            jax.ShapeDtypeStruct((RING, 2 * wide, rows), BF16),
            jax.ShapeDtypeStruct((rows, hidden_width), BF16),
            jax.ShapeDtypeStruct((rows, width), BF16),
            jax.ShapeDtypeStruct((rows, width), BF16),
            jax.ShapeDtypeStruct((2, width, rows), BF16),
            jax.ShapeDtypeStruct((width, rows), BF16),
            jax.ShapeDtypeStruct((rows, width), F32),
            jax.ShapeDtypeStruct((1, width), F32),
        ),
        compiler_params=pltpu.CompilerParams(vmem_limit_bytes=63 << 20),
        name="ffn_both_ways",
    )(core, tokens, mixed_t, w_out, gain, cot, *gate, *up, *down)


def settle_kernel(*refs):
    count = 6
    sources, gains, rest = refs[:count], refs[count], refs[count + 1 :]
    targets, gain_targets, rest = rest[: count + 2], rest[count + 2 : count + 6], rest[count + 6 :]
    held, in_sem, out_sem = rest[:count], rest[count], rest[count + 1]
    loads = [
        pltpu.make_async_copy(source, hold, in_sem.at[index])
        for index, (source, hold) in enumerate(zip(sources, held))
    ]
    for load in loads:
        load.start()
    stores, row = [], 0
    for index, load in enumerate(loads):
        load.wait()
        if index < count - 1:
            pieces = [(held[index], targets[index])]
        else:
            pieces = []
            for target in targets[index:]:
                pieces.append((held[index].at[pl.ds(row, target.shape[0])], target))
                row += target.shape[0]
        for piece, target in pieces:
            store = pltpu.make_async_copy(piece, target, out_sem.at[len(stores)])
            store.start()
            stores.append(store)
    for index, target in enumerate(gain_targets):
        target[...] = gains[index : index + 1, 0 : target.shape[1]]
    for store in stores:
        store.wait()


def settle_call(tokens, gate_t, up_t, down_t, out_t, qkv_t, gains):
    sources = (tokens, gate_t, up_t, down_t, out_t, qkv_t)
    lanes = qkv_t.shape[1]
    query = HEADS * HEAD_DIM // RING
    pair = KV_HEADS * HEAD_DIM // RING
    shapes = [source.shape for source in sources[:-1]]
    shapes += [(query, lanes), (pair, lanes), (pair, lanes)]
    gain_shapes = [(1, gains.shape[1])] * 2 + [(1, HEAD_DIM)] * 2
    return pl.pallas_call(
        settle_kernel,
        out_shape=tuple(jax.ShapeDtypeStruct(shape, F32) for shape in shapes + gain_shapes),
        in_specs=[HBM_SPEC] * len(sources) + [VMEM_SPEC],
        out_specs=(HBM_SPEC,) * len(shapes) + (VMEM_SPEC,) * 4,
        scratch_shapes=[pltpu.VMEM(source.shape, F32) for source in sources]
        + [pltpu.SemaphoreType.DMA((6,)), pltpu.SemaphoreType.DMA((8,))],
        compiler_params=pltpu.CompilerParams(vmem_limit_bytes=63 << 20),
        name="settle_results",
    )(*sources, gains)


def heads_body(
    tokens,
    seg_ids,
    doc_pos,
    attn_gain,
    w_query,
    w_key,
    w_value,
    query_gain,
    key_gain,
    w_out,
    ffn_gain,
    w_gate,
    w_up,
    w_down,
    d_output,
):
    rows = tokens.shape[1]
    (
        qkv,
        starts,
        normed_low,
        mixed_far,
        mixed_home,
        inverse_total,
        o_full,
        table,
        query_raw,
        key_raw,
        kvq_full,
        gate_far,
        up_far,
        down_far,
    ) = front_call(
        1,
        (
            attn_gain[None, :],
            doc_pos,
            query_gain[None, :],
            key_gain[None, :],
            head_frequencies(rows),
        ),
        (tokens[0], w_query, w_key, w_value, w_out, w_gate, w_up, w_down),
    )
    mixed_t = mixed_home.reshape(HEADS * HEAD_DIM, rows)
    cot_low = d_output[0]
    (
        pair,
        hidden_low,
        output,
        ffn_low,
        side,
        grad_mixed,
        grad_middle,
        ffn_terms,
    ) = ffn_call(
        lax.axis_index("fsdp").astype(jnp.int32)[None],
        tokens[0],
        mixed_t,
        o_full,
        ffn_gain[None, :],
        cot_low,
        (w_gate, gate_far),
        (w_up, up_far),
        (w_down, down_far),
    )
    gate_t, up_t, down_t, out_t, qkv_grads, d_tokens, gain_totals = back_call(
        3,
        (
            pair,
            hidden_low,
            side,
            ffn_low,
            mixed_t,
            grad_mixed.reshape(HALF, 2 * HEAD_DIM, rows),
            qkv,
            starts,
            mixed_far,
            inverse_total,
            table,
            normed_low,
            attn_gain[None, :],
            ffn_terms,
        ),
        (tokens[0], query_raw, key_raw, kvq_full, grad_middle),
    )
    d_tokens, gate, up, down, out, query, key, value, attn, ffn, query_gains, key_gains = (
        settle_call(d_tokens, gate_t, up_t, down_t, out_t, qkv_grads, gain_totals)
    )
    return (
        output[None],
        d_tokens[None],
        attn[0],
        query.T,
        key.T,
        value.T,
        query_gains[0],
        key_gains[0],
        out.T,
        ffn[0],
        gate.T,
        up.T,
        down.T,
    )


def solution(mesh):
    in_specs = (
        P("fsdp", "ctx", None),
        P("fsdp", "ctx"),
        P("fsdp", "ctx"),
        P(),
        P("fsdp", None),
        P("fsdp", None),
        P("fsdp", None),
        P(),
        P(),
        P("fsdp", None),
        P(),
        P("fsdp", None),
        P("fsdp", None),
        P("fsdp", None),
        P("fsdp", "ctx", None),
    )
    out_specs = (
        P("fsdp", "ctx", None),
        P("fsdp", "ctx", None),
        P(),
        P("fsdp", "ctx"),
        P("fsdp", "ctx"),
        P("fsdp", "ctx"),
        P(),
        P(),
        P("fsdp", "ctx"),
        P(),
        P("fsdp", "ctx"),
        P("fsdp", "ctx"),
        P("fsdp", "ctx"),
    )
    chosen = heads_body if (mesh.shape["ctx"], mesh.shape["fsdp"]) == (HEADS, 2) else ring_body
    return jax.shard_map(chosen, mesh=mesh, in_specs=in_specs, out_specs=out_specs, check_vma=False)
```

```python
import functools

import jax
import jax.numpy as jnp
import numpy as np
from jax import lax
from jax.experimental import pallas as pl
from jax.experimental.pallas import tpu as pltpu
from jax.sharding import PartitionSpec as P

HEADS = 16
KV_HEADS = 8
HEAD_DIM = 64
HOPS = 8


EPSILON = 1e-05
THETA = 1000000.0
MASKED = -1e30


def from_behind(block, axis, distance):
    devices = range(lax.axis_size(axis))
    route = [(i - distance, i) for i in devices if i - distance in devices]
    return lax.ppermute(block, axis, route)


def rms_norm(values, norm_gain):
    return (
        values * lax.rsqrt(jnp.mean(values * values, axis=-1, keepdims=True) + EPSILON) * norm_gain
    )


def rms_back(values, norm_gain, upstream):
    inverse = lax.rsqrt(jnp.mean(values * values, axis=-1, keepdims=True) + EPSILON)
    scaled = upstream * norm_gain
    row_width = values.shape[-1]
    d_values = (
        inverse * scaled
        - values * inverse**3 * jnp.sum(scaled * values, axis=-1, keepdims=True) / row_width
    )
    return (d_values, upstream * values * inverse)


def rotary(values, positions, turn_sign):
    half_dim = values.shape[-1] // 2
    inverse_freq = THETA ** (-(2.0 / values.shape[-1]) * jnp.arange(half_dim, dtype=jnp.float32))
    angles = positions.astype(jnp.float32)[:, None] * inverse_freq[None, :]
    cosine = jnp.cos(angles)[:, None, :]
    sine_part = turn_sign * jnp.sin(angles)[:, None, :]
    first_half = values[..., :half_dim]
    second_half = values[..., half_dim:]
    return jnp.concatenate(
        [
            first_half * cosine - second_half * sine_part,
            second_half * cosine + first_half * sine_part,
        ],
        axis=-1,
    )


def outer_product(left_mat, right_mat):
    return lax.dot_general(
        left_mat, right_mat, (((0,), (0,)), ((), ())), preferred_element_type=jnp.float32
    )


def against(left_mat, right_mat):
    return lax.dot_general(
        left_mat, right_mat, (((1,), (1,)), ((), ())), preferred_element_type=jnp.float32
    )


def ring_body(
    tokens,
    seg_ids,
    doc_pos,
    attn_gain,
    w_query,
    w_key,
    w_value,
    query_gain,
    key_gain,
    w_out,
    ffn_gain,
    w_gate,
    w_up,
    w_down,
    d_output,
):
    cycle_place = lax.axis_index("ctx")
    tok_rows = tokens.shape[1]
    resid_in = tokens[0].astype(jnp.float32)
    seg_local = seg_ids[0]
    pos_local = doc_pos[0]
    q_per_kv = HEADS // KV_HEADS
    group_cols = q_per_kv * HEAD_DIM
    score_scale = HEAD_DIM ** (-0.5)
    q_full, k_full, v_full, o_full = (
        lax.all_gather(w_query, "fsdp", axis=0, tiled=True),
        lax.all_gather(w_key, "fsdp", axis=0, tiled=True),
        lax.all_gather(w_value, "fsdp", axis=0, tiled=True),
        lax.all_gather(w_out, "fsdp", axis=0, tiled=True),
    )
    gate_full, up_full, down_full = (
        lax.all_gather(w_gate, "fsdp", axis=0, tiled=True),
        lax.all_gather(w_up, "fsdp", axis=0, tiled=True),
        lax.all_gather(w_down, "fsdp", axis=0, tiled=True),
    )
    normed = rms_norm(resid_in, attn_gain)
    normed_low = normed.astype(jnp.bfloat16)
    query_raw = jnp.dot(normed_low, q_full, preferred_element_type=jnp.float32).reshape(
        tok_rows, HEADS, HEAD_DIM
    )
    key_raw = jnp.dot(normed_low, k_full, preferred_element_type=jnp.float32).reshape(
        tok_rows, KV_HEADS, HEAD_DIM
    )
    value_raw = jnp.dot(normed_low, v_full, preferred_element_type=jnp.float32)
    query_rot = rotary(rms_norm(query_raw, query_gain), pos_local, 1.0)
    key_rot = rotary(rms_norm(key_raw, key_gain), pos_local, 1.0)
    query_low = query_rot.astype(jnp.bfloat16).reshape(tok_rows, HEADS * HEAD_DIM)
    key_low = key_rot.astype(jnp.bfloat16).reshape(tok_rows, KV_HEADS * HEAD_DIM)
    value_low = value_raw.astype(jnp.bfloat16)
    own_kv = (key_low, value_low, seg_local)
    kv_blocks = [own_kv]
    carried = own_kv
    for hop_index in range(HOPS):
        carried = from_behind((carried[0], carried[1], carried[2]), "ctx", 1)
        kv_blocks.append(carried)
    key_all = jnp.concatenate([kv_entry[0] for kv_entry in kv_blocks], axis=0)
    value_all = jnp.concatenate([kv_entry[1] for kv_entry in kv_blocks], axis=0)
    seg_all = jnp.concatenate([kv_entry[2] for kv_entry in kv_blocks], axis=0)
    key_owner = cycle_place - jnp.arange(HOPS + 1, dtype=jnp.int32)
    owner_valid = jnp.repeat(key_owner >= 0, tok_rows)
    key_index = (
        key_owner[:, None] * tok_rows + jnp.arange(tok_rows, dtype=jnp.int32)[None, :]
    ).reshape(-1)
    query_index = cycle_place * tok_rows + jnp.arange(tok_rows, dtype=jnp.int32)
    allowed = (
        (seg_local[:, None] == seg_all[None, :])
        & (key_index[None, :] <= query_index[:, None])
        & owner_valid[None, :]
    )

    def group_scores(kv_group):
        query_part = lax.dynamic_slice_in_dim(query_low, kv_group * group_cols, group_cols, 1)
        query_part = query_part.reshape(tok_rows, q_per_kv, HEAD_DIM)
        key_part = lax.dynamic_slice_in_dim(key_all, kv_group * HEAD_DIM, HEAD_DIM, 1)
        value_part = lax.dynamic_slice_in_dim(value_all, kv_group * HEAD_DIM, HEAD_DIM, 1)
        scores = (
            jnp.einsum("trd,kd->rtk", query_part, key_part, preferred_element_type=jnp.float32)
            * score_scale
        )
        return (jnp.where(allowed[None], scores, MASKED), query_part, key_part, value_part)

    def forward_group(kv_group):
        scores, query_part, key_part, value_part = group_scores(kv_group)
        row_top = jnp.max(scores, axis=-1, keepdims=True)
        log_total = row_top + jnp.log(jnp.sum(jnp.exp(scores - row_top), axis=-1, keepdims=True))
        attn_probs = jnp.exp(scores - log_total)
        mixed_part = jnp.einsum(
            "rtk,kd->trd",
            attn_probs.astype(jnp.bfloat16),
            value_part,
            preferred_element_type=jnp.float32,
        )
        return (mixed_part.reshape(tok_rows, group_cols), log_total[..., 0])

    mixed_groups, total_groups = lax.map(forward_group, jnp.arange(KV_HEADS, dtype=jnp.int32))
    mixed = mixed_groups.transpose(1, 0, 2).reshape(tok_rows, HEADS * HEAD_DIM)
    mixed_low = mixed.astype(jnp.bfloat16)
    middle = resid_in + jnp.dot(mixed_low, o_full, preferred_element_type=jnp.float32)
    ffn_low = rms_norm(middle, ffn_gain).astype(jnp.bfloat16)
    gate_pre = jnp.dot(ffn_low, gate_full, preferred_element_type=jnp.float32)
    up_pre = jnp.dot(ffn_low, up_full, preferred_element_type=jnp.float32)
    gate_sig = jax.nn.sigmoid(gate_pre)
    gate_act = gate_pre * gate_sig
    hidden_low = (gate_act * up_pre).astype(jnp.bfloat16)
    result = middle + jnp.dot(hidden_low, down_full, preferred_element_type=jnp.float32)
    output = result.astype(jnp.bfloat16)[None]
    cot_low = d_output[0]
    cotangent = cot_low.astype(jnp.float32)
    grad_w_down = outer_product(hidden_low, cot_low)
    grad_hidden = against(cot_low, down_full)
    gate_back = (grad_hidden * up_pre * (gate_sig * (1.0 + gate_pre * (1.0 - gate_sig)))).astype(
        jnp.bfloat16
    )
    up_back = (grad_hidden * gate_act).astype(jnp.bfloat16)
    grad_w_gate = outer_product(ffn_low, gate_back)
    grad_w_up = outer_product(ffn_low, up_back)
    grad_ffn_in = against(gate_back, gate_full) + against(up_back, up_full)
    middle_part, ffn_terms = rms_back(middle, ffn_gain, grad_ffn_in)
    grad_middle = cotangent + middle_part
    middle_low = grad_middle.astype(jnp.bfloat16)
    grad_w_out = outer_product(mixed_low, middle_low)
    grad_mixed = against(middle_low, o_full).astype(jnp.bfloat16)

    def backward_group(kv_group):
        scores, query_part, key_part, value_part = group_scores(kv_group)
        attn_probs = jnp.exp(scores - total_groups[kv_group][..., None])
        mixed_grad_part = lax.dynamic_slice_in_dim(grad_mixed, kv_group * group_cols, group_cols, 1)
        mixed_grad_part = mixed_grad_part.reshape(tok_rows, q_per_kv, HEAD_DIM)
        grad_probs = jnp.einsum(
            "trd,kd->rtk", mixed_grad_part, value_part, preferred_element_type=jnp.float32
        )
        grad_value = jnp.einsum(
            "rtk,trd->kd",
            attn_probs.astype(jnp.bfloat16),
            mixed_grad_part,
            preferred_element_type=jnp.float32,
        )
        row_delta = jnp.sum(grad_probs * attn_probs, axis=-1, keepdims=True)
        grad_scores = (attn_probs * (grad_probs - row_delta)).astype(jnp.bfloat16)
        grad_query = (
            jnp.einsum("rtk,kd->trd", grad_scores, key_part, preferred_element_type=jnp.float32)
            * score_scale
        )
        grad_key = (
            jnp.einsum("rtk,trd->kd", grad_scores, query_part, preferred_element_type=jnp.float32)
            * score_scale
        )
        return (grad_query.reshape(tok_rows, group_cols), grad_key, grad_value)

    query_groups, key_groups, value_groups = lax.map(
        backward_group, jnp.arange(KV_HEADS, dtype=jnp.int32)
    )
    grad_query_rot = query_groups.transpose(1, 0, 2).reshape(tok_rows, HEADS, HEAD_DIM)
    key_blocks = key_groups.transpose(1, 0, 2).reshape(HOPS + 1, tok_rows, KV_HEADS * HEAD_DIM)
    value_blocks = value_groups.transpose(1, 0, 2).reshape(HOPS + 1, tok_rows, KV_HEADS * HEAD_DIM)
    home_key = key_blocks[HOPS]
    home_value = value_blocks[HOPS]
    for hop_index in range(HOPS, 0, -1):
        moved_key, moved_value = (
            from_behind(home_key.astype(jnp.bfloat16), "ctx", -1).astype(home_key.dtype),
            from_behind(home_value.astype(jnp.bfloat16), "ctx", -1).astype(home_value.dtype),
        )
        home_key = moved_key + key_blocks[hop_index - 1]
        home_value = moved_value + value_blocks[hop_index - 1]
    query_turned = rotary(grad_query_rot, pos_local, -1.0)
    key_turned = rotary(home_key.reshape(tok_rows, KV_HEADS, HEAD_DIM), pos_local, -1.0)
    query_back, query_terms = rms_back(query_raw, query_gain, query_turned)
    key_back, key_terms = rms_back(key_raw, key_gain, key_turned)
    query_back = query_back.reshape(tok_rows, HEADS * HEAD_DIM).astype(jnp.bfloat16)
    key_back = key_back.reshape(tok_rows, KV_HEADS * HEAD_DIM).astype(jnp.bfloat16)
    value_back = home_value.astype(jnp.bfloat16)
    grad_w_query = outer_product(normed_low, query_back)
    grad_w_key = outer_product(normed_low, key_back)
    grad_w_value = outer_product(normed_low, value_back)
    grad_normed = (
        against(query_back, q_full) + against(key_back, k_full) + against(value_back, v_full)
    )
    input_part, attn_terms = rms_back(resid_in, attn_gain, grad_normed)
    d_tokens = (grad_middle + input_part)[None]
    gain_totals = lax.psum(
        (
            jnp.sum(attn_terms, axis=0),
            jnp.sum(ffn_terms, axis=0),
            jnp.sum(query_terms, axis=(0, 1)),
            jnp.sum(key_terms, axis=(0, 1)),
        ),
        ("ctx", "fsdp"),
    )
    weight_grads = (
        grad_w_query,
        grad_w_key,
        grad_w_value,
        grad_w_out,
        grad_w_gate,
        grad_w_up,
        grad_w_down,
    )
    spread = (
        lax.psum_scatter(
            weight_grads[0].astype(jnp.bfloat16), "fsdp", scatter_dimension=0, tiled=True
        ).astype(jnp.float32),
        lax.psum_scatter(
            weight_grads[1].astype(jnp.bfloat16), "fsdp", scatter_dimension=0, tiled=True
        ).astype(jnp.float32),
        lax.psum_scatter(
            weight_grads[2].astype(jnp.bfloat16), "fsdp", scatter_dimension=0, tiled=True
        ).astype(jnp.float32),
        lax.psum_scatter(
            weight_grads[3].astype(jnp.bfloat16), "fsdp", scatter_dimension=0, tiled=True
        ).astype(jnp.float32),
        lax.psum_scatter(
            weight_grads[4].astype(jnp.bfloat16), "fsdp", scatter_dimension=0, tiled=True
        ).astype(jnp.float32),
        lax.psum_scatter(
            weight_grads[5].astype(jnp.bfloat16), "fsdp", scatter_dimension=0, tiled=True
        ).astype(jnp.float32),
        lax.psum_scatter(
            weight_grads[6].astype(jnp.bfloat16), "fsdp", scatter_dimension=0, tiled=True
        ).astype(jnp.float32),
    )
    shares = (
        lax.psum_scatter(spread[0], "ctx", scatter_dimension=1, tiled=True),
        lax.psum_scatter(spread[1], "ctx", scatter_dimension=1, tiled=True),
        lax.psum_scatter(spread[2], "ctx", scatter_dimension=1, tiled=True),
        lax.psum_scatter(spread[3], "ctx", scatter_dimension=1, tiled=True),
        lax.psum_scatter(spread[4], "ctx", scatter_dimension=1, tiled=True),
        lax.psum_scatter(spread[5], "ctx", scatter_dimension=1, tiled=True),
        lax.psum_scatter(spread[6], "ctx", scatter_dimension=1, tiled=True),
    )
    return (
        output,
        d_tokens,
        gain_totals[0],
        shares[0],
        shares[1],
        shares[2],
        gain_totals[2],
        gain_totals[3],
        shares[3],
        gain_totals[1],
        shares[4],
        shares[5],
        shares[6],
    )


MESH = pl.DeviceIdType.MESH
BLOCK = 256
RING = 16
HALF = 8
EDGE = 128
DOWN_CHUNKS = ((0, 3), (3, 3), (6, 3))
EARLY = (2,)
VMEM_SPEC = pl.BlockSpec(memory_space=pltpu.VMEM)
HBM_SPEC = pl.BlockSpec(memory_space=pltpu.HBM)
SMEM_SPEC = pl.BlockSpec(memory_space=pltpu.SMEM)
F32 = jnp.float32
BF16 = jnp.bfloat16


def dot_dims(left_mat, right_mat, left_dim, right_dim):
    return lax.dot_general(
        left_mat, right_mat, (((left_dim,), (right_dim,)), ((), ())), preferred_element_type=F32
    )


def transposed(block):
    return block.astype(F32).T.astype(BF16)


def flip(bit, turned):
    return bit + turned - 2 * bit * turned


def block_owner(chain, place, other, slot):
    x, y, z = lax.rem(place, 2), lax.rem(place // 2, 2), place // 4
    turned, depth = slot // 4, lax.rem(lax.rem(slot, 4) + z, 4)
    first, second = flip((x, y)[chain], other), flip((y, x)[chain], turned)
    return depth * 4 + (second * 2 + first if chain == 0 else first * 2 + second)


class Spread:
    def __init__(self, chain, compute, base, sent, came, hold, skip, send_sems, recv_sems):
        place, self.core = lax.axis_index("ctx"), lax.axis_index("fsdp")
        x, y, self.z = lax.rem(place, 2), lax.rem(place // 2, 2), place // 4
        self.chain, self.base = chain, base
        self.first, self.second = (x, y) if chain == 0 else (y, x)
        self.compute, self.sent, self.came = compute, sent, came
        self.hold, self.skip = hold, skip
        self.send_sems, self.recv_sems = send_sems, recv_sems

    def at(self, first, second, depth):
        low = second * 2 + first if self.chain == 0 else first * 2 + second
        return depth * 4 + low

    def deep(self, depth):
        return lax.rem(self.z + depth, 4)

    def owner(self, slot):
        return self.at(self.first, flip(self.second, slot // 4), self.deep(lax.rem(slot, 4)))

    def copy(self, stage, slot):
        if stage == 0:
            peer = self.at(1 - self.first, self.second, self.z)
            source, target, sem = self.sent.at[slot], self.came[0].at[slot], slot
        elif stage == 1:
            peer = self.at(self.first, 1 - self.second, self.z)
            source, target, sem = self.hold.at[4 + slot - self.skip], self.came[1].at[slot], 8 + slot
        else:
            peer = self.at(self.first, self.second, self.deep(slot))
            source, target, sem = self.hold.at[slot - self.skip], self.came[2].at[slot - 1], 11 + slot
        return pltpu.make_async_remote_copy(
            src_ref=source,
            dst_ref=target,
            send_sem=self.send_sems.at[self.chain, sem],
            recv_sem=self.recv_sems.at[self.chain, sem],
            device_id=(peer, self.core),
            device_id_type=MESH,
        )

    def stage_one(self, turned, depth):
        slot = turned * 4 + depth
        owner = self.at(1 - self.first, flip(self.second, turned), self.deep(depth))
        for row, value in self.compute(self.chain, owner, None):
            row -= self.base
            self.sent[slot, row : row + value.shape[0], :] = value.astype(BF16)
        self.copy(0, slot).start()

    def sums(self, slot):
        for row, value in self.compute(self.chain, self.owner(slot), slot):
            if row >= self.base:
                low = row - self.base
                value = value + self.came[0][slot, low : low + value.shape[0], :].astype(F32)
            yield slice(row, row + value.shape[0]), value

    def stage_two(self, depth):
        self.copy(0, 4 + depth).wait_recv()
        for window, value in self.sums(4 + depth):
            self.hold[4 + depth - self.skip, window, :] = value.astype(BF16)
        self.copy(1, depth).start()

    def stage_three(self, depth):
        self.copy(0, depth).wait_recv()
        self.copy(1, depth).wait_recv()
        for window, value in self.sums(depth):
            value = value + self.came[1][depth, window, :].astype(F32)
            self.hold[depth - self.skip, window, :] = value.astype(BF16)
        self.copy(2, depth).start()

    def close(self, finish):
        self.copy(0, 0).wait_recv()
        self.copy(1, 0).wait_recv()
        for depth in range(1, 4):
            self.copy(2, depth).wait_recv()
        for window, value in self.sums(0):
            value = value + self.came[1][0, window, :].astype(F32)
            for depth in range(3):
                value = value + self.came[2][depth, window, :].astype(F32)
            finish(self.chain, window.start, value)

    def drain(self):
        for slot in range(8):
            self.copy(0, slot).wait_send()
        for depth in range(4):
            self.copy(1, depth).wait_send()
        for depth in range(1, 4):
            self.copy(2, depth).wait_send()


class DeepSpread:
    def __init__(self, compute, sent, came, send_sems, recv_sems):
        self.place, self.core = lax.axis_index("ctx"), lax.axis_index("fsdp")
        self.x, self.y = lax.rem(self.place, 2), lax.rem(self.place // 2, 2)
        self.compute, self.sent, self.came = compute, sent, came
        self.send_sems, self.recv_sems = send_sems, recv_sems

    def copy(self, stage, slot):
        if stage == 0:
            peer = lax.rem(self.place + 4 * slot, RING)
            source, target, sem = self.sent.at[slot - 1], self.came[0].at[slot - 1], slot - 1
        elif stage == 1:
            peer = self.place + 1 - 2 * self.x
            local = flip(self.y, slot) * 2 + 1 - self.x
            source, target, sem = self.came[0].at[0, local], self.came[1].at[slot], 3 + slot
        else:
            peer = self.place + 2 - 4 * self.y
            local = (1 - self.y) * 2 + self.x
            source, target, sem = self.came[0].at[0, local], self.came[2].at[0], 5
        return pltpu.make_async_remote_copy(
            src_ref=source,
            dst_ref=target,
            send_sem=self.send_sems.at[sem],
            recv_sem=self.recv_sems.at[sem],
            device_id=(peer, self.core),
            device_id_type=MESH,
        )

    def stage_one(self, slot):
        first = lax.rem(self.place // 4 + slot, 4) * 4
        value = self.compute(first, 4)
        rows = value.shape[0] // 4
        for local in range(4):
            for chunk in range(value.shape[1] // 256):
                self.sent[slot - 1, local, chunk * rows : (chunk + 1) * rows, :] = value[
                    local * rows : (local + 1) * rows, chunk * 256 : (chunk + 1) * 256
                ].astype(BF16)
        self.copy(0, slot).start()

    def arrived(self, local):
        value = self.compute(self.place - lax.rem(self.place, 4) + local, 1)
        rows = value.shape[0]
        for chunk in range(value.shape[1] // 256):
            window = slice(chunk * rows, (chunk + 1) * rows)
            total = value[:, chunk * 256 : (chunk + 1) * 256]
            for slot in range(3):
                total = total + self.came[0][slot, local, window, :].astype(F32)
            yield window, total

    def stage_two(self):
        for slot in range(1, 4):
            self.copy(0, slot).wait_recv()
        for slot in (1, 0):
            local = flip(self.y, slot) * 2 + 1 - self.x
            for window, total in self.arrived(local):
                self.came[0][0, local, window, :] = total.astype(BF16)
            self.copy(1, slot).start()

    def stage_three(self):
        self.copy(1, 1).wait_recv()
        local = (1 - self.y) * 2 + self.x
        for window, total in self.arrived(local):
            total = total + self.came[1][1, window, :].astype(F32)
            self.came[0][0, local, window, :] = total.astype(BF16)
        self.copy(2, 0).start()

    def close(self, finish):
        self.copy(1, 0).wait_recv()
        self.copy(2, 0).wait_recv()
        for window, total in self.arrived(lax.rem(self.place, 4)):
            total = total + self.came[1][0, window, :].astype(F32)
            finish(window, total + self.came[2][0, window, :].astype(F32))

    def drain(self):
        for slot in range(1, 4):
            self.copy(0, slot).wait_send()
        for slot in range(2):
            self.copy(1, slot).wait_send()
        self.copy(2, 0).wait_send()


def greet(peers):
    barrier = pltpu.get_barrier_semaphore()
    for peer in peers:
        pl.semaphore_signal(barrier, inc=1, device_id=peer, device_id_type=MESH)
    pl.semaphore_wait(barrier, len(peers))


def turn_back(values, cosine, sine):
    half = HEAD_DIM // 2
    first, second = values[:half], values[half:]
    return jnp.concatenate(
        [first * cosine + second * sine, second * cosine - first * sine], axis=0
    )


def column_norm_back(values, gain, upstream):
    inverse = lax.rsqrt(jnp.mean(values * values, axis=0, keepdims=True) + EPSILON)
    scaled = upstream * gain
    total = jnp.sum(scaled * values, axis=0, keepdims=True) / values.shape[0]
    return inverse * scaled - values * inverse**3 * total, upstream * values * inverse


def back_kernel(
    pair_hbm,
    hidden_hbm,
    side_hbm,
    ffn_hbm,
    mixed_hbm,
    home_hbm,
    qkv_hbm,
    start_ref,
    part_hbm,
    inv_ref,
    table_ref,
    normed_hbm,
    attn_gain_ref,
    ffn_terms_ref,
    tokens_hbm,
    query_hbm,
    key_hbm,
    weights_hbm,
    middle_hbm,
    swap_hbm,
    near_hbm,
    gate_out,
    up_out,
    down_out,
    out_out,
    grads_out,
    tokens_out,
    gains_out,
    side_own,
    ffn_ref,
    mixed_ref,
    home_ref,
    qkv_ref,
    part_ref,
    normed_ref,
    rows_of,
    ffn_near,
    side_far,
    hidden_own,
    hidden_far,
    ffn_far,
    mixed_far,
    normed_far,
    cot_far,
    back_own,
    back_far,
    extra_own,
    extra_far,
    turned_own,
    turned_far,
    gain_own,
    gain_came,
    gain_all,
    sent_a,
    came_a0,
    hold_a,
    came_a1,
    came_a2,
    sent_b,
    came_b0,
    hold_b,
    came_b1,
    came_b2,
    sent_c,
    came_c0,
    came_c1,
    came_c2,
    deep_send,
    deep_recv,
    tail_sent_a,
    tail_came_a0,
    tail_came_a1,
    tail_came_a2,
    tail_sent_b,
    tail_came_b0,
    tail_came_b1,
    tail_came_b2,
    send_sems,
    recv_sems,
    tail_send,
    tail_recv,
    cot_send,
    cot_recv,
    back_send,
    back_recv,
    core_send,
    core_recv,
    gain_send,
    gain_recv,
    extra_send,
    extra_recv,
    load_sem,
    stage_sem,
    rows_sem,
    mate_send,
    mate_recv,
    relay_send,
    relay_recv,
    swap_send,
    swap_recv,
    near_sem,
):
    place, core = lax.axis_index("ctx"), lax.axis_index("fsdp")
    part, member = place // HALF, lax.rem(place, HALF)
    base = part * HALF - 1
    x, y, z = lax.rem(place, 2), lax.rem(place // 2, 2), place // 4
    wide = rows_of.shape[3]
    narrow = side_own.shape[1] // RING
    half_hidden = hidden_far.shape[1]
    half_width = ffn_far.shape[1]
    heads, pairs = query_hbm.shape[0], key_hbm.shape[0]
    scale = HEAD_DIM**-0.5
    partner = (place, 1 - core)

    def half(part, size):
        return pl.ds(pl.multiple_of(part * size, 128), size)

    stages = [
        pltpu.make_async_copy(source, target, stage_sem.at[index])
        for index, (source, target) in enumerate(
            (
                (home_hbm, home_ref),
                (side_hbm, side_own),
                (ffn_hbm, ffn_ref),
                (mixed_hbm, mixed_ref),
                (qkv_hbm, qkv_ref),
                (part_hbm, part_ref),
                (normed_hbm, normed_ref),
            )
        )
    ]
    own_hidden = pltpu.make_async_copy(
        hidden_hbm.at[:, half(core, half_hidden)], hidden_own, load_sem.at[0]
    )
    for stage in stages[:4]:
        stage.start()
    own_hidden.start()
    for stage in stages[4:]:
        stage.start()
    middle_load = pltpu.make_async_copy(middle_hbm, tokens_out, load_sem.at[1])
    middle_load.start()
    near = (place + 1 - 2 * x, place + 2 - 4 * y)
    greet([(lax.rem(place + step, RING), core) for step in range(1, RING)] + [partner])

    def remote(source, target, send, recv, peer):
        return pltpu.make_async_remote_copy(
            src_ref=source,
            dst_ref=target,
            send_sem=send,
            recv_sem=recv,
            device_id=peer,
            device_id_type=MESH,
        )

    def mate(step):
        return (part * HALF + lax.rem(member + step, HALF), core)

    def cot_copy(step):
        return remote(
            home_ref.at[lax.rem(member + step, HALF)],
            cot_far.at[member],
            cot_send.at[step],
            cot_recv.at[step],
            mate(step),
        )

    def core_copy(source, target, sem):
        return remote(source, target, core_send.at[sem], core_recv.at[sem], partner)

    def back_rows(chain, owner):
        return pair_hbm.at[owner, pl.ds(chain * wide, wide)]

    def owner_of(chain, slot):
        return block_owner(chain, place, 0, slot)

    def own_loads(chain, slot):
        loads = [
            pltpu.make_async_copy(
                back_rows(chain, owner_of(chain, slot)),
                rows_of.at[0, chain, slot],
                rows_sem.at[0, chain, slot],
            )
        ]
        if slot % 4 in EARLY:
            loads.append(
                pltpu.make_async_copy(
                    swap_hbm.at[chain, slot],
                    rows_of.at[2, chain, slot],
                    rows_sem.at[1, chain, slot],
                )
            )
        return loads

    def swap_copy(chain, slot):
        return remote(
            back_rows(chain, block_owner(chain, place, 1, slot)),
            rows_of.at[2, chain, slot],
            swap_send.at[chain, slot],
            swap_recv.at[chain, slot],
            (near[chain], core),
        )

    def swap(depth):
        for slot in (4 + depth, depth):
            for chain in range(2):
                swap_copy(chain, slot).start()

    def relay(depth):
        for slot in (4 + depth, depth):
            for chain in range(2):
                swap_copy(chain, slot).wait_recv()
                relay_copy(chain, slot).start()

    def mate_copy(chain, slot):
        return remote(
            back_rows(chain, owner_of(chain, slot)),
            rows_of.at[1, chain, slot],
            mate_send.at[chain, slot],
            mate_recv.at[chain, slot],
            partner,
        )

    def relay_copy(chain, slot):
        return remote(
            swap_hbm.at[chain, slot] if slot % 4 in EARLY else rows_of.at[2, chain, slot],
            rows_of.at[3, chain, slot],
            relay_send.at[chain, slot],
            relay_recv.at[chain, slot],
            partner,
        )

    near_load = pltpu.make_async_copy(near_hbm, ffn_near, near_sem)
    sides = [
        core_copy(ffn_hbm.at[:, half(1 - core, half_width)], ffn_far, 0),
        core_copy(mixed_hbm.at[half(1 - core, half_width), :], mixed_far, 1),
        core_copy(side_hbm, side_far, 2),
        core_copy(hidden_hbm.at[:, half(1 - core, half_hidden)], hidden_far, 3),
    ]
    stages[0].wait()
    for step in range(1, HALF):
        cot_copy(step).start()
    for copy in sides:
        copy.start()
    near_load.start()
    for depth in (2, 1, 3, 0):
        for slot in (4 + depth, depth):
            for chain in range(2):
                for load in own_loads(chain, slot):
                    load.start()
                mate_copy(chain, slot).start()
                if depth in EARLY:
                    relay_copy(chain, slot).start()
    normed_copy = core_copy(normed_hbm.at[:, half(1 - core, half_width)], normed_far, 4)
    normed_copy.start()
    cot_far[member] = home_ref[member]

    def down_product(rows, split):
        cols = slice(split[0] * 256, (split[0] + split[1]) * 256)
        down = jnp.dot(side_own[0, rows, :], hidden_own[:, cols], preferred_element_type=F32)
        return down + jnp.dot(side_far[0, rows, :], hidden_far[:, cols], preferred_element_type=F32)

    def deep_compute(owner, count):
        rows = pl.ds(pl.multiple_of(owner * narrow, 16), count * narrow)
        return down_product(rows, DOWN_CHUNKS[2])

    def deep_finish(window, value):
        chunk = DOWN_CHUNKS[2][0] + window.start // narrow
        down_out[:, chunk * 256 : chunk * 256 + 256] = value

    def compute(chain, owner, slot):
        lanes = pl.ds(chain * 256, 256)
        own_lanes = pl.ds(pl.multiple_of(core * half_width + chain * 256, 128), 256)
        rows = pl.ds(pl.multiple_of(owner * narrow, 16), narrow)
        values = []
        if slot is not None:
            for load in own_loads(chain, slot):
                load.wait()
            mate_copy(chain, slot).wait_recv()
            relay_copy(chain, slot).wait_recv()
            wide_sum = jnp.dot(
                rows_of[0, chain, slot],
                ffn_ref[:, half(core, half_width)],
                preferred_element_type=F32,
            )
            for source, columns in (
                (1, ffn_far[...]),
                (2, ffn_near[chain, 0]),
                (3, ffn_near[chain, 1]),
            ):
                wide_sum += jnp.dot(
                    rows_of[source, chain, slot], columns, preferred_element_type=F32
                )
            values += [(0, wide_sum[:, :256]), (wide, wide_sum[:, 256:])]
        chunks = DOWN_CHUNKS[chain][1]
        down = down_product(rows, DOWN_CHUNKS[chain])
        row = 2 * wide
        for chunk in range(chunks):
            values.append((row, down[:, chunk * 256 : chunk * 256 + 256]))
            row += narrow
        out = dot_dims(side_own[1, rows, :], mixed_ref[own_lanes, :], 1, 1)
        out += dot_dims(side_far[1, rows, :], mixed_far[lanes, :], 1, 1)
        values.append((row, out))
        return values

    def finish(chain, row, value):
        lanes = slice(chain * 256, chain * 256 + 256)
        if row < 2 * wide:
            target, low = (gate_out, up_out)[chain], row // wide * 256
            target[:, low : low + 256] = value
            return
        chunk = (row - 2 * wide) // narrow
        if chunk == DOWN_CHUNKS[chain][1]:
            out_out[:, lanes] = value
        else:
            chunk += DOWN_CHUNKS[chain][0]
            down_out[:, chunk * 256 : chunk * 256 + 256] = value

    chains = (
        Spread(
            0,
            compute,
            2 * wide,
            sent_a,
            (came_a0, came_a1, came_a2),
            hold_a,
            1,
            send_sems,
            recv_sems,
        ),
        Spread(
            1,
            compute,
            2 * wide,
            sent_b,
            (came_b0, came_b1, came_b2),
            hold_b,
            1,
            send_sems,
            recv_sems,
        ),
    )
    own_hidden.wait()
    for stage in stages[1:4]:
        stage.wait()
    for copy in sides:
        copy.wait_recv()

    def near_side(depth):
        for chain in chains:
            chain.stage_one(1, depth)

    def far_side(depth):
        for chain in chains:
            chain.stage_one(0, depth)

    def onward(depth):
        for chain in chains:
            chain.stage_two(depth)

    def deeper(depth):
        for chain in chains:
            chain.stage_three(depth)

    along = DeepSpread(
        deep_compute, sent_c, (came_c0, came_c1, came_c2), deep_send, deep_recv
    )
    near_side(2)
    for slot in (2, 1, 3):
        along.stage_one(slot)
    far_side(2)
    near_side(1)
    swap(1)
    near_load.wait()
    for stage in stages[4:]:
        stage.wait()

    def back_copy(step):
        return remote(
            back_own.at[lax.rem(member + step, HALF)],
            back_far.at[member],
            back_send.at[step],
            back_recv.at[step],
            mate(step),
        )

    def extra_copy(group):
        return remote(
            extra_own,
            extra_far.at[group],
            extra_send.at[group],
            extra_recv.at[group],
            (HALF - 1, core),
        )

    def attention(
        scaled, cots, natural, delta_ref, query_acc, key_nat, value_nat, pair_acc
    ):
        def widen(ref, i, row):
            return jnp.concatenate(
                [ref[i, row : row + HEAD_DIM, :], ref[i, row + HEAD_DIM : row + 2 * HEAD_DIM, :]],
                axis=1,
            )

        def prepare(i, nothing):
            @pl.when(i != member)
            def _():
                cot_copy(lax.rem(member - i + HALF, HALF)).wait_recv()

            query = widen(qkv_ref, i + 1, 0) * jnp.asarray(scale, BF16)
            cot = widen(cot_far, i, 0)
            scaled[i] = query
            cots[i] = cot
            natural[i] = transposed(jnp.concatenate([query, cot], axis=0))
            delta_ref[i] = jnp.sum(
                cot.astype(F32) * widen(part_ref, i, 0).astype(F32), axis=0, keepdims=True
            )
            query_acc[i] = jnp.zeros(query_acc.shape[1:], F32)
            return nothing

        def per_key(j, nothing):
            key_t = qkv_ref[j, 2 * HEAD_DIM : 3 * HEAD_DIM, :]
            key_nat[...] = transposed(key_t)
            value_nat[...] = transposed(qkv_ref[j, 3 * HEAD_DIM : 4 * HEAD_DIM, :])
            shape = (BLOCK, 2 * BLOCK)
            key_place = (base + j) * BLOCK + lax.broadcasted_iota(jnp.int32, shape, 0)

            def step(diagonal, i):
                start = jnp.concatenate([start_ref[i - 1]] * 2, axis=1)
                scores = jnp.dot(key_nat[...], scaled[i - 1], preferred_element_type=F32)
                grad_probs = jnp.dot(value_nat[...], cots[i - 1], preferred_element_type=F32)
                ok = key_place >= start
                if diagonal:
                    places = (base + i) * BLOCK + lax.broadcasted_iota(jnp.int32, (1, BLOCK), 1)
                    ok = ok & (key_place <= jnp.concatenate([places] * 2, axis=1))
                probs = jnp.where(ok, jnp.exp(scores) * inv_ref[i - 1], 0.0)
                grad_scores = (probs * (grad_probs - delta_ref[i - 1])).astype(BF16)
                both_low = jnp.concatenate([grad_scores, probs.astype(BF16)], axis=0)
                query_acc[i - 1] += jnp.dot(
                    qkv_ref[j, 2 * HEAD_DIM : 3 * HEAD_DIM, :],
                    grad_scores,
                    preferred_element_type=F32,
                )
                return jnp.dot(both_low, natural[i - 1], preferred_element_type=F32)

            @pl.when(j == 0)
            def _():
                pair_acc[...] = jnp.zeros(pair_acc.shape, F32)

            @pl.when(j > 0)
            def _():
                pair_acc[...] = step(True, j)

            def one(i, carry):
                pair_acc[...] += step(False, i)
                return carry

            def two(index, carry):
                i = j + 1 + 2 * index
                pair_acc[...] += step(False, i) + step(False, i + 1)
                return carry

            count = (HALF - j) // 2
            lax.fori_loop(0, count, two, 0)
            lax.fori_loop(j + 1 + 2 * count, HALF + 1, one, 0)
            first = lax.broadcasted_iota(jnp.int32, (BLOCK, 2 * HEAD_DIM), 1) < HEAD_DIM
            merged = jnp.where(first, pair_acc[0:BLOCK, :], pair_acc[BLOCK:, :]).T.astype(BF16)

            @pl.when(j == 0)
            def _():
                extra_own[...] = merged
                extra_copy(member).start()

            @pl.when(j > 0)
            def _():
                query_grad = (query_acc[j - 1] * scale).astype(BF16)
                back_own[j - 1, 0:HEAD_DIM, :] = query_grad[:, :BLOCK]
                back_own[j - 1, HEAD_DIM : 2 * HEAD_DIM, :] = query_grad[:, BLOCK:]
                back_own[j - 1, 2 * HEAD_DIM : 4 * HEAD_DIM, :] = merged

            @pl.when((j > 0) & (j - 1 != member))
            def _():
                back_copy(lax.rem(j - 1 - member + HALF, HALF)).start()

            @pl.when(j == 1)
            def _():
                onward(2)
                far_side(1)
                swap(3)

            @pl.when(j == 2)
            def _():
                near_side(3)
                far_side(3)
                swap(0)

            @pl.when(j == 4)
            def _():
                relay(1)
                onward(1)

            @pl.when(j == 6)
            def _():
                deeper(2)

            return nothing

        lax.fori_loop(0, HALF, prepare, 0)
        lax.fori_loop(1 - part, HALF + 1, per_key, 0)
        back_far[member] = back_own[member]

    pl.run_scoped(
        attention,
        pltpu.VMEM((HALF, HEAD_DIM, 2 * BLOCK), BF16),
        pltpu.VMEM((HALF, HEAD_DIM, 2 * BLOCK), BF16),
        pltpu.VMEM((HALF, 2 * BLOCK, 2 * HEAD_DIM), BF16),
        pltpu.VMEM((HALF, 1, 2 * BLOCK), F32),
        pltpu.VMEM((HALF, HEAD_DIM, 2 * BLOCK), F32),
        pltpu.VMEM((BLOCK, HEAD_DIM), BF16),
        pltpu.VMEM((BLOCK, HEAD_DIM), BF16),
        pltpu.VMEM((2 * BLOCK, 2 * HEAD_DIM), F32),
    )

    turned_copy = core_copy(turned_own, turned_far, 5)

    def tail_compute(chain, owner, slot):
        lanes = slice(chain * 256, chain * 256 + 256)
        own_lanes = pl.ds(pl.multiple_of(core * half_width + chain * 256, 128), 256)
        values, row = [], 0
        for size, base in ((heads, 2 * pairs), (pairs, 0), (pairs, pairs)):
            count = size * HEAD_DIM // RING
            rows = pl.ds(pl.multiple_of(base * HEAD_DIM + owner * count, 16), count)
            value = jnp.dot(
                turned_own[rows, :], normed_ref[:, own_lanes], preferred_element_type=F32
            )
            value += jnp.dot(turned_far[rows, :], normed_far[:, lanes], preferred_element_type=F32)
            values.append((row, value))
            row += count
        return values

    def tail_finish(chain, row, value):
        grads_out[row : row + value.shape[0], chain * 256 : chain * 256 + 256] = value

    tails = (
        Spread(
            0,
            tail_compute,
            0,
            tail_sent_a,
            (tail_came_a0, tail_came_a1, tail_came_a2),
            tail_came_a0,
            0,
            tail_send,
            tail_recv,
        ),
        Spread(
            1,
            tail_compute,
            0,
            tail_sent_b,
            (tail_came_b0, tail_came_b1, tail_came_b2),
            tail_came_b0,
            0,
            tail_send,
            tail_recv,
        ),
    )

    def finish_all(natural, summed, query_ref, key_ref, tokens_ref, weights_ref):
        loads = [
            pltpu.make_async_copy(query_hbm, query_ref, load_sem.at[2]),
            pltpu.make_async_copy(key_hbm, key_ref, load_sem.at[3]),
            pltpu.make_async_copy(tokens_hbm, tokens_ref, load_sem.at[4]),
            pltpu.make_async_copy(weights_hbm, weights_ref, load_sem.at[5]),
        ]
        for copy in loads:
            copy.start()
        half_dim = HEAD_DIM // 2
        cosine, sine = table_ref[0:half_dim, :], table_ref[half_dim:HEAD_DIM, :]
        query_gain = table_ref[HEAD_DIM : 2 * HEAD_DIM, :]
        key_gain = table_ref[2 * HEAD_DIM : 3 * HEAD_DIM, :]

        def head_rows(index):
            return pl.ds(pl.multiple_of(index * HEAD_DIM, HEAD_DIM), HEAD_DIM)

        def query_head(head, total):
            low = pl.multiple_of(lax.rem(head, 2) * HEAD_DIM, HEAD_DIM)
            upstream = turn_back(
                back_far[head // 2, pl.ds(low, HEAD_DIM), :].astype(F32), cosine, sine
            )
            back, terms = column_norm_back(query_ref[head], query_gain, upstream)
            turned_own[head_rows(2 * pairs + head), :] = back.astype(BF16)
            return total + terms

        def key_head(pair, total):
            upstream = back_far[pair, 2 * HEAD_DIM : 4 * HEAD_DIM, :].astype(F32)
            upstream += extra_far[pair].astype(F32)
            back, terms = column_norm_back(
                key_ref[pair],
                key_gain,
                turn_back(upstream[:HEAD_DIM], cosine, sine),
            )
            turned_own[head_rows(pair), :] = back.astype(BF16)
            turned_own[head_rows(pairs + pair), :] = upstream[HEAD_DIM:].astype(BF16)
            return total + terms


        relay(3)
        near_side(0)
        deeper(1)
        far_side(0)
        onward(3)

        def arrive(step, nothing):
            back_copy(step).wait_recv()
            return nothing

        lax.fori_loop(1, HALF, arrive, 0)

        def extra_arrive(group, nothing):
            extra_copy(group).wait_recv()
            return nothing

        @pl.when(place == HALF - 1)
        def _():
            lax.fori_loop(0, HALF, extra_arrive, 0)

        @pl.when(place != HALF - 1)
        def _():
            extra_far[...] = jnp.zeros(extra_far.shape, BF16)

        for copy in loads:
            copy.wait()
        nothing = jnp.zeros((HEAD_DIM, BLOCK), F32)
        query_terms = lax.fori_loop(0, heads, query_head, nothing)
        key_terms = lax.fori_loop(0, pairs, key_head, nothing)
        turned_copy.start()
        for row in range(0, turned_own.shape[0], 128):
            natural[:, row : row + 128] = turned_own[row : row + 128, :].astype(F32).T.astype(BF16)
        normed_copy.wait_recv()
        turned_copy.wait_recv()

        def tail_one(index, carry):
            for chain in tails:
                chain.stage_one(1 - index // 4, lax.rem(index + 1, 4))
            return carry

        lax.fori_loop(0, 8, tail_one, 0)
        relay(0)
        onward(0)
        deeper(3)
        summed[...] = dot_dims(natural[...], weights_ref[...], 1, 1)
        middle_load.wait()

        def token_rows(index, total):
            rows = pl.ds(pl.multiple_of(index * 32, 32), 32)
            values, upstream = tokens_ref[rows, :].astype(F32), summed[rows, :]
            inverse = lax.rsqrt(jnp.mean(values * values, axis=-1, keepdims=True) + EPSILON)
            scaled = upstream * attn_gain_ref[...]
            weight = jnp.sum(scaled * values, axis=-1, keepdims=True) / values.shape[1]
            tokens_out[rows, :] += inverse * scaled - values * inverse**3 * weight
            return total + jnp.sum(upstream * values * inverse, axis=0, keepdims=True)

        terms = lax.fori_loop(
            0, BLOCK // 32, token_rows, jnp.zeros((1, tokens_ref.shape[1]), F32)
        )
        gain_own[...] = jnp.zeros(gain_own.shape, F32)
        gain_own[0:1, :] = terms
        gain_own[1:2, :] = ffn_terms_ref[...]
        gain_own[2:3, 0:HEAD_DIM] = jnp.sum(query_terms.T, axis=0, keepdims=True)
        gain_own[3:4, 0:HEAD_DIM] = jnp.sum(key_terms.T, axis=0, keepdims=True)

    width = normed_ref.shape[1]
    pl.run_scoped(
        finish_all,
        pltpu.VMEM((BLOCK, turned_own.shape[0]), BF16),
        pltpu.VMEM((BLOCK, width), F32),
        pltpu.VMEM((heads, HEAD_DIM, BLOCK), F32),
        pltpu.VMEM((pairs, HEAD_DIM, BLOCK), F32),
        pltpu.VMEM((BLOCK, width), BF16),
        pltpu.VMEM(weights_hbm.shape, BF16),
    )

    def tail_two(index, carry):
        for chain in tails:
            chain.stage_two(lax.rem(index + 1, 4))
        return carry

    def tail_three(depth, carry):
        for chain in tails:
            chain.stage_three(depth)
        return carry

    gain_swap = core_copy(gain_own, gain_came, 22)
    gain_swap.start()
    along.stage_two()

    def gain_copy(step):
        peer = (lax.rem(place + step, RING), core)
        return remote(
            gain_all.at[place], gain_all.at[place], gain_send.at[step], gain_recv.at[step], peer
        )

    def gain_start(step, carry):
        gain_copy(step).start()
        return carry

    def gain_arrive(step, carry):
        gain_copy(step).wait()
        return carry

    gain_swap.wait()
    gain_all[place] = gain_own[...] + gain_came[...]
    lax.fori_loop(1, RING, gain_start, 0)
    lax.fori_loop(0, 4, tail_two, 0)
    along.stage_three()
    lax.fori_loop(1, 4, tail_three, 0)
    along.close(deep_finish)
    for chain in chains:
        chain.close(finish)
    for chain in tails:
        chain.close(tail_finish)
    lax.fori_loop(1, RING, gain_arrive, 0)

    def gain_sum(index, total):
        return total + gain_all[index]

    gains_out[...] = lax.fori_loop(1, RING, gain_sum, gain_all[0])

    def settle(step, nothing):
        back_copy(step).wait_send()
        cot_copy(step).wait_send()
        return nothing

    lax.fori_loop(1, HALF, settle, 0)

    @pl.when(part == 1)
    def _():
        extra_copy(member).wait_send()

    for copy in sides + [normed_copy, turned_copy]:
        copy.wait_send()
    for slot in range(8):
        for chain in range(2):
            mate_copy(chain, slot).wait_send()
            relay_copy(chain, slot).wait_send()
            if slot % 4 not in EARLY:
                swap_copy(chain, slot).wait_send()
    for chain in chains + tails + (along,):
        chain.drain()


def back_call(call_id, inputs, loads):
    hidden, side, ffn_low = inputs[1:4]
    rows, hidden_width = hidden.shape
    width = ffn_low.shape[1]
    wide, narrow = hidden_width // RING, width // RING
    total = (HEADS + 2 * KV_HEADS) * HEAD_DIM

    def buffers(sizes):
        return [
            pltpu.VMEM((slots, sizes[chain], 256), BF16)
            for chain in range(2)
            for slots in (8, 8, 4, 3)
        ]

    def chain_buffers(split):
        rest = (split[1] + 1) * narrow
        shapes = ((8, rest), (8, rest), (7, 2 * wide + rest), (4, 2 * wide + rest), (3, 2 * wide + rest))
        return [pltpu.VMEM((*shape, 256), BF16) for shape in shapes]

    dma = pltpu.SemaphoreType.DMA
    specs = [VMEM_SPEC] * (len(inputs) + len(loads))
    staged = (2, 3, 4, 5, 6, 8, 11)
    for index in (0, 1, *staged, *range(len(inputs), len(specs))):
        specs[index] = HBM_SPEC
    return pl.pallas_call(
        back_kernel,
        out_shape=(
            jax.ShapeDtypeStruct((wide, width // 2), F32),
            jax.ShapeDtypeStruct((wide, width // 2), F32),
            jax.ShapeDtypeStruct((narrow, hidden_width // 2), F32),
            jax.ShapeDtypeStruct((narrow, width // 2), F32),
            jax.ShapeDtypeStruct((total // RING, width // 2), F32),
            jax.ShapeDtypeStruct((rows, width), F32),
            jax.ShapeDtypeStruct((4, width), F32),
        ),
        in_specs=specs,
        out_specs=(VMEM_SPEC,) * 7,
        scratch_shapes=[pltpu.VMEM(inputs[index].shape, BF16) for index in staged]
        + [
            pltpu.VMEM((4, 2, 8, wide, rows), BF16),
            pltpu.VMEM((2, 2, rows, width // 2), BF16),
            pltpu.VMEM(side.shape, BF16),
            pltpu.VMEM((rows, hidden_width // 2), BF16),
            pltpu.VMEM((rows, hidden_width // 2), BF16),
            pltpu.VMEM((rows, width // 2), BF16),
            pltpu.VMEM((width // 2, rows), BF16),
            pltpu.VMEM((rows, width // 2), BF16),
            pltpu.VMEM((HALF, 2 * HEAD_DIM, rows), BF16),
            pltpu.VMEM((HALF, 4 * HEAD_DIM, rows), BF16),
            pltpu.VMEM((HALF, 4 * HEAD_DIM, rows), BF16),
            pltpu.VMEM((2 * HEAD_DIM, rows), BF16),
            pltpu.VMEM((HALF, 2 * HEAD_DIM, rows), BF16),
            pltpu.VMEM((total, rows), BF16),
            pltpu.VMEM((total, rows), BF16),
            pltpu.VMEM((4, width), F32),
            pltpu.VMEM((4, width), F32),
            pltpu.VMEM((RING, 4, width), F32),
        ]
        + chain_buffers(DOWN_CHUNKS[0])
        + chain_buffers(DOWN_CHUNKS[1])
        + [pltpu.VMEM((*lead, DOWN_CHUNKS[2][1] * narrow, 256), BF16) for lead in ((3, 4), (3, 4), (2,), (1,))]
        + [dma((6,)), dma((6,))]
        + buffers((total // RING, total // RING))
        + [dma((2, 15))] * 4
        + [dma((HALF,))] * 4
        + [dma((23,))] * 2
        + [dma((RING,))] * 2
        + [dma((HALF,))] * 2
        + [dma((6,)), dma((7,))]
        + [dma((2, 2, 8))]
        + [dma((2, 8))] * 6
        + [dma],
        compiler_params=pltpu.CompilerParams(
            collective_id=call_id, has_side_effects=True, vmem_limit_bytes=63 << 20
        ),
        name="backward_spread",
    )(*inputs, *loads)


def head_frequencies(rows):
    half = HEAD_DIM // 2
    frequencies = THETA ** (-(2.0 / HEAD_DIM) * np.arange(half, dtype=np.float32))
    return jnp.asarray(np.repeat(frequencies.astype(np.float32)[:, None], rows, axis=1))


def front_kernel(
    gain_ref,
    place_ref,
    query_gain_ref,
    key_gain_ref,
    frequency_ref,
    tokens_hbm,
    w_query_hbm,
    w_key_hbm,
    w_value_hbm,
    w_out_hbm,
    w_gate_hbm,
    w_up_hbm,
    w_down_hbm,
    qkv_out,
    starts_out,
    normed_out,
    part_out,
    mixed_out,
    inv_out,
    out_full,
    table_ref,
    query_hbm,
    key_hbm,
    weights_hbm,
    gate_far,
    up_far,
    down_far,
    home,
    key_nat,
    totals,
    accs,
    tokens_ref,
    query_out,
    key_out,
    weights_out,
    own_start_ref,
    keep_sem,
    own_sem,
    send_sem,
    recv_sem,
    start_send,
    start_recv,
    mixed_send,
    mixed_recv,
    kv_send,
    kv_recv,
    extra_send,
    extra_recv,
    core_send,
    core_recv,
):
    place, core = lax.axis_index("ctx"), lax.axis_index("fsdp")
    part, member = place // HALF, lax.rem(place, HALF)
    rows = tokens_ref.shape[0]
    depth = w_query_hbm.shape[0]
    partner = (place, 1 - core)
    tokens_load = pltpu.make_async_copy(tokens_hbm, tokens_ref, keep_sem.at[0])
    tokens_load.start()
    places = place * rows + lax.broadcasted_iota(jnp.int32, (1, rows), 1)
    own_start_ref[...] = places - place_ref[...]
    angles = frequency_ref[...] * place_ref[...].astype(F32)
    half = HEAD_DIM // 2
    table_ref[0:half, :] = jnp.cos(angles)
    table_ref[half:HEAD_DIM, :] = jnp.sin(angles)
    for index, source in enumerate((query_gain_ref, key_gain_ref)):
        table_ref[(index + 1) * HEAD_DIM : (index + 2) * HEAD_DIM, :] = jnp.broadcast_to(
            source[...], (rows, HEAD_DIM)
        ).T
    greet([partner] + [(lax.rem(place + step, RING), core) for step in range(1, RING)])

    def remote(source, target, send, recv, peer):
        return pltpu.make_async_remote_copy(
            src_ref=source,
            dst_ref=target,
            send_sem=send,
            recv_sem=recv,
            device_id=peer,
            device_id_type=MESH,
        )

    def mate(step):
        return (part * HALF + lax.rem(member + step, HALF), core)

    copies, near_copies = [], []

    def share(source, target, near_target=None):
        index = len(copies)
        copy = remote(source, target, core_send.at[index], core_recv.at[index], partner)
        copy.start()
        copies.append(copy)
        if near_target is not None:
            near = pltpu.make_async_copy(source, near_target, own_sem.at[index])
            near.start()
            near_copies.append(near)

    column = 0
    own_depth = pl.ds(pl.multiple_of(core * depth, 128), depth)
    for source in (w_key_hbm, w_value_hbm, w_query_hbm):
        window = pl.ds(column, source.shape[1])
        target = weights_out.at[own_depth, window]
        share(source, target, target)
        column += source.shape[1]

    target = out_full.at[own_depth, :]
    share(w_out_hbm, target, target)
    for source, target in ((w_gate_hbm, gate_far), (w_up_hbm, up_far), (w_down_hbm, down_far)):
        share(source, target)

    def start_copy(step):
        return remote(
            own_start_ref,
            starts_out.at[member],
            start_send.at[step],
            start_recv.at[step],
            mate(step),
        )

    for step in range(1, HALF):
        start_copy(step).start()
    starts_out[member] = own_start_ref[...]

    def norm_rows(index, nothing):
        window = pl.ds(pl.multiple_of(index * 32, 32), 32)
        values = tokens_ref[window, :].astype(F32)
        inverse = lax.rsqrt(jnp.mean(values * values, axis=-1, keepdims=True) + EPSILON)
        normed_out[window, :] = (values * inverse * gain_ref[...]).astype(BF16)
        return nothing

    tokens_load.wait()
    lax.fori_loop(0, rows // 32, norm_rows, 0)
    cosine, sine = table_ref[0:half, :], table_ref[half:HEAD_DIM, :]
    query_gain = table_ref[HEAD_DIM : 2 * HEAD_DIM, :]
    key_gain = table_ref[2 * HEAD_DIM : 3 * HEAD_DIM, :]

    def project(column, count):
        window = pl.ds(column, count)
        product = jnp.dot(normed_out[...], weights_out[:, window], preferred_element_type=F32)
        return product.T

    def turned(values, gain):
        mean = jnp.mean(values * values, axis=0, keepdims=True)
        values = values * lax.rsqrt(mean + EPSILON) * gain
        first, second = values[:half], values[half:]
        return jnp.concatenate(
            [first * cosine - second * sine, second * cosine + first * sine], axis=0
        ).astype(BF16)

    kv_width = KV_HEADS * HEAD_DIM
    copies[0].wait_recv()
    near_copies[0].wait()

    def key_chunk(index, nothing):
        products = project(pl.multiple_of(index * 256, 256), 256)
        for offset in range(4):
            raw = products[offset * HEAD_DIM : (offset + 1) * HEAD_DIM]
            group = index * 4 + offset
            key_out[group] = raw
            home[group, 2 * HEAD_DIM : 3 * HEAD_DIM, :] = turned(raw, key_gain)
        return nothing

    lax.fori_loop(0, KV_HEADS // 4, key_chunk, 0)
    copies[1].wait_recv()
    near_copies[1].wait()

    def value_chunk(index, nothing):
        products = project(pl.multiple_of(kv_width + index * 256, 256), 256)
        for offset in range(4):
            value = products[offset * HEAD_DIM : (offset + 1) * HEAD_DIM].astype(BF16)
            home[index * 4 + offset, 3 * HEAD_DIM : 4 * HEAD_DIM, :] = value
        return nothing

    lax.fori_loop(0, KV_HEADS // 4, value_chunk, 0)

    window = pl.ds(2 * HEAD_DIM, 2 * HEAD_DIM)

    def kv_copy(step):
        return remote(
            home.at[lax.rem(member + step, HALF), window],
            qkv_out.at[1 + member, window],
            kv_send.at[step],
            kv_recv.at[step],
            mate(step),
        )

    def kv_start(step, nothing):
        kv_copy(HALF - step).start()
        return nothing

    def extra_copy(group):
        return remote(
            home.at[group, window, pl.ds(rows - EDGE, EDGE)],
            qkv_out.at[0, window, pl.ds(rows - EDGE, EDGE)],
            extra_send.at[group],
            extra_recv.at[group],
            (HALF + group, core),
        )

    def extra_start(group, nothing):
        extra_copy(group).start()
        return nothing

    @pl.when(place == HALF - 1)
    def _():
        lax.fori_loop(0, HALF, extra_start, 0)

    lax.fori_loop(1, HALF, kv_start, 0)
    copies[2].wait_recv()
    near_copies[2].wait()

    def block_copy(step):
        peer = mate(step)
        return remote(
            home.at[lax.rem(member + step, HALF), pl.ds(0, 2 * HEAD_DIM)],
            qkv_out.at[1 + member, pl.ds(0, 2 * HEAD_DIM)],
            send_sem.at[step],
            recv_sem.at[step],
            peer,
        )

    def query_chunk(turn, nothing):
        index = lax.rem(member // 2 - turn + 4, 4)
        products = project(pl.multiple_of(2 * kv_width + index * 256, 256), 256)
        for offset in range(4):
            raw = products[offset * HEAD_DIM : (offset + 1) * HEAD_DIM]
            query_out[index * 4 + offset] = raw
            low = (offset % 2) * HEAD_DIM
            home[index * 2 + offset // 2, low : low + HEAD_DIM, :] = turned(
                raw, query_gain
            )
        for offset in range(2):
            group = index * 2 + offset

            @pl.when(group != member)
            def _():
                block_copy(lax.rem(group - member + HALF, HALF)).start()

        return nothing

    lax.fori_loop(0, HEADS // 4, query_chunk, 0)
    keeps = [
        pltpu.make_async_copy(source, target, keep_sem.at[1 + index])
        for index, (source, target) in enumerate(
            ((query_out, query_hbm), (key_out, key_hbm), (weights_out, weights_hbm))
        )
    ]
    for keep in keeps:
        keep.start()
    qkv_out[1 + member] = home[member]
    base = part * HALF - 1

    def mixed_copy(step):
        peer = mate(step)
        return remote(
            part_out.at[lax.rem(member + step, HALF)],
            mixed_out.at[member],
            mixed_send.at[step],
            mixed_recv.at[step],
            peer,
        )

    def query_of(i):
        query_t = jnp.concatenate(
            [qkv_out[i, 0:HEAD_DIM, :], qkv_out[i, HEAD_DIM : 2 * HEAD_DIM, :]], axis=1
        ) * jnp.asarray(HEAD_DIM**-0.5, BF16)
        return query_t, jnp.concatenate([starts_out[i - 1]] * 2, axis=1)

    def meet(query_t, keys, values, ok, carry):
        total, acc = carry
        probs = jnp.exp(jnp.dot(keys, query_t, preferred_element_type=F32))
        probs = jnp.where(ok(lax.broadcasted_iota(jnp.int32, probs.shape, 0)), probs, 0.0)
        total = total + jnp.sum(probs, axis=0, keepdims=True)
        return total, acc + jnp.dot(values, probs.astype(BF16), preferred_element_type=F32)

    def inner(i):
        @pl.when(i - 1 != member)
        def _():
            step = lax.rem(member - i + 1 + HALF, HALF)
            start_copy(step).wait_recv()
            kv_copy(step).wait_recv()
            block_copy(step).wait_recv()

        key_nat[i] = transposed(qkv_out[i, 2 * HEAD_DIM : 3 * HEAD_DIM, :])
        query_t, start = query_of(i)
        places = (base + i) * BLOCK + lax.broadcasted_iota(jnp.int32, (1, BLOCK), 1)
        query_place = jnp.concatenate([places] * 2, axis=1)

        def step(diagonal, j, carry):
            def ok(offset):
                key_place = (base + j) * BLOCK + offset
                if diagonal:
                    return (key_place >= start) & (key_place <= query_place)
                return key_place >= start

            values = qkv_out[j, 3 * HEAD_DIM : 4 * HEAD_DIM, :]
            return meet(query_t, key_nat[j], values, ok, carry)

        carry = (jnp.zeros((1, 2 * BLOCK), F32), jnp.zeros((HEAD_DIM, 2 * BLOCK), F32))
        pairs = (i - 1) // 2

        def two(index, carry):
            return step(False, 2 * index + 2, step(False, 2 * index + 1, carry))

        carry = lax.fori_loop(0, pairs, two, carry)
        carry = lax.fori_loop(2 * pairs + 1, i, functools.partial(step, False), carry)
        totals[i - 1], accs[i - 1] = step(True, i, carry)

    def outer(i):
        @pl.when((part == 1) & (i == 1))
        def _():
            extra_copy(member).wait_recv()
            qkv_out[0, 2 * HEAD_DIM :, 0 : rows - EDGE] = jnp.zeros(
                (2 * HEAD_DIM, rows - EDGE), BF16
            )
            key_nat[0] = transposed(qkv_out[0, 2 * HEAD_DIM : 3 * HEAD_DIM, :])

        @pl.when(part == 1)
        def _():
            query_t, start = query_of(i)

            def ok(offset):
                return HALF * BLOCK - EDGE + offset >= start

            values = qkv_out[0, 3 * HEAD_DIM : 4 * HEAD_DIM, rows - EDGE :]
            totals[i - 1], accs[i - 1] = meet(
                query_t, key_nat[0, rows - EDGE :, :], values, ok, (totals[i - 1], accs[i - 1])
            )

        inverse = 1.0 / totals[i - 1]
        low = (accs[i - 1] * inverse).astype(BF16)
        part_out[i - 1, 0:HEAD_DIM, :] = low[:, :BLOCK]
        part_out[i - 1, HEAD_DIM:, :] = low[:, BLOCK:]
        inv_out[i - 1] = inverse

        @pl.when(i - 1 != member)
        def _():
            mixed_copy(lax.rem(i - 1 - member + HALF, HALF)).start()

    def per_query(i, nothing):
        @pl.when(i <= HALF)
        def _():
            inner(i)

        @pl.when(i > lag)
        def _():
            outer(i - lag)

        return nothing

    lag = 3
    lax.fori_loop(1, HALF + lag + 1, per_query, 0)
    mixed_out[member] = part_out[member]

    def settle(step, nothing):
        block_copy(step).wait_send()
        kv_copy(step).wait_send()
        start_copy(step).wait_send()
        mixed_copy(step).wait()
        return nothing

    lax.fori_loop(1, HALF, settle, 0)

    def extra_settle(group, nothing):
        extra_copy(group).wait_send()
        return nothing

    @pl.when(place == HALF - 1)
    def _():
        lax.fori_loop(0, HALF, extra_settle, 0)

    for copy in copies[:3]:
        copy.wait_send()
    for copy in copies[3:]:
        copy.wait()
    for near in near_copies[3:] + keeps:
        near.wait()


def front_call(call_id, inputs, loads):
    rows, width = loads[0].shape
    half_depth, hidden_width = loads[5].shape
    total = (HEADS + 2 * KV_HEADS) * HEAD_DIM
    dma = pltpu.SemaphoreType.DMA
    query_raw = (HEADS, HEAD_DIM, rows)
    key_raw = (KV_HEADS, HEAD_DIM, rows)
    return pl.pallas_call(
        front_kernel,
        out_shape=(
            jax.ShapeDtypeStruct((HALF + 1, 4 * HEAD_DIM, rows), BF16),
            jax.ShapeDtypeStruct((HALF, 1, rows), jnp.int32),
            jax.ShapeDtypeStruct((rows, width), BF16),
            jax.ShapeDtypeStruct((HALF, 2 * HEAD_DIM, rows), BF16),
            jax.ShapeDtypeStruct((HALF, 2 * HEAD_DIM, rows), BF16),
            jax.ShapeDtypeStruct((HALF, 1, 2 * rows), F32),
            jax.ShapeDtypeStruct((width, width), BF16),
            jax.ShapeDtypeStruct((3 * HEAD_DIM, rows), F32),
            jax.ShapeDtypeStruct(query_raw, F32),
            jax.ShapeDtypeStruct(key_raw, F32),
            jax.ShapeDtypeStruct((width, total), BF16),
            jax.ShapeDtypeStruct((half_depth, hidden_width), BF16),
            jax.ShapeDtypeStruct((half_depth, hidden_width), BF16),
            jax.ShapeDtypeStruct((hidden_width // 2, width), BF16),
        ),
        in_specs=[VMEM_SPEC] * len(inputs) + [HBM_SPEC] * len(loads),
        out_specs=(VMEM_SPEC,) * 8 + (HBM_SPEC,) * 6,
        scratch_shapes=[
            pltpu.VMEM((HALF, 4 * HEAD_DIM, rows), BF16),
            pltpu.VMEM((HALF + 1, rows, HEAD_DIM), BF16),
            pltpu.VMEM((HALF, 1, 2 * rows), F32),
            pltpu.VMEM((HALF, HEAD_DIM, 2 * rows), F32),
            pltpu.VMEM((rows, width), BF16),
            pltpu.VMEM(query_raw, F32),
            pltpu.VMEM(key_raw, F32),
            pltpu.VMEM((width, total), BF16),
            pltpu.VMEM((1, rows), jnp.int32),
            dma((4,)),
            dma((4,)),
        ]
        + [dma((HALF,))] * 10
        + [dma((7,))] * 2,
        compiler_params=pltpu.CompilerParams(
            collective_id=call_id, has_side_effects=True, vmem_limit_bytes=63 << 20
        ),
        name="front_heads",
    )(*inputs, *loads)


def ffn_kernel(
    tokens_ref,
    mixed_ref,
    w_out_ref,
    gain_ref,
    cot_ref,
    gate_own,
    gate_far,
    up_own,
    up_far,
    down_own,
    down_far,
    pair_out,
    hidden_out,
    output_out,
    ffn_out,
    side_out,
    mixed_back_out,
    grad_middle_out,
    terms_out,
    swap_out,
    near_out,
    middle,
    result,
    upstream,
    middle_low,
    swap_send,
    swap_recv,
    near_send,
    near_recv,
):
    step = pl.program_id(0)
    place, core = lax.axis_index("ctx"), lax.axis_index("fsdp")
    x, y, z = lax.rem(place, 2), lax.rem(place // 2, 2), place // 4
    near = (place + 1 - 2 * x, place + 2 - 4 * y)
    wide = pair_out.shape[1] // 2
    half_width = gate_own.shape[0]
    strip_owners = pair_out.shape[0] // 4
    plane = lax.rem(z + 6 - step, 4)

    def remote(source, target, send, recv, peer):
        return pltpu.make_async_remote_copy(
            src_ref=source,
            dst_ref=target,
            send_sem=send,
            recv_sem=recv,
            device_id=peer,
            device_id_type=MESH,
        )

    def near_copy(chain, other):
        target = core if other == 0 else 1 - core
        lanes = pl.ds(pl.multiple_of(target * half_width, 128), half_width)
        return remote(
            ffn_out.at[:, lanes],
            near_out.at[chain, other],
            near_send.at[chain, other],
            near_recv.at[chain, other],
            (near[chain], target),
        )

    def swap_copy(chain, slot):
        return remote(
            pair_out.at[block_owner(chain, place, 1, slot), pl.ds(chain * wide, wide)],
            swap_out.at[chain, slot],
            swap_send.at[chain, slot],
            swap_recv.at[chain, slot],
            (near[chain], core),
        )

    rows, width = tokens_ref.shape
    strip = 32

    def strips(work):
        def one(index, carry):
            return work(pl.ds(pl.multiple_of(index * strip, strip), strip), carry)

        return one

    @pl.when(step == 0)
    def _():
        mixed = mixed_ref[...].astype(F32).T.astype(BF16)
        middle[...] = tokens_ref[...].astype(F32) + jnp.dot(
            mixed, w_out_ref[...], preferred_element_type=F32
        )

        def norm(window, carry):
            values = middle[window, :]
            inverse = lax.rsqrt(jnp.mean(values * values, axis=-1, keepdims=True) + EPSILON)
            ffn_out[window, :] = (values * inverse * gain_ref[...]).astype(BF16)
            result[window, :] = values
            return carry

        lax.fori_loop(0, rows // strip, strips(norm), 0)
        greet([(peer, target) for peer in near for target in (core, 1 - core)])
        for chain in range(2):
            for other in range(2):
                near_copy(chain, other).start()
        upstream[...] = jnp.zeros(upstream.shape, F32)
        side_out[0] = cot_ref[...].astype(F32).T.astype(BF16)

    own = pl.ds(pl.multiple_of(core * half_width, 128), half_width)
    far = pl.ds(pl.multiple_of((1 - core) * half_width, 128), half_width)

    def strip_of_hidden(down_ref):
        def ahead(near_ref, far_ref):
            return jnp.dot(ffn_out[:, own], near_ref[...], preferred_element_type=F32) + jnp.dot(
                ffn_out[:, far], far_ref[...], preferred_element_type=F32
            )

        gate_pre, up_pre = ahead(gate_own, gate_far), ahead(up_own, up_far)
        grad_hidden = dot_dims(cot_ref[...], down_ref[...], 1, 1)
        gate_sig = jax.nn.sigmoid(gate_pre)
        gate_act = gate_pre * gate_sig
        hidden_out[...] = (gate_act * up_pre).astype(BF16)
        gate_back = (
            grad_hidden * up_pre * (gate_sig * (1.0 + gate_pre * (1.0 - gate_sig)))
        ).astype(BF16)
        up_back = (grad_hidden * gate_act).astype(BF16)
        result[...] += jnp.dot(hidden_out[...], down_ref[...], preferred_element_type=F32)
        for window, gate_ref, up_ref in ((own, gate_own, up_own), (far, gate_far, up_far)):
            upstream[:, window] += dot_dims(gate_back, gate_ref[...], 1, 1) + dot_dims(
                up_back, up_ref[...], 1, 1
            )
        for base, back in ((0, gate_back), (wide, up_back)):
            turned = back.astype(F32).T.astype(BF16)
            for index in range(strip_owners):
                pair_out[plane * strip_owners + index, base : base + wide, :] = turned[
                    index * wide : (index + 1) * wide
                ]

        @pl.when(step < len(EARLY))
        def _():
            for turned_side in range(2):
                for chain in range(2):
                    swap_copy(chain, turned_side * 4 + 2 - step).start()


    @pl.when(plane // 2 == core)
    def _():
        strip_of_hidden(down_own)

    @pl.when(plane // 2 != core)
    def _():
        strip_of_hidden(down_far)

    @pl.when(step == pl.num_programs(0) - 1)
    def _():
        output_out[...] = result[...].astype(BF16)

        def back(window, total):
            values, grads = middle[window, :], upstream[window, :]
            inverse = lax.rsqrt(jnp.mean(values * values, axis=-1, keepdims=True) + EPSILON)
            scaled = grads * gain_ref[...]
            weight = jnp.sum(scaled * values, axis=-1, keepdims=True) / width
            grad_middle = cot_ref[window, :].astype(F32) + (
                inverse * scaled - values * inverse**3 * weight
            )
            grad_middle_out[window, :] = grad_middle
            middle_low[window, :] = grad_middle.astype(BF16)
            return total + jnp.sum(grads * values * inverse, axis=0, keepdims=True)

        terms_out[...] = lax.fori_loop(
            0, rows // strip, strips(back), jnp.zeros((1, width), F32)
        )
        mixed_back_out[...] = dot_dims(w_out_ref[...], middle_low[...], 1, 1).astype(BF16)
        side_out[1] = middle_low[...].astype(F32).T.astype(BF16)
        for chain in range(2):
            for other in range(2):
                near_copy(chain, other).wait()

        for depth in EARLY:
            for slot in (4 + depth, depth):
                for chain in range(2):
                    swap_copy(chain, slot).wait()


def ffn_call(call_id, tokens, mixed_t, w_out, gain, cot, gate, up, down):
    rows, width = tokens.shape
    half_depth, hidden_width = gate[0].shape
    steps = 4
    chunk = hidden_width // steps
    wide = hidden_width // RING

    def whole(*shape):
        return pl.BlockSpec(shape, lambda i: (0,) * len(shape))

    def turn(i):
        return lax.rem(lax.axis_index("ctx") // 4 + 6 - i, steps)

    columns = pl.BlockSpec((half_depth, chunk), lambda i: (0, turn(i)))
    return pl.pallas_call(
        ffn_kernel,
        grid_spec=pl.GridSpec(
            grid=(steps,),
            in_specs=[
                whole(rows, width),
                whole(width, rows),
                whole(width, width),
                whole(1, width),
                whole(rows, width),
                columns,
                columns,
                columns,
                columns,
                pl.BlockSpec((chunk, width), lambda i: (lax.rem(turn(i), 2), 0)),
                pl.BlockSpec((chunk, width), lambda i: (lax.rem(turn(i), 2), 0)),
            ],
            out_specs=(
                whole(RING, 2 * wide, rows),
                pl.BlockSpec((rows, chunk), lambda i: (0, turn(i))),
                whole(rows, width),
                whole(rows, width),
                whole(2, width, rows),
                whole(width, rows),
                whole(rows, width),
                whole(1, width),
                HBM_SPEC,
                HBM_SPEC,
            ),
            scratch_shapes=[pltpu.VMEM((rows, width), F32)] * 3
            + [pltpu.VMEM((rows, width), BF16)]
            + [pltpu.SemaphoreType.DMA((2, 8))] * 2
            + [pltpu.SemaphoreType.DMA((2, 2))] * 2,
        ),
        out_shape=(
            jax.ShapeDtypeStruct((RING, 2 * wide, rows), BF16),
            jax.ShapeDtypeStruct((rows, hidden_width), BF16),
            jax.ShapeDtypeStruct((rows, width), BF16),
            jax.ShapeDtypeStruct((rows, width), BF16),
            jax.ShapeDtypeStruct((2, width, rows), BF16),
            jax.ShapeDtypeStruct((width, rows), BF16),
            jax.ShapeDtypeStruct((rows, width), F32),
            jax.ShapeDtypeStruct((1, width), F32),
            jax.ShapeDtypeStruct((2, 8, wide, rows), BF16),
            jax.ShapeDtypeStruct((2, 2, rows, half_depth), BF16),
        ),
        compiler_params=pltpu.CompilerParams(
            collective_id=call_id, has_side_effects=True, vmem_limit_bytes=63 << 20
        ),
        name="ffn_both_ways",
    )(tokens, mixed_t, w_out, gain, cot, *gate, *up, *down)


def settle_kernel(*refs):
    count = 6
    sources, gains, rest = refs[:count], refs[count], refs[count + 1 :]
    targets, gain_targets, rest = rest[: count + 2], rest[count + 2 : count + 6], rest[count + 6 :]
    held, in_sem, out_sem = rest[:count], rest[count], rest[count + 1]
    loads = [
        pltpu.make_async_copy(source, hold, in_sem.at[index])
        for index, (source, hold) in enumerate(zip(sources, held))
    ]
    for load in loads:
        load.start()
    stores, row = [], 0
    for index, load in enumerate(loads):
        load.wait()
        if index < count - 1:
            pieces = [(held[index], targets[index])]
        else:
            pieces = []
            for target in targets[index:]:
                pieces.append((held[index].at[pl.ds(row, target.shape[0])], target))
                row += target.shape[0]
        for piece, target in pieces:
            store = pltpu.make_async_copy(piece, target, out_sem.at[len(stores)])
            store.start()
            stores.append(store)
    for index, target in enumerate(gain_targets):
        target[...] = gains[index : index + 1, 0 : target.shape[1]]
    for store in stores:
        store.wait()


def settle_call(tokens, gate_t, up_t, down_t, out_t, qkv_t, gains):
    sources = (tokens, gate_t, up_t, down_t, out_t, qkv_t)
    lanes = qkv_t.shape[1]
    query = HEADS * HEAD_DIM // RING
    pair = KV_HEADS * HEAD_DIM // RING
    shapes = [source.shape for source in sources[:-1]]
    shapes += [(query, lanes), (pair, lanes), (pair, lanes)]
    gain_shapes = [(1, gains.shape[1])] * 2 + [(1, HEAD_DIM)] * 2
    return pl.pallas_call(
        settle_kernel,
        out_shape=tuple(jax.ShapeDtypeStruct(shape, F32) for shape in shapes + gain_shapes),
        in_specs=[HBM_SPEC] * len(sources) + [VMEM_SPEC],
        out_specs=(HBM_SPEC,) * len(shapes) + (VMEM_SPEC,) * 4,
        scratch_shapes=[pltpu.VMEM(source.shape, F32) for source in sources]
        + [pltpu.SemaphoreType.DMA((6,)), pltpu.SemaphoreType.DMA((8,))],
        compiler_params=pltpu.CompilerParams(vmem_limit_bytes=63 << 20),
        name="settle_results",
    )(*sources, gains)


def heads_body(
    tokens,
    seg_ids,
    doc_pos,
    attn_gain,
    w_query,
    w_key,
    w_value,
    query_gain,
    key_gain,
    w_out,
    ffn_gain,
    w_gate,
    w_up,
    w_down,
    d_output,
):
    rows = tokens.shape[1]
    (
        qkv,
        starts,
        normed_low,
        mixed_far,
        mixed_home,
        inverse_total,
        o_full,
        table,
        query_raw,
        key_raw,
        kvq_full,
        gate_far,
        up_far,
        down_far,
    ) = front_call(
        1,
        (
            attn_gain[None, :],
            doc_pos,
            query_gain[None, :],
            key_gain[None, :],
            head_frequencies(rows),
        ),
        (tokens[0], w_query, w_key, w_value, w_out, w_gate, w_up, w_down),
    )
    mixed_t = mixed_home.reshape(HEADS * HEAD_DIM, rows)
    cot_low = d_output[0]
    (
        pair,
        hidden_low,
        output,
        ffn_low,
        side,
        grad_mixed,
        grad_middle,
        ffn_terms,
        swapped,
        ffn_near,
    ) = ffn_call(
        2,
        tokens[0],
        mixed_t,
        o_full,
        ffn_gain[None, :],
        cot_low,
        (w_gate, gate_far),
        (w_up, up_far),
        (w_down, down_far),
    )
    gate_t, up_t, down_t, out_t, qkv_grads, d_tokens, gain_totals = back_call(
        3,
        (
            pair,
            hidden_low,
            side,
            ffn_low,
            mixed_t,
            grad_mixed.reshape(HALF, 2 * HEAD_DIM, rows),
            qkv,
            starts,
            mixed_far,
            inverse_total,
            table,
            normed_low,
            attn_gain[None, :],
            ffn_terms,
        ),
        (tokens[0], query_raw, key_raw, kvq_full, grad_middle, swapped, ffn_near),
    )
    d_tokens, gate, up, down, out, query, key, value, attn, ffn, query_gains, key_gains = (
        settle_call(d_tokens, gate_t, up_t, down_t, out_t, qkv_grads, gain_totals)
    )
    return (
        output[None],
        d_tokens[None],
        attn[0],
        query.T,
        key.T,
        value.T,
        query_gains[0],
        key_gains[0],
        out.T,
        ffn[0],
        gate.T,
        up.T,
        down.T,
    )


def solution(mesh):
    in_specs = (
        P("fsdp", "ctx", None),
        P("fsdp", "ctx"),
        P("fsdp", "ctx"),
        P(),
        P("fsdp", None),
        P("fsdp", None),
        P("fsdp", None),
        P(),
        P(),
        P("fsdp", None),
        P(),
        P("fsdp", None),
        P("fsdp", None),
        P("fsdp", None),
        P("fsdp", "ctx", None),
    )
    out_specs = (
        P("fsdp", "ctx", None),
        P("fsdp", "ctx", None),
        P(),
        P("fsdp", "ctx"),
        P("fsdp", "ctx"),
        P("fsdp", "ctx"),
        P(),
        P(),
        P("fsdp", "ctx"),
        P(),
        P("fsdp", "ctx"),
        P("fsdp", "ctx"),
        P("fsdp", "ctx"),
    )
    chosen = heads_body if (mesh.shape["ctx"], mesh.shape["fsdp"]) == (HEADS, 2) else ring_body
    return jax.shard_map(chosen, mesh=mesh, in_specs=in_specs, out_specs=out_specs, check_vma=False)
```

```python
import functools

import jax
import jax.numpy as jnp
import numpy as np
from jax import lax
from jax.experimental import pallas as pl
from jax.experimental.pallas import tpu as pltpu
from jax.sharding import PartitionSpec as P

HEADS = 16
KV_HEADS = 8
HEAD_DIM = 64
HOPS = 8


EPSILON = 1e-05
THETA = 1000000.0
MASKED = -1e30


def from_behind(block, axis, distance):
    devices = range(lax.axis_size(axis))
    route = [(i - distance, i) for i in devices if i - distance in devices]
    return lax.ppermute(block, axis, route)


def rms_norm(values, norm_gain):
    return (
        values * lax.rsqrt(jnp.mean(values * values, axis=-1, keepdims=True) + EPSILON) * norm_gain
    )


def rms_back(values, norm_gain, upstream):
    inverse = lax.rsqrt(jnp.mean(values * values, axis=-1, keepdims=True) + EPSILON)
    scaled = upstream * norm_gain
    row_width = values.shape[-1]
    d_values = (
        inverse * scaled
        - values * inverse**3 * jnp.sum(scaled * values, axis=-1, keepdims=True) / row_width
    )
    return (d_values, upstream * values * inverse)


def rotary(values, positions, turn_sign):
    half_dim = values.shape[-1] // 2
    inverse_freq = THETA ** (-(2.0 / values.shape[-1]) * jnp.arange(half_dim, dtype=jnp.float32))
    angles = positions.astype(jnp.float32)[:, None] * inverse_freq[None, :]
    cosine = jnp.cos(angles)[:, None, :]
    sine_part = turn_sign * jnp.sin(angles)[:, None, :]
    first_half = values[..., :half_dim]
    second_half = values[..., half_dim:]
    return jnp.concatenate(
        [
            first_half * cosine - second_half * sine_part,
            second_half * cosine + first_half * sine_part,
        ],
        axis=-1,
    )


def outer_product(left_mat, right_mat):
    return lax.dot_general(
        left_mat, right_mat, (((0,), (0,)), ((), ())), preferred_element_type=jnp.float32
    )


def against(left_mat, right_mat):
    return lax.dot_general(
        left_mat, right_mat, (((1,), (1,)), ((), ())), preferred_element_type=jnp.float32
    )


def ring_body(
    tokens,
    seg_ids,
    doc_pos,
    attn_gain,
    w_query,
    w_key,
    w_value,
    query_gain,
    key_gain,
    w_out,
    ffn_gain,
    w_gate,
    w_up,
    w_down,
    d_output,
):
    cycle_place = lax.axis_index("ctx")
    tok_rows = tokens.shape[1]
    resid_in = tokens[0].astype(jnp.float32)
    seg_local = seg_ids[0]
    pos_local = doc_pos[0]
    q_per_kv = HEADS // KV_HEADS
    group_cols = q_per_kv * HEAD_DIM
    score_scale = HEAD_DIM ** (-0.5)
    q_full, k_full, v_full, o_full = (
        lax.all_gather(w_query, "fsdp", axis=0, tiled=True),
        lax.all_gather(w_key, "fsdp", axis=0, tiled=True),
        lax.all_gather(w_value, "fsdp", axis=0, tiled=True),
        lax.all_gather(w_out, "fsdp", axis=0, tiled=True),
    )
    gate_full, up_full, down_full = (
        lax.all_gather(w_gate, "fsdp", axis=0, tiled=True),
        lax.all_gather(w_up, "fsdp", axis=0, tiled=True),
        lax.all_gather(w_down, "fsdp", axis=0, tiled=True),
    )
    normed = rms_norm(resid_in, attn_gain)
    normed_low = normed.astype(jnp.bfloat16)
    query_raw = jnp.dot(normed_low, q_full, preferred_element_type=jnp.float32).reshape(
        tok_rows, HEADS, HEAD_DIM
    )
    key_raw = jnp.dot(normed_low, k_full, preferred_element_type=jnp.float32).reshape(
        tok_rows, KV_HEADS, HEAD_DIM
    )
    value_raw = jnp.dot(normed_low, v_full, preferred_element_type=jnp.float32)
    query_rot = rotary(rms_norm(query_raw, query_gain), pos_local, 1.0)
    key_rot = rotary(rms_norm(key_raw, key_gain), pos_local, 1.0)
    query_low = query_rot.astype(jnp.bfloat16).reshape(tok_rows, HEADS * HEAD_DIM)
    key_low = key_rot.astype(jnp.bfloat16).reshape(tok_rows, KV_HEADS * HEAD_DIM)
    value_low = value_raw.astype(jnp.bfloat16)
    own_kv = (key_low, value_low, seg_local)
    kv_blocks = [own_kv]
    carried = own_kv
    for hop_index in range(HOPS):
        carried = from_behind((carried[0], carried[1], carried[2]), "ctx", 1)
        kv_blocks.append(carried)
    key_all = jnp.concatenate([kv_entry[0] for kv_entry in kv_blocks], axis=0)
    value_all = jnp.concatenate([kv_entry[1] for kv_entry in kv_blocks], axis=0)
    seg_all = jnp.concatenate([kv_entry[2] for kv_entry in kv_blocks], axis=0)
    key_owner = cycle_place - jnp.arange(HOPS + 1, dtype=jnp.int32)
    owner_valid = jnp.repeat(key_owner >= 0, tok_rows)
    key_index = (
        key_owner[:, None] * tok_rows + jnp.arange(tok_rows, dtype=jnp.int32)[None, :]
    ).reshape(-1)
    query_index = cycle_place * tok_rows + jnp.arange(tok_rows, dtype=jnp.int32)
    allowed = (
        (seg_local[:, None] == seg_all[None, :])
        & (key_index[None, :] <= query_index[:, None])
        & owner_valid[None, :]
    )

    def group_scores(kv_group):
        query_part = lax.dynamic_slice_in_dim(query_low, kv_group * group_cols, group_cols, 1)
        query_part = query_part.reshape(tok_rows, q_per_kv, HEAD_DIM)
        key_part = lax.dynamic_slice_in_dim(key_all, kv_group * HEAD_DIM, HEAD_DIM, 1)
        value_part = lax.dynamic_slice_in_dim(value_all, kv_group * HEAD_DIM, HEAD_DIM, 1)
        scores = (
            jnp.einsum("trd,kd->rtk", query_part, key_part, preferred_element_type=jnp.float32)
            * score_scale
        )
        return (jnp.where(allowed[None], scores, MASKED), query_part, key_part, value_part)

    def forward_group(kv_group):
        scores, query_part, key_part, value_part = group_scores(kv_group)
        row_top = jnp.max(scores, axis=-1, keepdims=True)
        log_total = row_top + jnp.log(jnp.sum(jnp.exp(scores - row_top), axis=-1, keepdims=True))
        attn_probs = jnp.exp(scores - log_total)
        mixed_part = jnp.einsum(
            "rtk,kd->trd",
            attn_probs.astype(jnp.bfloat16),
            value_part,
            preferred_element_type=jnp.float32,
        )
        return (mixed_part.reshape(tok_rows, group_cols), log_total[..., 0])

    mixed_groups, total_groups = lax.map(forward_group, jnp.arange(KV_HEADS, dtype=jnp.int32))
    mixed = mixed_groups.transpose(1, 0, 2).reshape(tok_rows, HEADS * HEAD_DIM)
    mixed_low = mixed.astype(jnp.bfloat16)
    middle = resid_in + jnp.dot(mixed_low, o_full, preferred_element_type=jnp.float32)
    ffn_low = rms_norm(middle, ffn_gain).astype(jnp.bfloat16)
    gate_pre = jnp.dot(ffn_low, gate_full, preferred_element_type=jnp.float32)
    up_pre = jnp.dot(ffn_low, up_full, preferred_element_type=jnp.float32)
    gate_sig = jax.nn.sigmoid(gate_pre)
    gate_act = gate_pre * gate_sig
    hidden_low = (gate_act * up_pre).astype(jnp.bfloat16)
    result = middle + jnp.dot(hidden_low, down_full, preferred_element_type=jnp.float32)
    output = result.astype(jnp.bfloat16)[None]
    cot_low = d_output[0]
    cotangent = cot_low.astype(jnp.float32)
    grad_w_down = outer_product(hidden_low, cot_low)
    grad_hidden = against(cot_low, down_full)
    gate_back = (grad_hidden * up_pre * (gate_sig * (1.0 + gate_pre * (1.0 - gate_sig)))).astype(
        jnp.bfloat16
    )
    up_back = (grad_hidden * gate_act).astype(jnp.bfloat16)
    grad_w_gate = outer_product(ffn_low, gate_back)
    grad_w_up = outer_product(ffn_low, up_back)
    grad_ffn_in = against(gate_back, gate_full) + against(up_back, up_full)
    middle_part, ffn_terms = rms_back(middle, ffn_gain, grad_ffn_in)
    grad_middle = cotangent + middle_part
    middle_low = grad_middle.astype(jnp.bfloat16)
    grad_w_out = outer_product(mixed_low, middle_low)
    grad_mixed = against(middle_low, o_full).astype(jnp.bfloat16)

    def backward_group(kv_group):
        scores, query_part, key_part, value_part = group_scores(kv_group)
        attn_probs = jnp.exp(scores - total_groups[kv_group][..., None])
        mixed_grad_part = lax.dynamic_slice_in_dim(grad_mixed, kv_group * group_cols, group_cols, 1)
        mixed_grad_part = mixed_grad_part.reshape(tok_rows, q_per_kv, HEAD_DIM)
        grad_probs = jnp.einsum(
            "trd,kd->rtk", mixed_grad_part, value_part, preferred_element_type=jnp.float32
        )
        grad_value = jnp.einsum(
            "rtk,trd->kd",
            attn_probs.astype(jnp.bfloat16),
            mixed_grad_part,
            preferred_element_type=jnp.float32,
        )
        row_delta = jnp.sum(grad_probs * attn_probs, axis=-1, keepdims=True)
        grad_scores = (attn_probs * (grad_probs - row_delta)).astype(jnp.bfloat16)
        grad_query = (
            jnp.einsum("rtk,kd->trd", grad_scores, key_part, preferred_element_type=jnp.float32)
            * score_scale
        )
        grad_key = (
            jnp.einsum("rtk,trd->kd", grad_scores, query_part, preferred_element_type=jnp.float32)
            * score_scale
        )
        return (grad_query.reshape(tok_rows, group_cols), grad_key, grad_value)

    query_groups, key_groups, value_groups = lax.map(
        backward_group, jnp.arange(KV_HEADS, dtype=jnp.int32)
    )
    grad_query_rot = query_groups.transpose(1, 0, 2).reshape(tok_rows, HEADS, HEAD_DIM)
    key_blocks = key_groups.transpose(1, 0, 2).reshape(HOPS + 1, tok_rows, KV_HEADS * HEAD_DIM)
    value_blocks = value_groups.transpose(1, 0, 2).reshape(HOPS + 1, tok_rows, KV_HEADS * HEAD_DIM)
    home_key = key_blocks[HOPS]
    home_value = value_blocks[HOPS]
    for hop_index in range(HOPS, 0, -1):
        moved_key, moved_value = (
            from_behind(home_key.astype(jnp.bfloat16), "ctx", -1).astype(home_key.dtype),
            from_behind(home_value.astype(jnp.bfloat16), "ctx", -1).astype(home_value.dtype),
        )
        home_key = moved_key + key_blocks[hop_index - 1]
        home_value = moved_value + value_blocks[hop_index - 1]
    query_turned = rotary(grad_query_rot, pos_local, -1.0)
    key_turned = rotary(home_key.reshape(tok_rows, KV_HEADS, HEAD_DIM), pos_local, -1.0)
    query_back, query_terms = rms_back(query_raw, query_gain, query_turned)
    key_back, key_terms = rms_back(key_raw, key_gain, key_turned)
    query_back = query_back.reshape(tok_rows, HEADS * HEAD_DIM).astype(jnp.bfloat16)
    key_back = key_back.reshape(tok_rows, KV_HEADS * HEAD_DIM).astype(jnp.bfloat16)
    value_back = home_value.astype(jnp.bfloat16)
    grad_w_query = outer_product(normed_low, query_back)
    grad_w_key = outer_product(normed_low, key_back)
    grad_w_value = outer_product(normed_low, value_back)
    grad_normed = (
        against(query_back, q_full) + against(key_back, k_full) + against(value_back, v_full)
    )
    input_part, attn_terms = rms_back(resid_in, attn_gain, grad_normed)
    d_tokens = (grad_middle + input_part)[None]
    gain_totals = lax.psum(
        (
            jnp.sum(attn_terms, axis=0),
            jnp.sum(ffn_terms, axis=0),
            jnp.sum(query_terms, axis=(0, 1)),
            jnp.sum(key_terms, axis=(0, 1)),
        ),
        ("ctx", "fsdp"),
    )
    weight_grads = (
        grad_w_query,
        grad_w_key,
        grad_w_value,
        grad_w_out,
        grad_w_gate,
        grad_w_up,
        grad_w_down,
    )
    spread = (
        lax.psum_scatter(
            weight_grads[0].astype(jnp.bfloat16), "fsdp", scatter_dimension=0, tiled=True
        ).astype(jnp.float32),
        lax.psum_scatter(
            weight_grads[1].astype(jnp.bfloat16), "fsdp", scatter_dimension=0, tiled=True
        ).astype(jnp.float32),
        lax.psum_scatter(
            weight_grads[2].astype(jnp.bfloat16), "fsdp", scatter_dimension=0, tiled=True
        ).astype(jnp.float32),
        lax.psum_scatter(
            weight_grads[3].astype(jnp.bfloat16), "fsdp", scatter_dimension=0, tiled=True
        ).astype(jnp.float32),
        lax.psum_scatter(
            weight_grads[4].astype(jnp.bfloat16), "fsdp", scatter_dimension=0, tiled=True
        ).astype(jnp.float32),
        lax.psum_scatter(
            weight_grads[5].astype(jnp.bfloat16), "fsdp", scatter_dimension=0, tiled=True
        ).astype(jnp.float32),
        lax.psum_scatter(
            weight_grads[6].astype(jnp.bfloat16), "fsdp", scatter_dimension=0, tiled=True
        ).astype(jnp.float32),
    )
    shares = (
        lax.psum_scatter(spread[0], "ctx", scatter_dimension=1, tiled=True),
        lax.psum_scatter(spread[1], "ctx", scatter_dimension=1, tiled=True),
        lax.psum_scatter(spread[2], "ctx", scatter_dimension=1, tiled=True),
        lax.psum_scatter(spread[3], "ctx", scatter_dimension=1, tiled=True),
        lax.psum_scatter(spread[4], "ctx", scatter_dimension=1, tiled=True),
        lax.psum_scatter(spread[5], "ctx", scatter_dimension=1, tiled=True),
        lax.psum_scatter(spread[6], "ctx", scatter_dimension=1, tiled=True),
    )
    return (
        output,
        d_tokens,
        gain_totals[0],
        shares[0],
        shares[1],
        shares[2],
        gain_totals[2],
        gain_totals[3],
        shares[3],
        gain_totals[1],
        shares[4],
        shares[5],
        shares[6],
    )


MESH = pl.DeviceIdType.MESH
BLOCK = 256
RING = 16
HALF = 8
EDGE = 128
DOWN_CHUNKS = ((0, 3), (3, 3), (6, 3))
EARLY = (2,)
VMEM_SPEC = pl.BlockSpec(memory_space=pltpu.VMEM)
HBM_SPEC = pl.BlockSpec(memory_space=pltpu.HBM)
SMEM_SPEC = pl.BlockSpec(memory_space=pltpu.SMEM)
F32 = jnp.float32
BF16 = jnp.bfloat16


def dot_dims(left_mat, right_mat, left_dim, right_dim):
    return lax.dot_general(
        left_mat, right_mat, (((left_dim,), (right_dim,)), ((), ())), preferred_element_type=F32
    )


def transposed(block):
    return block.astype(F32).T.astype(BF16)


def flip(bit, turned):
    return bit + turned - 2 * bit * turned


def block_owner(chain, place, other, slot):
    x, y, z = lax.rem(place, 2), lax.rem(place // 2, 2), place // 4
    turned, depth = slot // 4, lax.rem(lax.rem(slot, 4) + z, 4)
    first, second = flip((x, y)[chain], other), flip((y, x)[chain], turned)
    return depth * 4 + (second * 2 + first if chain == 0 else first * 2 + second)


class Spread:
    def __init__(self, chain, compute, base, sent, came, hold, skip, send_sems, recv_sems):
        place, self.core = lax.axis_index("ctx"), lax.axis_index("fsdp")
        x, y, self.z = lax.rem(place, 2), lax.rem(place // 2, 2), place // 4
        self.chain, self.base = chain, base
        self.first, self.second = (x, y) if chain == 0 else (y, x)
        self.compute, self.sent, self.came = compute, sent, came
        self.hold, self.skip = hold, skip
        self.send_sems, self.recv_sems = send_sems, recv_sems

    def at(self, first, second, depth):
        low = second * 2 + first if self.chain == 0 else first * 2 + second
        return depth * 4 + low

    def deep(self, depth):
        return lax.rem(self.z + depth, 4)

    def owner(self, slot):
        return self.at(self.first, flip(self.second, slot // 4), self.deep(lax.rem(slot, 4)))

    def copy(self, stage, slot):
        if stage == 0:
            peer = self.at(1 - self.first, self.second, self.z)
            source, target, sem = self.sent.at[slot], self.came[0].at[slot], slot
        elif stage == 1:
            peer = self.at(self.first, 1 - self.second, self.z)
            source, target, sem = self.hold.at[4 + slot - self.skip], self.came[1].at[slot], 8 + slot
        else:
            peer = self.at(self.first, self.second, self.deep(slot))
            source, target, sem = self.hold.at[slot - self.skip], self.came[2].at[slot - 1], 11 + slot
        return pltpu.make_async_remote_copy(
            src_ref=source,
            dst_ref=target,
            send_sem=self.send_sems.at[self.chain, sem],
            recv_sem=self.recv_sems.at[self.chain, sem],
            device_id=(peer, self.core),
            device_id_type=MESH,
        )

    def stage_one(self, turned, depth):
        slot = turned * 4 + depth
        owner = self.at(1 - self.first, flip(self.second, turned), self.deep(depth))
        for row, value in self.compute(self.chain, owner, None):
            row -= self.base
            self.sent[slot, row : row + value.shape[0], :] = value.astype(BF16)
        self.copy(0, slot).start()

    def sums(self, slot):
        for row, value in self.compute(self.chain, self.owner(slot), slot):
            if row >= self.base:
                low = row - self.base
                value = value + self.came[0][slot, low : low + value.shape[0], :].astype(F32)
            yield slice(row, row + value.shape[0]), value

    def stage_two(self, depth):
        self.copy(0, 4 + depth).wait_recv()
        for window, value in self.sums(4 + depth):
            self.hold[4 + depth - self.skip, window, :] = value.astype(BF16)
        self.copy(1, depth).start()

    def stage_three(self, depth):
        self.copy(0, depth).wait_recv()
        self.copy(1, depth).wait_recv()
        for window, value in self.sums(depth):
            value = value + self.came[1][depth, window, :].astype(F32)
            self.hold[depth - self.skip, window, :] = value.astype(BF16)
        self.copy(2, depth).start()

    def close(self, finish):
        self.copy(0, 0).wait_recv()
        self.copy(1, 0).wait_recv()
        for depth in range(1, 4):
            self.copy(2, depth).wait_recv()
        for window, value in self.sums(0):
            value = value + self.came[1][0, window, :].astype(F32)
            for depth in range(3):
                value = value + self.came[2][depth, window, :].astype(F32)
            finish(self.chain, window.start, value)

    def drain(self):
        for slot in range(8):
            self.copy(0, slot).wait_send()
        for depth in range(4):
            self.copy(1, depth).wait_send()
        for depth in range(1, 4):
            self.copy(2, depth).wait_send()


class DeepSpread:
    def __init__(self, compute, sent, came, send_sems, recv_sems):
        self.place, self.core = lax.axis_index("ctx"), lax.axis_index("fsdp")
        self.x, self.y = lax.rem(self.place, 2), lax.rem(self.place // 2, 2)
        self.compute, self.sent, self.came = compute, sent, came
        self.send_sems, self.recv_sems = send_sems, recv_sems

    def copy(self, stage, slot):
        if stage == 0:
            peer = lax.rem(self.place + 4 * slot, RING)
            source, target, sem = self.sent.at[slot - 1], self.came[0].at[slot - 1], slot - 1
        elif stage == 1:
            peer = self.place + 1 - 2 * self.x
            local = flip(self.y, slot) * 2 + 1 - self.x
            source, target, sem = self.came[0].at[0, local], self.came[1].at[slot], 3 + slot
        else:
            peer = self.place + 2 - 4 * self.y
            local = (1 - self.y) * 2 + self.x
            source, target, sem = self.came[0].at[0, local], self.came[2].at[0], 5
        return pltpu.make_async_remote_copy(
            src_ref=source,
            dst_ref=target,
            send_sem=self.send_sems.at[sem],
            recv_sem=self.recv_sems.at[sem],
            device_id=(peer, self.core),
            device_id_type=MESH,
        )

    def stage_one(self, slot):
        first = lax.rem(self.place // 4 + slot, 4) * 4
        value = self.compute(first, 4)
        rows = value.shape[0] // 4
        for local in range(4):
            for chunk in range(value.shape[1] // 256):
                self.sent[slot - 1, local, chunk * rows : (chunk + 1) * rows, :] = value[
                    local * rows : (local + 1) * rows, chunk * 256 : (chunk + 1) * 256
                ].astype(BF16)
        self.copy(0, slot).start()

    def arrived(self, local):
        value = self.compute(self.place - lax.rem(self.place, 4) + local, 1)
        rows = value.shape[0]
        for chunk in range(value.shape[1] // 256):
            window = slice(chunk * rows, (chunk + 1) * rows)
            total = value[:, chunk * 256 : (chunk + 1) * 256]
            for slot in range(3):
                total = total + self.came[0][slot, local, window, :].astype(F32)
            yield window, total

    def stage_two(self):
        for slot in range(1, 4):
            self.copy(0, slot).wait_recv()
        for slot in (1, 0):
            local = flip(self.y, slot) * 2 + 1 - self.x
            for window, total in self.arrived(local):
                self.came[0][0, local, window, :] = total.astype(BF16)
            self.copy(1, slot).start()

    def stage_three(self):
        self.copy(1, 1).wait_recv()
        local = (1 - self.y) * 2 + self.x
        for window, total in self.arrived(local):
            total = total + self.came[1][1, window, :].astype(F32)
            self.came[0][0, local, window, :] = total.astype(BF16)
        self.copy(2, 0).start()

    def close(self, finish):
        self.copy(1, 0).wait_recv()
        self.copy(2, 0).wait_recv()
        for window, total in self.arrived(lax.rem(self.place, 4)):
            total = total + self.came[1][0, window, :].astype(F32)
            finish(window, total + self.came[2][0, window, :].astype(F32))

    def drain(self):
        for slot in range(1, 4):
            self.copy(0, slot).wait_send()
        for slot in range(2):
            self.copy(1, slot).wait_send()
        self.copy(2, 0).wait_send()


def greet(peers):
    barrier = pltpu.get_barrier_semaphore()
    for peer in peers:
        pl.semaphore_signal(barrier, inc=1, device_id=peer, device_id_type=MESH)
    pl.semaphore_wait(barrier, len(peers))


def turn_back(values, cosine, sine):
    half = HEAD_DIM // 2
    first, second = values[:half], values[half:]
    return jnp.concatenate(
        [first * cosine + second * sine, second * cosine - first * sine], axis=0
    )


def column_norm_back(values, gain, upstream):
    inverse = lax.rsqrt(jnp.mean(values * values, axis=0, keepdims=True) + EPSILON)
    scaled = upstream * gain
    total = jnp.sum(scaled * values, axis=0, keepdims=True) / values.shape[0]
    return inverse * scaled - values * inverse**3 * total, upstream * values * inverse


def back_kernel(
    pair_hbm,
    hidden_hbm,
    side_hbm,
    ffn_hbm,
    mixed_hbm,
    home_hbm,
    qkv_hbm,
    start_ref,
    part_hbm,
    inv_ref,
    table_ref,
    normed_hbm,
    attn_gain_ref,
    ffn_terms_ref,
    tokens_hbm,
    query_hbm,
    key_hbm,
    weights_hbm,
    middle_hbm,
    swap_hbm,
    near_hbm,
    gate_out,
    up_out,
    down_out,
    out_out,
    grads_out,
    tokens_out,
    gains_out,
    side_own,
    ffn_ref,
    mixed_ref,
    home_ref,
    qkv_ref,
    part_ref,
    normed_ref,
    rows_of,
    ffn_near,
    side_far,
    hidden_own,
    hidden_far,
    ffn_far,
    mixed_far,
    normed_far,
    cot_far,
    back_own,
    back_far,
    extra_own,
    extra_far,
    turned_own,
    turned_far,
    gain_own,
    gain_came,
    gain_all,
    sent_a,
    came_a0,
    hold_a,
    came_a1,
    came_a2,
    sent_b,
    came_b0,
    hold_b,
    came_b1,
    came_b2,
    sent_c,
    came_c0,
    came_c1,
    came_c2,
    deep_send,
    deep_recv,
    tail_sent_a,
    tail_came_a0,
    tail_came_a1,
    tail_came_a2,
    tail_sent_b,
    tail_came_b0,
    tail_came_b1,
    tail_came_b2,
    send_sems,
    recv_sems,
    tail_send,
    tail_recv,
    cot_send,
    cot_recv,
    back_send,
    back_recv,
    core_send,
    core_recv,
    gain_send,
    gain_recv,
    extra_send,
    extra_recv,
    load_sem,
    stage_sem,
    rows_sem,
    mate_send,
    mate_recv,
    relay_send,
    relay_recv,
    swap_send,
    swap_recv,
    near_sem,
):
    place, core = lax.axis_index("ctx"), lax.axis_index("fsdp")
    part, member = place // HALF, lax.rem(place, HALF)
    base = part * HALF - 1
    x, y, z = lax.rem(place, 2), lax.rem(place // 2, 2), place // 4
    wide = rows_of.shape[3]
    narrow = side_own.shape[1] // RING
    half_hidden = hidden_far.shape[1]
    half_width = ffn_far.shape[1]
    heads, pairs = query_hbm.shape[0], key_hbm.shape[0]
    scale = HEAD_DIM**-0.5
    partner = (place, 1 - core)

    def half(part, size):
        return pl.ds(pl.multiple_of(part * size, 128), size)

    stages = [
        pltpu.make_async_copy(source, target, stage_sem.at[index])
        for index, (source, target) in enumerate(
            (
                (home_hbm, home_ref),
                (side_hbm, side_own),
                (ffn_hbm, ffn_ref),
                (mixed_hbm, mixed_ref),
                (qkv_hbm, qkv_ref),
                (part_hbm, part_ref),
                (normed_hbm, normed_ref),
            )
        )
    ]
    own_hidden = pltpu.make_async_copy(
        hidden_hbm.at[:, half(core, half_hidden)], hidden_own, load_sem.at[0]
    )
    for stage in stages[:4]:
        stage.start()
    own_hidden.start()
    for stage in stages[4:]:
        stage.start()
    middle_load = pltpu.make_async_copy(middle_hbm, tokens_out, load_sem.at[1])
    middle_load.start()
    near = (place + 1 - 2 * x, place + 2 - 4 * y)
    greet([(lax.rem(place + step, RING), core) for step in range(1, RING)] + [partner])

    def remote(source, target, send, recv, peer):
        return pltpu.make_async_remote_copy(
            src_ref=source,
            dst_ref=target,
            send_sem=send,
            recv_sem=recv,
            device_id=peer,
            device_id_type=MESH,
        )

    def mate(step):
        return (part * HALF + lax.rem(member + step, HALF), core)

    def cot_copy(step):
        return remote(
            home_ref.at[lax.rem(member + step, HALF)],
            cot_far.at[member],
            cot_send.at[step],
            cot_recv.at[step],
            mate(step),
        )

    def core_copy(source, target, sem):
        return remote(source, target, core_send.at[sem], core_recv.at[sem], partner)

    def back_rows(chain, owner):
        return pair_hbm.at[owner, pl.ds(chain * wide, wide)]

    def owner_of(chain, slot):
        return block_owner(chain, place, 0, slot)

    def own_loads(chain, slot):
        loads = [
            pltpu.make_async_copy(
                back_rows(chain, owner_of(chain, slot)),
                rows_of.at[0, chain, slot],
                rows_sem.at[0, chain, slot],
            )
        ]
        if slot % 4 in EARLY:
            loads.append(
                pltpu.make_async_copy(
                    swap_hbm.at[chain, slot],
                    rows_of.at[2, chain, slot],
                    rows_sem.at[1, chain, slot],
                )
            )
        return loads

    def swap_copy(chain, slot):
        return remote(
            back_rows(chain, block_owner(chain, place, 1, slot)),
            rows_of.at[2, chain, slot],
            swap_send.at[chain, slot],
            swap_recv.at[chain, slot],
            (near[chain], core),
        )

    def swap(depth):
        for slot in (4 + depth, depth):
            for chain in range(2):
                swap_copy(chain, slot).start()

    def relay(depth):
        for slot in (4 + depth, depth):
            for chain in range(2):
                swap_copy(chain, slot).wait_recv()
                relay_copy(chain, slot).start()

    def mate_copy(chain, slot):
        return remote(
            back_rows(chain, owner_of(chain, slot)),
            rows_of.at[1, chain, slot],
            mate_send.at[chain, slot],
            mate_recv.at[chain, slot],
            partner,
        )

    def relay_copy(chain, slot):
        return remote(
            swap_hbm.at[chain, slot] if slot % 4 in EARLY else rows_of.at[2, chain, slot],
            rows_of.at[3, chain, slot],
            relay_send.at[chain, slot],
            relay_recv.at[chain, slot],
            partner,
        )

    near_load = pltpu.make_async_copy(near_hbm, ffn_near, near_sem)
    sides = [
        core_copy(ffn_hbm.at[:, half(1 - core, half_width)], ffn_far, 0),
        core_copy(mixed_hbm.at[half(1 - core, half_width), :], mixed_far, 1),
        core_copy(side_hbm, side_far, 2),
        core_copy(hidden_hbm.at[:, half(1 - core, half_hidden)], hidden_far, 3),
    ]
    stages[0].wait()
    for step in range(1, HALF):
        cot_copy(step).start()
    for copy in sides:
        copy.start()
    near_load.start()
    for depth in (2, 1, 3, 0):
        for slot in (4 + depth, depth):
            for chain in range(2):
                for load in own_loads(chain, slot):
                    load.start()
                mate_copy(chain, slot).start()
                if depth in EARLY:
                    relay_copy(chain, slot).start()
    normed_copy = core_copy(normed_hbm.at[:, half(1 - core, half_width)], normed_far, 4)
    normed_copy.start()
    cot_far[member] = home_ref[member]

    def down_product(rows, split):
        cols = slice(split[0] * 256, (split[0] + split[1]) * 256)
        down = jnp.dot(side_own[0, rows, :], hidden_own[:, cols], preferred_element_type=F32)
        return down + jnp.dot(side_far[0, rows, :], hidden_far[:, cols], preferred_element_type=F32)

    def deep_compute(owner, count):
        rows = pl.ds(pl.multiple_of(owner * narrow, 16), count * narrow)
        return down_product(rows, DOWN_CHUNKS[2])

    def deep_finish(window, value):
        chunk = DOWN_CHUNKS[2][0] + window.start // narrow
        down_out[:, chunk * 256 : chunk * 256 + 256] = value

    def compute(chain, owner, slot):
        lanes = pl.ds(chain * 256, 256)
        own_lanes = pl.ds(pl.multiple_of(core * half_width + chain * 256, 128), 256)
        rows = pl.ds(pl.multiple_of(owner * narrow, 16), narrow)
        values = []
        if slot is not None:
            for load in own_loads(chain, slot):
                load.wait()
            mate_copy(chain, slot).wait_recv()
            relay_copy(chain, slot).wait_recv()
            wide_sum = jnp.dot(
                rows_of[0, chain, slot],
                ffn_ref[:, half(core, half_width)],
                preferred_element_type=F32,
            )
            for source, columns in (
                (1, ffn_far[...]),
                (2, ffn_near[chain, 0]),
                (3, ffn_near[chain, 1]),
            ):
                wide_sum += jnp.dot(
                    rows_of[source, chain, slot], columns, preferred_element_type=F32
                )
            values += [(0, wide_sum[:, :256]), (wide, wide_sum[:, 256:])]
        chunks = DOWN_CHUNKS[chain][1]
        down = down_product(rows, DOWN_CHUNKS[chain])
        row = 2 * wide
        for chunk in range(chunks):
            values.append((row, down[:, chunk * 256 : chunk * 256 + 256]))
            row += narrow
        out = dot_dims(side_own[1, rows, :], mixed_ref[own_lanes, :], 1, 1)
        out += dot_dims(side_far[1, rows, :], mixed_far[lanes, :], 1, 1)
        values.append((row, out))
        return values

    def finish(chain, row, value):
        lanes = slice(chain * 256, chain * 256 + 256)
        if row < 2 * wide:
            target, low = (gate_out, up_out)[chain], row // wide * 256
            target[:, low : low + 256] = value
            return
        chunk = (row - 2 * wide) // narrow
        if chunk == DOWN_CHUNKS[chain][1]:
            out_out[:, lanes] = value
        else:
            chunk += DOWN_CHUNKS[chain][0]
            down_out[:, chunk * 256 : chunk * 256 + 256] = value

    chains = (
        Spread(
            0,
            compute,
            2 * wide,
            sent_a,
            (came_a0, came_a1, came_a2),
            hold_a,
            1,
            send_sems,
            recv_sems,
        ),
        Spread(
            1,
            compute,
            2 * wide,
            sent_b,
            (came_b0, came_b1, came_b2),
            hold_b,
            1,
            send_sems,
            recv_sems,
        ),
    )
    own_hidden.wait()
    for stage in stages[1:4]:
        stage.wait()
    for copy in sides:
        copy.wait_recv()

    def near_side(depth):
        for chain in chains:
            chain.stage_one(1, depth)

    def far_side(depth):
        for chain in chains:
            chain.stage_one(0, depth)

    def onward(depth):
        for chain in chains:
            chain.stage_two(depth)

    def deeper(depth):
        for chain in chains:
            chain.stage_three(depth)

    along = DeepSpread(
        deep_compute, sent_c, (came_c0, came_c1, came_c2), deep_send, deep_recv
    )
    near_side(2)
    for slot in (2, 1, 3):
        along.stage_one(slot)
    far_side(2)
    near_side(1)
    swap(1)
    near_load.wait()
    for stage in stages[4:]:
        stage.wait()

    def back_copy(step):
        return remote(
            back_own.at[lax.rem(member + step, HALF)],
            back_far.at[member],
            back_send.at[step],
            back_recv.at[step],
            mate(step),
        )

    def extra_copy(group):
        return remote(
            extra_own,
            extra_far.at[group],
            extra_send.at[group],
            extra_recv.at[group],
            (HALF - 1, core),
        )

    def attention(
        scaled, cots, natural, delta_ref, query_acc, key_nat, value_nat, pair_acc
    ):
        def widen(ref, i, row):
            return jnp.concatenate(
                [ref[i, row : row + HEAD_DIM, :], ref[i, row + HEAD_DIM : row + 2 * HEAD_DIM, :]],
                axis=1,
            )

        def prepare(i, nothing):
            @pl.when(i != member)
            def _():
                cot_copy(lax.rem(member - i + HALF, HALF)).wait_recv()

            query = widen(qkv_ref, i + 1, 0) * jnp.asarray(scale, BF16)
            cot = widen(cot_far, i, 0)
            scaled[i] = query
            cots[i] = cot
            natural[i] = transposed(jnp.concatenate([query, cot], axis=0))
            delta_ref[i] = jnp.sum(
                cot.astype(F32) * widen(part_ref, i, 0).astype(F32), axis=0, keepdims=True
            )
            query_acc[i] = jnp.zeros(query_acc.shape[1:], F32)
            return nothing

        def per_key(j, nothing):
            key_t = qkv_ref[j, 2 * HEAD_DIM : 3 * HEAD_DIM, :]
            key_nat[...] = transposed(key_t)
            value_nat[...] = transposed(qkv_ref[j, 3 * HEAD_DIM : 4 * HEAD_DIM, :])
            shape = (BLOCK, 2 * BLOCK)
            key_place = (base + j) * BLOCK + lax.broadcasted_iota(jnp.int32, shape, 0)

            def step(diagonal, i):
                start = jnp.concatenate([start_ref[i - 1]] * 2, axis=1)
                scores = jnp.dot(key_nat[...], scaled[i - 1], preferred_element_type=F32)
                grad_probs = jnp.dot(value_nat[...], cots[i - 1], preferred_element_type=F32)
                ok = key_place >= start
                if diagonal:
                    places = (base + i) * BLOCK + lax.broadcasted_iota(jnp.int32, (1, BLOCK), 1)
                    ok = ok & (key_place <= jnp.concatenate([places] * 2, axis=1))
                probs = jnp.where(ok, jnp.exp(scores) * inv_ref[i - 1], 0.0)
                grad_scores = (probs * (grad_probs - delta_ref[i - 1])).astype(BF16)
                both_low = jnp.concatenate([grad_scores, probs.astype(BF16)], axis=0)
                query_acc[i - 1] += jnp.dot(
                    qkv_ref[j, 2 * HEAD_DIM : 3 * HEAD_DIM, :],
                    grad_scores,
                    preferred_element_type=F32,
                )
                return jnp.dot(both_low, natural[i - 1], preferred_element_type=F32)

            @pl.when(j == 0)
            def _():
                pair_acc[...] = jnp.zeros(pair_acc.shape, F32)

            @pl.when(j > 0)
            def _():
                pair_acc[...] = step(True, j)

            def one(i, carry):
                pair_acc[...] += step(False, i)
                return carry

            def two(index, carry):
                i = j + 1 + 2 * index
                pair_acc[...] += step(False, i) + step(False, i + 1)
                return carry

            count = (HALF - j) // 2
            lax.fori_loop(0, count, two, 0)
            lax.fori_loop(j + 1 + 2 * count, HALF + 1, one, 0)
            first = lax.broadcasted_iota(jnp.int32, (BLOCK, 2 * HEAD_DIM), 1) < HEAD_DIM
            merged = jnp.where(first, pair_acc[0:BLOCK, :], pair_acc[BLOCK:, :]).T.astype(BF16)

            @pl.when(j == 0)
            def _():
                extra_own[...] = merged
                extra_copy(member).start()

            @pl.when(j > 0)
            def _():
                query_grad = (query_acc[j - 1] * scale).astype(BF16)
                back_own[j - 1, 0:HEAD_DIM, :] = query_grad[:, :BLOCK]
                back_own[j - 1, HEAD_DIM : 2 * HEAD_DIM, :] = query_grad[:, BLOCK:]
                back_own[j - 1, 2 * HEAD_DIM : 4 * HEAD_DIM, :] = merged

            @pl.when((j > 0) & (j - 1 != member))
            def _():
                back_copy(lax.rem(j - 1 - member + HALF, HALF)).start()

            @pl.when(j == 1)
            def _():
                onward(2)
                far_side(1)
                swap(3)

            @pl.when(j == 2)
            def _():
                near_side(3)
                far_side(3)

            @pl.when(j == 4)
            def _():
                relay(1)
                onward(1)
                swap(0)

            @pl.when(j == 6)
            def _():
                deeper(2)

            return nothing

        lax.fori_loop(0, HALF, prepare, 0)
        lax.fori_loop(1 - part, HALF + 1, per_key, 0)
        back_far[member] = back_own[member]

    pl.run_scoped(
        attention,
        pltpu.VMEM((HALF, HEAD_DIM, 2 * BLOCK), BF16),
        pltpu.VMEM((HALF, HEAD_DIM, 2 * BLOCK), BF16),
        pltpu.VMEM((HALF, 2 * BLOCK, 2 * HEAD_DIM), BF16),
        pltpu.VMEM((HALF, 1, 2 * BLOCK), F32),
        pltpu.VMEM((HALF, HEAD_DIM, 2 * BLOCK), F32),
        pltpu.VMEM((BLOCK, HEAD_DIM), BF16),
        pltpu.VMEM((BLOCK, HEAD_DIM), BF16),
        pltpu.VMEM((2 * BLOCK, 2 * HEAD_DIM), F32),
    )

    turned_copy = core_copy(turned_own, turned_far, 5)

    def tail_compute(chain, owner, slot):
        lanes = slice(chain * 256, chain * 256 + 256)
        own_lanes = pl.ds(pl.multiple_of(core * half_width + chain * 256, 128), 256)
        values, row = [], 0
        for size, base in ((heads, 2 * pairs), (pairs, 0), (pairs, pairs)):
            count = size * HEAD_DIM // RING
            rows = pl.ds(pl.multiple_of(base * HEAD_DIM + owner * count, 16), count)
            value = jnp.dot(
                turned_own[rows, :], normed_ref[:, own_lanes], preferred_element_type=F32
            )
            value += jnp.dot(turned_far[rows, :], normed_far[:, lanes], preferred_element_type=F32)
            values.append((row, value))
            row += count
        return values

    def tail_finish(chain, row, value):
        grads_out[row : row + value.shape[0], chain * 256 : chain * 256 + 256] = value

    tails = (
        Spread(
            0,
            tail_compute,
            0,
            tail_sent_a,
            (tail_came_a0, tail_came_a1, tail_came_a2),
            tail_came_a0,
            0,
            tail_send,
            tail_recv,
        ),
        Spread(
            1,
            tail_compute,
            0,
            tail_sent_b,
            (tail_came_b0, tail_came_b1, tail_came_b2),
            tail_came_b0,
            0,
            tail_send,
            tail_recv,
        ),
    )

    def finish_all(natural, summed, query_ref, key_ref, tokens_ref, weights_ref):
        loads = [
            pltpu.make_async_copy(query_hbm, query_ref, load_sem.at[2]),
            pltpu.make_async_copy(key_hbm, key_ref, load_sem.at[3]),
            pltpu.make_async_copy(tokens_hbm, tokens_ref, load_sem.at[4]),
            pltpu.make_async_copy(weights_hbm, weights_ref, load_sem.at[5]),
        ]
        for copy in loads:
            copy.start()
        half_dim = HEAD_DIM // 2
        cosine, sine = table_ref[0:half_dim, :], table_ref[half_dim:HEAD_DIM, :]
        query_gain = table_ref[HEAD_DIM : 2 * HEAD_DIM, :]
        key_gain = table_ref[2 * HEAD_DIM : 3 * HEAD_DIM, :]

        def head_rows(index):
            return pl.ds(pl.multiple_of(index * HEAD_DIM, HEAD_DIM), HEAD_DIM)

        def query_head(head, total):
            low = pl.multiple_of(lax.rem(head, 2) * HEAD_DIM, HEAD_DIM)
            upstream = turn_back(
                back_far[head // 2, pl.ds(low, HEAD_DIM), :].astype(F32), cosine, sine
            )
            back, terms = column_norm_back(query_ref[head], query_gain, upstream)
            turned_own[head_rows(2 * pairs + head), :] = back.astype(BF16)
            return total + terms

        def key_head(pair, total):
            upstream = back_far[pair, 2 * HEAD_DIM : 4 * HEAD_DIM, :].astype(F32)
            upstream += extra_far[pair].astype(F32)
            back, terms = column_norm_back(
                key_ref[pair],
                key_gain,
                turn_back(upstream[:HEAD_DIM], cosine, sine),
            )
            turned_own[head_rows(pair), :] = back.astype(BF16)
            turned_own[head_rows(pairs + pair), :] = upstream[HEAD_DIM:].astype(BF16)
            return total + terms


        along.stage_two()
        relay(3)
        near_side(0)
        onward(3)
        deeper(1)
        far_side(0)

        def arrive(step, nothing):
            back_copy(step).wait_recv()
            return nothing

        lax.fori_loop(1, HALF, arrive, 0)

        def extra_arrive(group, nothing):
            extra_copy(group).wait_recv()
            return nothing

        @pl.when(place == HALF - 1)
        def _():
            lax.fori_loop(0, HALF, extra_arrive, 0)

        @pl.when(place != HALF - 1)
        def _():
            extra_far[...] = jnp.zeros(extra_far.shape, BF16)

        for copy in loads:
            copy.wait()
        nothing = jnp.zeros((HEAD_DIM, BLOCK), F32)
        query_terms = lax.fori_loop(0, heads, query_head, nothing)
        key_terms = lax.fori_loop(0, pairs, key_head, nothing)
        turned_copy.start()
        for row in range(0, turned_own.shape[0], 128):
            natural[:, row : row + 128] = turned_own[row : row + 128, :].astype(F32).T.astype(BF16)
        normed_copy.wait_recv()
        turned_copy.wait_recv()

        def tail_one(index, carry):
            for chain in tails:
                chain.stage_one(1 - index // 4, lax.rem(index + 1, 4))
            return carry

        lax.fori_loop(0, 8, tail_one, 0)
        along.stage_three()
        relay(0)
        onward(0)
        deeper(3)
        summed[...] = dot_dims(natural[...], weights_ref[...], 1, 1)
        middle_load.wait()

        def token_rows(index, total):
            rows = pl.ds(pl.multiple_of(index * 32, 32), 32)
            values, upstream = tokens_ref[rows, :].astype(F32), summed[rows, :]
            inverse = lax.rsqrt(jnp.mean(values * values, axis=-1, keepdims=True) + EPSILON)
            scaled = upstream * attn_gain_ref[...]
            weight = jnp.sum(scaled * values, axis=-1, keepdims=True) / values.shape[1]
            tokens_out[rows, :] += inverse * scaled - values * inverse**3 * weight
            return total + jnp.sum(upstream * values * inverse, axis=0, keepdims=True)

        terms = lax.fori_loop(
            0, BLOCK // 32, token_rows, jnp.zeros((1, tokens_ref.shape[1]), F32)
        )
        gain_own[...] = jnp.zeros(gain_own.shape, F32)
        gain_own[0:1, :] = terms
        gain_own[1:2, :] = ffn_terms_ref[...]
        gain_own[2:3, 0:HEAD_DIM] = jnp.sum(query_terms.T, axis=0, keepdims=True)
        gain_own[3:4, 0:HEAD_DIM] = jnp.sum(key_terms.T, axis=0, keepdims=True)

    width = normed_ref.shape[1]
    pl.run_scoped(
        finish_all,
        pltpu.VMEM((BLOCK, turned_own.shape[0]), BF16),
        pltpu.VMEM((BLOCK, width), F32),
        pltpu.VMEM((heads, HEAD_DIM, BLOCK), F32),
        pltpu.VMEM((pairs, HEAD_DIM, BLOCK), F32),
        pltpu.VMEM((BLOCK, width), BF16),
        pltpu.VMEM(weights_hbm.shape, BF16),
    )

    def tail_two(index, carry):
        for chain in tails:
            chain.stage_two(lax.rem(index + 1, 4))
        return carry

    def tail_three(depth, carry):
        for chain in tails:
            chain.stage_three(depth)
        return carry

    gain_swap = core_copy(gain_own, gain_came, 22)
    gain_swap.start()

    def gain_copy(step):
        peer = (lax.rem(place + step, RING), core)
        return remote(
            gain_all.at[place], gain_all.at[place], gain_send.at[step], gain_recv.at[step], peer
        )

    def gain_start(step, carry):
        gain_copy(step).start()
        return carry

    def gain_arrive(step, carry):
        gain_copy(step).wait()
        return carry

    gain_swap.wait()
    gain_all[place] = gain_own[...] + gain_came[...]
    lax.fori_loop(1, RING, gain_start, 0)
    lax.fori_loop(0, 4, tail_two, 0)
    lax.fori_loop(1, 4, tail_three, 0)
    along.close(deep_finish)
    for chain in chains:
        chain.close(finish)
    for chain in tails:
        chain.close(tail_finish)
    lax.fori_loop(1, RING, gain_arrive, 0)

    def gain_sum(index, total):
        return total + gain_all[index]

    gains_out[...] = lax.fori_loop(1, RING, gain_sum, gain_all[0])

    def settle(step, nothing):
        back_copy(step).wait_send()
        cot_copy(step).wait_send()
        return nothing

    lax.fori_loop(1, HALF, settle, 0)

    @pl.when(part == 1)
    def _():
        extra_copy(member).wait_send()

    for copy in sides + [normed_copy, turned_copy]:
        copy.wait_send()
    for slot in range(8):
        for chain in range(2):
            mate_copy(chain, slot).wait_send()
            relay_copy(chain, slot).wait_send()
            if slot % 4 not in EARLY:
                swap_copy(chain, slot).wait_send()
    for chain in chains + tails + (along,):
        chain.drain()


def back_call(call_id, inputs, loads):
    hidden, side, ffn_low = inputs[1:4]
    rows, hidden_width = hidden.shape
    width = ffn_low.shape[1]
    wide, narrow = hidden_width // RING, width // RING
    total = (HEADS + 2 * KV_HEADS) * HEAD_DIM

    def buffers(sizes):
        return [
            pltpu.VMEM((slots, sizes[chain], 256), BF16)
            for chain in range(2)
            for slots in (8, 8, 4, 3)
        ]

    def chain_buffers(split):
        rest = (split[1] + 1) * narrow
        shapes = ((8, rest), (8, rest), (7, 2 * wide + rest), (4, 2 * wide + rest), (3, 2 * wide + rest))
        return [pltpu.VMEM((*shape, 256), BF16) for shape in shapes]

    dma = pltpu.SemaphoreType.DMA
    specs = [VMEM_SPEC] * (len(inputs) + len(loads))
    staged = (2, 3, 4, 5, 6, 8, 11)
    for index in (0, 1, *staged, *range(len(inputs), len(specs))):
        specs[index] = HBM_SPEC
    return pl.pallas_call(
        back_kernel,
        out_shape=(
            jax.ShapeDtypeStruct((wide, width // 2), F32),
            jax.ShapeDtypeStruct((wide, width // 2), F32),
            jax.ShapeDtypeStruct((narrow, hidden_width // 2), F32),
            jax.ShapeDtypeStruct((narrow, width // 2), F32),
            jax.ShapeDtypeStruct((total // RING, width // 2), F32),
            jax.ShapeDtypeStruct((rows, width), F32),
            jax.ShapeDtypeStruct((4, width), F32),
        ),
        in_specs=specs,
        out_specs=(VMEM_SPEC,) * 7,
        scratch_shapes=[pltpu.VMEM(inputs[index].shape, BF16) for index in staged]
        + [
            pltpu.VMEM((4, 2, 8, wide, rows), BF16),
            pltpu.VMEM((2, 2, rows, width // 2), BF16),
            pltpu.VMEM(side.shape, BF16),
            pltpu.VMEM((rows, hidden_width // 2), BF16),
            pltpu.VMEM((rows, hidden_width // 2), BF16),
            pltpu.VMEM((rows, width // 2), BF16),
            pltpu.VMEM((width // 2, rows), BF16),
            pltpu.VMEM((rows, width // 2), BF16),
            pltpu.VMEM((HALF, 2 * HEAD_DIM, rows), BF16),
            pltpu.VMEM((HALF, 4 * HEAD_DIM, rows), BF16),
            pltpu.VMEM((HALF, 4 * HEAD_DIM, rows), BF16),
            pltpu.VMEM((2 * HEAD_DIM, rows), BF16),
            pltpu.VMEM((HALF, 2 * HEAD_DIM, rows), BF16),
            pltpu.VMEM((total, rows), BF16),
            pltpu.VMEM((total, rows), BF16),
            pltpu.VMEM((4, width), F32),
            pltpu.VMEM((4, width), F32),
            pltpu.VMEM((RING, 4, width), F32),
        ]
        + chain_buffers(DOWN_CHUNKS[0])
        + chain_buffers(DOWN_CHUNKS[1])
        + [pltpu.VMEM((*lead, DOWN_CHUNKS[2][1] * narrow, 256), BF16) for lead in ((3, 4), (3, 4), (2,), (1,))]
        + [dma((6,)), dma((6,))]
        + buffers((total // RING, total // RING))
        + [dma((2, 15))] * 4
        + [dma((HALF,))] * 4
        + [dma((23,))] * 2
        + [dma((RING,))] * 2
        + [dma((HALF,))] * 2
        + [dma((6,)), dma((7,))]
        + [dma((2, 2, 8))]
        + [dma((2, 8))] * 6
        + [dma],
        compiler_params=pltpu.CompilerParams(
            collective_id=call_id, has_side_effects=True, vmem_limit_bytes=63 << 20
        ),
        name="backward_spread",
    )(*inputs, *loads)


def head_frequencies(rows):
    half = HEAD_DIM // 2
    frequencies = THETA ** (-(2.0 / HEAD_DIM) * np.arange(half, dtype=np.float32))
    return jnp.asarray(np.repeat(frequencies.astype(np.float32)[:, None], rows, axis=1))


def front_kernel(
    gain_ref,
    place_ref,
    query_gain_ref,
    key_gain_ref,
    frequency_ref,
    tokens_hbm,
    w_query_hbm,
    w_key_hbm,
    w_value_hbm,
    w_out_hbm,
    w_gate_hbm,
    w_up_hbm,
    w_down_hbm,
    qkv_out,
    starts_out,
    normed_out,
    part_out,
    mixed_out,
    inv_out,
    out_full,
    table_ref,
    query_hbm,
    key_hbm,
    weights_hbm,
    gate_far,
    up_far,
    down_far,
    home,
    key_nat,
    totals,
    accs,
    tokens_ref,
    query_out,
    key_out,
    weights_out,
    own_start_ref,
    keep_sem,
    own_sem,
    send_sem,
    recv_sem,
    start_send,
    start_recv,
    mixed_send,
    mixed_recv,
    kv_send,
    kv_recv,
    extra_send,
    extra_recv,
    core_send,
    core_recv,
):
    place, core = lax.axis_index("ctx"), lax.axis_index("fsdp")
    part, member = place // HALF, lax.rem(place, HALF)
    rows = tokens_ref.shape[0]
    depth = w_query_hbm.shape[0]
    partner = (place, 1 - core)
    tokens_load = pltpu.make_async_copy(tokens_hbm, tokens_ref, keep_sem.at[0])
    tokens_load.start()
    places = place * rows + lax.broadcasted_iota(jnp.int32, (1, rows), 1)
    own_start_ref[...] = places - place_ref[...]
    angles = frequency_ref[...] * place_ref[...].astype(F32)
    half = HEAD_DIM // 2
    table_ref[0:half, :] = jnp.cos(angles)
    table_ref[half:HEAD_DIM, :] = jnp.sin(angles)
    for index, source in enumerate((query_gain_ref, key_gain_ref)):
        table_ref[(index + 1) * HEAD_DIM : (index + 2) * HEAD_DIM, :] = jnp.broadcast_to(
            source[...], (rows, HEAD_DIM)
        ).T
    greet([partner] + [(lax.rem(place + step, RING), core) for step in range(1, RING)])

    def remote(source, target, send, recv, peer):
        return pltpu.make_async_remote_copy(
            src_ref=source,
            dst_ref=target,
            send_sem=send,
            recv_sem=recv,
            device_id=peer,
            device_id_type=MESH,
        )

    def mate(step):
        return (part * HALF + lax.rem(member + step, HALF), core)

    copies, near_copies = [], []

    def share(source, target, near_target=None):
        index = len(copies)
        copy = remote(source, target, core_send.at[index], core_recv.at[index], partner)
        copy.start()
        copies.append(copy)
        if near_target is not None:
            near = pltpu.make_async_copy(source, near_target, own_sem.at[index])
            near.start()
            near_copies.append(near)

    column = 0
    own_depth = pl.ds(pl.multiple_of(core * depth, 128), depth)
    for source in (w_key_hbm, w_value_hbm, w_query_hbm):
        window = pl.ds(column, source.shape[1])
        target = weights_out.at[own_depth, window]
        share(source, target, target)
        column += source.shape[1]

    target = out_full.at[own_depth, :]
    share(w_out_hbm, target, target)
    for source, target in ((w_gate_hbm, gate_far), (w_up_hbm, up_far), (w_down_hbm, down_far)):
        share(source, target)

    def start_copy(step):
        return remote(
            own_start_ref,
            starts_out.at[member],
            start_send.at[step],
            start_recv.at[step],
            mate(step),
        )

    for step in range(1, HALF):
        start_copy(step).start()
    starts_out[member] = own_start_ref[...]

    def norm_rows(index, nothing):
        window = pl.ds(pl.multiple_of(index * 32, 32), 32)
        values = tokens_ref[window, :].astype(F32)
        inverse = lax.rsqrt(jnp.mean(values * values, axis=-1, keepdims=True) + EPSILON)
        normed_out[window, :] = (values * inverse * gain_ref[...]).astype(BF16)
        return nothing

    tokens_load.wait()
    lax.fori_loop(0, rows // 32, norm_rows, 0)
    cosine, sine = table_ref[0:half, :], table_ref[half:HEAD_DIM, :]
    query_gain = table_ref[HEAD_DIM : 2 * HEAD_DIM, :]
    key_gain = table_ref[2 * HEAD_DIM : 3 * HEAD_DIM, :]

    def project(column, count):
        window = pl.ds(column, count)
        product = jnp.dot(normed_out[...], weights_out[:, window], preferred_element_type=F32)
        return product.T

    def turned(values, gain):
        mean = jnp.mean(values * values, axis=0, keepdims=True)
        values = values * lax.rsqrt(mean + EPSILON) * gain
        first, second = values[:half], values[half:]
        return jnp.concatenate(
            [first * cosine - second * sine, second * cosine + first * sine], axis=0
        ).astype(BF16)

    kv_width = KV_HEADS * HEAD_DIM
    copies[0].wait_recv()
    near_copies[0].wait()

    def key_chunk(index, nothing):
        products = project(pl.multiple_of(index * 256, 256), 256)
        for offset in range(4):
            raw = products[offset * HEAD_DIM : (offset + 1) * HEAD_DIM]
            group = index * 4 + offset
            key_out[group] = raw
            home[group, 2 * HEAD_DIM : 3 * HEAD_DIM, :] = turned(raw, key_gain)
        return nothing

    lax.fori_loop(0, KV_HEADS // 4, key_chunk, 0)
    copies[1].wait_recv()
    near_copies[1].wait()

    def value_chunk(index, nothing):
        products = project(pl.multiple_of(kv_width + index * 256, 256), 256)
        for offset in range(4):
            value = products[offset * HEAD_DIM : (offset + 1) * HEAD_DIM].astype(BF16)
            home[index * 4 + offset, 3 * HEAD_DIM : 4 * HEAD_DIM, :] = value
        return nothing

    lax.fori_loop(0, KV_HEADS // 4, value_chunk, 0)

    window = pl.ds(2 * HEAD_DIM, 2 * HEAD_DIM)

    def kv_copy(step):
        return remote(
            home.at[lax.rem(member + step, HALF), window],
            qkv_out.at[1 + member, window],
            kv_send.at[step],
            kv_recv.at[step],
            mate(step),
        )

    def kv_start(step, nothing):
        kv_copy(HALF - step).start()
        return nothing

    def extra_copy(group):
        return remote(
            home.at[group, window, pl.ds(rows - EDGE, EDGE)],
            qkv_out.at[0, window, pl.ds(rows - EDGE, EDGE)],
            extra_send.at[group],
            extra_recv.at[group],
            (HALF + group, core),
        )

    def extra_start(group, nothing):
        extra_copy(group).start()
        return nothing

    @pl.when(place == HALF - 1)
    def _():
        lax.fori_loop(0, HALF, extra_start, 0)

    lax.fori_loop(1, HALF, kv_start, 0)
    copies[2].wait_recv()
    near_copies[2].wait()

    def block_copy(step):
        peer = mate(step)
        return remote(
            home.at[lax.rem(member + step, HALF), pl.ds(0, 2 * HEAD_DIM)],
            qkv_out.at[1 + member, pl.ds(0, 2 * HEAD_DIM)],
            send_sem.at[step],
            recv_sem.at[step],
            peer,
        )

    def query_chunk(turn, nothing):
        index = lax.rem(member // 2 - turn + 4, 4)
        products = project(pl.multiple_of(2 * kv_width + index * 256, 256), 256)
        for offset in range(4):
            raw = products[offset * HEAD_DIM : (offset + 1) * HEAD_DIM]
            query_out[index * 4 + offset] = raw
            low = (offset % 2) * HEAD_DIM
            home[index * 2 + offset // 2, low : low + HEAD_DIM, :] = turned(
                raw, query_gain
            )
        for offset in range(2):
            group = index * 2 + offset

            @pl.when(group != member)
            def _():
                block_copy(lax.rem(group - member + HALF, HALF)).start()

        return nothing

    lax.fori_loop(0, HEADS // 4, query_chunk, 0)
    keeps = [
        pltpu.make_async_copy(source, target, keep_sem.at[1 + index])
        for index, (source, target) in enumerate(
            ((query_out, query_hbm), (key_out, key_hbm), (weights_out, weights_hbm))
        )
    ]
    for keep in keeps:
        keep.start()
    qkv_out[1 + member] = home[member]
    base = part * HALF - 1

    def mixed_copy(step):
        peer = mate(step)
        return remote(
            part_out.at[lax.rem(member + step, HALF)],
            mixed_out.at[member],
            mixed_send.at[step],
            mixed_recv.at[step],
            peer,
        )

    def query_of(i):
        query_t = jnp.concatenate(
            [qkv_out[i, 0:HEAD_DIM, :], qkv_out[i, HEAD_DIM : 2 * HEAD_DIM, :]], axis=1
        ) * jnp.asarray(HEAD_DIM**-0.5, BF16)
        return query_t, jnp.concatenate([starts_out[i - 1]] * 2, axis=1)

    def meet(query_t, keys, values, ok, carry):
        total, acc = carry
        probs = jnp.exp(jnp.dot(keys, query_t, preferred_element_type=F32))
        probs = jnp.where(ok(lax.broadcasted_iota(jnp.int32, probs.shape, 0)), probs, 0.0)
        total = total + jnp.sum(probs, axis=0, keepdims=True)
        return total, acc + jnp.dot(values, probs.astype(BF16), preferred_element_type=F32)

    def fetch(i, nothing):
        @pl.when(i - 1 != member)
        def _():
            step = lax.rem(member - i + 1 + HALF, HALF)
            start_copy(step).wait_recv()
            kv_copy(step).wait_recv()
            block_copy(step).wait_recv()

        key_nat[i] = transposed(qkv_out[i, 2 * HEAD_DIM : 3 * HEAD_DIM, :])
        return nothing

    def inner(i):
        query_t, start = query_of(i)
        places = (base + i) * BLOCK + lax.broadcasted_iota(jnp.int32, (1, BLOCK), 1)
        query_place = jnp.concatenate([places] * 2, axis=1)

        def step(diagonal, j, carry):
            def ok(offset):
                key_place = (base + j) * BLOCK + offset
                if diagonal:
                    return (key_place >= start) & (key_place <= query_place)
                return key_place >= start

            values = qkv_out[j, 3 * HEAD_DIM : 4 * HEAD_DIM, :]
            return meet(query_t, key_nat[j], values, ok, carry)

        carry = (jnp.zeros((1, 2 * BLOCK), F32), jnp.zeros((HEAD_DIM, 2 * BLOCK), F32))
        pairs = (i - 1) // 2

        def two(index, carry):
            return step(False, 2 * index + 2, step(False, 2 * index + 1, carry))

        carry = lax.fori_loop(0, pairs, two, carry)
        carry = lax.fori_loop(2 * pairs + 1, i, functools.partial(step, False), carry)
        totals[i - 1], accs[i - 1] = step(True, i, carry)

    def outer(i):
        @pl.when((part == 1) & (i == 1))
        def _():
            extra_copy(member).wait_recv()
            qkv_out[0, 2 * HEAD_DIM :, 0 : rows - EDGE] = jnp.zeros(
                (2 * HEAD_DIM, rows - EDGE), BF16
            )
            key_nat[0] = transposed(qkv_out[0, 2 * HEAD_DIM : 3 * HEAD_DIM, :])

        @pl.when(part == 1)
        def _():
            query_t, start = query_of(i)

            def ok(offset):
                return HALF * BLOCK - EDGE + offset >= start

            values = qkv_out[0, 3 * HEAD_DIM : 4 * HEAD_DIM, rows - EDGE :]
            totals[i - 1], accs[i - 1] = meet(
                query_t, key_nat[0, rows - EDGE :, :], values, ok, (totals[i - 1], accs[i - 1])
            )

        inverse = 1.0 / totals[i - 1]
        low = (accs[i - 1] * inverse).astype(BF16)
        part_out[i - 1, 0:HEAD_DIM, :] = low[:, :BLOCK]
        part_out[i - 1, HEAD_DIM:, :] = low[:, BLOCK:]
        inv_out[i - 1] = inverse

        @pl.when(i - 1 != member)
        def _():
            mixed_copy(lax.rem(i - 1 - member + HALF, HALF)).start()

    def order(turn):
        return turn + turn // 5 * (5 + lax.rem(turn + 3 + member, 4) - turn)

    def per_query(turn, nothing):
        @pl.when(turn <= 4)
        def _():
            fetch(turn, 0)

        @pl.when(turn == 5)
        def _():
            lax.fori_loop(5, HALF + 1, fetch, 0)

        @pl.when(turn <= HALF)
        def _():
            inner(order(turn))

        @pl.when(turn > lag)
        def _():
            outer(order(turn - lag))

        return nothing

    lag = 1
    lax.fori_loop(1, HALF + lag + 1, per_query, 0)
    mixed_out[member] = part_out[member]

    def settle(step, nothing):
        block_copy(step).wait_send()
        kv_copy(step).wait_send()
        start_copy(step).wait_send()
        mixed_copy(step).wait()
        return nothing

    lax.fori_loop(1, HALF, settle, 0)

    def extra_settle(group, nothing):
        extra_copy(group).wait_send()
        return nothing

    @pl.when(place == HALF - 1)
    def _():
        lax.fori_loop(0, HALF, extra_settle, 0)

    for copy in copies[:3]:
        copy.wait_send()
    for copy in copies[3:]:
        copy.wait()
    for near in near_copies[3:] + keeps:
        near.wait()


def front_call(call_id, inputs, loads):
    rows, width = loads[0].shape
    half_depth, hidden_width = loads[5].shape
    total = (HEADS + 2 * KV_HEADS) * HEAD_DIM
    dma = pltpu.SemaphoreType.DMA
    query_raw = (HEADS, HEAD_DIM, rows)
    key_raw = (KV_HEADS, HEAD_DIM, rows)
    return pl.pallas_call(
        front_kernel,
        out_shape=(
            jax.ShapeDtypeStruct((HALF + 1, 4 * HEAD_DIM, rows), BF16),
            jax.ShapeDtypeStruct((HALF, 1, rows), jnp.int32),
            jax.ShapeDtypeStruct((rows, width), BF16),
            jax.ShapeDtypeStruct((HALF, 2 * HEAD_DIM, rows), BF16),
            jax.ShapeDtypeStruct((HALF, 2 * HEAD_DIM, rows), BF16),
            jax.ShapeDtypeStruct((HALF, 1, 2 * rows), F32),
            jax.ShapeDtypeStruct((width, width), BF16),
            jax.ShapeDtypeStruct((3 * HEAD_DIM, rows), F32),
            jax.ShapeDtypeStruct(query_raw, F32),
            jax.ShapeDtypeStruct(key_raw, F32),
            jax.ShapeDtypeStruct((width, total), BF16),
            jax.ShapeDtypeStruct((half_depth, hidden_width), BF16),
            jax.ShapeDtypeStruct((half_depth, hidden_width), BF16),
            jax.ShapeDtypeStruct((hidden_width // 2, width), BF16),
        ),
        in_specs=[VMEM_SPEC] * len(inputs) + [HBM_SPEC] * len(loads),
        out_specs=(VMEM_SPEC,) * 8 + (HBM_SPEC,) * 6,
        scratch_shapes=[
            pltpu.VMEM((HALF, 4 * HEAD_DIM, rows), BF16),
            pltpu.VMEM((HALF + 1, rows, HEAD_DIM), BF16),
            pltpu.VMEM((HALF, 1, 2 * rows), F32),
            pltpu.VMEM((HALF, HEAD_DIM, 2 * rows), F32),
            pltpu.VMEM((rows, width), BF16),
            pltpu.VMEM(query_raw, F32),
            pltpu.VMEM(key_raw, F32),
            pltpu.VMEM((width, total), BF16),
            pltpu.VMEM((1, rows), jnp.int32),
            dma((4,)),
            dma((4,)),
        ]
        + [dma((HALF,))] * 10
        + [dma((7,))] * 2,
        compiler_params=pltpu.CompilerParams(
            collective_id=call_id, has_side_effects=True, vmem_limit_bytes=63 << 20
        ),
        name="front_heads",
    )(*inputs, *loads)


def ffn_kernel(
    tokens_ref,
    mixed_ref,
    w_out_ref,
    gain_ref,
    cot_ref,
    gate_own,
    gate_far,
    up_own,
    up_far,
    down_own,
    down_far,
    pair_hbm,
    hidden_out,
    output_out,
    ffn_out,
    side_out,
    mixed_back_out,
    grad_middle_out,
    terms_out,
    swap_out,
    near_out,
    pair_out,
    pair_sem,
    middle,
    result,
    upstream,
    middle_low,
    swap_send,
    swap_recv,
    near_send,
    near_recv,
):
    step = pl.program_id(0)
    place, core = lax.axis_index("ctx"), lax.axis_index("fsdp")
    x, y, z = lax.rem(place, 2), lax.rem(place // 2, 2), place // 4
    near = (place + 1 - 2 * x, place + 2 - 4 * y)
    wide = pair_out.shape[1] // 2
    half_width = gate_own.shape[0]
    strip_owners = pair_out.shape[0] // 4
    plane = lax.rem(z + 6 - step, 4)

    def remote(source, target, send, recv, peer):
        return pltpu.make_async_remote_copy(
            src_ref=source,
            dst_ref=target,
            send_sem=send,
            recv_sem=recv,
            device_id=peer,
            device_id_type=MESH,
        )

    def keep_pair(turn):
        window = pl.ds(lax.rem(z + 6 - turn, 4) * strip_owners, strip_owners)
        return pltpu.make_async_copy(pair_out.at[window], pair_hbm.at[window], pair_sem.at[turn])

    def near_copy(chain, other):
        target = core if other == 0 else 1 - core
        lanes = pl.ds(pl.multiple_of(target * half_width, 128), half_width)
        return remote(
            ffn_out.at[:, lanes],
            near_out.at[chain, other],
            near_send.at[chain, other],
            near_recv.at[chain, other],
            (near[chain], target),
        )

    def swap_copy(chain, slot):
        return remote(
            pair_out.at[block_owner(chain, place, 1, slot), pl.ds(chain * wide, wide)],
            swap_out.at[chain, slot],
            swap_send.at[chain, slot],
            swap_recv.at[chain, slot],
            (near[chain], core),
        )

    rows, width = tokens_ref.shape
    strip = 32

    def strips(work):
        def one(index, carry):
            return work(pl.ds(pl.multiple_of(index * strip, strip), strip), carry)

        return one

    @pl.when(step == 0)
    def _():
        mixed = mixed_ref[...].astype(F32).T.astype(BF16)
        middle[...] = tokens_ref[...].astype(F32) + jnp.dot(
            mixed, w_out_ref[...], preferred_element_type=F32
        )

        def norm(window, carry):
            values = middle[window, :]
            inverse = lax.rsqrt(jnp.mean(values * values, axis=-1, keepdims=True) + EPSILON)
            ffn_out[window, :] = (values * inverse * gain_ref[...]).astype(BF16)
            result[window, :] = values
            return carry

        lax.fori_loop(0, rows // strip, strips(norm), 0)
        greet([(peer, target) for peer in near for target in (core, 1 - core)])
        for chain in range(2):
            for other in range(2):
                near_copy(chain, other).start()
        upstream[...] = jnp.zeros(upstream.shape, F32)
        side_out[0] = cot_ref[...].astype(F32).T.astype(BF16)

    own = pl.ds(pl.multiple_of(core * half_width, 128), half_width)
    far = pl.ds(pl.multiple_of((1 - core) * half_width, 128), half_width)

    def strip_of_hidden(down_ref):
        def ahead(near_ref, far_ref):
            return jnp.dot(ffn_out[:, own], near_ref[...], preferred_element_type=F32) + jnp.dot(
                ffn_out[:, far], far_ref[...], preferred_element_type=F32
            )

        gate_pre, up_pre = ahead(gate_own, gate_far), ahead(up_own, up_far)
        grad_hidden = dot_dims(cot_ref[...], down_ref[...], 1, 1)
        gate_sig = jax.nn.sigmoid(gate_pre)
        gate_act = gate_pre * gate_sig
        hidden_out[...] = (gate_act * up_pre).astype(BF16)
        gate_back = (
            grad_hidden * up_pre * (gate_sig * (1.0 + gate_pre * (1.0 - gate_sig)))
        ).astype(BF16)
        up_back = (grad_hidden * gate_act).astype(BF16)
        result[...] += jnp.dot(hidden_out[...], down_ref[...], preferred_element_type=F32)
        for window, gate_ref, up_ref in ((own, gate_own, up_own), (far, gate_far, up_far)):
            upstream[:, window] += dot_dims(gate_back, gate_ref[...], 1, 1) + dot_dims(
                up_back, up_ref[...], 1, 1
            )
        for base, back in ((0, gate_back), (wide, up_back)):
            turned = back.astype(F32).T.astype(BF16)
            for index in range(strip_owners):
                pair_out[plane * strip_owners + index, base : base + wide, :] = turned[
                    index * wide : (index + 1) * wide
                ]
        keep_pair(step).start()

        @pl.when(step < len(EARLY))
        def _():
            for turned_side in range(2):
                for chain in range(2):
                    swap_copy(chain, turned_side * 4 + 2 - step).start()


    @pl.when(plane // 2 == core)
    def _():
        strip_of_hidden(down_own)

    @pl.when(plane // 2 != core)
    def _():
        strip_of_hidden(down_far)

    @pl.when(step == pl.num_programs(0) - 1)
    def _():
        output_out[...] = result[...].astype(BF16)

        def back(window, total):
            values, grads = middle[window, :], upstream[window, :]
            inverse = lax.rsqrt(jnp.mean(values * values, axis=-1, keepdims=True) + EPSILON)
            scaled = grads * gain_ref[...]
            weight = jnp.sum(scaled * values, axis=-1, keepdims=True) / width
            grad_middle = cot_ref[window, :].astype(F32) + (
                inverse * scaled - values * inverse**3 * weight
            )
            grad_middle_out[window, :] = grad_middle
            middle_low[window, :] = grad_middle.astype(BF16)
            return total + jnp.sum(grads * values * inverse, axis=0, keepdims=True)

        terms_out[...] = lax.fori_loop(
            0, rows // strip, strips(back), jnp.zeros((1, width), F32)
        )
        mixed_back_out[...] = dot_dims(w_out_ref[...], middle_low[...], 1, 1).astype(BF16)
        side_out[1] = middle_low[...].astype(F32).T.astype(BF16)
        for turn in range(4):
            keep_pair(turn).wait()
        for chain in range(2):
            for other in range(2):
                near_copy(chain, other).wait()

        for depth in EARLY:
            for slot in (4 + depth, depth):
                for chain in range(2):
                    swap_copy(chain, slot).wait()


def ffn_call(call_id, tokens, mixed_t, w_out, gain, cot, gate, up, down):
    rows, width = tokens.shape
    half_depth, hidden_width = gate[0].shape
    steps = 4
    chunk = hidden_width // steps
    wide = hidden_width // RING

    def whole(*shape):
        return pl.BlockSpec(shape, lambda i: (0,) * len(shape))

    def turn(i):
        return lax.rem(lax.axis_index("ctx") // 4 + 6 - i, steps)

    columns = pl.BlockSpec((half_depth, chunk), lambda i: (0, turn(i)))
    return pl.pallas_call(
        ffn_kernel,
        grid_spec=pl.GridSpec(
            grid=(steps,),
            in_specs=[
                whole(rows, width),
                whole(width, rows),
                whole(width, width),
                whole(1, width),
                whole(rows, width),
                columns,
                columns,
                columns,
                columns,
                pl.BlockSpec((chunk, width), lambda i: (lax.rem(turn(i), 2), 0)),
                pl.BlockSpec((chunk, width), lambda i: (lax.rem(turn(i), 2), 0)),
            ],
            out_specs=(
                HBM_SPEC,
                pl.BlockSpec((rows, chunk), lambda i: (0, turn(i))),
                whole(rows, width),
                whole(rows, width),
                whole(2, width, rows),
                whole(width, rows),
                whole(rows, width),
                whole(1, width),
                HBM_SPEC,
                HBM_SPEC,
            ),
            scratch_shapes=[
                pltpu.VMEM((RING, 2 * wide, rows), BF16),
                pltpu.SemaphoreType.DMA((4,)),
            ]
            + [pltpu.VMEM((rows, width), F32)] * 3
            + [pltpu.VMEM((rows, width), BF16)]
            + [pltpu.SemaphoreType.DMA((2, 8))] * 2
            + [pltpu.SemaphoreType.DMA((2, 2))] * 2,
        ),
        out_shape=(
            jax.ShapeDtypeStruct((RING, 2 * wide, rows), BF16),
            jax.ShapeDtypeStruct((rows, hidden_width), BF16),
            jax.ShapeDtypeStruct((rows, width), BF16),
            jax.ShapeDtypeStruct((rows, width), BF16),
            jax.ShapeDtypeStruct((2, width, rows), BF16),
            jax.ShapeDtypeStruct((width, rows), BF16),
            jax.ShapeDtypeStruct((rows, width), F32),
            jax.ShapeDtypeStruct((1, width), F32),
            jax.ShapeDtypeStruct((2, 8, wide, rows), BF16),
            jax.ShapeDtypeStruct((2, 2, rows, half_depth), BF16),
        ),
        compiler_params=pltpu.CompilerParams(
            collective_id=call_id, has_side_effects=True, vmem_limit_bytes=63 << 20
        ),
        name="ffn_both_ways",
    )(tokens, mixed_t, w_out, gain, cot, *gate, *up, *down)


def settle_kernel(*refs):
    count = 7
    sources, gains, rest = refs[:count], refs[count], refs[count + 1 :]
    targets, gain_targets, rest = rest[: count + 2], rest[count + 2 : count + 6], rest[count + 6 :]
    held, in_sem, out_sem = rest[:count], rest[count], rest[count + 1]
    loads = [
        pltpu.make_async_copy(source, hold, in_sem.at[index])
        for index, (source, hold) in enumerate(zip(sources, held))
    ]
    for load in loads:
        load.start()
    stores, row = [], 0
    for index, load in enumerate(loads):
        load.wait()
        if index < count - 1:
            pieces = [(held[index], targets[index])]
        else:
            pieces = []
            for target in targets[index:]:
                pieces.append((held[index].at[pl.ds(row, target.shape[0])], target))
                row += target.shape[0]
        for piece, target in pieces:
            store = pltpu.make_async_copy(piece, target, out_sem.at[len(stores)])
            store.start()
            stores.append(store)
    for index, target in enumerate(gain_targets):
        target[...] = gains[index : index + 1, 0 : target.shape[1]]
    for store in stores:
        store.wait()


def settle_call(output, tokens, gate_t, up_t, down_t, out_t, qkv_t, gains):
    sources = (output, tokens, gate_t, up_t, down_t, out_t, qkv_t)
    lanes = qkv_t.shape[1]
    query = HEADS * HEAD_DIM // RING
    pair = KV_HEADS * HEAD_DIM // RING
    shapes = [source.shape for source in sources[:-1]]
    shapes += [(query, lanes), (pair, lanes), (pair, lanes)]
    gain_shapes = [(1, gains.shape[1])] * 2 + [(1, HEAD_DIM)] * 2
    return pl.pallas_call(
        settle_kernel,
        out_shape=(jax.ShapeDtypeStruct(output.shape, output.dtype),)
        + tuple(jax.ShapeDtypeStruct(shape, F32) for shape in shapes[1:] + gain_shapes),
        in_specs=[HBM_SPEC] * len(sources) + [VMEM_SPEC],
        out_specs=(HBM_SPEC,) * len(shapes) + (VMEM_SPEC,) * 4,
        scratch_shapes=[pltpu.VMEM(source.shape, source.dtype) for source in sources]
        + [pltpu.SemaphoreType.DMA((7,)), pltpu.SemaphoreType.DMA((9,))],
        compiler_params=pltpu.CompilerParams(vmem_limit_bytes=63 << 20),
        name="settle_results",
    )(*sources, gains)


def heads_body(
    tokens,
    seg_ids,
    doc_pos,
    attn_gain,
    w_query,
    w_key,
    w_value,
    query_gain,
    key_gain,
    w_out,
    ffn_gain,
    w_gate,
    w_up,
    w_down,
    d_output,
):
    rows = tokens.shape[1]
    (
        qkv,
        starts,
        normed_low,
        mixed_far,
        mixed_home,
        inverse_total,
        o_full,
        table,
        query_raw,
        key_raw,
        kvq_full,
        gate_far,
        up_far,
        down_far,
    ) = front_call(
        1,
        (
            attn_gain[None, :],
            doc_pos,
            query_gain[None, :],
            key_gain[None, :],
            head_frequencies(rows),
        ),
        (tokens[0], w_query, w_key, w_value, w_out, w_gate, w_up, w_down),
    )
    mixed_t = mixed_home.reshape(HEADS * HEAD_DIM, rows)
    cot_low = d_output[0]
    (
        pair,
        hidden_low,
        output,
        ffn_low,
        side,
        grad_mixed,
        grad_middle,
        ffn_terms,
        swapped,
        ffn_near,
    ) = ffn_call(
        2,
        tokens[0],
        mixed_t,
        o_full,
        ffn_gain[None, :],
        cot_low,
        (w_gate, gate_far),
        (w_up, up_far),
        (w_down, down_far),
    )
    gate_t, up_t, down_t, out_t, qkv_grads, d_tokens, gain_totals = back_call(
        3,
        (
            pair,
            hidden_low,
            side,
            ffn_low,
            mixed_t,
            grad_mixed.reshape(HALF, 2 * HEAD_DIM, rows),
            qkv,
            starts,
            mixed_far,
            inverse_total,
            table,
            normed_low,
            attn_gain[None, :],
            ffn_terms,
        ),
        (tokens[0], query_raw, key_raw, kvq_full, grad_middle, swapped, ffn_near),
    )
    output, d_tokens, gate, up, down, out, query, key, value, attn, ffn, query_gains, key_gains = (
        settle_call(output, d_tokens, gate_t, up_t, down_t, out_t, qkv_grads, gain_totals)
    )
    return (
        output[None],
        d_tokens[None],
        attn[0],
        query.T,
        key.T,
        value.T,
        query_gains[0],
        key_gains[0],
        out.T,
        ffn[0],
        gate.T,
        up.T,
        down.T,
    )


def solution(mesh):
    in_specs = (
        P("fsdp", "ctx", None),
        P("fsdp", "ctx"),
        P("fsdp", "ctx"),
        P(),
        P("fsdp", None),
        P("fsdp", None),
        P("fsdp", None),
        P(),
        P(),
        P("fsdp", None),
        P(),
        P("fsdp", None),
        P("fsdp", None),
        P("fsdp", None),
        P("fsdp", "ctx", None),
    )
    out_specs = (
        P("fsdp", "ctx", None),
        P("fsdp", "ctx", None),
        P(),
        P("fsdp", "ctx"),
        P("fsdp", "ctx"),
        P("fsdp", "ctx"),
        P(),
        P(),
        P("fsdp", "ctx"),
        P(),
        P("fsdp", "ctx"),
        P("fsdp", "ctx"),
        P("fsdp", "ctx"),
    )
    chosen = heads_body if (mesh.shape["ctx"], mesh.shape["fsdp"]) == (HEADS, 2) else ring_body
    return jax.shard_map(chosen, mesh=mesh, in_specs=in_specs, out_specs=out_specs, check_vma=False)
```

```python
import functools

import jax
import jax.numpy as jnp
import numpy as np
from jax import lax
from jax.experimental import pallas as pl
from jax.experimental.pallas import tpu as pltpu
from jax.sharding import PartitionSpec as P

HEADS = 16
KV_HEADS = 8
HEAD_DIM = 64
HOPS = 8


EPSILON = 1e-05
THETA = 1000000.0
MASKED = -1e30


def from_behind(block, axis, distance):
    devices = range(lax.axis_size(axis))
    route = [(i - distance, i) for i in devices if i - distance in devices]
    return lax.ppermute(block, axis, route)


def rms_norm(values, norm_gain):
    return (
        values * lax.rsqrt(jnp.mean(values * values, axis=-1, keepdims=True) + EPSILON) * norm_gain
    )


def rms_back(values, norm_gain, upstream):
    inverse = lax.rsqrt(jnp.mean(values * values, axis=-1, keepdims=True) + EPSILON)
    scaled = upstream * norm_gain
    row_width = values.shape[-1]
    d_values = (
        inverse * scaled
        - values * inverse**3 * jnp.sum(scaled * values, axis=-1, keepdims=True) / row_width
    )
    return (d_values, upstream * values * inverse)


def rotary(values, positions, turn_sign):
    half_dim = values.shape[-1] // 2
    inverse_freq = THETA ** (-(2.0 / values.shape[-1]) * jnp.arange(half_dim, dtype=jnp.float32))
    angles = positions.astype(jnp.float32)[:, None] * inverse_freq[None, :]
    cosine = jnp.cos(angles)[:, None, :]
    sine_part = turn_sign * jnp.sin(angles)[:, None, :]
    first_half = values[..., :half_dim]
    second_half = values[..., half_dim:]
    return jnp.concatenate(
        [
            first_half * cosine - second_half * sine_part,
            second_half * cosine + first_half * sine_part,
        ],
        axis=-1,
    )


def outer_product(left_mat, right_mat):
    return lax.dot_general(
        left_mat, right_mat, (((0,), (0,)), ((), ())), preferred_element_type=jnp.float32
    )


def against(left_mat, right_mat):
    return lax.dot_general(
        left_mat, right_mat, (((1,), (1,)), ((), ())), preferred_element_type=jnp.float32
    )


def ring_body(
    tokens,
    seg_ids,
    doc_pos,
    attn_gain,
    w_query,
    w_key,
    w_value,
    query_gain,
    key_gain,
    w_out,
    ffn_gain,
    w_gate,
    w_up,
    w_down,
    d_output,
):
    cycle_place = lax.axis_index("ctx")
    tok_rows = tokens.shape[1]
    resid_in = tokens[0].astype(jnp.float32)
    seg_local = seg_ids[0]
    pos_local = doc_pos[0]
    q_per_kv = HEADS // KV_HEADS
    group_cols = q_per_kv * HEAD_DIM
    score_scale = HEAD_DIM ** (-0.5)
    q_full, k_full, v_full, o_full = (
        lax.all_gather(w_query, "fsdp", axis=0, tiled=True),
        lax.all_gather(w_key, "fsdp", axis=0, tiled=True),
        lax.all_gather(w_value, "fsdp", axis=0, tiled=True),
        lax.all_gather(w_out, "fsdp", axis=0, tiled=True),
    )
    gate_full, up_full, down_full = (
        lax.all_gather(w_gate, "fsdp", axis=0, tiled=True),
        lax.all_gather(w_up, "fsdp", axis=0, tiled=True),
        lax.all_gather(w_down, "fsdp", axis=0, tiled=True),
    )
    normed = rms_norm(resid_in, attn_gain)
    normed_low = normed.astype(jnp.bfloat16)
    query_raw = jnp.dot(normed_low, q_full, preferred_element_type=jnp.float32).reshape(
        tok_rows, HEADS, HEAD_DIM
    )
    key_raw = jnp.dot(normed_low, k_full, preferred_element_type=jnp.float32).reshape(
        tok_rows, KV_HEADS, HEAD_DIM
    )
    value_raw = jnp.dot(normed_low, v_full, preferred_element_type=jnp.float32)
    query_rot = rotary(rms_norm(query_raw, query_gain), pos_local, 1.0)
    key_rot = rotary(rms_norm(key_raw, key_gain), pos_local, 1.0)
    query_low = query_rot.astype(jnp.bfloat16).reshape(tok_rows, HEADS * HEAD_DIM)
    key_low = key_rot.astype(jnp.bfloat16).reshape(tok_rows, KV_HEADS * HEAD_DIM)
    value_low = value_raw.astype(jnp.bfloat16)
    own_kv = (key_low, value_low, seg_local)
    kv_blocks = [own_kv]
    carried = own_kv
    for hop_index in range(HOPS):
        carried = from_behind((carried[0], carried[1], carried[2]), "ctx", 1)
        kv_blocks.append(carried)
    key_all = jnp.concatenate([kv_entry[0] for kv_entry in kv_blocks], axis=0)
    value_all = jnp.concatenate([kv_entry[1] for kv_entry in kv_blocks], axis=0)
    seg_all = jnp.concatenate([kv_entry[2] for kv_entry in kv_blocks], axis=0)
    key_owner = cycle_place - jnp.arange(HOPS + 1, dtype=jnp.int32)
    owner_valid = jnp.repeat(key_owner >= 0, tok_rows)
    key_index = (
        key_owner[:, None] * tok_rows + jnp.arange(tok_rows, dtype=jnp.int32)[None, :]
    ).reshape(-1)
    query_index = cycle_place * tok_rows + jnp.arange(tok_rows, dtype=jnp.int32)
    allowed = (
        (seg_local[:, None] == seg_all[None, :])
        & (key_index[None, :] <= query_index[:, None])
        & owner_valid[None, :]
    )

    def group_scores(kv_group):
        query_part = lax.dynamic_slice_in_dim(query_low, kv_group * group_cols, group_cols, 1)
        query_part = query_part.reshape(tok_rows, q_per_kv, HEAD_DIM)
        key_part = lax.dynamic_slice_in_dim(key_all, kv_group * HEAD_DIM, HEAD_DIM, 1)
        value_part = lax.dynamic_slice_in_dim(value_all, kv_group * HEAD_DIM, HEAD_DIM, 1)
        scores = (
            jnp.einsum("trd,kd->rtk", query_part, key_part, preferred_element_type=jnp.float32)
            * score_scale
        )
        return (jnp.where(allowed[None], scores, MASKED), query_part, key_part, value_part)

    def forward_group(kv_group):
        scores, query_part, key_part, value_part = group_scores(kv_group)
        row_top = jnp.max(scores, axis=-1, keepdims=True)
        log_total = row_top + jnp.log(jnp.sum(jnp.exp(scores - row_top), axis=-1, keepdims=True))
        attn_probs = jnp.exp(scores - log_total)
        mixed_part = jnp.einsum(
            "rtk,kd->trd",
            attn_probs.astype(jnp.bfloat16),
            value_part,
            preferred_element_type=jnp.float32,
        )
        return (mixed_part.reshape(tok_rows, group_cols), log_total[..., 0])

    mixed_groups, total_groups = lax.map(forward_group, jnp.arange(KV_HEADS, dtype=jnp.int32))
    mixed = mixed_groups.transpose(1, 0, 2).reshape(tok_rows, HEADS * HEAD_DIM)
    mixed_low = mixed.astype(jnp.bfloat16)
    middle = resid_in + jnp.dot(mixed_low, o_full, preferred_element_type=jnp.float32)
    ffn_low = rms_norm(middle, ffn_gain).astype(jnp.bfloat16)
    gate_pre = jnp.dot(ffn_low, gate_full, preferred_element_type=jnp.float32)
    up_pre = jnp.dot(ffn_low, up_full, preferred_element_type=jnp.float32)
    gate_sig = jax.nn.sigmoid(gate_pre)
    gate_act = gate_pre * gate_sig
    hidden_low = (gate_act * up_pre).astype(jnp.bfloat16)
    result = middle + jnp.dot(hidden_low, down_full, preferred_element_type=jnp.float32)
    output = result.astype(jnp.bfloat16)[None]
    cot_low = d_output[0]
    cotangent = cot_low.astype(jnp.float32)
    grad_w_down = outer_product(hidden_low, cot_low)
    grad_hidden = against(cot_low, down_full)
    gate_back = (grad_hidden * up_pre * (gate_sig * (1.0 + gate_pre * (1.0 - gate_sig)))).astype(
        jnp.bfloat16
    )
    up_back = (grad_hidden * gate_act).astype(jnp.bfloat16)
    grad_w_gate = outer_product(ffn_low, gate_back)
    grad_w_up = outer_product(ffn_low, up_back)
    grad_ffn_in = against(gate_back, gate_full) + against(up_back, up_full)
    middle_part, ffn_terms = rms_back(middle, ffn_gain, grad_ffn_in)
    grad_middle = cotangent + middle_part
    middle_low = grad_middle.astype(jnp.bfloat16)
    grad_w_out = outer_product(mixed_low, middle_low)
    grad_mixed = against(middle_low, o_full).astype(jnp.bfloat16)

    def backward_group(kv_group):
        scores, query_part, key_part, value_part = group_scores(kv_group)
        attn_probs = jnp.exp(scores - total_groups[kv_group][..., None])
        mixed_grad_part = lax.dynamic_slice_in_dim(grad_mixed, kv_group * group_cols, group_cols, 1)
        mixed_grad_part = mixed_grad_part.reshape(tok_rows, q_per_kv, HEAD_DIM)
        grad_probs = jnp.einsum(
            "trd,kd->rtk", mixed_grad_part, value_part, preferred_element_type=jnp.float32
        )
        grad_value = jnp.einsum(
            "rtk,trd->kd",
            attn_probs.astype(jnp.bfloat16),
            mixed_grad_part,
            preferred_element_type=jnp.float32,
        )
        row_delta = jnp.sum(grad_probs * attn_probs, axis=-1, keepdims=True)
        grad_scores = (attn_probs * (grad_probs - row_delta)).astype(jnp.bfloat16)
        grad_query = (
            jnp.einsum("rtk,kd->trd", grad_scores, key_part, preferred_element_type=jnp.float32)
            * score_scale
        )
        grad_key = (
            jnp.einsum("rtk,trd->kd", grad_scores, query_part, preferred_element_type=jnp.float32)
            * score_scale
        )
        return (grad_query.reshape(tok_rows, group_cols), grad_key, grad_value)

    query_groups, key_groups, value_groups = lax.map(
        backward_group, jnp.arange(KV_HEADS, dtype=jnp.int32)
    )
    grad_query_rot = query_groups.transpose(1, 0, 2).reshape(tok_rows, HEADS, HEAD_DIM)
    key_blocks = key_groups.transpose(1, 0, 2).reshape(HOPS + 1, tok_rows, KV_HEADS * HEAD_DIM)
    value_blocks = value_groups.transpose(1, 0, 2).reshape(HOPS + 1, tok_rows, KV_HEADS * HEAD_DIM)
    home_key = key_blocks[HOPS]
    home_value = value_blocks[HOPS]
    for hop_index in range(HOPS, 0, -1):
        moved_key, moved_value = (
            from_behind(home_key.astype(jnp.bfloat16), "ctx", -1).astype(home_key.dtype),
            from_behind(home_value.astype(jnp.bfloat16), "ctx", -1).astype(home_value.dtype),
        )
        home_key = moved_key + key_blocks[hop_index - 1]
        home_value = moved_value + value_blocks[hop_index - 1]
    query_turned = rotary(grad_query_rot, pos_local, -1.0)
    key_turned = rotary(home_key.reshape(tok_rows, KV_HEADS, HEAD_DIM), pos_local, -1.0)
    query_back, query_terms = rms_back(query_raw, query_gain, query_turned)
    key_back, key_terms = rms_back(key_raw, key_gain, key_turned)
    query_back = query_back.reshape(tok_rows, HEADS * HEAD_DIM).astype(jnp.bfloat16)
    key_back = key_back.reshape(tok_rows, KV_HEADS * HEAD_DIM).astype(jnp.bfloat16)
    value_back = home_value.astype(jnp.bfloat16)
    grad_w_query = outer_product(normed_low, query_back)
    grad_w_key = outer_product(normed_low, key_back)
    grad_w_value = outer_product(normed_low, value_back)
    grad_normed = (
        against(query_back, q_full) + against(key_back, k_full) + against(value_back, v_full)
    )
    input_part, attn_terms = rms_back(resid_in, attn_gain, grad_normed)
    d_tokens = (grad_middle + input_part)[None]
    gain_totals = lax.psum(
        (
            jnp.sum(attn_terms, axis=0),
            jnp.sum(ffn_terms, axis=0),
            jnp.sum(query_terms, axis=(0, 1)),
            jnp.sum(key_terms, axis=(0, 1)),
        ),
        ("ctx", "fsdp"),
    )
    weight_grads = (
        grad_w_query,
        grad_w_key,
        grad_w_value,
        grad_w_out,
        grad_w_gate,
        grad_w_up,
        grad_w_down,
    )
    spread = (
        lax.psum_scatter(
            weight_grads[0].astype(jnp.bfloat16), "fsdp", scatter_dimension=0, tiled=True
        ).astype(jnp.float32),
        lax.psum_scatter(
            weight_grads[1].astype(jnp.bfloat16), "fsdp", scatter_dimension=0, tiled=True
        ).astype(jnp.float32),
        lax.psum_scatter(
            weight_grads[2].astype(jnp.bfloat16), "fsdp", scatter_dimension=0, tiled=True
        ).astype(jnp.float32),
        lax.psum_scatter(
            weight_grads[3].astype(jnp.bfloat16), "fsdp", scatter_dimension=0, tiled=True
        ).astype(jnp.float32),
        lax.psum_scatter(
            weight_grads[4].astype(jnp.bfloat16), "fsdp", scatter_dimension=0, tiled=True
        ).astype(jnp.float32),
        lax.psum_scatter(
            weight_grads[5].astype(jnp.bfloat16), "fsdp", scatter_dimension=0, tiled=True
        ).astype(jnp.float32),
        lax.psum_scatter(
            weight_grads[6].astype(jnp.bfloat16), "fsdp", scatter_dimension=0, tiled=True
        ).astype(jnp.float32),
    )
    shares = (
        lax.psum_scatter(spread[0], "ctx", scatter_dimension=1, tiled=True),
        lax.psum_scatter(spread[1], "ctx", scatter_dimension=1, tiled=True),
        lax.psum_scatter(spread[2], "ctx", scatter_dimension=1, tiled=True),
        lax.psum_scatter(spread[3], "ctx", scatter_dimension=1, tiled=True),
        lax.psum_scatter(spread[4], "ctx", scatter_dimension=1, tiled=True),
        lax.psum_scatter(spread[5], "ctx", scatter_dimension=1, tiled=True),
        lax.psum_scatter(spread[6], "ctx", scatter_dimension=1, tiled=True),
    )
    return (
        output,
        d_tokens,
        gain_totals[0],
        shares[0],
        shares[1],
        shares[2],
        gain_totals[2],
        gain_totals[3],
        shares[3],
        gain_totals[1],
        shares[4],
        shares[5],
        shares[6],
    )


MESH = pl.DeviceIdType.MESH
BLOCK = 256
RING = 16
HALF = 8
EDGE = 128
DOWN_CHUNKS = ((0, 3), (3, 3), (6, 3))
EARLY = (2,)
VMEM_SPEC = pl.BlockSpec(memory_space=pltpu.VMEM)
HBM_SPEC = pl.BlockSpec(memory_space=pltpu.HBM)
SMEM_SPEC = pl.BlockSpec(memory_space=pltpu.SMEM)
F32 = jnp.float32
BF16 = jnp.bfloat16


def dot_dims(left_mat, right_mat, left_dim, right_dim):
    return lax.dot_general(
        left_mat, right_mat, (((left_dim,), (right_dim,)), ((), ())), preferred_element_type=F32
    )


def transposed(block):
    return block.astype(F32).T.astype(BF16)


def flip(bit, turned):
    return bit + turned - 2 * bit * turned


def block_owner(chain, place, other, slot):
    x, y, z = lax.rem(place, 2), lax.rem(place // 2, 2), place // 4
    turned, depth = slot // 4, lax.rem(lax.rem(slot, 4) + z, 4)
    first, second = flip((x, y)[chain], other), flip((y, x)[chain], turned)
    return depth * 4 + (second * 2 + first if chain == 0 else first * 2 + second)


class Spread:
    def __init__(self, chain, compute, base, sent, came, hold, skip, send_sems, recv_sems):
        place, self.core = lax.axis_index("ctx"), lax.axis_index("fsdp")
        x, y, self.z = lax.rem(place, 2), lax.rem(place // 2, 2), place // 4
        self.chain, self.base = chain, base
        self.first, self.second = (x, y) if chain == 0 else (y, x)
        self.compute, self.sent, self.came = compute, sent, came
        self.hold, self.skip = hold, skip
        self.send_sems, self.recv_sems = send_sems, recv_sems

    def at(self, first, second, depth):
        low = second * 2 + first if self.chain == 0 else first * 2 + second
        return depth * 4 + low

    def deep(self, depth):
        return lax.rem(self.z + depth, 4)

    def owner(self, slot):
        return self.at(self.first, flip(self.second, slot // 4), self.deep(lax.rem(slot, 4)))

    def copy(self, stage, slot):
        if stage == 0:
            peer = self.at(1 - self.first, self.second, self.z)
            source, target, sem = self.sent.at[slot], self.came[0].at[slot], slot
        elif stage == 1:
            peer = self.at(self.first, 1 - self.second, self.z)
            source, target, sem = self.hold.at[4 + slot - self.skip], self.came[1].at[slot], 8 + slot
        else:
            peer = self.at(self.first, self.second, self.deep(slot))
            source, target, sem = self.hold.at[slot - self.skip], self.came[2].at[slot - 1], 11 + slot
        return pltpu.make_async_remote_copy(
            src_ref=source,
            dst_ref=target,
            send_sem=self.send_sems.at[self.chain, sem],
            recv_sem=self.recv_sems.at[self.chain, sem],
            device_id=(peer, self.core),
            device_id_type=MESH,
        )

    def stage_one(self, turned, depth):
        slot = turned * 4 + depth
        owner = self.at(1 - self.first, flip(self.second, turned), self.deep(depth))
        for row, value in self.compute(self.chain, owner, None):
            row -= self.base
            self.sent[slot, row : row + value.shape[0], :] = value.astype(BF16)
        self.copy(0, slot).start()

    def sums(self, slot):
        for row, value in self.compute(self.chain, self.owner(slot), slot):
            if row >= self.base:
                low = row - self.base
                value = value + self.came[0][slot, low : low + value.shape[0], :].astype(F32)
            yield slice(row, row + value.shape[0]), value

    def stage_two(self, depth):
        self.copy(0, 4 + depth).wait_recv()
        for window, value in self.sums(4 + depth):
            self.hold[4 + depth - self.skip, window, :] = value.astype(BF16)
        self.copy(1, depth).start()

    def stage_three(self, depth):
        self.copy(0, depth).wait_recv()
        self.copy(1, depth).wait_recv()
        for window, value in self.sums(depth):
            value = value + self.came[1][depth, window, :].astype(F32)
            self.hold[depth - self.skip, window, :] = value.astype(BF16)
        self.copy(2, depth).start()

    def close(self, finish):
        self.copy(0, 0).wait_recv()
        self.copy(1, 0).wait_recv()
        for depth in range(1, 4):
            self.copy(2, depth).wait_recv()
        for window, value in self.sums(0):
            value = value + self.came[1][0, window, :].astype(F32)
            for depth in range(3):
                value = value + self.came[2][depth, window, :].astype(F32)
            finish(self.chain, window.start, value)

    def drain(self):
        for slot in range(8):
            self.copy(0, slot).wait_send()
        for depth in range(4):
            self.copy(1, depth).wait_send()
        for depth in range(1, 4):
            self.copy(2, depth).wait_send()


class DeepSpread:
    def __init__(self, compute, sent, came, send_sems, recv_sems):
        self.place, self.core = lax.axis_index("ctx"), lax.axis_index("fsdp")
        self.x, self.y = lax.rem(self.place, 2), lax.rem(self.place // 2, 2)
        self.compute, self.sent, self.came = compute, sent, came
        self.send_sems, self.recv_sems = send_sems, recv_sems

    def copy(self, stage, slot):
        if stage == 0:
            peer = lax.rem(self.place + 4 * slot, RING)
            source, target, sem = self.sent.at[slot - 1], self.came[0].at[slot - 1], slot - 1
        elif stage == 1:
            peer = self.place + 1 - 2 * self.x
            local = flip(self.y, slot) * 2 + 1 - self.x
            source, target, sem = self.came[0].at[0, local], self.came[1].at[slot], 3 + slot
        else:
            peer = self.place + 2 - 4 * self.y
            local = (1 - self.y) * 2 + self.x
            source, target, sem = self.came[0].at[0, local], self.came[2].at[0], 5
        return pltpu.make_async_remote_copy(
            src_ref=source,
            dst_ref=target,
            send_sem=self.send_sems.at[sem],
            recv_sem=self.recv_sems.at[sem],
            device_id=(peer, self.core),
            device_id_type=MESH,
        )

    def stage_one(self, slot):
        first = lax.rem(self.place // 4 + slot, 4) * 4
        value = self.compute(first, 4)
        rows = value.shape[0] // 4
        for local in range(4):
            for chunk in range(value.shape[1] // 256):
                self.sent[slot - 1, local, chunk * rows : (chunk + 1) * rows, :] = value[
                    local * rows : (local + 1) * rows, chunk * 256 : (chunk + 1) * 256
                ].astype(BF16)
        self.copy(0, slot).start()

    def arrived(self, local):
        value = self.compute(self.place - lax.rem(self.place, 4) + local, 1)
        rows = value.shape[0]
        for chunk in range(value.shape[1] // 256):
            window = slice(chunk * rows, (chunk + 1) * rows)
            total = value[:, chunk * 256 : (chunk + 1) * 256]
            for slot in range(3):
                total = total + self.came[0][slot, local, window, :].astype(F32)
            yield window, total

    def stage_two(self):
        for slot in range(1, 4):
            self.copy(0, slot).wait_recv()
        for slot in (1, 0):
            local = flip(self.y, slot) * 2 + 1 - self.x
            for window, total in self.arrived(local):
                self.came[0][0, local, window, :] = total.astype(BF16)
            self.copy(1, slot).start()

    def stage_three(self):
        self.copy(1, 1).wait_recv()
        local = (1 - self.y) * 2 + self.x
        for window, total in self.arrived(local):
            total = total + self.came[1][1, window, :].astype(F32)
            self.came[0][0, local, window, :] = total.astype(BF16)
        self.copy(2, 0).start()

    def close(self, finish):
        self.copy(1, 0).wait_recv()
        self.copy(2, 0).wait_recv()
        for window, total in self.arrived(lax.rem(self.place, 4)):
            total = total + self.came[1][0, window, :].astype(F32)
            finish(window, total + self.came[2][0, window, :].astype(F32))

    def drain(self):
        for slot in range(1, 4):
            self.copy(0, slot).wait_send()
        for slot in range(2):
            self.copy(1, slot).wait_send()
        self.copy(2, 0).wait_send()


def greet(peers):
    barrier = pltpu.get_barrier_semaphore()
    for peer in peers:
        pl.semaphore_signal(barrier, inc=1, device_id=peer, device_id_type=MESH)
    pl.semaphore_wait(barrier, len(peers))


def turn_back(values, cosine, sine):
    half = HEAD_DIM // 2
    first, second = values[:half], values[half:]
    return jnp.concatenate(
        [first * cosine + second * sine, second * cosine - first * sine], axis=0
    )


def column_norm_back(values, gain, upstream):
    inverse = lax.rsqrt(jnp.mean(values * values, axis=0, keepdims=True) + EPSILON)
    scaled = upstream * gain
    total = jnp.sum(scaled * values, axis=0, keepdims=True) / values.shape[0]
    return inverse * scaled - values * inverse**3 * total, upstream * values * inverse


def back_kernel(
    pair_hbm,
    hidden_hbm,
    side_hbm,
    ffn_hbm,
    mixed_hbm,
    home_hbm,
    qkv_hbm,
    start_ref,
    part_hbm,
    inv_ref,
    table_ref,
    normed_hbm,
    attn_gain_ref,
    ffn_terms_ref,
    tokens_hbm,
    query_hbm,
    key_hbm,
    weights_hbm,
    middle_hbm,
    swap_hbm,
    near_hbm,
    gate_out,
    up_out,
    down_out,
    out_out,
    grads_out,
    tokens_out,
    gains_out,
    side_own,
    ffn_ref,
    mixed_ref,
    home_ref,
    qkv_ref,
    part_ref,
    normed_ref,
    rows_of,
    ffn_near,
    side_far,
    hidden_own,
    hidden_far,
    ffn_far,
    mixed_far,
    normed_far,
    cot_far,
    back_own,
    back_far,
    extra_own,
    extra_far,
    turned_own,
    turned_far,
    gain_own,
    gain_came,
    gain_all,
    sent_a,
    came_a0,
    hold_a,
    came_a1,
    came_a2,
    sent_b,
    came_b0,
    hold_b,
    came_b1,
    came_b2,
    sent_c,
    came_c0,
    came_c1,
    came_c2,
    deep_send,
    deep_recv,
    tail_sent_a,
    tail_came_a0,
    tail_came_a1,
    tail_came_a2,
    tail_sent_b,
    tail_came_b0,
    tail_came_b1,
    tail_came_b2,
    send_sems,
    recv_sems,
    tail_send,
    tail_recv,
    cot_send,
    cot_recv,
    back_send,
    back_recv,
    core_send,
    core_recv,
    gain_send,
    gain_recv,
    extra_send,
    extra_recv,
    load_sem,
    stage_sem,
    rows_sem,
    mate_send,
    mate_recv,
    relay_send,
    relay_recv,
    swap_send,
    swap_recv,
    near_sem,
):
    place, core = lax.axis_index("ctx"), lax.axis_index("fsdp")
    part, member = place // HALF, lax.rem(place, HALF)
    base = part * HALF - 1
    x, y, z = lax.rem(place, 2), lax.rem(place // 2, 2), place // 4
    wide = rows_of.shape[3]
    narrow = side_own.shape[1] // RING
    half_hidden = hidden_far.shape[1]
    half_width = ffn_far.shape[1]
    heads, pairs = query_hbm.shape[0], key_hbm.shape[0]
    scale = HEAD_DIM**-0.5
    partner = (place, 1 - core)

    def half(part, size):
        return pl.ds(pl.multiple_of(part * size, 128), size)

    stages = [
        pltpu.make_async_copy(source, target, stage_sem.at[index])
        for index, (source, target) in enumerate(
            (
                (home_hbm, home_ref),
                (side_hbm, side_own),
                (ffn_hbm, ffn_ref),
                (mixed_hbm, mixed_ref),
                (qkv_hbm, qkv_ref),
                (part_hbm, part_ref),
                (normed_hbm, normed_ref),
            )
        )
    ]
    own_hidden = pltpu.make_async_copy(
        hidden_hbm.at[:, half(core, half_hidden)], hidden_own, load_sem.at[0]
    )
    for stage in stages[:4]:
        stage.start()
    own_hidden.start()
    for stage in stages[4:]:
        stage.start()
    middle_load = pltpu.make_async_copy(middle_hbm, tokens_out, load_sem.at[1])
    middle_load.start()
    near = (place + 1 - 2 * x, place + 2 - 4 * y)
    greet([(lax.rem(place + step, RING), core) for step in range(1, RING)] + [partner])

    def remote(source, target, send, recv, peer):
        return pltpu.make_async_remote_copy(
            src_ref=source,
            dst_ref=target,
            send_sem=send,
            recv_sem=recv,
            device_id=peer,
            device_id_type=MESH,
        )

    def mate(step):
        return (part * HALF + lax.rem(member + step, HALF), core)

    def cot_copy(step):
        return remote(
            home_ref.at[lax.rem(member + step, HALF)],
            cot_far.at[member],
            cot_send.at[step],
            cot_recv.at[step],
            mate(step),
        )

    def core_copy(source, target, sem):
        return remote(source, target, core_send.at[sem], core_recv.at[sem], partner)

    def back_rows(chain, owner):
        return pair_hbm.at[owner, pl.ds(chain * wide, wide)]

    def owner_of(chain, slot):
        return block_owner(chain, place, 0, slot)

    def own_loads(chain, slot):
        loads = [
            pltpu.make_async_copy(
                back_rows(chain, owner_of(chain, slot)),
                rows_of.at[0, chain, slot],
                rows_sem.at[0, chain, slot],
            )
        ]
        if slot % 4 in EARLY:
            loads.append(
                pltpu.make_async_copy(
                    swap_hbm.at[chain, slot],
                    rows_of.at[2, chain, slot],
                    rows_sem.at[1, chain, slot],
                )
            )
        return loads

    def swap_copy(chain, slot):
        return remote(
            back_rows(chain, block_owner(chain, place, 1, slot)),
            rows_of.at[2, chain, slot],
            swap_send.at[chain, slot],
            swap_recv.at[chain, slot],
            (near[chain], core),
        )

    def swap(depth):
        for slot in (4 + depth, depth):
            for chain in range(2):
                swap_copy(chain, slot).start()

    def relay(depth):
        for slot in (4 + depth, depth):
            for chain in range(2):
                swap_copy(chain, slot).wait_recv()
                relay_copy(chain, slot).start()

    def mate_copy(chain, slot):
        return remote(
            back_rows(chain, owner_of(chain, slot)),
            rows_of.at[1, chain, slot],
            mate_send.at[chain, slot],
            mate_recv.at[chain, slot],
            partner,
        )

    def relay_copy(chain, slot):
        return remote(
            swap_hbm.at[chain, slot] if slot % 4 in EARLY else rows_of.at[2, chain, slot],
            rows_of.at[3, chain, slot],
            relay_send.at[chain, slot],
            relay_recv.at[chain, slot],
            partner,
        )

    near_load = pltpu.make_async_copy(near_hbm, ffn_near, near_sem)
    sides = [
        core_copy(ffn_hbm.at[:, half(1 - core, half_width)], ffn_far, 0),
        core_copy(mixed_hbm.at[half(1 - core, half_width), :], mixed_far, 1),
        core_copy(side_hbm, side_far, 2),
        core_copy(hidden_hbm.at[:, half(1 - core, half_hidden)], hidden_far, 3),
    ]
    stages[0].wait()
    for step in range(1, HALF):
        cot_copy(step).start()
    for copy in sides:
        copy.start()
    near_load.start()
    for depth in (2, 1, 3, 0):
        for slot in (4 + depth, depth):
            for chain in range(2):
                for load in own_loads(chain, slot):
                    load.start()
                mate_copy(chain, slot).start()
                if depth in EARLY:
                    relay_copy(chain, slot).start()
    normed_copy = core_copy(normed_hbm.at[:, half(1 - core, half_width)], normed_far, 4)
    normed_copy.start()
    cot_far[member] = home_ref[member]

    def down_product(rows, split):
        cols = slice(split[0] * 256, (split[0] + split[1]) * 256)
        down = jnp.dot(side_own[0, rows, :], hidden_own[:, cols], preferred_element_type=F32)
        return down + jnp.dot(side_far[0, rows, :], hidden_far[:, cols], preferred_element_type=F32)

    def deep_compute(owner, count):
        rows = pl.ds(pl.multiple_of(owner * narrow, 16), count * narrow)
        return down_product(rows, DOWN_CHUNKS[2])

    def deep_finish(window, value):
        chunk = DOWN_CHUNKS[2][0] + window.start // narrow
        down_out[:, chunk * 256 : chunk * 256 + 256] = value

    def compute(chain, owner, slot):
        lanes = pl.ds(chain * 256, 256)
        own_lanes = pl.ds(pl.multiple_of(core * half_width + chain * 256, 128), 256)
        rows = pl.ds(pl.multiple_of(owner * narrow, 16), narrow)
        values = []
        if slot is not None:
            for load in own_loads(chain, slot):
                load.wait()
            mate_copy(chain, slot).wait_recv()
            relay_copy(chain, slot).wait_recv()
            wide_sum = jnp.dot(
                rows_of[0, chain, slot],
                ffn_ref[:, half(core, half_width)],
                preferred_element_type=F32,
            )
            for source, columns in (
                (1, ffn_far[...]),
                (2, ffn_near[chain, 0]),
                (3, ffn_near[chain, 1]),
            ):
                wide_sum += jnp.dot(
                    rows_of[source, chain, slot], columns, preferred_element_type=F32
                )
            values += [(0, wide_sum[:, :256]), (wide, wide_sum[:, 256:])]
        chunks = DOWN_CHUNKS[chain][1]
        down = down_product(rows, DOWN_CHUNKS[chain])
        row = 2 * wide
        for chunk in range(chunks):
            values.append((row, down[:, chunk * 256 : chunk * 256 + 256]))
            row += narrow
        out = dot_dims(side_own[1, rows, :], mixed_ref[own_lanes, :], 1, 1)
        out += dot_dims(side_far[1, rows, :], mixed_far[lanes, :], 1, 1)
        values.append((row, out))
        return values

    def finish(chain, row, value):
        lanes = slice(chain * 256, chain * 256 + 256)
        if row < 2 * wide:
            target, low = (gate_out, up_out)[chain], row // wide * 256
            target[:, low : low + 256] = value
            return
        chunk = (row - 2 * wide) // narrow
        if chunk == DOWN_CHUNKS[chain][1]:
            out_out[:, lanes] = value
        else:
            chunk += DOWN_CHUNKS[chain][0]
            down_out[:, chunk * 256 : chunk * 256 + 256] = value

    chains = (
        Spread(
            0,
            compute,
            2 * wide,
            sent_a,
            (came_a0, came_a1, came_a2),
            hold_a,
            1,
            send_sems,
            recv_sems,
        ),
        Spread(
            1,
            compute,
            2 * wide,
            sent_b,
            (came_b0, came_b1, came_b2),
            hold_b,
            1,
            send_sems,
            recv_sems,
        ),
    )
    own_hidden.wait()
    for stage in stages[1:4]:
        stage.wait()
    for copy in sides:
        copy.wait_recv()

    def near_side(depth):
        for chain in chains:
            chain.stage_one(1, depth)

    def far_side(depth):
        for chain in chains:
            chain.stage_one(0, depth)

    def onward(depth):
        for chain in chains:
            chain.stage_two(depth)

    def deeper(depth):
        for chain in chains:
            chain.stage_three(depth)

    along = DeepSpread(
        deep_compute, sent_c, (came_c0, came_c1, came_c2), deep_send, deep_recv
    )
    near_side(2)
    for slot in (2, 1, 3):
        along.stage_one(slot)
    far_side(2)
    near_side(1)
    swap(1)
    near_load.wait()
    for stage in stages[4:]:
        stage.wait()

    def back_copy(step):
        return remote(
            back_own.at[lax.rem(member + step, HALF)],
            back_far.at[member],
            back_send.at[step],
            back_recv.at[step],
            mate(step),
        )

    def extra_copy(group):
        return remote(
            extra_own,
            extra_far.at[group],
            extra_send.at[group],
            extra_recv.at[group],
            (HALF - 1, core),
        )

    def attention(
        scaled, cots, natural, delta_ref, query_acc, key_nat, value_nat, pair_acc
    ):
        def widen(ref, i, row):
            return jnp.concatenate(
                [ref[i, row : row + HEAD_DIM, :], ref[i, row + HEAD_DIM : row + 2 * HEAD_DIM, :]],
                axis=1,
            )

        def prepare(i, nothing):
            @pl.when(i != member)
            def _():
                cot_copy(lax.rem(member - i + HALF, HALF)).wait_recv()

            query = widen(qkv_ref, i + 1, 0) * jnp.asarray(scale, BF16)
            cot = widen(cot_far, i, 0)
            scaled[i] = query
            cots[i] = cot
            natural[i] = transposed(jnp.concatenate([query, cot], axis=0))
            delta_ref[i] = jnp.sum(
                cot.astype(F32) * widen(part_ref, i, 0).astype(F32), axis=0, keepdims=True
            )
            query_acc[i] = jnp.zeros(query_acc.shape[1:], F32)
            return nothing

        def per_key(j, nothing):
            key_t = qkv_ref[j, 2 * HEAD_DIM : 3 * HEAD_DIM, :]
            key_nat[...] = transposed(key_t)
            value_nat[...] = transposed(qkv_ref[j, 3 * HEAD_DIM : 4 * HEAD_DIM, :])
            shape = (BLOCK, 2 * BLOCK)
            key_place = (base + j) * BLOCK + lax.broadcasted_iota(jnp.int32, shape, 0)

            def step(diagonal, i):
                start = jnp.concatenate([start_ref[i - 1]] * 2, axis=1)
                scores = jnp.dot(key_nat[...], scaled[i - 1], preferred_element_type=F32)
                grad_probs = jnp.dot(value_nat[...], cots[i - 1], preferred_element_type=F32)
                ok = key_place >= start
                if diagonal:
                    places = (base + i) * BLOCK + lax.broadcasted_iota(jnp.int32, (1, BLOCK), 1)
                    ok = ok & (key_place <= jnp.concatenate([places] * 2, axis=1))
                probs = jnp.where(ok, jnp.exp(scores) * inv_ref[i - 1], 0.0)
                grad_scores = (probs * (grad_probs - delta_ref[i - 1])).astype(BF16)
                both_low = jnp.concatenate([grad_scores, probs.astype(BF16)], axis=0)
                query_acc[i - 1] += jnp.dot(
                    qkv_ref[j, 2 * HEAD_DIM : 3 * HEAD_DIM, :],
                    grad_scores,
                    preferred_element_type=F32,
                )
                return jnp.dot(both_low, natural[i - 1], preferred_element_type=F32)

            @pl.when(j == 0)
            def _():
                pair_acc[...] = jnp.zeros(pair_acc.shape, F32)

            @pl.when(j > 0)
            def _():
                pair_acc[...] = step(True, j)

            def one(i, carry):
                pair_acc[...] += step(False, i)
                return carry

            def two(index, carry):
                i = j + 1 + 2 * index
                pair_acc[...] += step(False, i) + step(False, i + 1)
                return carry

            count = (HALF - j) // 2
            lax.fori_loop(0, count, two, 0)
            lax.fori_loop(j + 1 + 2 * count, HALF + 1, one, 0)
            first = lax.broadcasted_iota(jnp.int32, (BLOCK, 2 * HEAD_DIM), 1) < HEAD_DIM
            merged = jnp.where(first, pair_acc[0:BLOCK, :], pair_acc[BLOCK:, :]).T.astype(BF16)

            @pl.when(j == 0)
            def _():
                extra_own[...] = merged
                extra_copy(member).start()

            @pl.when(j > 0)
            def _():
                query_grad = (query_acc[j - 1] * scale).astype(BF16)
                back_own[j - 1, 0:HEAD_DIM, :] = query_grad[:, :BLOCK]
                back_own[j - 1, HEAD_DIM : 2 * HEAD_DIM, :] = query_grad[:, BLOCK:]
                back_own[j - 1, 2 * HEAD_DIM : 4 * HEAD_DIM, :] = merged

            @pl.when((j > 0) & (j - 1 != member))
            def _():
                back_copy(lax.rem(j - 1 - member + HALF, HALF)).start()

            @pl.when(j == 1)
            def _():
                onward(2)
                far_side(1)
                swap(3)

            @pl.when(j == 2)
            def _():
                near_side(3)
                far_side(3)

            @pl.when(j == 4)
            def _():
                relay(1)
                onward(1)
                swap(0)

            @pl.when(j == 6)
            def _():
                deeper(2)

            return nothing

        lax.fori_loop(0, HALF, prepare, 0)
        lax.fori_loop(1 - part, HALF + 1, per_key, 0)
        back_far[member] = back_own[member]

    pl.run_scoped(
        attention,
        pltpu.VMEM((HALF, HEAD_DIM, 2 * BLOCK), BF16),
        pltpu.VMEM((HALF, HEAD_DIM, 2 * BLOCK), BF16),
        pltpu.VMEM((HALF, 2 * BLOCK, 2 * HEAD_DIM), BF16),
        pltpu.VMEM((HALF, 1, 2 * BLOCK), F32),
        pltpu.VMEM((HALF, HEAD_DIM, 2 * BLOCK), F32),
        pltpu.VMEM((BLOCK, HEAD_DIM), BF16),
        pltpu.VMEM((BLOCK, HEAD_DIM), BF16),
        pltpu.VMEM((2 * BLOCK, 2 * HEAD_DIM), F32),
    )

    turned_copy = core_copy(turned_own, turned_far, 5)

    def tail_compute(chain, owner, slot):
        lanes = slice(chain * 256, chain * 256 + 256)
        own_lanes = pl.ds(pl.multiple_of(core * half_width + chain * 256, 128), 256)
        values, row = [], 0
        for size, base in ((heads, 2 * pairs), (pairs, 0), (pairs, pairs)):
            count = size * HEAD_DIM // RING
            rows = pl.ds(pl.multiple_of(base * HEAD_DIM + owner * count, 16), count)
            value = jnp.dot(
                turned_own[rows, :], normed_ref[:, own_lanes], preferred_element_type=F32
            )
            value += jnp.dot(turned_far[rows, :], normed_far[:, lanes], preferred_element_type=F32)
            values.append((row, value))
            row += count
        return values

    def tail_finish(chain, row, value):
        grads_out[row : row + value.shape[0], chain * 256 : chain * 256 + 256] = value

    tails = (
        Spread(
            0,
            tail_compute,
            0,
            tail_sent_a,
            (tail_came_a0, tail_came_a1, tail_came_a2),
            tail_came_a0,
            0,
            tail_send,
            tail_recv,
        ),
        Spread(
            1,
            tail_compute,
            0,
            tail_sent_b,
            (tail_came_b0, tail_came_b1, tail_came_b2),
            tail_came_b0,
            0,
            tail_send,
            tail_recv,
        ),
    )

    def finish_all(natural, summed, query_ref, key_ref, tokens_ref, weights_ref):
        loads = [
            pltpu.make_async_copy(query_hbm, query_ref, load_sem.at[2]),
            pltpu.make_async_copy(key_hbm, key_ref, load_sem.at[3]),
            pltpu.make_async_copy(tokens_hbm, tokens_ref, load_sem.at[4]),
            pltpu.make_async_copy(weights_hbm, weights_ref, load_sem.at[5]),
        ]
        for copy in loads:
            copy.start()
        half_dim = HEAD_DIM // 2
        cosine, sine = table_ref[0:half_dim, :], table_ref[half_dim:HEAD_DIM, :]
        query_gain = table_ref[HEAD_DIM : 2 * HEAD_DIM, :]
        key_gain = table_ref[2 * HEAD_DIM : 3 * HEAD_DIM, :]

        def head_rows(index):
            return pl.ds(pl.multiple_of(index * HEAD_DIM, HEAD_DIM), HEAD_DIM)

        def query_head(head, total):
            low = pl.multiple_of(lax.rem(head, 2) * HEAD_DIM, HEAD_DIM)
            upstream = turn_back(
                back_far[head // 2, pl.ds(low, HEAD_DIM), :].astype(F32), cosine, sine
            )
            back, terms = column_norm_back(query_ref[head], query_gain, upstream)
            turned_own[head_rows(2 * pairs + head), :] = back.astype(BF16)
            return total + terms

        def key_head(pair, total):
            upstream = back_far[pair, 2 * HEAD_DIM : 4 * HEAD_DIM, :].astype(F32)
            upstream += extra_far[pair].astype(F32)
            back, terms = column_norm_back(
                key_ref[pair],
                key_gain,
                turn_back(upstream[:HEAD_DIM], cosine, sine),
            )
            turned_own[head_rows(pair), :] = back.astype(BF16)
            turned_own[head_rows(pairs + pair), :] = upstream[HEAD_DIM:].astype(BF16)
            return total + terms


        along.stage_two()
        relay(3)
        near_side(0)
        onward(3)
        deeper(1)
        far_side(0)

        def arrive(step, nothing):
            back_copy(step).wait_recv()
            return nothing

        lax.fori_loop(1, HALF, arrive, 0)

        def extra_arrive(group, nothing):
            extra_copy(group).wait_recv()
            return nothing

        @pl.when(place == HALF - 1)
        def _():
            lax.fori_loop(0, HALF, extra_arrive, 0)

        @pl.when(place != HALF - 1)
        def _():
            extra_far[...] = jnp.zeros(extra_far.shape, BF16)

        for copy in loads:
            copy.wait()
        nothing = jnp.zeros((HEAD_DIM, BLOCK), F32)
        query_terms = lax.fori_loop(0, heads, query_head, nothing)
        key_terms = lax.fori_loop(0, pairs, key_head, nothing)
        turned_copy.start()
        for row in range(0, turned_own.shape[0], 128):
            natural[:, row : row + 128] = turned_own[row : row + 128, :].astype(F32).T.astype(BF16)
        normed_copy.wait_recv()
        turned_copy.wait_recv()

        def tail_one(index, carry):
            for chain in tails:
                chain.stage_one(1 - index // 4, lax.rem(index + 1, 4))
            return carry

        lax.fori_loop(0, 8, tail_one, 0)
        along.stage_three()
        relay(0)
        onward(0)
        deeper(3)
        summed[...] = dot_dims(natural[...], weights_ref[...], 1, 1)
        middle_load.wait()

        def token_rows(index, total):
            rows = pl.ds(pl.multiple_of(index * 32, 32), 32)
            values, upstream = tokens_ref[rows, :].astype(F32), summed[rows, :]
            inverse = lax.rsqrt(jnp.mean(values * values, axis=-1, keepdims=True) + EPSILON)
            scaled = upstream * attn_gain_ref[...]
            weight = jnp.sum(scaled * values, axis=-1, keepdims=True) / values.shape[1]
            tokens_out[rows, :] += inverse * scaled - values * inverse**3 * weight
            return total + jnp.sum(upstream * values * inverse, axis=0, keepdims=True)

        terms = lax.fori_loop(
            0, BLOCK // 32, token_rows, jnp.zeros((1, tokens_ref.shape[1]), F32)
        )
        gain_own[...] = jnp.zeros(gain_own.shape, F32)
        gain_own[0:1, :] = terms
        gain_own[1:2, :] = ffn_terms_ref[...]
        gain_own[2:3, 0:HEAD_DIM] = jnp.sum(query_terms.T, axis=0, keepdims=True)
        gain_own[3:4, 0:HEAD_DIM] = jnp.sum(key_terms.T, axis=0, keepdims=True)

    width = normed_ref.shape[1]
    pl.run_scoped(
        finish_all,
        pltpu.VMEM((BLOCK, turned_own.shape[0]), BF16),
        pltpu.VMEM((BLOCK, width), F32),
        pltpu.VMEM((heads, HEAD_DIM, BLOCK), F32),
        pltpu.VMEM((pairs, HEAD_DIM, BLOCK), F32),
        pltpu.VMEM((BLOCK, width), BF16),
        pltpu.VMEM(weights_hbm.shape, BF16),
    )

    def tail_two(index, carry):
        for chain in tails:
            chain.stage_two(lax.rem(index + 1, 4))
        return carry

    def tail_three(depth, carry):
        for chain in tails:
            chain.stage_three(depth)
        return carry

    gain_swap = core_copy(gain_own, gain_came, 22)
    gain_swap.start()

    def gain_copy(step):
        peer = (lax.rem(place + step, RING), core)
        return remote(
            gain_all.at[place], gain_all.at[place], gain_send.at[step], gain_recv.at[step], peer
        )

    def gain_start(step, carry):
        gain_copy(step).start()
        return carry

    def gain_arrive(step, carry):
        gain_copy(step).wait()
        return carry

    gain_swap.wait()
    gain_all[place] = gain_own[...] + gain_came[...]
    lax.fori_loop(1, RING, gain_start, 0)
    lax.fori_loop(0, 4, tail_two, 0)
    lax.fori_loop(1, 4, tail_three, 0)
    along.close(deep_finish)
    for chain in chains:
        chain.close(finish)
    for chain in tails:
        chain.close(tail_finish)
    lax.fori_loop(1, RING, gain_arrive, 0)

    def gain_sum(index, total):
        return total + gain_all[index]

    gains_out[...] = lax.fori_loop(1, RING, gain_sum, gain_all[0])

    def settle(step, nothing):
        back_copy(step).wait_send()
        cot_copy(step).wait_send()
        return nothing

    lax.fori_loop(1, HALF, settle, 0)

    @pl.when(part == 1)
    def _():
        extra_copy(member).wait_send()

    for copy in sides + [normed_copy, turned_copy]:
        copy.wait_send()
    for slot in range(8):
        for chain in range(2):
            mate_copy(chain, slot).wait_send()
            relay_copy(chain, slot).wait_send()
            if slot % 4 not in EARLY:
                swap_copy(chain, slot).wait_send()
    for chain in chains + tails + (along,):
        chain.drain()


def back_call(call_id, inputs, loads):
    hidden, side, ffn_low = inputs[1:4]
    rows, hidden_width = hidden.shape
    width = ffn_low.shape[1]
    wide, narrow = hidden_width // RING, width // RING
    total = (HEADS + 2 * KV_HEADS) * HEAD_DIM

    def buffers(sizes):
        return [
            pltpu.VMEM((slots, sizes[chain], 256), BF16)
            for chain in range(2)
            for slots in (8, 8, 4, 3)
        ]

    def chain_buffers(split):
        rest = (split[1] + 1) * narrow
        shapes = ((8, rest), (8, rest), (7, 2 * wide + rest), (4, 2 * wide + rest), (3, 2 * wide + rest))
        return [pltpu.VMEM((*shape, 256), BF16) for shape in shapes]

    dma = pltpu.SemaphoreType.DMA
    specs = [VMEM_SPEC] * (len(inputs) + len(loads))
    staged = (2, 3, 4, 5, 6, 8, 11)
    for index in (0, 1, *staged, *range(len(inputs), len(specs))):
        specs[index] = HBM_SPEC
    return pl.pallas_call(
        back_kernel,
        out_shape=(
            jax.ShapeDtypeStruct((wide, width // 2), F32),
            jax.ShapeDtypeStruct((wide, width // 2), F32),
            jax.ShapeDtypeStruct((narrow, hidden_width // 2), F32),
            jax.ShapeDtypeStruct((narrow, width // 2), F32),
            jax.ShapeDtypeStruct((total // RING, width // 2), F32),
            jax.ShapeDtypeStruct((rows, width), F32),
            jax.ShapeDtypeStruct((4, width), F32),
        ),
        in_specs=specs,
        out_specs=(VMEM_SPEC,) * 7,
        scratch_shapes=[pltpu.VMEM(inputs[index].shape, BF16) for index in staged]
        + [
            pltpu.VMEM((4, 2, 8, wide, rows), BF16),
            pltpu.VMEM((2, 2, rows, width // 2), BF16),
            pltpu.VMEM(side.shape, BF16),
            pltpu.VMEM((rows, hidden_width // 2), BF16),
            pltpu.VMEM((rows, hidden_width // 2), BF16),
            pltpu.VMEM((rows, width // 2), BF16),
            pltpu.VMEM((width // 2, rows), BF16),
            pltpu.VMEM((rows, width // 2), BF16),
            pltpu.VMEM((HALF, 2 * HEAD_DIM, rows), BF16),
            pltpu.VMEM((HALF, 4 * HEAD_DIM, rows), BF16),
            pltpu.VMEM((HALF, 4 * HEAD_DIM, rows), BF16),
            pltpu.VMEM((2 * HEAD_DIM, rows), BF16),
            pltpu.VMEM((HALF, 2 * HEAD_DIM, rows), BF16),
            pltpu.VMEM((total, rows), BF16),
            pltpu.VMEM((total, rows), BF16),
            pltpu.VMEM((4, width), F32),
            pltpu.VMEM((4, width), F32),
            pltpu.VMEM((RING, 4, width), F32),
        ]
        + chain_buffers(DOWN_CHUNKS[0])
        + chain_buffers(DOWN_CHUNKS[1])
        + [pltpu.VMEM((*lead, DOWN_CHUNKS[2][1] * narrow, 256), BF16) for lead in ((3, 4), (3, 4), (2,), (1,))]
        + [dma((6,)), dma((6,))]
        + buffers((total // RING, total // RING))
        + [dma((2, 15))] * 4
        + [dma((HALF,))] * 4
        + [dma((23,))] * 2
        + [dma((RING,))] * 2
        + [dma((HALF,))] * 2
        + [dma((6,)), dma((7,))]
        + [dma((2, 2, 8))]
        + [dma((2, 8))] * 6
        + [dma],
        compiler_params=pltpu.CompilerParams(
            collective_id=call_id, has_side_effects=True, vmem_limit_bytes=63 << 20
        ),
        name="backward_spread",
    )(*inputs, *loads)


def head_frequencies(rows):
    half = HEAD_DIM // 2
    frequencies = THETA ** (-(2.0 / HEAD_DIM) * np.arange(half, dtype=np.float32))
    return jnp.asarray(np.repeat(frequencies.astype(np.float32)[:, None], rows, axis=1))


def front_kernel(
    gain_ref,
    place_ref,
    query_gain_ref,
    key_gain_ref,
    frequency_ref,
    tokens_hbm,
    w_query_hbm,
    w_key_hbm,
    w_value_hbm,
    w_out_hbm,
    w_gate_hbm,
    w_up_hbm,
    w_down_hbm,
    qkv_out,
    starts_out,
    normed_out,
    part_out,
    mixed_out,
    inv_out,
    out_full,
    table_ref,
    query_hbm,
    key_hbm,
    weights_hbm,
    gate_far,
    up_far,
    down_far,
    home,
    key_nat,
    totals,
    accs,
    tokens_ref,
    query_out,
    key_out,
    weights_out,
    own_start_ref,
    keep_sem,
    own_sem,
    send_sem,
    recv_sem,
    start_send,
    start_recv,
    mixed_send,
    mixed_recv,
    kv_send,
    kv_recv,
    extra_send,
    extra_recv,
    core_send,
    core_recv,
):
    place, core = lax.axis_index("ctx"), lax.axis_index("fsdp")
    part, member = place // HALF, lax.rem(place, HALF)
    rows = tokens_ref.shape[0]
    depth = w_query_hbm.shape[0]
    partner = (place, 1 - core)
    tokens_load = pltpu.make_async_copy(tokens_hbm, tokens_ref, keep_sem.at[0])
    tokens_load.start()
    places = place * rows + lax.broadcasted_iota(jnp.int32, (1, rows), 1)
    own_start_ref[...] = places - place_ref[...]
    angles = frequency_ref[...] * place_ref[...].astype(F32)
    half = HEAD_DIM // 2
    table_ref[0:half, :] = jnp.cos(angles)
    table_ref[half:HEAD_DIM, :] = jnp.sin(angles)
    for index, source in enumerate((query_gain_ref, key_gain_ref)):
        table_ref[(index + 1) * HEAD_DIM : (index + 2) * HEAD_DIM, :] = jnp.broadcast_to(
            source[...], (rows, HEAD_DIM)
        ).T
    greet([partner] + [(lax.rem(place + step, RING), core) for step in range(1, RING)])

    def remote(source, target, send, recv, peer):
        return pltpu.make_async_remote_copy(
            src_ref=source,
            dst_ref=target,
            send_sem=send,
            recv_sem=recv,
            device_id=peer,
            device_id_type=MESH,
        )

    def mate(step):
        return (part * HALF + lax.rem(member + step, HALF), core)

    copies, near_copies = [], []

    def share(source, target, near_target=None):
        index = len(copies)
        copy = remote(source, target, core_send.at[index], core_recv.at[index], partner)
        copy.start()
        copies.append(copy)
        if near_target is not None:
            near = pltpu.make_async_copy(source, near_target, own_sem.at[index])
            near.start()
            near_copies.append(near)

    column = 0
    own_depth = pl.ds(pl.multiple_of(core * depth, 128), depth)
    for source in (w_key_hbm, w_value_hbm, w_query_hbm):
        window = pl.ds(column, source.shape[1])
        target = weights_out.at[own_depth, window]
        share(source, target, target)
        column += source.shape[1]

    target = out_full.at[own_depth, :]
    share(w_out_hbm, target, target)
    for source, target in ((w_gate_hbm, gate_far), (w_up_hbm, up_far), (w_down_hbm, down_far)):
        share(source, target)

    def start_copy(step):
        return remote(
            own_start_ref,
            starts_out.at[member],
            start_send.at[step],
            start_recv.at[step],
            mate(step),
        )

    for step in range(1, HALF):
        start_copy(step).start()
    starts_out[member] = own_start_ref[...]

    def norm_rows(index, nothing):
        window = pl.ds(pl.multiple_of(index * 32, 32), 32)
        values = tokens_ref[window, :].astype(F32)
        inverse = lax.rsqrt(jnp.mean(values * values, axis=-1, keepdims=True) + EPSILON)
        normed_out[window, :] = (values * inverse * gain_ref[...]).astype(BF16)
        return nothing

    tokens_load.wait()
    lax.fori_loop(0, rows // 32, norm_rows, 0)
    cosine, sine = table_ref[0:half, :], table_ref[half:HEAD_DIM, :]
    query_gain = table_ref[HEAD_DIM : 2 * HEAD_DIM, :]
    key_gain = table_ref[2 * HEAD_DIM : 3 * HEAD_DIM, :]

    def project(column, count):
        window = pl.ds(column, count)
        product = jnp.dot(normed_out[...], weights_out[:, window], preferred_element_type=F32)
        return product.T

    def turned(values, gain):
        mean = jnp.mean(values * values, axis=0, keepdims=True)
        values = values * lax.rsqrt(mean + EPSILON) * gain
        first, second = values[:half], values[half:]
        return jnp.concatenate(
            [first * cosine - second * sine, second * cosine + first * sine], axis=0
        ).astype(BF16)

    kv_width = KV_HEADS * HEAD_DIM
    copies[0].wait_recv()
    near_copies[0].wait()

    def key_chunk(index, nothing):
        products = project(pl.multiple_of(index * 256, 256), 256)
        for offset in range(4):
            raw = products[offset * HEAD_DIM : (offset + 1) * HEAD_DIM]
            group = index * 4 + offset
            key_out[group] = raw
            home[group, 2 * HEAD_DIM : 3 * HEAD_DIM, :] = turned(raw, key_gain)
        return nothing

    lax.fori_loop(0, KV_HEADS // 4, key_chunk, 0)
    copies[1].wait_recv()
    near_copies[1].wait()

    def value_chunk(index, nothing):
        products = project(pl.multiple_of(kv_width + index * 256, 256), 256)
        for offset in range(4):
            value = products[offset * HEAD_DIM : (offset + 1) * HEAD_DIM].astype(BF16)
            home[index * 4 + offset, 3 * HEAD_DIM : 4 * HEAD_DIM, :] = value
        return nothing

    lax.fori_loop(0, KV_HEADS // 4, value_chunk, 0)

    window = pl.ds(2 * HEAD_DIM, 2 * HEAD_DIM)

    def kv_copy(step):
        return remote(
            home.at[lax.rem(member + step, HALF), window],
            qkv_out.at[1 + member, window],
            kv_send.at[step],
            kv_recv.at[step],
            mate(step),
        )

    def kv_start(step, nothing):
        kv_copy(HALF - step).start()
        return nothing

    def extra_copy(group):
        return remote(
            home.at[group, window, pl.ds(rows - EDGE, EDGE)],
            qkv_out.at[0, window, pl.ds(rows - EDGE, EDGE)],
            extra_send.at[group],
            extra_recv.at[group],
            (HALF + group, core),
        )

    def extra_start(group, nothing):
        extra_copy(group).start()
        return nothing

    @pl.when(place == HALF - 1)
    def _():
        lax.fori_loop(0, HALF, extra_start, 0)

    lax.fori_loop(1, HALF, kv_start, 0)
    copies[2].wait_recv()
    near_copies[2].wait()

    def block_copy(step):
        peer = mate(step)
        return remote(
            home.at[lax.rem(member + step, HALF), pl.ds(0, 2 * HEAD_DIM)],
            qkv_out.at[1 + member, pl.ds(0, 2 * HEAD_DIM)],
            send_sem.at[step],
            recv_sem.at[step],
            peer,
        )

    def query_chunk(turn, nothing):
        index = lax.rem(member // 2 - turn + 4, 4)
        products = project(pl.multiple_of(2 * kv_width + index * 256, 256), 256)
        for offset in range(4):
            raw = products[offset * HEAD_DIM : (offset + 1) * HEAD_DIM]
            query_out[index * 4 + offset] = raw
            low = (offset % 2) * HEAD_DIM
            home[index * 2 + offset // 2, low : low + HEAD_DIM, :] = turned(
                raw, query_gain
            )
        for offset in range(2):
            group = index * 2 + offset

            @pl.when(group != member)
            def _():
                block_copy(lax.rem(group - member + HALF, HALF)).start()

        return nothing

    lax.fori_loop(0, HEADS // 4, query_chunk, 0)
    keeps = [
        pltpu.make_async_copy(source, target, keep_sem.at[1 + index])
        for index, (source, target) in enumerate(
            ((query_out, query_hbm), (key_out, key_hbm), (weights_out, weights_hbm))
        )
    ]
    for keep in keeps:
        keep.start()
    qkv_out[1 + member] = home[member]
    base = part * HALF - 1

    def mixed_copy(step):
        peer = mate(step)
        return remote(
            part_out.at[lax.rem(member + step, HALF)],
            mixed_out.at[member],
            mixed_send.at[step],
            mixed_recv.at[step],
            peer,
        )

    def query_of(i):
        query_t = jnp.concatenate(
            [qkv_out[i, 0:HEAD_DIM, :], qkv_out[i, HEAD_DIM : 2 * HEAD_DIM, :]], axis=1
        ) * jnp.asarray(HEAD_DIM**-0.5, BF16)
        return query_t, jnp.concatenate([starts_out[i - 1]] * 2, axis=1)

    def meet(query_t, keys, values, ok, carry):
        total, acc = carry
        probs = jnp.exp(jnp.dot(keys, query_t, preferred_element_type=F32))
        probs = jnp.where(ok(lax.broadcasted_iota(jnp.int32, probs.shape, 0)), probs, 0.0)
        total = total + jnp.sum(probs, axis=0, keepdims=True)
        return total, acc + jnp.dot(values, probs.astype(BF16), preferred_element_type=F32)

    def fetch(i, nothing):
        @pl.when(i - 1 != member)
        def _():
            step = lax.rem(member - i + 1 + HALF, HALF)
            start_copy(step).wait_recv()
            kv_copy(step).wait_recv()
            block_copy(step).wait_recv()

        key_nat[i] = transposed(qkv_out[i, 2 * HEAD_DIM : 3 * HEAD_DIM, :])
        return nothing

    def inner(i):
        query_t, start = query_of(i)
        places = (base + i) * BLOCK + lax.broadcasted_iota(jnp.int32, (1, BLOCK), 1)
        query_place = jnp.concatenate([places] * 2, axis=1)

        def step(diagonal, j, carry):
            def ok(offset):
                key_place = (base + j) * BLOCK + offset
                if diagonal:
                    return (key_place >= start) & (key_place <= query_place)
                return key_place >= start

            values = qkv_out[j, 3 * HEAD_DIM : 4 * HEAD_DIM, :]
            return meet(query_t, key_nat[j], values, ok, carry)

        carry = (jnp.zeros((1, 2 * BLOCK), F32), jnp.zeros((HEAD_DIM, 2 * BLOCK), F32))
        pairs = (i - 1) // 2

        def two(index, carry):
            return step(False, 2 * index + 2, step(False, 2 * index + 1, carry))

        carry = lax.fori_loop(0, pairs, two, carry)
        carry = lax.fori_loop(2 * pairs + 1, i, functools.partial(step, False), carry)
        totals[i - 1], accs[i - 1] = step(True, i, carry)

    def outer(i):
        @pl.when((part == 1) & (i == 1))
        def _():
            extra_copy(member).wait_recv()
            qkv_out[0, 2 * HEAD_DIM :, 0 : rows - EDGE] = jnp.zeros(
                (2 * HEAD_DIM, rows - EDGE), BF16
            )
            key_nat[0] = transposed(qkv_out[0, 2 * HEAD_DIM : 3 * HEAD_DIM, :])

        @pl.when(part == 1)
        def _():
            query_t, start = query_of(i)

            def ok(offset):
                return HALF * BLOCK - EDGE + offset >= start

            values = qkv_out[0, 3 * HEAD_DIM : 4 * HEAD_DIM, rows - EDGE :]
            totals[i - 1], accs[i - 1] = meet(
                query_t, key_nat[0, rows - EDGE :, :], values, ok, (totals[i - 1], accs[i - 1])
            )

        inverse = 1.0 / totals[i - 1]
        low = (accs[i - 1] * inverse).astype(BF16)
        part_out[i - 1, 0:HEAD_DIM, :] = low[:, :BLOCK]
        part_out[i - 1, HEAD_DIM:, :] = low[:, BLOCK:]
        inv_out[i - 1] = inverse

        @pl.when(i - 1 != member)
        def _():
            mixed_copy(lax.rem(i - 1 - member + HALF, HALF)).start()

    def order(turn):
        return turn + turn // 5 * (5 + lax.rem(turn + 3 + member, 4) - turn)

    def per_query(turn, nothing):
        @pl.when(turn <= 4)
        def _():
            fetch(turn, 0)

        @pl.when(turn == 5)
        def _():
            lax.fori_loop(5, HALF + 1, fetch, 0)

        @pl.when(turn <= HALF)
        def _():
            inner(order(turn))

        @pl.when(turn > lag)
        def _():
            outer(order(turn - lag))

        return nothing

    lag = 0
    lax.fori_loop(1, HALF + lag + 1, per_query, 0)
    mixed_out[member] = part_out[member]

    def settle(step, nothing):
        block_copy(step).wait_send()
        kv_copy(step).wait_send()
        start_copy(step).wait_send()
        mixed_copy(step).wait()
        return nothing

    lax.fori_loop(1, HALF, settle, 0)

    def extra_settle(group, nothing):
        extra_copy(group).wait_send()
        return nothing

    @pl.when(place == HALF - 1)
    def _():
        lax.fori_loop(0, HALF, extra_settle, 0)

    for copy in copies[:3]:
        copy.wait_send()
    for copy in copies[3:]:
        copy.wait()
    for near in near_copies[3:] + keeps:
        near.wait()


def front_call(call_id, inputs, loads):
    rows, width = loads[0].shape
    half_depth, hidden_width = loads[5].shape
    total = (HEADS + 2 * KV_HEADS) * HEAD_DIM
    dma = pltpu.SemaphoreType.DMA
    query_raw = (HEADS, HEAD_DIM, rows)
    key_raw = (KV_HEADS, HEAD_DIM, rows)
    return pl.pallas_call(
        front_kernel,
        out_shape=(
            jax.ShapeDtypeStruct((HALF + 1, 4 * HEAD_DIM, rows), BF16),
            jax.ShapeDtypeStruct((HALF, 1, rows), jnp.int32),
            jax.ShapeDtypeStruct((rows, width), BF16),
            jax.ShapeDtypeStruct((HALF, 2 * HEAD_DIM, rows), BF16),
            jax.ShapeDtypeStruct((HALF, 2 * HEAD_DIM, rows), BF16),
            jax.ShapeDtypeStruct((HALF, 1, 2 * rows), F32),
            jax.ShapeDtypeStruct((width, width), BF16),
            jax.ShapeDtypeStruct((3 * HEAD_DIM, rows), F32),
            jax.ShapeDtypeStruct(query_raw, F32),
            jax.ShapeDtypeStruct(key_raw, F32),
            jax.ShapeDtypeStruct((width, total), BF16),
            jax.ShapeDtypeStruct((half_depth, hidden_width), BF16),
            jax.ShapeDtypeStruct((half_depth, hidden_width), BF16),
            jax.ShapeDtypeStruct((hidden_width // 2, width), BF16),
        ),
        in_specs=[VMEM_SPEC] * len(inputs) + [HBM_SPEC] * len(loads),
        out_specs=(VMEM_SPEC,) * 8 + (HBM_SPEC,) * 6,
        scratch_shapes=[
            pltpu.VMEM((HALF, 4 * HEAD_DIM, rows), BF16),
            pltpu.VMEM((HALF + 1, rows, HEAD_DIM), BF16),
            pltpu.VMEM((HALF, 1, 2 * rows), F32),
            pltpu.VMEM((HALF, HEAD_DIM, 2 * rows), F32),
            pltpu.VMEM((rows, width), BF16),
            pltpu.VMEM(query_raw, F32),
            pltpu.VMEM(key_raw, F32),
            pltpu.VMEM((width, total), BF16),
            pltpu.VMEM((1, rows), jnp.int32),
            dma((4,)),
            dma((4,)),
        ]
        + [dma((HALF,))] * 10
        + [dma((7,))] * 2,
        compiler_params=pltpu.CompilerParams(
            collective_id=call_id, has_side_effects=True, vmem_limit_bytes=63 << 20
        ),
        name="front_heads",
    )(*inputs, *loads)


def ffn_kernel(
    tokens_ref,
    mixed_ref,
    w_out_ref,
    gain_ref,
    cot_ref,
    gate_own,
    gate_far,
    up_own,
    up_far,
    down_own,
    down_far,
    pair_hbm,
    hidden_out,
    output_out,
    ffn_out,
    side_out,
    mixed_back_out,
    grad_middle_out,
    terms_out,
    swap_out,
    near_out,
    pair_out,
    pair_sem,
    middle,
    result,
    upstream,
    middle_low,
    swap_send,
    swap_recv,
    near_send,
    near_recv,
):
    step = pl.program_id(0)
    place, core = lax.axis_index("ctx"), lax.axis_index("fsdp")
    x, y, z = lax.rem(place, 2), lax.rem(place // 2, 2), place // 4
    near = (place + 1 - 2 * x, place + 2 - 4 * y)
    wide = pair_out.shape[1] // 2
    half_width = gate_own.shape[0]
    strip_owners = pair_out.shape[0] // 4
    plane = lax.rem(z + 6 - step, 4)

    def remote(source, target, send, recv, peer):
        return pltpu.make_async_remote_copy(
            src_ref=source,
            dst_ref=target,
            send_sem=send,
            recv_sem=recv,
            device_id=peer,
            device_id_type=MESH,
        )

    def keep_pair(turn):
        window = pl.ds(lax.rem(z + 6 - turn, 4) * strip_owners, strip_owners)
        return pltpu.make_async_copy(pair_out.at[window], pair_hbm.at[window], pair_sem.at[turn])

    def near_copy(chain, other):
        target = core if other == 0 else 1 - core
        lanes = pl.ds(pl.multiple_of(target * half_width, 128), half_width)
        return remote(
            ffn_out.at[:, lanes],
            near_out.at[chain, other],
            near_send.at[chain, other],
            near_recv.at[chain, other],
            (near[chain], target),
        )

    def swap_copy(chain, slot):
        return remote(
            pair_out.at[block_owner(chain, place, 1, slot), pl.ds(chain * wide, wide)],
            swap_out.at[chain, slot],
            swap_send.at[chain, slot],
            swap_recv.at[chain, slot],
            (near[chain], core),
        )

    rows, width = tokens_ref.shape
    strip = 32

    def strips(work):
        def one(index, carry):
            return work(pl.ds(pl.multiple_of(index * strip, strip), strip), carry)

        return one

    @pl.when(step == 0)
    def _():
        mixed = mixed_ref[...].astype(F32).T.astype(BF16)
        middle[...] = tokens_ref[...].astype(F32) + jnp.dot(
            mixed, w_out_ref[...], preferred_element_type=F32
        )

        def norm(window, carry):
            values = middle[window, :]
            inverse = lax.rsqrt(jnp.mean(values * values, axis=-1, keepdims=True) + EPSILON)
            ffn_out[window, :] = (values * inverse * gain_ref[...]).astype(BF16)
            result[window, :] = values
            return carry

        lax.fori_loop(0, rows // strip, strips(norm), 0)
        greet([(peer, target) for peer in near for target in (core, 1 - core)])
        for chain in range(2):
            for other in range(2):
                near_copy(chain, other).start()
        upstream[...] = jnp.zeros(upstream.shape, F32)
        side_out[0] = cot_ref[...].astype(F32).T.astype(BF16)

    own = pl.ds(pl.multiple_of(core * half_width, 128), half_width)
    far = pl.ds(pl.multiple_of((1 - core) * half_width, 128), half_width)

    def strip_of_hidden(down_ref):
        def ahead(near_ref, far_ref):
            return jnp.dot(ffn_out[:, own], near_ref[...], preferred_element_type=F32) + jnp.dot(
                ffn_out[:, far], far_ref[...], preferred_element_type=F32
            )

        gate_pre, up_pre = ahead(gate_own, gate_far), ahead(up_own, up_far)
        grad_hidden = dot_dims(cot_ref[...], down_ref[...], 1, 1)
        gate_sig = jax.nn.sigmoid(gate_pre)
        gate_act = gate_pre * gate_sig
        hidden_out[...] = (gate_act * up_pre).astype(BF16)
        gate_back = (
            grad_hidden * up_pre * (gate_sig * (1.0 + gate_pre * (1.0 - gate_sig)))
        ).astype(BF16)
        up_back = (grad_hidden * gate_act).astype(BF16)
        result[...] += jnp.dot(hidden_out[...], down_ref[...], preferred_element_type=F32)
        for window, gate_ref, up_ref in ((own, gate_own, up_own), (far, gate_far, up_far)):
            upstream[:, window] += dot_dims(gate_back, gate_ref[...], 1, 1) + dot_dims(
                up_back, up_ref[...], 1, 1
            )
        for base, back in ((0, gate_back), (wide, up_back)):
            turned = back.astype(F32).T.astype(BF16)
            for index in range(strip_owners):
                pair_out[plane * strip_owners + index, base : base + wide, :] = turned[
                    index * wide : (index + 1) * wide
                ]
        keep_pair(step).start()

        @pl.when(step < len(EARLY))
        def _():
            for turned_side in range(2):
                for chain in range(2):
                    swap_copy(chain, turned_side * 4 + 2 - step).start()


    @pl.when(plane // 2 == core)
    def _():
        strip_of_hidden(down_own)

    @pl.when(plane // 2 != core)
    def _():
        strip_of_hidden(down_far)

    @pl.when(step == pl.num_programs(0) - 1)
    def _():
        output_out[...] = result[...].astype(BF16)

        def back(window, total):
            values, grads = middle[window, :], upstream[window, :]
            inverse = lax.rsqrt(jnp.mean(values * values, axis=-1, keepdims=True) + EPSILON)
            scaled = grads * gain_ref[...]
            weight = jnp.sum(scaled * values, axis=-1, keepdims=True) / width
            grad_middle = cot_ref[window, :].astype(F32) + (
                inverse * scaled - values * inverse**3 * weight
            )
            grad_middle_out[window, :] = grad_middle
            middle_low[window, :] = grad_middle.astype(BF16)
            return total + jnp.sum(grads * values * inverse, axis=0, keepdims=True)

        terms_out[...] = lax.fori_loop(
            0, rows // strip, strips(back), jnp.zeros((1, width), F32)
        )
        mixed_back_out[...] = dot_dims(w_out_ref[...], middle_low[...], 1, 1).astype(BF16)
        side_out[1] = middle_low[...].astype(F32).T.astype(BF16)
        for turn in range(4):
            keep_pair(turn).wait()
        for chain in range(2):
            for other in range(2):
                near_copy(chain, other).wait()

        for depth in EARLY:
            for slot in (4 + depth, depth):
                for chain in range(2):
                    swap_copy(chain, slot).wait()


def ffn_call(call_id, tokens, mixed_t, w_out, gain, cot, gate, up, down):
    rows, width = tokens.shape
    half_depth, hidden_width = gate[0].shape
    steps = 4
    chunk = hidden_width // steps
    wide = hidden_width // RING

    def whole(*shape):
        return pl.BlockSpec(shape, lambda i: (0,) * len(shape))

    def turn(i):
        return lax.rem(lax.axis_index("ctx") // 4 + 6 - i, steps)

    columns = pl.BlockSpec((half_depth, chunk), lambda i: (0, turn(i)))
    return pl.pallas_call(
        ffn_kernel,
        grid_spec=pl.GridSpec(
            grid=(steps,),
            in_specs=[
                whole(rows, width),
                whole(width, rows),
                whole(width, width),
                whole(1, width),
                whole(rows, width),
                columns,
                columns,
                columns,
                columns,
                pl.BlockSpec((chunk, width), lambda i: (lax.rem(turn(i), 2), 0)),
                pl.BlockSpec((chunk, width), lambda i: (lax.rem(turn(i), 2), 0)),
            ],
            out_specs=(
                HBM_SPEC,
                pl.BlockSpec((rows, chunk), lambda i: (0, turn(i))),
                whole(rows, width),
                whole(rows, width),
                whole(2, width, rows),
                whole(width, rows),
                whole(rows, width),
                whole(1, width),
                HBM_SPEC,
                HBM_SPEC,
            ),
            scratch_shapes=[
                pltpu.VMEM((RING, 2 * wide, rows), BF16),
                pltpu.SemaphoreType.DMA((4,)),
            ]
            + [pltpu.VMEM((rows, width), F32)] * 3
            + [pltpu.VMEM((rows, width), BF16)]
            + [pltpu.SemaphoreType.DMA((2, 8))] * 2
            + [pltpu.SemaphoreType.DMA((2, 2))] * 2,
        ),
        out_shape=(
            jax.ShapeDtypeStruct((RING, 2 * wide, rows), BF16),
            jax.ShapeDtypeStruct((rows, hidden_width), BF16),
            jax.ShapeDtypeStruct((rows, width), BF16),
            jax.ShapeDtypeStruct((rows, width), BF16),
            jax.ShapeDtypeStruct((2, width, rows), BF16),
            jax.ShapeDtypeStruct((width, rows), BF16),
            jax.ShapeDtypeStruct((rows, width), F32),
            jax.ShapeDtypeStruct((1, width), F32),
            jax.ShapeDtypeStruct((2, 8, wide, rows), BF16),
            jax.ShapeDtypeStruct((2, 2, rows, half_depth), BF16),
        ),
        compiler_params=pltpu.CompilerParams(
            collective_id=call_id, has_side_effects=True, vmem_limit_bytes=63 << 20
        ),
        name="ffn_both_ways",
    )(tokens, mixed_t, w_out, gain, cot, *gate, *up, *down)


def settle_kernel(*refs):
    count = 7
    sources, gains, rest = refs[:count], refs[count], refs[count + 1 :]
    targets, gain_targets, rest = rest[: count + 2], rest[count + 2 : count + 6], rest[count + 6 :]
    held, in_sem, out_sem = rest[:count], rest[count], rest[count + 1]
    loads = [
        pltpu.make_async_copy(source, hold, in_sem.at[index])
        for index, (source, hold) in enumerate(zip(sources, held))
    ]
    for load in loads:
        load.start()
    stores, row = [], 0
    for index, load in enumerate(loads):
        load.wait()
        if index < count - 1:
            pieces = [(held[index], targets[index])]
        else:
            pieces = []
            for target in targets[index:]:
                pieces.append((held[index].at[pl.ds(row, target.shape[0])], target))
                row += target.shape[0]
        for piece, target in pieces:
            store = pltpu.make_async_copy(piece, target, out_sem.at[len(stores)])
            store.start()
            stores.append(store)
    for index, target in enumerate(gain_targets):
        target[...] = gains[index : index + 1, 0 : target.shape[1]]
    for store in stores:
        store.wait()


def settle_call(output, tokens, gate_t, up_t, down_t, out_t, qkv_t, gains):
    sources = (output, tokens, gate_t, up_t, down_t, out_t, qkv_t)
    lanes = qkv_t.shape[1]
    query = HEADS * HEAD_DIM // RING
    pair = KV_HEADS * HEAD_DIM // RING
    shapes = [source.shape for source in sources[:-1]]
    shapes += [(query, lanes), (pair, lanes), (pair, lanes)]
    gain_shapes = [(1, gains.shape[1])] * 2 + [(1, HEAD_DIM)] * 2
    return pl.pallas_call(
        settle_kernel,
        out_shape=(jax.ShapeDtypeStruct(output.shape, output.dtype),)
        + tuple(jax.ShapeDtypeStruct(shape, F32) for shape in shapes[1:] + gain_shapes),
        in_specs=[HBM_SPEC] * len(sources) + [VMEM_SPEC],
        out_specs=(HBM_SPEC,) * len(shapes) + (VMEM_SPEC,) * 4,
        scratch_shapes=[pltpu.VMEM(source.shape, source.dtype) for source in sources]
        + [pltpu.SemaphoreType.DMA((7,)), pltpu.SemaphoreType.DMA((9,))],
        compiler_params=pltpu.CompilerParams(vmem_limit_bytes=63 << 20),
        name="settle_results",
    )(*sources, gains)


def heads_body(
    tokens,
    seg_ids,
    doc_pos,
    attn_gain,
    w_query,
    w_key,
    w_value,
    query_gain,
    key_gain,
    w_out,
    ffn_gain,
    w_gate,
    w_up,
    w_down,
    d_output,
):
    rows = tokens.shape[1]
    (
        qkv,
        starts,
        normed_low,
        mixed_far,
        mixed_home,
        inverse_total,
        o_full,
        table,
        query_raw,
        key_raw,
        kvq_full,
        gate_far,
        up_far,
        down_far,
    ) = front_call(
        1,
        (
            attn_gain[None, :],
            doc_pos,
            query_gain[None, :],
            key_gain[None, :],
            head_frequencies(rows),
        ),
        (tokens[0], w_query, w_key, w_value, w_out, w_gate, w_up, w_down),
    )
    mixed_t = mixed_home.reshape(HEADS * HEAD_DIM, rows)
    cot_low = d_output[0]
    (
        pair,
        hidden_low,
        output,
        ffn_low,
        side,
        grad_mixed,
        grad_middle,
        ffn_terms,
        swapped,
        ffn_near,
    ) = ffn_call(
        2,
        tokens[0],
        mixed_t,
        o_full,
        ffn_gain[None, :],
        cot_low,
        (w_gate, gate_far),
        (w_up, up_far),
        (w_down, down_far),
    )
    gate_t, up_t, down_t, out_t, qkv_grads, d_tokens, gain_totals = back_call(
        3,
        (
            pair,
            hidden_low,
            side,
            ffn_low,
            mixed_t,
            grad_mixed.reshape(HALF, 2 * HEAD_DIM, rows),
            qkv,
            starts,
            mixed_far,
            inverse_total,
            table,
            normed_low,
            attn_gain[None, :],
            ffn_terms,
        ),
        (tokens[0], query_raw, key_raw, kvq_full, grad_middle, swapped, ffn_near),
    )
    output, d_tokens, gate, up, down, out, query, key, value, attn, ffn, query_gains, key_gains = (
        settle_call(output, d_tokens, gate_t, up_t, down_t, out_t, qkv_grads, gain_totals)
    )
    return (
        output[None],
        d_tokens[None],
        attn[0],
        query.T,
        key.T,
        value.T,
        query_gains[0],
        key_gains[0],
        out.T,
        ffn[0],
        gate.T,
        up.T,
        down.T,
    )


def solution(mesh):
    in_specs = (
        P("fsdp", "ctx", None),
        P("fsdp", "ctx"),
        P("fsdp", "ctx"),
        P(),
        P("fsdp", None),
        P("fsdp", None),
        P("fsdp", None),
        P(),
        P(),
        P("fsdp", None),
        P(),
        P("fsdp", None),
        P("fsdp", None),
        P("fsdp", None),
        P("fsdp", "ctx", None),
    )
    out_specs = (
        P("fsdp", "ctx", None),
        P("fsdp", "ctx", None),
        P(),
        P("fsdp", "ctx"),
        P("fsdp", "ctx"),
        P("fsdp", "ctx"),
        P(),
        P(),
        P("fsdp", "ctx"),
        P(),
        P("fsdp", "ctx"),
        P("fsdp", "ctx"),
        P("fsdp", "ctx"),
    )
    chosen = heads_body if (mesh.shape["ctx"], mesh.shape["fsdp"]) == (HEADS, 2) else ring_body
    return jax.shard_map(chosen, mesh=mesh, in_specs=in_specs, out_specs=out_specs, check_vma=False)
```
